32 devices in a mesh: rep: 4 (over y, x), fsdp: 8 (over z, core).
Axes of the slice: x: 2, y: 2, z: 4, core: 2. Of those that a mesh axis runs over, the one named last changes fastest.
Arguments:
- tokens: bfloat16 [4, 4096, 1024], P('rep', 'fsdp'), may hold values from -6 to 6
- image_ids: int32 [4, 4096], P('rep', 'fsdp'), may hold values from 0 to 4, never falling along the last dimension, each value on 1 to 1024 neighbouring positions
- ln1_gain: bfloat16 [1024], P('fsdp'), may hold values from 0.099609375 to 1.8984375
- ln1_bias: bfloat16 [1024], P('fsdp'), may hold values from -3 to 3
- qkv_weight: bfloat16 [1024, 3072], P('fsdp'), may hold values from -0.1875 to 0.1875
- query_bias: bfloat16 [1024], P('fsdp'), may hold values from -3 to 3
- value_bias: bfloat16 [1024], P('fsdp'), may hold values from -3 to 3
- proj_weight: bfloat16 [1024, 1024], P('fsdp'), may hold values from -1.5 to 1.5
- proj_bias: bfloat16 [1024], P('fsdp'), may hold values from -3 to 3
- scale_attn: bfloat16 [1024], P('fsdp'), may hold values from 0.5 to 1.5
- ln2_gain: bfloat16 [1024], P('fsdp'), may hold values from 0.099609375 to 1.8984375
- ln2_bias: bfloat16 [1024], P('fsdp'), may hold values from -3 to 3
- fc1_weight: bfloat16 [1024, 4096], P('fsdp'), may hold values from -0.1875 to 0.1875
- fc1_bias: bfloat16 [4096], P('fsdp'), may hold values from -3 to 3
- fc2_weight: bfloat16 [4096, 1024], P('fsdp'), may hold values from -0.09375 to 0.09375
- fc2_bias: bfloat16 [1024], P('fsdp'), may hold values from -3 to 3
- scale_mlp: bfloat16 [1024], P('fsdp'), may hold values from 0.5 to 1.5
- cotangent: bfloat16 [4, 4096, 1024], P('rep', 'fsdp'), may hold values from -6 to 6
Outputs:
- output: bfloat16 [4, 4096, 1024], P('rep', 'fsdp')
- input_grad: float32 [4, 4096, 1024], P('rep', 'fsdp')
- grad_ln1_gain: float32 [1024], P('fsdp')
- grad_ln1_bias: float32 [1024], P('fsdp')
- grad_qkv_weight: float32 [1024, 3072], P('fsdp')
- grad_query_bias: float32 [1024], P('fsdp')
- grad_value_bias: float32 [1024], P('fsdp')
- grad_proj_weight: float32 [1024, 1024], P('fsdp')
- grad_proj_bias: float32 [1024], P('fsdp')
- grad_scale_attn: float32 [1024], P('fsdp')
- grad_ln2_gain: float32 [1024], P('fsdp')
- grad_ln2_bias: float32 [1024], P('fsdp')
- grad_fc1_weight: float32 [1024, 4096], P('fsdp')
- grad_fc1_bias: float32 [4096], P('fsdp')
- grad_fc2_weight: float32 [4096, 1024], P('fsdp')
- grad_fc2_bias: float32 [1024], P('fsdp')
- grad_scale_mlp: float32 [1024], P('fsdp')
The draws below stay inside these ranges and needn't reach their ends.
Inputs may be any that keep to these rules, and one draw needn't show every extreme that they name: `image_ids`: within each replica group the image numbers never fall along the tokens, every number from 0 up is used, and each image holds 1 to 1024 tokens, one of them exactly 1024.
All inputs are finite; a program needn't handle non-finite values.
Results may differ from the reference program's by a relative error of at most 0.012.
The reference program's roundings to bfloat16 on the way count: a program that leaves them out, or rounds other values in their place, can miss the bound.
Values may be sent and summed in bfloat16 or wider, within the bound.
No kernel may reach another device: no remote copies, remote signals or barrier semaphores. Data moves between devices by JAX's collectives and lax.ppermute only.
A program may use at most 256 MiB of HBM per device.

```python
import math
import jax
import jax.numpy as jnp
import numpy as np
from jax import lax

D = 1024
HEADS = 16
HEAD_DIM = 64
FF = 4096
GROUP_TOK = 4096
TOKENS = 16384
IMAGES = 5
MOST_IMG = 1024
N_REP = 4


def block_scale(stream_key, extent, cuts, smallest, top_value):
    def one(dim, shards_of):
        draws = jax.random.uniform(jax.random.fold_in(jax.random.fold_in(stream_key, 6), dim), (shards_of,), jnp.float32, smallest / len(cuts), top_value / len(cuts))
        return jnp.repeat(jnp.exp(draws), extent[dim] // shards_of).reshape((-1,) + (1,) * (len(extent) - dim - 1))

    level = one(*cuts[0])
    for cut in cuts[1:]:
        level = level * one(*cut)
    return level


def length_profile(amount, total, bound, skew):
    portions = [(1 << 20) // math.isqrt(grade ** skew) + 1 for grade in range(2, amount + 1)]
    surplus, given = total - bound - (amount - 1), [1] * (amount - 1)
    while surplus > 0:
        candidates = [i for i in range(amount - 1) if given[i] < bound]
        pool, left = sum([portions[i] for i in candidates]), surplus
        for i in candidates:
            more = min(bound - given[i], max(1, left * portions[i] // pool), surplus)
            given[i] = given[i] + more
            surplus = surplus - more
    return np.array([bound] + given)


def ragged_sizes(own_key, count, total, limit, lean):
    if count == 2:
        one = jax.random.randint(own_key, (), max(1, total - limit), min(limit, total - 1) + 1)
        return jnp.stack([one, total - one])
    tallies = jnp.asarray(length_profile(count, total, limit, lean), jnp.int32)
    pairs = (count - 1) // 2
    donor, sink = tallies[1:1 + 2 * pairs:2], tallies[2:2 + 2 * pairs:2]
    slack = jnp.minimum(donor - 1, limit - sink)
    shifted = jax.random.randint(jax.random.fold_in(own_key, 1), (pairs,), 0, 1 << 20) % (slack + 1)
    tallies = tallies.at[1:1 + 2 * pairs:2].set(donor - shifted).at[2:2 + 2 * pairs:2].set(sink + shifted)
    return tallies[jax.random.permutation(jax.random.fold_in(own_key, 2), count)]


def normal_values(rng, dims, width, limit, pieces=(), dtype=jnp.bfloat16):
    gain = block_scale(rng, dims, pieces, -0.22, 0.18) if pieces else 1.0
    entries = jax.random.normal(rng, dims, jnp.float32) * width * gain
    return jnp.minimum(jnp.maximum(entries, -limit), limit).astype(dtype)


def setup_inputs(seed: int = 0) -> dict:
    seeds = jax.random.split(jax.random.key(seed), 19)
    return {
        "tokens": normal_values(seeds[0], (N_REP, GROUP_TOK, D), 1.0, 6.0, ((0, 4), (1, 8))),
        "image_ids": jax.vmap(lambda own: jnp.searchsorted(jnp.cumsum(ragged_sizes(own, IMAGES, GROUP_TOK, MOST_IMG, 2)), jnp.arange(GROUP_TOK), side="right"))(jax.random.split(seeds[1], N_REP)).reshape((N_REP, GROUP_TOK)).astype(jnp.int32),
        "ln1_gain": jnp.clip(1.0 + 0.18 * jax.random.normal(seeds[2], (D,), jnp.float32), 0.099609375, 1.8984375).astype(jnp.bfloat16),
        "ln1_bias": normal_values(seeds[3], (D,), 0.5, 3.0, ((0, 8),)),
        "qkv_weight": normal_values(seeds[4], (D, 3 * D), D ** -0.5, 0.1875, ((0, 8),)),
        "query_bias": normal_values(seeds[5], (D,), 0.5, 3.0, ((0, 8),)),
        "value_bias": normal_values(seeds[6], (D,), 0.5, 3.0, ((0, 8),)),
        "proj_weight": normal_values(seeds[7], (D, D), 16 ** -0.5, 1.5, ((0, 8),)),
        "proj_bias": normal_values(seeds[8], (D,), 0.5, 3.0, ((0, 8),)),
        "scale_attn": jnp.clip(0.5 + 1.0 * jax.random.uniform(seeds[9], (D,), jnp.float32) ** block_scale(seeds[9], (D,), ((0, 8),), -0.2, 0.2), 0.5, 1.5).astype(jnp.bfloat16),
        "ln2_gain": jnp.clip(1.0 + 0.18 * jax.random.normal(seeds[10], (D,), jnp.float32), 0.099609375, 1.8984375).astype(jnp.bfloat16),
        "ln2_bias": normal_values(seeds[11], (D,), 0.5, 3.0, ((0, 8),)),
        "fc1_weight": normal_values(seeds[12], (D, FF), D ** -0.5, 0.1875, ((0, 8),)),
        "fc1_bias": normal_values(seeds[13], (FF,), 0.5, 3.0, ((0, 8),)),
        "fc2_weight": normal_values(seeds[14], (FF, D), FF ** -0.5, 0.09375, ((0, 8),)),
        "fc2_bias": normal_values(seeds[15], (D,), 0.5, 3.0, ((0, 8),)),
        "scale_mlp": jnp.clip(0.5 + 1.0 * jax.random.uniform(seeds[16], (D,), jnp.float32) ** block_scale(seeds[16], (D,), ((0, 8),), -0.2, 0.2), 0.5, 1.5).astype(jnp.bfloat16),
        "cotangent": normal_values(seeds[17], (N_REP, GROUP_TOK, D), 1.0, 6.0, ((0, 4), (1, 8))),
    }


EPSILON = 1e-06
MASKED = -1e+30

def layer_norm(features, gain_vec, bias_vec):
    row_mean = lax.optimization_barrier(jnp.mean(features, axis=-1, keepdims=True))
    centred = features - row_mean
    variance = lax.optimization_barrier(jnp.mean(centred * centred, axis=-1, keepdims=True))
    inverse = lax.rsqrt(variance + EPSILON)
    normal = centred * inverse
    return (normal * gain_vec + bias_vec, normal, inverse)

def norm_back(gradient, normal, inverse, gain_vec):
    scaled = gradient * gain_vec
    mean_first = lax.optimization_barrier(jnp.mean(scaled, axis=-1, keepdims=True))
    mean_second = lax.optimization_barrier(jnp.mean(scaled * normal, axis=-1, keepdims=True))
    return inverse * (scaled - mean_first - normal * mean_second)

def gelu_pair(values):
    cumulative = 0.5 * (1.0 + lax.erf(values * 2.0 ** (-0.5)))
    density = jnp.exp(-0.5 * values * values) * (2.0 * math.pi) ** (-0.5)
    return (values * cumulative, cumulative + values * density)

def heads_of(matrix):
    return matrix.reshape(matrix.shape[0], HEADS, HEAD_DIM).astype(jnp.float32)

def window_scores(query_block, key_block, query_tag, key_tag):
    scores = jnp.einsum('qhd,khd->hqk', query_block, key_block) * HEAD_DIM ** (-0.5)
    same_image = query_tag[:, None] == key_tag[None, :]
    return jnp.where(same_image[None], scores, MASKED)

def attend(queries, key_rows, value_rows, image_tag, block_rows, reach_rows):
    group_rows = queries.shape[0]
    padded_keys = jnp.pad(key_rows, ((reach_rows, reach_rows), (0, 0)))
    padded_values = jnp.pad(value_rows, ((reach_rows, reach_rows), (0, 0)))
    padded_tag = jnp.pad(image_tag, (reach_rows, reach_rows))
    window = block_rows + 2 * reach_rows
    offsets = (jnp.arange(group_rows // block_rows) * block_rows).astype(jnp.int32)

    def one_block(offset):
        query_block = heads_of(lax.dynamic_slice_in_dim(queries, offset, block_rows, 0))
        key_block = heads_of(lax.dynamic_slice_in_dim(padded_keys, offset, window, 0))
        value_block = heads_of(lax.dynamic_slice_in_dim(padded_values, offset, window, 0))
        scores = window_scores(query_block, key_block, lax.dynamic_slice_in_dim(image_tag, offset, block_rows, 0), lax.dynamic_slice_in_dim(padded_tag, offset, window, 0))
        row_max = lax.optimization_barrier(jnp.max(scores, axis=-1, keepdims=True))
        row_sum = lax.optimization_barrier(jnp.sum(jnp.exp(scores - row_max), axis=-1, keepdims=True))
        log_total = row_max + jnp.log(row_sum)
        attn_probs = lax.optimization_barrier(jnp.exp(scores - log_total).astype(jnp.bfloat16)).astype(jnp.float32)
        context = jnp.einsum('hqk,khd->qhd', attn_probs, value_block)
        return (context.reshape(block_rows, D).astype(jnp.bfloat16), log_total[..., 0])
    context, log_total = lax.map(one_block, offsets)
    return (context.reshape(group_rows, D), log_total)

def attend_back(queries, key_rows, value_rows, image_tag, context, context_grad, log_total, block_rows, reach_rows):
    group_rows = queries.shape[0]
    padded_keys = jnp.pad(key_rows, ((reach_rows, reach_rows), (0, 0)))
    padded_values = jnp.pad(value_rows, ((reach_rows, reach_rows), (0, 0)))
    padded_tag = jnp.pad(image_tag, (reach_rows, reach_rows))
    window = block_rows + 2 * reach_rows
    offsets = (jnp.arange(group_rows // block_rows) * block_rows).astype(jnp.int32)
    row_delta = lax.optimization_barrier(jnp.sum((context_grad.astype(jnp.float32) * context.astype(jnp.float32)).reshape(group_rows, HEADS, HEAD_DIM), axis=-1))
    empty = jnp.zeros((group_rows + 2 * reach_rows, D), jnp.float32)

    def one_block(running, inputs):
        offset, block_total = inputs
        key_grad, value_grad = running
        query_block = heads_of(lax.dynamic_slice_in_dim(queries, offset, block_rows, 0))
        key_block = heads_of(lax.dynamic_slice_in_dim(padded_keys, offset, window, 0))
        value_block = heads_of(lax.dynamic_slice_in_dim(padded_values, offset, window, 0))
        back_block = heads_of(lax.dynamic_slice_in_dim(context_grad, offset, block_rows, 0))
        delta_block = lax.dynamic_slice_in_dim(row_delta, offset, block_rows, 0).T
        scores = window_scores(query_block, key_block, lax.dynamic_slice_in_dim(image_tag, offset, block_rows, 0), lax.dynamic_slice_in_dim(padded_tag, offset, window, 0))
        exact_probs = jnp.exp(scores - block_total[..., None])
        rounded_probs = lax.optimization_barrier(exact_probs.astype(jnp.bfloat16)).astype(jnp.float32)
        prob_grad = jnp.einsum('qhd,khd->hqk', back_block, value_block)
        score_grad = (exact_probs * (prob_grad - delta_block[..., None]) * HEAD_DIM ** (-0.5)).astype(jnp.bfloat16)
        score_grad = lax.optimization_barrier(score_grad).astype(jnp.float32)
        query_part = jnp.einsum('hqk,khd->qhd', score_grad, key_block).reshape(block_rows, D)
        key_part = jnp.einsum('hqk,qhd->khd', score_grad, query_block).reshape(window, D)
        value_part = jnp.einsum('hqk,qhd->khd', rounded_probs, back_block).reshape(window, D)
        key_grad = lax.dynamic_update_slice_in_dim(key_grad, lax.dynamic_slice_in_dim(key_grad, offset, window, 0) + key_part, offset, 0)
        value_grad = lax.dynamic_update_slice_in_dim(value_grad, lax.dynamic_slice_in_dim(value_grad, offset, window, 0) + value_part, offset, 0)
        return ((key_grad, value_grad), query_part)
    (key_grad, value_grad), query_grad = lax.scan(one_block, (empty, empty), (offsets, log_total))
    return (query_grad.reshape(group_rows, D), key_grad[reach_rows:reach_rows + group_rows], value_grad[reach_rows:reach_rows + group_rows])

def reference(tokens, image_ids, ln1_gain, ln1_bias, qkv_weight, query_bias, value_bias, proj_weight, proj_bias, scale_attn, ln2_gain, ln2_bias, fc1_weight, fc1_bias, fc2_weight, fc2_bias, scale_mlp, cotangent):
    attn_gain = ln1_gain.astype(jnp.float32)
    attn_shift = ln1_bias.astype(jnp.float32)
    query_shift = query_bias.astype(jnp.float32)
    value_shift = value_bias.astype(jnp.float32)
    proj_shift = proj_bias.astype(jnp.float32)
    attn_scale = scale_attn.astype(jnp.float32)
    mlp_gain = ln2_gain.astype(jnp.float32)
    mlp_shift = ln2_bias.astype(jnp.float32)
    fc1_shift = fc1_bias.astype(jnp.float32)
    fc2_shift = fc2_bias.astype(jnp.float32)
    mlp_scale = scale_mlp.astype(jnp.float32)
    block_rows = math.gcd(GROUP_TOK, 512)
    reach_rows = MOST_IMG

    def group_step(running, inputs):
        token_rows, id_rows, cot_rows = inputs
        image_tag = id_rows + 1
        features = token_rows.astype(jnp.float32)
        attn_input, attn_normal, attn_inverse = layer_norm(features, attn_gain, attn_shift)
        attn_input = attn_input.astype(jnp.bfloat16)
        qkv_full = jnp.dot(attn_input, qkv_weight, preferred_element_type=jnp.float32)
        queries = (qkv_full[:, :D] + query_shift).astype(jnp.bfloat16)
        key_rows = qkv_full[:, D:2 * D].astype(jnp.bfloat16)
        value_rows = (qkv_full[:, 2 * D:] + value_shift).astype(jnp.bfloat16)
        context, log_total = attend(queries, key_rows, value_rows, image_tag, block_rows, reach_rows)
        attn_out = jnp.dot(context, proj_weight, preferred_element_type=jnp.float32) + proj_shift
        resid = features + attn_scale * attn_out
        mlp_input, mlp_normal, mlp_inverse = layer_norm(resid, mlp_gain, mlp_shift)
        mlp_input = mlp_input.astype(jnp.bfloat16)
        pre_act = jnp.dot(mlp_input, fc1_weight, preferred_element_type=jnp.float32) + fc1_shift
        activated, slope = gelu_pair(pre_act)
        activated = activated.astype(jnp.bfloat16)
        mlp_out = jnp.dot(activated, fc2_weight, preferred_element_type=jnp.float32) + fc2_shift
        output_rows = (resid + mlp_scale * mlp_out).astype(jnp.bfloat16)
        out_grad = cot_rows.astype(jnp.float32)
        mlp_grad_full = out_grad * mlp_scale
        mlp_grad = mlp_grad_full.astype(jnp.bfloat16)
        pre_grad_full = jnp.dot(mlp_grad, fc2_weight.T, preferred_element_type=jnp.float32) * slope
        pre_grad = pre_grad_full.astype(jnp.bfloat16)
        mlp_in_grad = jnp.dot(pre_grad, fc1_weight.T, preferred_element_type=jnp.float32)
        resid_grad = out_grad + norm_back(mlp_in_grad, mlp_normal, mlp_inverse, mlp_gain)
        attn_grad_full = resid_grad * attn_scale
        attn_grad = attn_grad_full.astype(jnp.bfloat16)
        context_grad = jnp.dot(attn_grad, proj_weight.T, preferred_element_type=jnp.float32).astype(jnp.bfloat16)
        query_grad, key_grad, value_grad = attend_back(queries, key_rows, value_rows, image_tag, context, context_grad, log_total, block_rows, reach_rows)
        qkv_grad = jnp.concatenate([query_grad, key_grad, value_grad], axis=1).astype(jnp.bfloat16)
        attn_in_grad = jnp.dot(qkv_grad, qkv_weight.T, preferred_element_type=jnp.float32)
        input_rows = resid_grad + norm_back(attn_in_grad, attn_normal, attn_inverse, attn_gain)
        grads = (lax.optimization_barrier(jnp.sum(attn_in_grad * attn_normal, axis=0)), lax.optimization_barrier(jnp.sum(attn_in_grad, axis=0)), jnp.dot(attn_input.T, qkv_grad, preferred_element_type=jnp.float32), lax.optimization_barrier(jnp.sum(query_grad, axis=0)), lax.optimization_barrier(jnp.sum(value_grad, axis=0)), jnp.dot(context.T, attn_grad, preferred_element_type=jnp.float32), lax.optimization_barrier(jnp.sum(attn_grad_full, axis=0)), lax.optimization_barrier(jnp.sum(resid_grad * attn_out, axis=0)), lax.optimization_barrier(jnp.sum(mlp_in_grad * mlp_normal, axis=0)), lax.optimization_barrier(jnp.sum(mlp_in_grad, axis=0)), jnp.dot(mlp_input.T, pre_grad, preferred_element_type=jnp.float32), lax.optimization_barrier(jnp.sum(pre_grad_full, axis=0)), jnp.dot(activated.T, mlp_grad, preferred_element_type=jnp.float32), lax.optimization_barrier(jnp.sum(mlp_grad_full, axis=0)), lax.optimization_barrier(jnp.sum(out_grad * mlp_out, axis=0)))
        running = tuple((total + part for total, part in zip(running, grads)))
        return (running, (output_rows, input_rows))
    params = (ln1_gain, ln1_bias, qkv_weight, query_bias, value_bias, proj_weight, proj_bias, scale_attn, ln2_gain, ln2_bias, fc1_weight, fc1_bias, fc2_weight, fc2_bias, scale_mlp)
    initial = tuple((jnp.zeros(param.shape, jnp.float32) for param in params))
    totals, (outputs, input_grads) = lax.scan(group_step, initial, (tokens, image_ids, cotangent))
    factor = 1.0 / math.sqrt(TOKENS)
    return (outputs, input_grads, totals[0] * factor, totals[1] * factor, totals[2] * factor, totals[3] * factor, totals[4] * factor, totals[5] * factor, totals[6] * factor, totals[7] * factor, totals[8] * factor, totals[9] * factor, totals[10] * factor, totals[11] * factor, totals[12] * factor, totals[13] * factor, totals[14] * factor)
```

```python
import functools
import math

import jax
import jax.numpy as jnp
from jax import lax
from jax.experimental import pallas as pl
from jax.experimental.pallas import tpu as pltpu
from jax.sharding import PartitionSpec as P

D = 1024
HEADS = 16
HEAD_DIM = 64
LANES = 128

EPSILON = 1e-06
MASKED = -1e30
BLOCK = 256

f32 = jnp.float32
bf16 = jnp.bfloat16


def normalize(features):
    row_mean = jnp.mean(features, axis=-1, keepdims=True)
    centred = features - row_mean
    variance = jnp.mean(centred * centred, axis=-1, keepdims=True)
    inverse = lax.rsqrt(variance + EPSILON)
    return centred * inverse, inverse


def norm_back(gradient, normal, inverse, gain_vec):
    scaled = gradient * gain_vec
    mean_first = jnp.mean(scaled, axis=-1, keepdims=True)
    mean_second = jnp.mean(scaled * normal, axis=-1, keepdims=True)
    return inverse * (scaled - mean_first - normal * mean_second)


def gelu_pair(values):
    cumulative = 0.5 * (1.0 + lax.erf(values * 2.0 ** (-0.5)))
    density = jnp.exp(-0.5 * values * values) * (2.0 * math.pi) ** (-0.5)
    return (values * cumulative, cumulative + values * density)


def dot(a, b):
    return jnp.dot(a, b, preferred_element_type=f32)


def dot_nt(a, b):
    return lax.dot_general(a, b, (((1,), (1,)), ((), ())), preferred_element_type=f32)


def dot_tn(a, b):
    return lax.dot_general(a, b, (((0,), (0,)), ((), ())), preferred_element_type=f32)


def swap_cores(value):
    size = lax.axis_size("fsdp")
    return lax.ppermute(value, "fsdp", [(i, i ^ 1) for i in range(size)])


def along_z(value, by):
    size = lax.axis_size("fsdp")
    return lax.ppermute(value, "fsdp", [(i, (i + 2 * by) % size) for i in range(size)])


def from_chip(value, by):
    size = lax.axis_size("fsdp")
    pairs = [(i, i + 2 * by) for i in range(size) if 0 <= i + 2 * by < size]
    return lax.ppermute(value, "fsdp", pairs)


def across_rep(value, bit):
    size = lax.axis_size("rep")
    return lax.ppermute(value, "rep", [(i, i ^ (1 << bit)) for i in range(size)])


def pick(value, index, axis):
    return lax.dynamic_index_in_dim(value, index, axis, keepdims=False)


def rep_bits():
    return lax.axis_size("rep").bit_length() - 1


def spread_over_rep(value, order):
    stacked, offsets = value[None], [0]
    for step, bit in enumerate(order):
        received = across_rep(stacked, bit)
        further = [o ^ (1 << bit) for o in offsets]
        if step + 1 < len(order):
            stacked, offsets = jnp.concatenate([stacked, received]), offsets + further
        else:
            return [(stacked, offsets), (received, further)]
    return [(stacked, offsets)]


def assemble_kernel(plan, index_ref, *refs):
    count = len(plan)
    sources, target, held, in_sems, out_sems = refs[:count], refs[count], refs[count + 1], refs[count + 2], refs[count + 3]
    here, rank = index_ref[0], index_ref[1]
    depth = target.shape[0]
    half = target.shape[2] // 2
    rows = target.shape[2]
    width = sources[0].shape[-1]
    waits = [[] for _ in range(depth)]
    number = 0
    for which, (colour, offsets) in enumerate(plan):
        lo = colour * half
        for m, offset in enumerate(offsets):
            for k in range(depth):
                place = lax.rem(here - k + depth, depth)
                copy = pltpu.make_async_copy(
                    sources[which].at[m, k],
                    held.at[place, rank ^ offset, pl.ds(lo, half)],
                    in_sems.at[number],
                )
                copy.start()
                waits[k].append(copy)
                number += 1
    outs = []
    ranks = target.shape[1]
    for k in range(depth):
        place = lax.rem(here - k + depth, depth)
        for copy in waits[k]:
            copy.wait()
        for i in range(ranks):
            out = pltpu.make_async_copy(held.at[place, i], target.at[place, i], out_sems.at[k, i])
            out.start()
            outs.append(out)
    for out in outs:
        out.wait()


def gather_group(own, here, rank):
    depth, ranks = lax.axis_size("fsdp") // 2, lax.axis_size("rep")
    pieces = [own] + [along_z(own, k) for k in range(1, depth)]
    rows, cols = own.shape
    half = rows // 2
    order = list(range(rep_bits()))
    upper = spread_over_rep(jnp.stack([p[:half] for p in pieces]), order)
    lower = spread_over_rep(jnp.stack([p[half:] for p in pieces]), order[::-1])
    sources, plan = [], []
    for colour, parts in enumerate((upper, lower)):
        for array, offsets in parts:
            sources.append(array)
            plan.append((colour, offsets))
    total = 2 * ranks * depth
    return pl.pallas_call(
        functools.partial(assemble_kernel, plan),
        out_shape=jax.ShapeDtypeStruct((depth, ranks, rows, cols), own.dtype),
        grid_spec=pltpu.PrefetchScalarGridSpec(
            num_scalar_prefetch=1,
            grid=(1,),
            in_specs=[pl.BlockSpec(memory_space=pl.ANY)] * len(sources),
            out_specs=pl.BlockSpec(memory_space=pl.ANY),
            scratch_shapes=[
                pltpu.VMEM((depth, ranks, rows, cols), own.dtype),
                pltpu.SemaphoreType.DMA((total,)),
                pltpu.SemaphoreType.DMA((depth, ranks)),
            ],
        ),
        compiler_params=pltpu.CompilerParams(vmem_limit_bytes=16 << 20),
        cost_estimate=pl.CostEstimate(
            flops=0, transcendentals=0, bytes_accessed=2 * depth * ranks * rows * cols * own.dtype.itemsize
        ),
        name="assemble",
    )(jnp.stack([here, rank]).astype(jnp.int32), *sources)


def merge_columns(gathered):
    depth, ranks, rows, cols = gathered.shape
    return jnp.concatenate(
        [gathered[:, i].reshape(depth * rows, cols) for i in range(ranks)], axis=1
    )


def reduce_group(grads, here, rank, orders):
    depth, ranks = lax.axis_size("fsdp") // 2, lax.axis_size("rep")
    width = grads.shape[1] // ranks
    rows = grads.shape[0] // depth
    shaped = grads.reshape(depth, rows, grads.shape[1])
    share = rows // len(orders)
    reduced = []
    for colour, order in enumerate(orders):
        block = lambda o: lax.dynamic_slice(
            shaped, (0, colour * share, (rank ^ o) * width), (depth, share, width)
        )
        held = {o: block(o) for o in range(ranks)}
        for bit in order:
            flip = 1 << bit
            kept = [o for o in held if not o & flip]
            received = across_rep(jnp.stack([held[o ^ flip] for o in kept]), bit)
            held = {
                o: (held[o].astype(f32) + received[i].astype(f32)).astype(bf16)
                for i, o in enumerate(kept)
            }
        reduced.append(held[0])
    reduced = reduced[0] if len(reduced) == 1 else jnp.concatenate(reduced, axis=1)
    total = pick(reduced, here, 0).astype(f32)
    for k in range(1, depth):
        sent = pick(reduced, lax.rem(here + k, depth), 0)
        total = total + along_z(sent, k).astype(f32)
    return total


def share_over_rep(mine, rank):
    stacked = mine[None]
    offsets = [0]
    for bit in range(rep_bits()):
        received = across_rep(stacked, bit)
        stacked = jnp.concatenate([stacked, received])
        offsets = offsets + [o ^ (1 << bit) for o in offsets]
    blocks = [pick(stacked, rank ^ i, 0) for i in range(lax.axis_size("rep"))]
    return jnp.concatenate(blocks, axis=1)


def spread_lanes(tags, width):
    return jnp.concatenate([tags] * (width // LANES), axis=1)


def project_kernel(need_ref, n_ref, w_ref, b_ref, q_ref, k_ref, v_ref):
    row = pl.program_id(0)
    wide = q_ref.shape[1]

    @pl.when(need_ref[row] > 0)
    def _():
        n = n_ref[...]
        for i, ref in enumerate((q_ref, k_ref, v_ref)):
            out = dot(n, w_ref[:, i * wide : (i + 1) * wide]) + b_ref[0:1, i * wide : (i + 1) * wide]
            if i == 0:
                out = out.astype(bf16).astype(f32) * HEAD_DIM ** (-0.5)
            ref[...] = out.astype(bf16)

    @pl.when(need_ref[row] == 0)
    def _():
        for ref in (q_ref, k_ref, v_ref):
            ref[...] = jnp.zeros_like(ref)


def project(need, normed, weight, bias, wide):
    rows = normed.shape[0]
    return pl.pallas_call(
        project_kernel,
        out_shape=[jax.ShapeDtypeStruct((rows, wide), bf16)] * 3,
        grid_spec=pltpu.PrefetchScalarGridSpec(
            num_scalar_prefetch=1,
            grid=(rows // BLOCK,),
            in_specs=[
                pl.BlockSpec((BLOCK, D), lambda i, s: (i, 0)),
                pl.BlockSpec(weight.shape, lambda i, s: (0, 0)),
                pl.BlockSpec((8, 3 * wide), lambda i, s: (0, 0)),
            ],
            out_specs=[pl.BlockSpec((BLOCK, wide), lambda i, s: (i, 0))] * 3,
        ),
        compiler_params=pltpu.CompilerParams(vmem_limit_bytes=32 << 20),
        cost_estimate=pl.CostEstimate(
            flops=2 * rows * D * 3 * wide, transcendentals=0, bytes_accessed=rows * D * 6
        ),
        name="project",
    )(need, normed, weight, bias)


def attend_kernel(lo_ref, hi_ref, q_ref, k_ref, v_ref, qt_ref, kt_ref, o_ref, lse_ref):
    i = pl.program_id(1)
    first = lax.broadcasted_iota(jnp.int32, (1, LANES), 1) < HEAD_DIM
    q = q_ref[...]
    zero = jnp.zeros_like(q)
    heads = (jnp.where(first, q, zero), jnp.where(first, zero, q))
    q_tags = spread_lanes(qt_ref[...], BLOCK)

    def step(j, carry):
        at = pl.multiple_of(j * BLOCK, BLOCK)
        k = k_ref[pl.ds(at, BLOCK), :]
        v = v_ref[pl.ds(at, BLOCK), :]
        same = q_tags == kt_ref[:, pl.ds(at, BLOCK)]
        acc = carry[4]
        stats, scales, parts = [], [], []
        for h in range(2):
            old_max, old_sum = carry[2 * h], carry[2 * h + 1]
            s = jnp.where(same, dot_nt(heads[h], k), MASKED)
            new_max = jnp.maximum(old_max, jnp.max(s, axis=1, keepdims=True))
            scale = jnp.exp(old_max - new_max)
            p = jnp.exp(s - new_max)
            stats += [new_max, old_sum * scale + jnp.sum(p, axis=1, keepdims=True)]
            vz = jnp.zeros_like(v)
            vh = jnp.where(first, v, vz) if h == 0 else jnp.where(first, vz, v)
            parts.append(dot(p.astype(bf16), vh))
            scales.append(scale)
        acc = acc * jnp.where(first, scales[0], scales[1]) + parts[0] + parts[1]
        return (*stats, acc)

    low = jnp.full((BLOCK, 1), MASKED, f32)
    none = jnp.zeros((BLOCK, 1), f32)
    ma, la, mb, lb, acc = lax.fori_loop(
        lo_ref[i], hi_ref[i], step, (low, none, low, none, jnp.zeros((BLOCK, LANES), f32))
    )
    o_ref[...] = (acc / jnp.where(first, la, lb)).astype(bf16)
    lse_ref[0] = jnp.where(first, ma + jnp.log(la), mb + jnp.log(lb))


def attend(lo, hi, q, k, v, tag_cols, tag_row, own_rows):
    window, wide = q.shape
    pairs = wide // LANES
    skip = (window - own_rows) // 2 // BLOCK
    blocks = own_rows // BLOCK
    return pl.pallas_call(
        attend_kernel,
        out_shape=[
            jax.ShapeDtypeStruct((own_rows, wide), bf16),
            jax.ShapeDtypeStruct((pairs, own_rows, LANES), f32),
        ],
        grid_spec=pltpu.PrefetchScalarGridSpec(
            num_scalar_prefetch=2,
            grid=(pairs, blocks),
            in_specs=[
                pl.BlockSpec((BLOCK, LANES), lambda p, i, a, b: (i + skip, p)),
                pl.BlockSpec((window, LANES), lambda p, i, a, b: (0, p)),
                pl.BlockSpec((window, LANES), lambda p, i, a, b: (0, p)),
                pl.BlockSpec((BLOCK, LANES), lambda p, i, a, b: (i + skip, 0)),
                pl.BlockSpec((1, window), lambda p, i, a, b: (0, 0)),
            ],
            out_specs=[
                pl.BlockSpec((BLOCK, LANES), lambda p, i, a, b: (i, p)),
                pl.BlockSpec((1, BLOCK, LANES), lambda p, i, a, b: (p, i, 0)),
            ],
        ),
        compiler_params=pltpu.CompilerParams(vmem_limit_bytes=32 << 20),
        cost_estimate=pl.CostEstimate(
            flops=4 * own_rows * own_rows * 4 * wide,
            transcendentals=own_rows * own_rows * 8,
            bytes_accessed=window * wide * 4,
        ),
        name="attend",
    )(lo, hi, q, k, v, tag_cols, tag_row)


def attend_back_kernel(
    start, stop, lo_ref, hi_ref, q_ref, k_ref, v_ref, g_ref, tc_ref, tr_ref, lse_ref, delta_ref,
    dq_ref, dk_ref, dv_ref, sum_ref, dk_acc, dv_acc, dq_acc,
):
    first = lax.broadcasted_iota(jnp.int32, (1, LANES), 1) < HEAD_DIM
    dk_acc[...] = jnp.zeros_like(dk_acc)
    dv_acc[...] = jnp.zeros_like(dv_acc)
    sum_ref[...] = jnp.zeros_like(sum_ref)

    def split(value):
        zero = jnp.zeros_like(value)
        return jnp.where(first, value, zero), jnp.where(first, zero, value)

    def query_block(i, carry):
        at_q = pl.multiple_of(i * BLOCK, BLOCK)
        own_q = jnp.logical_and(i >= start, i < stop)
        lo = jnp.where(own_q, lo_ref[i], jnp.maximum(lo_ref[i], start))
        hi = jnp.where(own_q, hi_ref[i], jnp.minimum(hi_ref[i], stop))

        @pl.when(own_q)
        def _():
            dq_acc[...] = jnp.zeros_like(dq_acc)

        def key_block(j, carry):
            at_k = pl.multiple_of(j * BLOCK, BLOCK)
            k = k_ref[pl.ds(at_k, BLOCK), :]
            v = v_ref[pl.ds(at_k, BLOCK), :]
            qs = split(q_ref[pl.ds(at_q, BLOCK), :])
            gs = split(g_ref[pl.ds(at_q, BLOCK), :])
            same = spread_lanes(tc_ref[pl.ds(at_k, BLOCK), :], BLOCK) == tr_ref[:, pl.ds(at_q, BLOCK)]
            ps, ds = [], []
            for h in range(2):
                s = dot_nt(k, qs[h])
                p = jnp.where(same, jnp.exp(s - lse_ref[0, h : h + 1, pl.ds(at_q, BLOCK)]), 0.0)
                dp = dot_nt(v, gs[h])
                d = p * (dp - delta_ref[0, h : h + 1, pl.ds(at_q, BLOCK)])
                ps.append(p.astype(bf16))
                ds.append(d.astype(bf16))

            @pl.when(jnp.logical_and(j >= start, j < stop))
            def _():
                at = pl.multiple_of((j - start) * BLOCK, BLOCK)
                dv_acc[pl.ds(at, BLOCK), :] += dot(ps[0], gs[0]) + dot(ps[1], gs[1])
                dk_acc[pl.ds(at, BLOCK), :] += dot(ds[0], qs[0]) + dot(ds[1], qs[1])

            @pl.when(own_q)
            def _():
                ks = split(k)
                dq_acc[...] += dot_tn(ds[0], ks[0]) + dot_tn(ds[1], ks[1])

            return carry

        lax.fori_loop(lo, hi, key_block, 0)

        @pl.when(own_q)
        def _():
            at = pl.multiple_of((i - start) * BLOCK, BLOCK)
            dq = dq_acc[...] * HEAD_DIM ** (-0.5)
            dq_ref[pl.ds(at, BLOCK), :] = dq.astype(bf16)
            sum_ref[0, 0:1, :] += jnp.sum(dq, axis=0, keepdims=True)

        return carry

    lax.fori_loop(0, q_ref.shape[0] // BLOCK, query_block, 0)
    dk_ref[...] = dk_acc[...].astype(bf16)
    dv_ref[...] = dv_acc[...].astype(bf16)
    sum_ref[0, 1:2, :] = jnp.sum(dv_acc[...], axis=0, keepdims=True)


def attend_back(lo, hi, q, k, v, g, tag_cols, tag_row, lse, delta, own_rows):
    window, wide = q.shape
    pairs = wide // LANES
    start = (window - own_rows) // 2 // BLOCK
    stop = start + own_rows // BLOCK
    whole = lambda: pl.BlockSpec((window, LANES), lambda p, a, b: (0, p))
    own = lambda: pl.BlockSpec((own_rows, LANES), lambda p, a, b: (0, p))
    stat = lambda: pl.BlockSpec((1, 2, window), lambda p, a, b: (p, 0, 0))
    return pl.pallas_call(
        functools.partial(attend_back_kernel, start, stop),
        out_shape=[jax.ShapeDtypeStruct((own_rows, wide), bf16)] * 3
        + [jax.ShapeDtypeStruct((pairs, 8, LANES), f32)],
        grid_spec=pltpu.PrefetchScalarGridSpec(
            num_scalar_prefetch=2,
            grid=(pairs,),
            in_specs=[
                whole(), whole(), whole(), whole(),
                pl.BlockSpec((window, LANES), lambda p, a, b: (0, 0)),
                pl.BlockSpec((1, window), lambda p, a, b: (0, 0)),
                stat(), stat(),
            ],
            out_specs=[own(), own(), own(), pl.BlockSpec((1, 8, LANES), lambda p, a, b: (p, 0, 0))],
            scratch_shapes=[
                pltpu.VMEM((own_rows, LANES), f32),
                pltpu.VMEM((own_rows, LANES), f32),
                pltpu.VMEM((BLOCK, LANES), f32),
            ],
        ),
        compiler_params=pltpu.CompilerParams(vmem_limit_bytes=40 << 20),
        cost_estimate=pl.CostEstimate(
            flops=10 * own_rows * own_rows * 4 * wide,
            transcendentals=own_rows * own_rows * 8,
            bytes_accessed=window * wide * 8,
        ),
        name="attend_back",
    )(lo, hi, q, k, v, g, tag_cols, tag_row, lse, delta)


def on_device(
    tokens, image_ids, ln1_gain, ln1_bias, qkv_weight, query_bias, value_bias, proj_weight,
    proj_bias, scale_attn, ln2_gain, ln2_bias, fc1_weight, fc1_bias, fc2_weight, fc2_bias,
    scale_mlp, cotangent,
):
    devices = lax.axis_size("fsdp")
    depth, ranks = devices // 2, lax.axis_size("rep")
    place = lax.axis_index("fsdp")
    rank = lax.axis_index("rep")
    here, core = place // 2, place % 2
    count = tokens.shape[1]
    chip = 2 * count
    head_rows = D // devices
    ff = fc1_weight.shape[1]
    unit_rows = ff // devices
    half_heads = D // 2

    def in_order(own, other, axis=0):
        return jnp.where(
            core == 0,
            jnp.concatenate([own, other], axis=axis),
            jnp.concatenate([other, own], axis=axis),
        )

    def mine(value):
        return lax.dynamic_slice_in_dim(value, core * count, count, 0)

    def others(value):
        return lax.dynamic_slice_in_dim(value, (1 - core) * count, count, 0)

    qkv_split = qkv_weight.reshape(head_rows, 3 * depth, 2, head_rows)
    fc1_split = fc1_weight.reshape(head_rows, depth, 2, unit_rows)

    def of_core(index):
        return jnp.concatenate(
            [
                pick(qkv_split, index, 2).reshape(head_rows, 3 * half_heads),
                pick(fc1_split, index, 2).reshape(head_rows, ff // 2),
            ],
            axis=1,
        )

    paired = in_order(of_core(core), swap_cores(of_core(1 - core)))
    proj_packed = jnp.concatenate([proj_weight[:, :half_heads], proj_weight[:, half_heads:]], axis=0)
    group1 = jnp.concatenate([paired[:, : 3 * half_heads], proj_packed], axis=1)
    group2 = paired[:, 3 * half_heads :]
    group3 = fc2_weight

    def own_columns(group):
        width = group.shape[1] // ranks
        return lax.dynamic_slice_in_dim(group, rank * width, width, 1)

    tok = tokens[0]
    behind, ahead = from_chip(tok, 1), from_chip(tok, -1)
    tok_other = swap_cores(jnp.concatenate([tok, behind, ahead, cotangent[0]]))
    cot_other = tok_other[3 * count :]
    window_tokens = jnp.concatenate(
        [
            in_order(behind, tok_other[count : 2 * count]),
            in_order(tok, tok_other[:count]),
            in_order(ahead, tok_other[2 * count : 3 * count]),
        ]
    )
    window = window_tokens.shape[0]

    small = (
        ln1_gain, ln1_bias, query_bias, value_bias, proj_bias, scale_attn, ln2_gain, ln2_bias,
        fc2_bias, scale_mlp, fc1_bias, (image_ids[0] + 1).astype(bf16),
    )
    sizes = [v.shape[0] for v in small]
    gathered = lax.all_gather(jnp.concatenate(small), "fsdp", axis=0)
    vectors, offset = [], 0
    for size in sizes:
        vectors.append(gathered[:, offset : offset + size].reshape(-1).astype(f32))
        offset += size
    (
        attn_gain, attn_shift, query_shift, value_shift, proj_shift, attn_scale, mlp_gain,
        mlp_shift, fc2_shift, mlp_scale, fc1_shift, all_tags,
    ) = vectors
    core_part = lambda vec: pick(vec.reshape(depth, 2, -1), core, 1).reshape(-1)
    query_shift, value_shift, fc1_shift = map(core_part, (query_shift, value_shift, fc1_shift))

    padded = jnp.concatenate(
        [jnp.zeros((chip,), f32), all_tags, jnp.full((chip,), 1e6, f32)]
    )
    tags = lax.dynamic_slice(padded, (here * chip,), (window,))
    firsts, lasts = tags[::BLOCK], tags[BLOCK - 1 :: BLOCK]
    real = firsts * (1e6 - firsts) > 0
    below = jnp.sum((tags[None, :] < firsts[:, None]).astype(jnp.int32), axis=1)
    upto = jnp.sum((tags[None, :] <= lasts[:, None]).astype(jnp.int32), axis=1)
    blocks = window // BLOCK
    block_lo = jnp.where(real, below // BLOCK, 0)
    block_hi = jnp.where(real, (upto + BLOCK - 1) // BLOCK, 0)
    own_lo, own_hi = chip // BLOCK, 2 * chip // BLOCK
    numbers = jnp.arange(blocks)
    need = jnp.logical_and(numbers >= block_lo[own_lo], numbers < block_hi[own_hi - 1])
    tag_cols = jnp.broadcast_to(tags[:, None], (window, LANES))
    tag_row = tags[None, :]

    normal_window, _ = normalize(window_tokens.astype(f32))
    normed1 = (normal_window * attn_gain + attn_shift).astype(bf16)

    full1 = merge_columns(gather_group(own_columns(group1), here, rank))
    full2 = merge_columns(gather_group(own_columns(group2), here, rank))
    full3 = merge_columns(gather_group(own_columns(group3), here, rank))
    qkv_matrix = full1[:, : 3 * half_heads]
    proj_matrix = (
        full1[:, 3 * half_heads :]
        .reshape(depth, 2, head_rows, half_heads)
        .transpose(0, 2, 1, 3)
        .reshape(half_heads, D)
    )
    fc1_matrix, fc2_matrix = full2, full3

    shifts = jnp.broadcast_to(
        jnp.concatenate([query_shift, jnp.zeros_like(query_shift), value_shift])[None],
        (8, 3 * half_heads),
    )
    queries, keys, values = project(
        need.astype(jnp.int32), normed1, qkv_matrix, shifts, half_heads
    )
    context, lse = attend(
        block_lo[own_lo:own_hi], block_hi[own_lo:own_hi], queries, keys, values, tag_cols, tag_row, chip
    )
    local_heads = half_heads // HEAD_DIM
    lse_rows = lse[:, :, ::HEAD_DIM].transpose(0, 2, 1).reshape(local_heads, chip)

    features = tok.astype(f32)
    sent = swap_cores(dot(others(context), proj_matrix))
    attn_out = dot(mine(context), proj_matrix) + sent + proj_shift
    resid = features + attn_scale * attn_out
    mlp_normal, mlp_inverse = normalize(resid)
    mlp_input = (mlp_normal * mlp_gain + mlp_shift).astype(bf16)
    mlp_input = jnp.concatenate([mlp_input, swap_cores(mlp_input)])
    pre_act = dot(mlp_input, fc1_matrix) + fc1_shift
    activated, slope = gelu_pair(pre_act)
    activated = activated.astype(bf16)

    out_grad = cotangent[0].astype(f32)
    mlp_grad_full = out_grad * mlp_scale
    mlp_grad = (jnp.concatenate([cotangent[0], cot_other]).astype(f32) * mlp_scale).astype(bf16)
    sent = swap_cores(dot(activated[count:], fc2_matrix))
    mlp_out = dot(activated[:count], fc2_matrix) + sent + fc2_shift
    output_rows = (resid + mlp_scale * mlp_out).astype(bf16)

    fc2_grad = dot_tn(activated, mlp_grad).astype(bf16)
    fc2_total = reduce_group(fc2_grad, here, rank, [list(range(rep_bits()))])

    pre_grad_full = dot_nt(mlp_grad, fc2_matrix) * slope
    pre_grad = pre_grad_full.astype(bf16)
    fc1_grad = dot_tn(mlp_input, pre_grad).astype(bf16)
    fc1_total = reduce_group(fc1_grad, here, rank, [list(range(rep_bits()))[::-1]])

    sent = swap_cores(dot_nt(pre_grad[count:], fc1_matrix))
    mlp_in_grad = dot_nt(pre_grad[:count], fc1_matrix) + sent
    resid_grad = out_grad + norm_back(mlp_in_grad, mlp_normal, mlp_inverse, mlp_gain)
    attn_grad_full = resid_grad * attn_scale
    attn_grad = attn_grad_full.astype(bf16)
    attn_grad = in_order(attn_grad, swap_cores(attn_grad))
    context_grad = dot_nt(attn_grad, proj_matrix).astype(bf16)
    row_delta = jnp.sum(
        (context_grad.astype(f32) * context.astype(f32)).reshape(chip, local_heads, HEAD_DIM), axis=-1
    ).T
    stats = jnp.concatenate([lse_rows, row_delta])
    grad_window = jnp.concatenate([from_chip(context_grad, 1), context_grad, from_chip(context_grad, -1)])
    stat_window = jnp.concatenate([from_chip(stats, 1), stats, from_chip(stats, -1)], axis=1)
    by_pair = lambda s: s.reshape(local_heads // 2, 2, window)

    query_grad, key_grad, value_grad, sums = attend_back(
        block_lo, block_hi, queries, keys, values, grad_window, tag_cols, tag_row,
        by_pair(stat_window[:local_heads]), by_pair(stat_window[local_heads:]), chip,
    )
    qkv_grad = jnp.concatenate([query_grad, key_grad, value_grad], axis=1)
    qkv_w_grad = dot_tn(normed1[chip : 2 * chip], qkv_grad).astype(bf16)
    proj_grad = dot_tn(context, attn_grad).astype(bf16)
    proj_grad = (
        proj_grad.reshape(depth, head_rows, 2, half_heads)
        .transpose(0, 2, 1, 3)
        .reshape(D, half_heads)
    )
    group1_total = reduce_group(
        jnp.concatenate([qkv_w_grad, proj_grad], axis=1), here, rank,
        [list(range(rep_bits())), list(range(rep_bits()))[::-1]],
    )

    sent = swap_cores(dot_nt(others(qkv_grad), qkv_matrix))
    attn_in_grad = dot_nt(mine(qkv_grad), qkv_matrix) + sent
    attn_normal, attn_inverse = normalize(features)
    input_rows = resid_grad + norm_back(attn_in_grad, attn_normal, attn_inverse, attn_gain)

    factor = 1.0 / math.sqrt(count * devices * ranks)

    def on_core(part):
        part = part.reshape(depth, 1, -1)
        zero = jnp.zeros_like(part)
        return jnp.where(
            core == 0,
            jnp.concatenate([part, zero], axis=1),
            jnp.concatenate([zero, part], axis=1),
        ).reshape(-1)

    columns = lambda value: jnp.sum(value, axis=0)
    partial = jnp.concatenate(
        [
            v.reshape(devices, -1)
            for v in (
                columns(attn_in_grad * attn_normal), columns(attn_in_grad),
                on_core(sums[:, 0]), on_core(sums[:, 1]),
                columns(attn_grad_full), columns(resid_grad * attn_out),
                columns(mlp_in_grad * mlp_normal), columns(mlp_in_grad),
                columns(mlp_grad_full), columns(out_grad * mlp_out),
                on_core(columns(pre_grad_full)),
            )
        ],
        axis=1,
    )
    totals = pick(lax.psum(partial, ("rep", "fsdp")), place, 0) * factor
    small_grads, offset = [], 0
    for size in sizes[:-1]:
        small_grads.append(totals[offset : offset + size])
        offset += size
    (
        grad_attn_gain, grad_attn_shift, grad_query_shift, grad_value_shift, grad_proj_shift,
        grad_attn_scale, grad_mlp_gain, grad_mlp_shift, grad_fc2_shift, grad_mlp_scale, grad_fc1_shift,
    ) = small_grads

    def finish(total):
        return share_over_rep(total.astype(bf16), rank)

    fc2_full = finish(fc2_total).astype(f32) * factor
    fc1_full = finish(fc1_total)
    first_full = finish(group1_total)
    rows_of = lambda value, index: lax.dynamic_slice_in_dim(value, index * head_rows, head_rows, 0)
    both = jnp.concatenate([first_full[:, : 3 * half_heads], fc1_full], axis=1)
    own_part, other_part = rows_of(both, core), swap_cores(rows_of(both, 1 - core))

    def interleave(own, other, blocks):
        own = own.reshape(head_rows, blocks, 1, -1)
        other = other.reshape(head_rows, blocks, 1, -1)
        joined = in_order(own, other, axis=2)
        return joined.reshape(head_rows, -1).astype(f32) * factor

    grad_qkv = interleave(own_part[:, : 3 * half_heads], other_part[:, : 3 * half_heads], 3 * depth)
    grad_fc1 = interleave(own_part[:, 3 * half_heads :], other_part[:, 3 * half_heads :], depth)
    proj_part = first_full[:, 3 * half_heads :]
    grad_proj = jnp.concatenate([proj_part[:head_rows], proj_part[head_rows:]], axis=1).astype(f32) * factor

    return (
        output_rows[None],
        input_rows[None],
        grad_attn_gain,
        grad_attn_shift,
        grad_qkv,
        grad_query_shift,
        grad_value_shift,
        grad_proj,
        grad_proj_shift,
        grad_attn_scale,
        grad_mlp_gain,
        grad_mlp_shift,
        grad_fc1,
        grad_fc1_shift,
        fc2_full,
        grad_fc2_shift,
        grad_mlp_scale,
    )


def solution(mesh):
    rows = P("fsdp", None)
    vec = P("fsdp")
    tok = P("rep", "fsdp", None)
    return jax.shard_map(
        on_device,
        mesh=mesh,
        in_specs=(
            tok, P("rep", "fsdp"), vec, vec, rows, vec, vec, rows, vec, vec, vec, vec, rows, vec,
            rows, vec, vec, tok,
        ),
        out_specs=(
            tok, tok, vec, vec, rows, vec, vec, rows, vec, vec, vec, vec, rows, vec, rows, vec, vec,
        ),
        check_vma=False,
    )
```

```python
import functools
import math

import jax
import jax.numpy as jnp
from jax import lax
from jax.experimental import pallas as pl
from jax.experimental.pallas import tpu as pltpu
from jax.sharding import PartitionSpec as P

D = 1024
HEADS = 16
HEAD_DIM = 64
LANES = 128

EPSILON = 1e-06
MASKED = -1e30
BLOCK = 256

f32 = jnp.float32
bf16 = jnp.bfloat16


def normalize(features):
    row_mean = jnp.mean(features, axis=-1, keepdims=True)
    centred = features - row_mean
    variance = jnp.mean(centred * centred, axis=-1, keepdims=True)
    inverse = lax.rsqrt(variance + EPSILON)
    return centred * inverse, inverse


def norm_back(gradient, normal, inverse, gain_vec):
    scaled = gradient * gain_vec
    mean_first = jnp.mean(scaled, axis=-1, keepdims=True)
    mean_second = jnp.mean(scaled * normal, axis=-1, keepdims=True)
    return inverse * (scaled - mean_first - normal * mean_second)


def gelu_pair(values):
    cumulative = 0.5 * (1.0 + lax.erf(values * 2.0 ** (-0.5)))
    density = jnp.exp(-0.5 * values * values) * (2.0 * math.pi) ** (-0.5)
    return (values * cumulative, cumulative + values * density)


def dot(a, b):
    return jnp.dot(a, b, preferred_element_type=f32)


def dot_nt(a, b):
    return lax.dot_general(a, b, (((1,), (1,)), ((), ())), preferred_element_type=f32)


def dot_tn(a, b):
    return lax.dot_general(a, b, (((0,), (0,)), ((), ())), preferred_element_type=f32)


def swap_cores(value):
    size = lax.axis_size("fsdp")
    return lax.ppermute(value, "fsdp", [(i, i ^ 1) for i in range(size)])


def along_z(value, by):
    size = lax.axis_size("fsdp")
    return lax.ppermute(value, "fsdp", [(i, (i + 2 * by) % size) for i in range(size)])


def from_chip(value, by):
    size = lax.axis_size("fsdp")
    pairs = [(i, i + 2 * by) for i in range(size) if 0 <= i + 2 * by < size]
    return lax.ppermute(value, "fsdp", pairs)


def across_rep(value, bit):
    size = lax.axis_size("rep")
    return lax.ppermute(value, "rep", [(i, i ^ (1 << bit)) for i in range(size)])


def pick(value, index, axis):
    return lax.dynamic_index_in_dim(value, index, axis, keepdims=False)


def rep_bits():
    return lax.axis_size("rep").bit_length() - 1


def tie(*values):
    return lax.optimization_barrier(values)


def fetch_z(own):
    return [own] + [along_z(own, k) for k in range(1, lax.axis_size("fsdp") // 2)]


class Gather:
    def __init__(self, pieces, rows, name):
        self.rows, self.cols, self.name = rows, pieces[0].shape[1], name
        half = rows // 2
        bits = list(range(rep_bits()))
        self.orders = [bits, bits[::-1]]
        self.parts = [
            [(jnp.stack([p[:half] for p in pieces])[None], [0])],
            [(jnp.stack([p[half:rows] for p in pieces])[None], [0])],
        ]
        self.at = 0

    def send(self, *values):
        whole = [
            (ps[0][0] if len(ps) == 1 else jnp.concatenate([a for a, _ in ps]), [o for _, os in ps for o in os])
            for ps in self.parts
        ]
        values, arrays = lax.optimization_barrier((values, [a for a, _ in whole]))
        self.parts = []
        for array, (_, offsets), order in zip(arrays, whole, self.orders):
            flip = 1 << order[self.at]
            received = across_rep(array, order[self.at])
            self.parts.append([(array, offsets), (received, [o ^ flip for o in offsets])])
        self.at += 1
        return values[0] if len(values) == 1 else values

    def arrive(self, value):
        value, arrays = lax.optimization_barrier((value, [a for ps in self.parts for a, _ in ps]))
        self.parts = [[(arrays.pop(0), o) for _, o in ps] for ps in self.parts]
        return value

    def assemble(self, here, rank, tail_rows=0):
        depth, ranks = lax.axis_size("fsdp") // 2, lax.axis_size("rep")
        sources, plan = [], []
        for number, parts in enumerate(self.parts):
            for array, offsets in parts:
                sources.append(array)
                plan.append((number, offsets))
        dtype = sources[0].dtype
        shape = (depth * self.rows, ranks * self.cols)
        shapes = [jax.ShapeDtypeStruct(shape, dtype)]
        if tail_rows:
            tail = shape[1] // 4
            shapes = [
                jax.ShapeDtypeStruct((shape[0], shape[1] - tail), dtype),
                jax.ShapeDtypeStruct((depth * tail_rows, 2 * tail), dtype),
            ]
        out = pl.pallas_call(
            functools.partial(assemble_kernel, plan, depth, self.rows, self.cols, tail_rows),
            out_shape=shapes,
            grid_spec=pltpu.PrefetchScalarGridSpec(
                num_scalar_prefetch=1,
                grid=(1,),
                in_specs=[pl.BlockSpec(memory_space=pl.ANY)] * len(sources),
                out_specs=[pl.BlockSpec(memory_space=pl.ANY)] * len(shapes),
                scratch_shapes=[
                    pltpu.VMEM(shape, dtype),
                    pltpu.SemaphoreType.DMA((2 * ranks * depth,)),
                    pltpu.SemaphoreType.DMA((3 * depth,)),
                ],
            ),
            compiler_params=pltpu.CompilerParams(vmem_limit_bytes=16 << 20),
            cost_estimate=pl.CostEstimate(
                flops=0, transcendentals=0, bytes_accessed=2 * shape[0] * shape[1] * dtype.itemsize
            ),
            name=self.name,
        )(jnp.stack([here, rank]).astype(jnp.int32), *sources)
        return out if tail_rows else out[0]


def assemble_kernel(plan, depth, rows, cols, tail_rows, index_ref, *refs):
    count = len(plan)
    sources = refs[:count]
    targets = refs[count : count + (2 if tail_rows else 1)]
    held, in_sems, out_sems = refs[-3:]
    here, rank = index_ref[0], index_ref[1]
    half = rows // 2
    waits = [[] for _ in range(depth)]
    number = 0
    for k in range(depth):
        place = lax.rem(here - k + depth, depth)
        for which, (colour, offsets) in enumerate(plan):
            for m, offset in enumerate(offsets):
                at_row = pl.multiple_of(place * rows + colour * half, half)
                at_col = pl.multiple_of((rank ^ offset) * cols, cols)
                copy = pltpu.make_async_copy(
                    sources[which].at[m, k],
                    held.at[pl.ds(at_row, half), pl.ds(at_col, cols)],
                    in_sems.at[number],
                )
                copy.start()
                waits[k].append(copy)
                number += 1
    outs = []
    main = targets[0].shape[1]
    for k in range(depth):
        place = lax.rem(here - k + depth, depth)
        for copy in waits[k]:
            copy.wait()
        base = pl.multiple_of(place * rows, rows)
        band = pl.ds(base, rows)
        out = pltpu.make_async_copy(held.at[band, pl.ds(0, main)], targets[0].at[band], out_sems.at[3 * k])
        out.start()
        outs.append(out)
        if tail_rows:
            wide = targets[1].shape[1] // 2
            for side in range(2):
                out = pltpu.make_async_copy(
                    held.at[pl.ds(base + side * tail_rows, tail_rows), pl.ds(main, wide)],
                    targets[1].at[
                        pl.ds(pl.multiple_of(place * tail_rows, tail_rows), tail_rows),
                        pl.ds(side * wide, wide),
                    ],
                    out_sems.at[3 * k + 1 + side],
                )
                out.start()
                outs.append(out)
    for out in outs:
        out.wait()


def halves(ranks, bit, held):
    flip = 1 << bit
    kept = [o for o in held if not o & flip]
    return kept, [o ^ flip for o in kept]


def relative_blocks(grads, rank, orders):
    depth, ranks = lax.axis_size("fsdp") // 2, lax.axis_size("rep")
    width = grads.shape[1] // ranks
    rows = grads.shape[0] // depth
    shaped = grads.reshape(depth, rows, grads.shape[1])
    share = rows // len(orders)
    first = []
    for n, order in enumerate(orders):
        block = lambda o: lax.dynamic_slice(
            shaped, (0, n * share, (rank ^ o) * width), (depth, share, width)
        )
        kept, given = halves(ranks, order[0], list(range(ranks)))
        first.append((jnp.stack([block(o) for o in kept]), jnp.stack([block(o) for o in given])))
    return first


class Reduce:
    def __init__(self, first, here, orders):
        self.here, self.orders, self.at = here, orders, 0
        ranks = lax.axis_size("rep")
        self.held = []
        for (keep, give), order in zip(first, orders):
            kept, given = halves(ranks, order[0], list(range(ranks)))
            self.held.append((kept, keep, give))

    def send(self, *values):
        values, gives = lax.optimization_barrier((values, [give for _, _, give in self.held]))
        self.received = [across_rep(g, order[self.at]) for g, order in zip(gives, self.orders)]
        self.at += 1
        return values[0] if len(values) == 1 else values

    def arrive(self, *values):
        values, received = lax.optimization_barrier((values, self.received))
        held = []
        for (kept, keep, _), got, order in zip(self.held, received, self.orders):
            total = (keep.astype(f32) + got.astype(f32)).astype(bf16)
            if self.at < len(order):
                stay, leave = halves(None, order[self.at], kept)
                take = lambda os: jnp.stack([total[kept.index(o)] for o in os])
                held.append((stay, take(stay), take(leave)))
            else:
                held.append((kept, total[0], None))
        self.held = held
        return values[0] if len(values) == 1 else values

    def send_z(self, *values):
        depth = lax.axis_size("fsdp") // 2
        parts = [keep for _, keep, _ in self.held]
        whole = parts[0] if len(parts) == 1 else jnp.concatenate(parts, axis=1)
        pieces = [pick(whole, lax.rem(self.here + k, depth), 0) for k in range(depth)]
        values, pieces = lax.optimization_barrier((values, pieces))
        self.pieces = [pieces[0]] + [along_z(p, k) for k, p in enumerate(pieces) if k]
        return values[0] if len(values) == 1 else values

    def arrive_z(self, *values):
        values, pieces = lax.optimization_barrier((values, self.pieces))
        total = pieces[0].astype(f32)
        for piece in pieces[1:]:
            total = total + piece.astype(f32)
        self.total = total
        return values[0] if len(values) == 1 else values


def rep_blocks(stacked, offsets, rank):
    blocks = []
    for i in range(len(offsets)):
        block = stacked[0]
        for entry, offset in enumerate(offsets):
            block = jnp.where((rank ^ offset) == i, stacked[entry], block)
        blocks.append(block)
    return jnp.concatenate(blocks, axis=1)


def whole_specs(arrays):
    return [pl.BlockSpec(a.shape, lambda *_, n=len(a.shape): (0,) * n) for a in arrays]


def slot_lists(sizes):
    slots = []
    for number, size in enumerate(sizes):
        for start in range(0, size, LANES):
            slots.append((number, start, min(LANES, size - start)))
    return slots


def pack_kernel(slots, *refs):
    *sources, out_ref, held = refs
    per_row = held.shape[1] // LANES
    held[...] = jnp.zeros_like(held)
    for slot, (number, start, size) in enumerate(slots):
        row, at = slot // per_row, slot % per_row * LANES
        held[row : row + 1, at : at + size] = sources[number][:, start : start + size].astype(f32)
    out_ref[...] = held[...].astype(out_ref.dtype)


def pack_small(vectors, width, slots):
    shape = (32 * LANES // width, width)
    vectors = [v.reshape(1, -1) for v in vectors]
    return pl.pallas_call(
        functools.partial(pack_kernel, slots),
        out_shape=jax.ShapeDtypeStruct(shape, bf16),
        scratch_shapes=[pltpu.VMEM(shape, f32)],
        name="pack_small",
    )(*vectors)


def unpack_kernel(slots, depth, index_ref, *refs):
    pieces, (vec_ref, unit_ref, tag_ref) = refs[:depth], refs[depth:]
    here, core = index_ref[0], index_ref[1]
    rows, width = pieces[0].shape
    per_row = width // LANES
    single = sum(1 for number, _, _ in slots if number < 10)
    vec_ref[...] = jnp.zeros_like(vec_ref)
    for k in range(depth):
        place = lax.rem(here - k + depth, depth)
        values = pieces[k][...].astype(f32)

        def part(side, slot, size):
            row, at = side * (rows // 2) + slot // per_row, slot % per_row * LANES
            return values[row : row + 1, at : at + size]

        for slot, (number, start, size) in enumerate(slots):
            own, other = part(0, slot, size), part(1, slot, size)
            first = jnp.where(core == 0, own, other)
            second = jnp.where(core == 0, other, own)
            if number < 10:
                at = pl.multiple_of(place * 2 * size, 2 * size)
                vec_ref[number : number + 1, pl.ds(at, 2 * size)] = jnp.concatenate([first, second], axis=1)
            elif number == 10:
                wide = unit_ref.shape[1] // depth
                unit_ref[0:1, pl.ds(pl.multiple_of(place * wide + start, LANES), LANES)] = own
            else:
                wide = tag_ref.shape[1] // depth
                at = pl.multiple_of(place * wide + start, LANES)
                tag_ref[0:1, pl.ds(at, LANES)] = first
                tag_ref[0:1, pl.ds(pl.multiple_of(at + wide // 2, LANES), LANES)] = second


def unpack_small(pieces, slots, rows, here, core, units, group_tokens):
    depth = len(pieces)
    extra, width = pieces[0].shape[0] - rows, pieces[0].shape[1]
    shapes = [(16, D), (1, units), (1, group_tokens)]
    return pl.pallas_call(
        functools.partial(unpack_kernel, slots, depth),
        out_shape=[jax.ShapeDtypeStruct(s, f32) for s in shapes],
        grid_spec=pltpu.PrefetchScalarGridSpec(
            num_scalar_prefetch=1,
            grid=(1,),
            in_specs=[pl.BlockSpec((extra, width), lambda i, a: (rows // extra, 0))] * depth,
            out_specs=[pl.BlockSpec(s, lambda i, a: (0, 0)) for s in shapes],
        ),
        name="unpack_small",
    )(jnp.stack([here, core]).astype(jnp.int32), *pieces)


def pack_grads_kernel(depth, sizes, index_ref, *refs):
    *sources, out_ref = refs
    core = index_ref[0]
    out_ref[...] = jnp.zeros_like(out_ref)
    for z in range(depth):
        for c in range(2):
            row = 16 * c
            for source, (size, of_core) in zip(sources, sizes):
                for start in range(0, size, LANES):
                    lanes = min(LANES, size - start)
                    at = (z if of_core else 2 * z + c) * size + start
                    value = source[0:1, at : at + lanes]
                    if of_core:
                        value = jnp.where(core == c, value, 0.0)
                    out_ref[z, row : row + 1, 0:lanes] = value
                    row += 1


def pack_grads(vectors, sizes, core, depth):
    return pl.pallas_call(
        functools.partial(pack_grads_kernel, depth, sizes),
        out_shape=jax.ShapeDtypeStruct((depth, 32, LANES), f32),
        grid_spec=pltpu.PrefetchScalarGridSpec(
            num_scalar_prefetch=1,
            grid=(1,),
            in_specs=whole_specs(vectors),
            out_specs=pl.BlockSpec((depth, 32, LANES), lambda i, a: (0, 0, 0)),
        ),
        name="pack_grads",
    )(core.reshape(1).astype(jnp.int32), *vectors)


def proj_grad_kernel(head_rows, c_ref, g_ref, out_ref):
    wide = out_ref.shape[1]
    for side in range(2):
        grad = dot_tn(c_ref[...], g_ref[:, side * wide : (side + 1) * wide]).astype(bf16)
        for z in range(grad.shape[0] // head_rows):
            at = (2 * z + side) * head_rows
            out_ref[at : at + head_rows, :] = grad[z * head_rows : (z + 1) * head_rows]


def packed_proj_grad(context, attn_grad, head_rows):
    wide = D // 2
    return pl.pallas_call(
        functools.partial(proj_grad_kernel, head_rows),
        out_shape=jax.ShapeDtypeStruct((D, wide), bf16),
        compiler_params=pltpu.CompilerParams(vmem_limit_bytes=32 << 20),
        cost_estimate=pl.CostEstimate(flops=2 * context.shape[0] * D * wide, transcendentals=0, bytes_accessed=6 << 20),
        name="proj_grad",
    )(context, attn_grad)


def qkv_grad_kernel(orders, ranks, depth, per, index_ref, n_ref, *refs):
    grads, p_ref = refs[: 3 * per], refs[3 * per]
    outs, held = refs[3 * per + 1 : -1], refs[-1]
    rank = index_ref[0]
    normed = n_ref[...]
    for number in range(3):
        pieces = [g[...] for g in grads[number * per : (number + 1) * per]]
        wide = per * LANES
        joined = pieces[0] if per == 1 else jnp.concatenate(pieces, axis=1)
        held[:, number * wide : (number + 1) * wide] = dot_tn(normed, joined).astype(bf16)
    held[:, 3 * per * LANES :] = p_ref[...]
    width = held.shape[1] // ranks
    rows = held.shape[0] // depth
    share = rows // len(orders)
    for n, order in enumerate(orders):
        for which, offsets in enumerate(halves(ranks, order[0], list(range(ranks)))):
            for i, o in enumerate(offsets):
                cols = pl.ds(pl.multiple_of((rank ^ o) * width, width), width)
                for z in range(depth):
                    at = z * rows + n * share
                    outs[2 * n + which][i, z] = held[at : at + share, cols]


def qkv_grad_blocks(normed, grads, proj_packed, part, parts, rank, orders):
    depth, ranks = lax.axis_size("fsdp") // 2, lax.axis_size("rep")
    per = len(grads) // 3
    cols = 4 * per * LANES
    block = (ranks // 2, depth, D // depth // len(orders), cols // ranks)
    tokens = normed.shape[0] // 3
    outs = pl.pallas_call(
        functools.partial(qkv_grad_kernel, orders, ranks, depth, per),
        out_shape=[jax.ShapeDtypeStruct(block, bf16)] * (2 * len(orders)),
        grid_spec=pltpu.PrefetchScalarGridSpec(
            num_scalar_prefetch=1,
            grid=(1,),
            in_specs=[pl.BlockSpec((tokens, D), lambda i, a: (1, 0))]
            + whole_specs(grads)
            + [pl.BlockSpec((D, per * LANES), lambda i, a: (0, part))],
            out_specs=[pl.BlockSpec(block, lambda i, a: (0, 0, 0, 0))] * (2 * len(orders)),
            scratch_shapes=[pltpu.VMEM((D, cols), bf16)],
        ),
        compiler_params=pltpu.CompilerParams(vmem_limit_bytes=40 << 20),
        cost_estimate=pl.CostEstimate(flops=2 * tokens * D * cols, transcendentals=0, bytes_accessed=8 << 20),
        name="qkv_grad",
    )(rank.reshape(1).astype(jnp.int32), normed, *grads, proj_packed)
    return [(outs[2 * n], outs[2 * n + 1]) for n in range(len(orders))]


def spread_lanes(tags, width):
    return jnp.concatenate([tags] * (width // LANES), axis=1)


def project_kernel(need_ref, n_ref, w_ref, b_ref, q_ref, k_ref, v_ref):
    row = pl.program_id(0)
    wide = q_ref.shape[1]

    @pl.when(need_ref[row] > 0)
    def _():
        n = n_ref[...]
        for i, ref in enumerate((q_ref, k_ref, v_ref)):
            out = dot(n, w_ref[:, i * wide : (i + 1) * wide]) + b_ref[0:1, i * wide : (i + 1) * wide]
            if i == 0:
                out = out.astype(bf16).astype(f32) * HEAD_DIM ** (-0.5)
            ref[...] = out.astype(bf16)

    @pl.when(need_ref[row] == 0)
    def _():
        for ref in (q_ref, k_ref, v_ref):
            ref[...] = jnp.zeros_like(ref)


def project(need, normed, weight, bias, wide):
    rows = normed.shape[0]
    return pl.pallas_call(
        project_kernel,
        out_shape=[jax.ShapeDtypeStruct((rows, wide), bf16)] * 3,
        grid_spec=pltpu.PrefetchScalarGridSpec(
            num_scalar_prefetch=1,
            grid=(rows // BLOCK,),
            in_specs=[
                pl.BlockSpec((BLOCK, D), lambda i, s: (i, 0)),
                pl.BlockSpec(weight.shape, lambda i, s: (0, 0)),
                pl.BlockSpec((1, 3 * wide), lambda i, s: (0, 0)),
            ],
            out_specs=[pl.BlockSpec((BLOCK, wide), lambda i, s: (i, 0))] * 3,
        ),
        compiler_params=pltpu.CompilerParams(vmem_limit_bytes=32 << 20),
        cost_estimate=pl.CostEstimate(
            flops=2 * rows * D * 3 * wide, transcendentals=0, bytes_accessed=rows * D * 6
        ),
        name="project",
    )(need, normed, weight, bias)


def norm_kernel(need_ref, info_ref, *refs):
    *sources, vec_ref, out_ref = refs
    row = pl.program_id(0)
    side = (row // info_ref[1]) % 2
    chip = row // (2 * info_ref[1])

    @pl.when(need_ref[row] > 0)
    def _():
        picked = jnp.where(chip == 0, sources[0][...], jnp.where(chip == 1, sources[2][...], sources[4][...]))
        theirs = jnp.where(chip == 0, sources[1][...], jnp.where(chip == 1, sources[3][...], sources[5][...]))
        picked = jnp.where(side == info_ref[0], picked, theirs)
        normal, _ = normalize(picked.astype(f32))
        out_ref[...] = (normal * vec_ref[0:1, :] + vec_ref[1:2, :]).astype(bf16)

    @pl.when(need_ref[row] == 0)
    def _():
        out_ref[...] = jnp.zeros_like(out_ref)


def norm_window(need, info, sources, vecs, window, count):
    per = count // BLOCK

    def spec(chip):
        def index(i, a, b):
            inside = jnp.clip(i - 2 * per * chip, 0, 2 * per - 1)
            return (inside % per, 0)

        return pl.BlockSpec((BLOCK, D), index)

    return pl.pallas_call(
        norm_kernel,
        out_shape=jax.ShapeDtypeStruct((window, D), bf16),
        grid_spec=pltpu.PrefetchScalarGridSpec(
            num_scalar_prefetch=2,
            grid=(window // BLOCK,),
            in_specs=[spec(i // 2) for i in range(6)] + [pl.BlockSpec(vecs.shape, lambda i, a, b: (0, 0))],
            out_specs=pl.BlockSpec((BLOCK, D), lambda i, a, b: (i, 0)),
        ),
        compiler_params=pltpu.CompilerParams(vmem_limit_bytes=24 << 20),
        cost_estimate=pl.CostEstimate(flops=window * D * 10, transcendentals=0, bytes_accessed=30 << 20),
        name="norm_window",
    )(need, info, *sources, vecs)


def attend_kernel(lo_ref, hi_ref, first_ref, last_ref, q_ref, k_ref, v_ref, qt_ref, kt_ref, o_ref, lse_ref, s_ref, m_ref):
    i = pl.program_id(0)
    left = lax.broadcasted_iota(jnp.int32, (1, LANES), 1) < HEAD_DIM
    lo, hi = lo_ref[i], hi_ref[i]
    base = (first_ref.shape[0] - pl.num_programs(0)) // 2
    q = q_ref[...]
    zero = jnp.zeros_like(q)
    heads = (jnp.where(left, q, zero), jnp.where(left, zero, q))
    m_ref[...] = jnp.full_like(m_ref, MASKED)
    one_image = first_ref[base + i] == last_ref[base + i]
    folds = BLOCK // LANES

    def fold(value, combine):
        parts = [value[:, n * LANES : (n + 1) * LANES] for n in range(folds)]
        return functools.reduce(combine, parts)

    def scores(j, carry):
        at = pl.multiple_of(j * BLOCK, BLOCK)
        k = k_ref[pl.ds(at, BLOCK), :]
        inside = one_image & (first_ref[j] == first_ref[base + i]) & (last_ref[j] == first_ref[base + i])

        @pl.when(inside)
        def _():
            for h in range(2):
                s = dot_nt(heads[h], k)
                s_ref[h, j] = s
                m_ref[h] = jnp.maximum(m_ref[h], fold(s, jnp.maximum))

        @pl.when(jnp.logical_not(inside))
        def _():
            same = spread_lanes(qt_ref[...], BLOCK) == kt_ref[:, pl.ds(at, BLOCK)]
            for h in range(2):
                s = jnp.where(same, dot_nt(heads[h], k), MASKED)
                s_ref[h, j] = s
                m_ref[h] = jnp.maximum(m_ref[h], fold(s, jnp.maximum))

        return carry

    lax.fori_loop(lo, hi, scores, 0)
    tops = [jnp.max(m_ref[h], axis=1, keepdims=True) for h in range(2)]
    m_ref[...] = jnp.zeros_like(m_ref)

    def powers(j, carry):
        for h in range(2):
            e = jnp.exp(s_ref[h, j] - tops[h])
            s_ref[h, j] = e
            m_ref[h] += fold(e, jnp.add)
        return carry

    lax.fori_loop(lo, hi, powers, 0)
    sums = [jnp.sum(m_ref[h], axis=1, keepdims=True) for h in range(2)]
    shares = [1.0 / s for s in sums]
    m_ref[...] = jnp.zeros_like(m_ref)

    def mix(j, carry):
        at = pl.multiple_of(j * BLOCK, BLOCK)
        v = v_ref[pl.ds(at, BLOCK), :]
        for h in range(2):
            m_ref[h] += dot((s_ref[h, j] * shares[h]).astype(bf16), v)
        return carry

    lax.fori_loop(lo, hi, mix, 0)
    o_ref[...] = jnp.where(left, m_ref[0], m_ref[1]).astype(bf16)
    for h in range(2):
        lse = jnp.broadcast_to(tops[h] + jnp.log(sums[h]), (BLOCK, LANES))
        lse_ref[0, h : h + 1, :] = lse.T[0:1, :]


def attend(lo, hi, firsts, lasts, q, k, v, tag_cols, tag_row, own_rows, pair):
    window = q.shape[0]
    blocks = own_rows // BLOCK
    skip = (window - own_rows) // 2 // BLOCK
    return pl.pallas_call(
        attend_kernel,
        out_shape=[
            jax.ShapeDtypeStruct((own_rows, LANES), bf16),
            jax.ShapeDtypeStruct((1, 2, own_rows), f32),
        ],
        grid_spec=pltpu.PrefetchScalarGridSpec(
            num_scalar_prefetch=4,
            grid=(blocks,),
            in_specs=[
                pl.BlockSpec((BLOCK, LANES), lambda i, *_: (i + skip, pair)),
                pl.BlockSpec((window, LANES), lambda i, *_: (0, pair)),
                pl.BlockSpec((window, LANES), lambda i, *_: (0, pair)),
                pl.BlockSpec((BLOCK, LANES), lambda i, *_: (i + skip, 0)),
                pl.BlockSpec((1, window), lambda i, *_: (0, 0)),
            ],
            out_specs=[
                pl.BlockSpec((BLOCK, LANES), lambda i, *_: (i, 0)),
                pl.BlockSpec((1, 2, BLOCK), lambda i, *_: (0, 0, i)),
            ],
            scratch_shapes=[
                pltpu.VMEM((2, window // BLOCK, BLOCK, BLOCK), f32),
                pltpu.VMEM((2, BLOCK, LANES), f32),
            ],
        ),
        compiler_params=pltpu.CompilerParams(vmem_limit_bytes=32 << 20),
        cost_estimate=pl.CostEstimate(
            flops=90 * own_rows * own_rows * LANES,
            transcendentals=own_rows * own_rows * 2,
            bytes_accessed=window * LANES * 6,
        ),
        name="attend",
    )(lo, hi, firsts, lasts, q, k, v, tag_cols, tag_row)


def attend_back_kernel(
    start, stop, lo_ref, hi_ref, q_ref, k_ref, v_ref, g_ref, tc_ref, tr_ref, lse_ref, delta_ref,
    dq_ref, dk_ref, dv_ref, sum_ref, dk_acc, dv_acc, dq_acc,
):
    first = lax.broadcasted_iota(jnp.int32, (1, LANES), 1) < HEAD_DIM
    dk_acc[...] = jnp.zeros_like(dk_acc)
    dv_acc[...] = jnp.zeros_like(dv_acc)
    sum_ref[...] = jnp.zeros_like(sum_ref)

    def split(value):
        zero = jnp.zeros_like(value)
        return jnp.where(first, value, zero), jnp.where(first, zero, value)

    def query_block(i, carry):
        at_q = pl.multiple_of(i * BLOCK, BLOCK)
        own_q = jnp.logical_and(i >= start, i < stop)
        lo = jnp.where(own_q, lo_ref[i], jnp.maximum(lo_ref[i], start))
        hi = jnp.where(own_q, hi_ref[i], jnp.minimum(hi_ref[i], stop))

        @pl.when(own_q)
        def _():
            dq_acc[...] = jnp.zeros_like(dq_acc)

        def key_block(j, carry):
            at_k = pl.multiple_of(j * BLOCK, BLOCK)
            k = k_ref[pl.ds(at_k, BLOCK), :]
            v = v_ref[pl.ds(at_k, BLOCK), :]
            qs = split(q_ref[pl.ds(at_q, BLOCK), :])
            gs = split(g_ref[pl.ds(at_q, BLOCK), :])
            same = spread_lanes(tc_ref[pl.ds(at_k, BLOCK), :], BLOCK) == tr_ref[:, pl.ds(at_q, BLOCK)]
            ps, ds = [], []
            for h in range(2):
                s = dot_nt(k, qs[h])
                p = jnp.where(same, jnp.exp(s - lse_ref[0, h : h + 1, pl.ds(at_q, BLOCK)]), 0.0)
                dp = dot_nt(v, gs[h])
                d = p * (dp - delta_ref[0, h : h + 1, pl.ds(at_q, BLOCK)])
                ps.append(p.astype(bf16))
                ds.append(d.astype(bf16))

            @pl.when(jnp.logical_and(j >= start, j < stop))
            def _():
                at = pl.multiple_of((j - start) * BLOCK, BLOCK)
                dv_acc[pl.ds(at, BLOCK), :] += dot(ps[0], gs[0]) + dot(ps[1], gs[1])
                dk_acc[pl.ds(at, BLOCK), :] += dot(ds[0], qs[0]) + dot(ds[1], qs[1])

            @pl.when(own_q)
            def _():
                ks = split(k)
                dq_acc[...] += dot_tn(ds[0], ks[0]) + dot_tn(ds[1], ks[1])

            return carry

        lax.fori_loop(lo, hi, key_block, 0)

        @pl.when(own_q)
        def _():
            at = pl.multiple_of((i - start) * BLOCK, BLOCK)
            dq = dq_acc[...] * HEAD_DIM ** (-0.5)
            dq_ref[pl.ds(at, BLOCK), :] = dq.astype(bf16)
            sum_ref[0, 0:1, :] += jnp.sum(dq, axis=0, keepdims=True)

        return carry

    lax.fori_loop(0, q_ref.shape[0] // BLOCK, query_block, 0)
    dk_ref[...] = dk_acc[...].astype(bf16)
    dv_ref[...] = dv_acc[...].astype(bf16)
    sum_ref[0, 1:2, :] = jnp.sum(dv_acc[...], axis=0, keepdims=True)


def attend_back(lo, hi, q, k, v, g, tag_cols, tag_row, lse, delta, own_rows, pair):
    window = q.shape[0]
    pairs, wide = 1, LANES
    start = (window - own_rows) // 2 // BLOCK
    stop = start + own_rows // BLOCK
    whole = lambda: pl.BlockSpec((window, LANES), lambda p, a, b: (0, pair))
    own = lambda: pl.BlockSpec((own_rows, LANES), lambda p, a, b: (0, p))
    stat = lambda: pl.BlockSpec((1, 2, window), lambda p, a, b: (pair, 0, 0))
    return pl.pallas_call(
        functools.partial(attend_back_kernel, start, stop),
        out_shape=[jax.ShapeDtypeStruct((own_rows, wide), bf16)] * 3
        + [jax.ShapeDtypeStruct((pairs, 8, LANES), f32)],
        grid_spec=pltpu.PrefetchScalarGridSpec(
            num_scalar_prefetch=2,
            grid=(pairs,),
            in_specs=[
                whole(), whole(), whole(), whole(),
                pl.BlockSpec((window, LANES), lambda p, a, b: (0, 0)),
                pl.BlockSpec((1, window), lambda p, a, b: (0, 0)),
                stat(), stat(),
            ],
            out_specs=[own(), own(), own(), pl.BlockSpec((1, 8, LANES), lambda p, a, b: (p, 0, 0))],
            scratch_shapes=[
                pltpu.VMEM((own_rows, LANES), f32),
                pltpu.VMEM((own_rows, LANES), f32),
                pltpu.VMEM((BLOCK, LANES), f32),
            ],
        ),
        compiler_params=pltpu.CompilerParams(vmem_limit_bytes=40 << 20),
        cost_estimate=pl.CostEstimate(
            flops=180 * own_rows * own_rows * LANES,
            transcendentals=own_rows * own_rows * 2,
            bytes_accessed=window * wide * 8,
        ),
        name="attend_back",
    )(lo, hi, q, k, v, g, tag_cols, tag_row, lse, delta)


def on_device(
    tokens, image_ids, ln1_gain, ln1_bias, qkv_weight, query_bias, value_bias, proj_weight,
    proj_bias, scale_attn, ln2_gain, ln2_bias, fc1_weight, fc1_bias, fc2_weight, fc2_bias,
    scale_mlp, cotangent,
):
    devices = lax.axis_size("fsdp")
    depth, ranks = devices // 2, lax.axis_size("rep")
    place = lax.axis_index("fsdp")
    rank = lax.axis_index("rep")
    here, core = place // 2, place % 2
    count = tokens.shape[1]
    chip = 2 * count
    head_rows = D // devices
    ff = fc1_weight.shape[1]
    unit_rows = ff // devices
    half_heads = D // 2
    local_heads = half_heads // HEAD_DIM
    pairs = half_heads // LANES
    bits = list(range(rep_bits()))

    def in_order(own, other, axis=0):
        return jnp.where(
            core == 0,
            jnp.concatenate([own, other], axis=axis),
            jnp.concatenate([other, own], axis=axis),
        )

    def mine(value):
        return lax.dynamic_slice_in_dim(value, core * count, count, 0)

    def others(value):
        return lax.dynamic_slice_in_dim(value, (1 - core) * count, count, 0)

    def every_other(value, width, start):
        cuts = range(start * width, value.shape[1], 2 * width)
        return jnp.concatenate([value[:, c : c + width] for c in cuts], axis=1)

    even = jnp.concatenate(
        [every_other(qkv_weight, head_rows, 0), every_other(fc1_weight, unit_rows, 0)], axis=1
    )
    odd = jnp.concatenate(
        [every_other(qkv_weight, head_rows, 1), every_other(fc1_weight, unit_rows, 1)], axis=1
    )
    kept, given = jnp.where(core == 0, even, odd), jnp.where(core == 0, odd, even)
    small = (
        ln1_gain, ln1_bias, query_bias, value_bias, proj_bias, scale_attn, ln2_gain, ln2_bias,
        fc2_bias, scale_mlp, fc1_bias, (image_ids[0] + 1).astype(bf16),
    )
    sizes = [v.shape[0] for v in small]
    slots = slot_lists(sizes)
    width = 2 * D // ranks
    small = pack_small(small, width, slots)
    paired = in_order(kept, swap_cores(given))
    small_other = swap_cores(small)
    proj_packed = jnp.concatenate([proj_weight[:, :half_heads], proj_weight[:, half_heads:]], axis=0)
    group1 = jnp.concatenate([paired[:, : 3 * half_heads], proj_packed], axis=1)
    group2 = paired[:, 3 * half_heads :]

    def own_columns(group):
        width = group.shape[1] // ranks
        return lax.dynamic_slice_in_dim(group, rank * width, width, 1)

    own1, own2, own3 = own_columns(group1), own_columns(group2), own_columns(fc2_weight)
    rows1, rows3 = own1.shape[0], own3.shape[0]
    tok_other = swap_cores(tokens[0])
    cot_other = swap_cores(cotangent[0])
    own1 = jnp.concatenate([own1, small, small_other])
    own1, own2, own3, tok, cot, tok_other, cot_other = tie(
        own1, own2, own3, tokens[0], cotangent[0], tok_other, cot_other
    )
    pieces1 = fetch_z(own1)
    tok, pieces1[1] = tie(tok, pieces1[1])
    behind, ahead = from_chip(tok, 1), from_chip(tok, -1)
    own2, *pieces1 = tie(own2, *pieces1)
    gather1 = Gather(pieces1, rows1, "gather1")
    own2, behind, ahead = gather1.send(own2, behind, ahead)
    behind_other, ahead_other = swap_cores(behind), swap_cores(ahead)
    pieces2 = fetch_z(own2)

    vec_rows, fc1_shift, all_tags = unpack_small(
        pieces1, slots, rows1, here, core, ff // 2, devices * count
    )
    vector = lambda i: vec_rows[i : i + 1]
    (
        attn_gain, attn_shift, query_shift, value_shift, proj_shift, attn_scale, mlp_gain,
        mlp_shift, fc2_shift, mlp_scale,
    ) = map(vector, range(10))
    core_part = lambda vec: jnp.where(
        core == 0, every_other(vec, head_rows, 0), every_other(vec, head_rows, 1)
    )

    window = 3 * chip
    padded = jnp.concatenate(
        [jnp.zeros((1, chip), f32), all_tags, jnp.full((1, chip), 1e6, f32)], axis=1
    )
    tag_row = lax.dynamic_slice(padded, (0, here * chip), (1, window))
    tags = tag_row.reshape(window)
    firsts, lasts = tags[::BLOCK], tags[BLOCK - 1 :: BLOCK]
    real = firsts * (1e6 - firsts) > 0
    below = jnp.sum((tag_row < firsts[:, None]).astype(jnp.int32), axis=1)
    upto = jnp.sum((tag_row <= lasts[:, None]).astype(jnp.int32), axis=1)
    blocks = window // BLOCK
    block_lo = jnp.where(real, below // BLOCK, 0)
    block_hi = jnp.where(real, (upto + BLOCK - 1) // BLOCK, 0)
    own_lo, own_hi = chip // BLOCK, 2 * chip // BLOCK
    numbers = jnp.arange(blocks)
    need = jnp.logical_and(numbers >= block_lo[own_lo], numbers < block_hi[own_hi - 1]).astype(jnp.int32)
    firsts, lasts = firsts.astype(jnp.int32), lasts.astype(jnp.int32)
    tag_cols = jnp.broadcast_to(tags[:, None], (window, LANES))

    info = jnp.stack([core, jnp.int32(count // BLOCK)]).astype(jnp.int32)
    normed1 = norm_window(
        need, info, (behind, behind_other, tok, tok_other, ahead, ahead_other), vec_rows, window, count
    )

    normed1 = gather1.arrive(normed1)
    normed1, own3 = gather1.send(normed1, own3)
    for _ in bits[2:]:
        normed1 = gather1.arrive(normed1)
        normed1 = gather1.send(normed1)
    normed1, *pieces2 = tie(normed1, *pieces2)
    gather2 = Gather(pieces2, rows1, "gather2")
    normed1, own3 = gather2.send(normed1, own3)
    pieces3 = fetch_z(own3)
    normed1 = gather1.arrive(normed1)
    qkv_matrix, proj_matrix = gather1.assemble(here, rank, head_rows)

    shifts = jnp.concatenate(
        [core_part(query_shift), jnp.zeros((1, half_heads), f32), core_part(value_shift)], axis=1
    )
    queries, keys, values = project(need, normed1, qkv_matrix, shifts, half_heads)

    contexts, lses = [], []
    los = block_lo[own_lo:own_hi]
    los, queries = tie(los, queries)
    for pair in range(pairs):
        if pair == 1:
            los = gather2.arrive(los)
            los, *pieces3 = tie(los, *pieces3)
            gather3 = Gather(pieces3, rows3, "gather3")
            los = gather2.send(los)
            los = gather3.send(los)
        if pair == 3:
            los = gather2.arrive(los)
            los = gather3.arrive(los)
            for _ in bits[2:]:
                los = gather2.send(los)
                los = gather2.arrive(los)
            los = gather3.send(los)
        context, lse = attend(
            los, block_hi[own_lo:own_hi], firsts, lasts, queries, keys, values, tag_cols,
            tag_row, chip, pair,
        )
        los, context = tie(los, context)
        contexts.append(context)
        lses.append(lse)
    context = jnp.concatenate(contexts, axis=1)
    lse_rows = jnp.concatenate(lses).reshape(local_heads, chip)
    fc1_matrix = gather2.assemble(here, rank)

    features = tok.astype(f32)
    sent = swap_cores(dot(others(context), proj_matrix))
    attn_out = dot(mine(context), proj_matrix) + sent + proj_shift
    resid = features + attn_scale * attn_out
    mlp_normal, mlp_inverse = normalize(resid)
    mlp_input = (mlp_normal * mlp_gain + mlp_shift).astype(bf16)
    mlp_input = jnp.concatenate([mlp_input, swap_cores(mlp_input)])
    pre_act = dot(mlp_input, fc1_matrix) + fc1_shift
    activated, slope = gelu_pair(pre_act)
    activated = activated.astype(bf16)

    out_grad = cot.astype(f32)
    mlp_grad_full = out_grad * mlp_scale
    mlp_grad = (jnp.concatenate([cot, cot_other]).astype(f32) * mlp_scale).astype(bf16)

    activated = gather3.arrive(activated)
    for _ in bits[2:]:
        activated = gather3.send(activated)
        activated = gather3.arrive(activated)
    fc2_matrix = gather3.assemble(here, rank)
    fc2_grad = dot_tn(activated, mlp_grad).astype(bf16)
    reduce3 = Reduce(relative_blocks(fc2_grad, rank, [bits]), here, [bits])
    activated, fc2_matrix = reduce3.send(activated, fc2_matrix)
    sent = swap_cores(dot(activated[count:], fc2_matrix))
    mlp_out = dot(activated[:count], fc2_matrix) + sent + fc2_shift
    output_rows = (resid + mlp_scale * mlp_out).astype(bf16)
    pre_grad_full = dot_nt(mlp_grad, fc2_matrix) * slope
    pre_grad = pre_grad_full.astype(bf16)
    fc1_bias_part = jnp.sum(pre_grad_full, axis=0, keepdims=True)

    fc1_grad = dot_tn(mlp_input, pre_grad).astype(bf16)
    reduce2 = Reduce(relative_blocks(fc1_grad, rank, [bits[::-1]]), here, [bits[::-1]])
    pre_grad = reduce2.send(pre_grad)
    sent = swap_cores(dot_nt(pre_grad[count:], fc1_matrix))
    mlp_in_grad = dot_nt(pre_grad[:count], fc1_matrix) + sent
    resid_grad = out_grad + norm_back(mlp_in_grad, mlp_normal, mlp_inverse, mlp_gain)
    attn_grad_full = resid_grad * attn_scale
    attn_grad = attn_grad_full.astype(bf16)
    attn_grad = in_order(attn_grad, swap_cores(attn_grad))
    context_grad = dot_nt(attn_grad, proj_matrix).astype(bf16)
    head_of = (
        lax.broadcasted_iota(jnp.int32, (local_heads, half_heads), 1) // HEAD_DIM
        == lax.broadcasted_iota(jnp.int32, (local_heads, half_heads), 0)
    ).astype(f32)
    row_delta = lax.dot_general(
        head_of, context_grad.astype(f32) * context.astype(f32), (((1,), (1,)), ((), ())),
        precision=lax.Precision.HIGHEST, preferred_element_type=f32,
    )
    stats = jnp.concatenate([lse_rows, row_delta])
    grads_behind, grads_ahead = from_chip(context_grad, 1), from_chip(context_grad, -1)
    stats_behind, stats_ahead = from_chip(stats, 1), from_chip(stats, -1)
    proj_grad = packed_proj_grad(context, attn_grad, head_rows)
    grad_window = jnp.concatenate([grads_behind, context_grad, grads_ahead])
    stat_window = jnp.concatenate([stats_behind, stats, stats_ahead], axis=1)
    by_pair = lambda s: s.reshape(pairs, 2, window)
    lse_window, delta_window = by_pair(stat_window[:local_heads]), by_pair(stat_window[local_heads:])

    half_pairs = pairs // 2
    half_width = half_heads // 2
    both = [bits, bits[::-1]]

    def first_group(parts, number):
        grads = [g for kind in zip(*parts) for g in kind]
        return Reduce(
            qkv_grad_blocks(normed1, grads, proj_grad, number, 2, rank, both), here, both
        )

    parts, sums = [], []
    lo, delta_window = tie(block_lo, delta_window)
    for pair in range(pairs):
        if pair == 0:
            lo = reduce3.arrive(lo)
            for _ in bits[2:]:
                lo = reduce3.arrive(reduce3.send(lo))
            lo = reduce3.send(lo)
        if pair == 1:
            lo = reduce3.arrive(lo)
            lo = reduce3.send_z(lo)
            lo = reduce2.arrive(lo)
            for _ in bits[2:]:
                lo = reduce2.arrive(reduce2.send(lo))
            lo = reduce2.send(lo)
        if pair == 2:
            lo = reduce2.arrive(lo)
            lo = reduce2.send_z(lo)
            reduce1a = first_group(parts, 0)
            lo = reduce1a.send(lo)
        if pair == 3:
            lo = reduce3.arrive_z(lo)
            lo = reduce2.arrive_z(lo)
            fc2_part = reduce3.total.astype(bf16)
            fc1_part = reduce2.total.astype(bf16)
            split = fc2_part.shape[0] // fc1_part.shape[0]
            mlp_part = jnp.concatenate([fc1_part, *jnp.split(fc2_part, split)], axis=1)[None]
            mlp_offsets = [0]
            lo, mlp_part = tie(lo, mlp_part)
            mlp_more = across_rep(mlp_part, 0)
            lo = reduce1a.arrive(lo)
            for _ in bits[2:]:
                lo = reduce1a.arrive(reduce1a.send(lo))
            lo = reduce1a.send(lo)
        *grads, total = attend_back(
            lo, block_hi, queries, keys, values, grad_window, tag_cols, tag_row, lse_window,
            delta_window, chip, pair,
        )
        lo, *grads = tie(lo, *grads)
        parts.append(grads)
        sums.append(total[0])

    reduce1b = first_group(parts[half_pairs:], 1)
    lo = reduce1b.send(lo)
    every = [jnp.concatenate(p, axis=1) for p in zip(*parts)]
    every[0], mlp_more, lo = tie(every[0], mlp_more, lo)
    for later in bits[1:] + [None]:
        mlp_part = jnp.concatenate([mlp_part, mlp_more])
        flip = 1 << (len(mlp_offsets).bit_length() - 1)
        mlp_offsets = mlp_offsets + [o ^ flip for o in mlp_offsets]
        if later is not None:
            mlp_more = across_rep(mlp_part, later)
    reduce1a.arrive(lo)
    every[0] = reduce1a.send_z(every[0])

    factor = 1.0 / math.sqrt(count * devices * ranks)
    qkv_grad = jnp.concatenate(every, axis=1)
    sent = swap_cores(dot_nt(others(qkv_grad), qkv_matrix))
    attn_in_grad = dot_nt(mine(qkv_grad), qkv_matrix) + sent
    for _ in bits[1:]:
        attn_in_grad = reduce1b.arrive(attn_in_grad)
        attn_in_grad = reduce1b.send(attn_in_grad)
    attn_normal, attn_inverse = normalize(features)
    input_rows = resid_grad + norm_back(attn_in_grad, attn_normal, attn_inverse, attn_gain)

    columns = lambda value: jnp.sum(value, axis=0, keepdims=True)
    vectors = (
        columns(attn_in_grad * attn_normal), columns(attn_in_grad),
        jnp.concatenate([s[0:1] for s in sums], axis=1), jnp.concatenate([s[1:2] for s in sums], axis=1),
        columns(attn_grad_full), columns(resid_grad * attn_out),
        columns(mlp_in_grad * mlp_normal), columns(mlp_in_grad),
        columns(mlp_grad_full), columns(out_grad * mlp_out), fc1_bias_part,
    )
    of_core = [number in (2, 3, 10) for number in range(11)]
    partial = pack_grads(vectors, list(zip(sizes, of_core)), core, depth)
    partial = reduce1b.arrive(partial)
    partial = reduce1b.send_z(partial)

    vec_total = pick(partial, here, 0)
    for k in range(1, depth):
        vec_total = vec_total + along_z(pick(partial, lax.rem(here + k, depth), 0), k)
    reduce1a.arrive_z(lo)
    vec_total = reduce1b.arrive_z(vec_total)
    first_part = jnp.concatenate([reduce1a.total, reduce1b.total], axis=1).astype(bf16)[None]
    first_offsets = [0]
    for bit in bits:
        received = across_rep(first_part, bit)
        vec_total = vec_total + across_rep(vec_total, bit)
        first_part = jnp.concatenate([first_part, received])
        first_offsets = first_offsets + [o ^ (1 << bit) for o in first_offsets]
    vec_half = vec_total.reshape(2, 16, LANES)
    totals = (pick(vec_half, core, 0) + swap_cores(pick(vec_half, 1 - core, 0))) * factor

    mlp_cols = fc1_part.shape[1]
    fc1_full = rep_blocks(mlp_part[:, :, :mlp_cols], mlp_offsets, rank)
    fc2_width = fc2_part.shape[1]
    grad_fc2 = jnp.concatenate(
        [
            rep_blocks(
                mlp_part[:, :, mlp_cols + n * fc2_width : mlp_cols + (n + 1) * fc2_width], mlp_offsets, rank
            )
            for n in range(split)
        ]
    ).astype(f32) * factor
    vec_width = D // ranks
    first_a = rep_blocks(first_part[:, :, :vec_width], first_offsets, rank)
    first_b = rep_blocks(first_part[:, :, vec_width:], first_offsets, rank)

    def rows_of(value, index):
        return lax.dynamic_slice_in_dim(value, index * head_rows, head_rows, 0)

    def interleave(own, other, width):
        cuts = range(0, own.shape[1], width)
        zipped = lambda a, b: jnp.concatenate(
            [v[:, c : c + width] for c in cuts for v in (a, b)], axis=1
        )
        return jnp.where(core == 0, zipped(own, other), zipped(other, own)).astype(f32) * factor

    fc1_other = swap_cores(rows_of(fc1_full, 1 - core))
    grad_fc1 = interleave(rows_of(fc1_full, core), fc1_other, unit_rows)
    qkv_full = jnp.concatenate(
        [
            part[:, n * half_width : (n + 1) * half_width]
            for n in range(3)
            for part in (first_a, first_b)
        ],
        axis=1,
    )
    grad_qkv = interleave(rows_of(qkv_full, core), swap_cores(rows_of(qkv_full, 1 - core)), head_rows)
    proj_part = jnp.concatenate([first_a[:, 3 * half_width :], first_b[:, 3 * half_width :]], axis=1)
    grad_proj = jnp.concatenate([proj_part[:head_rows], proj_part[head_rows:]], axis=1).astype(f32) * factor

    small_grads = [totals[i, : sizes[i]] for i in range(10)]
    lines = -(-sizes[10] // LANES)
    small_grads.append(totals[10 : 10 + lines].reshape(-1))
    (
        grad_attn_gain, grad_attn_shift, grad_query_shift, grad_value_shift, grad_proj_shift,
        grad_attn_scale, grad_mlp_gain, grad_mlp_shift, grad_fc2_shift, grad_mlp_scale, grad_fc1_shift,
    ) = small_grads

    return (
        output_rows[None],
        input_rows[None],
        grad_attn_gain,
        grad_attn_shift,
        grad_qkv,
        grad_query_shift,
        grad_value_shift,
        grad_proj,
        grad_proj_shift,
        grad_attn_scale,
        grad_mlp_gain,
        grad_mlp_shift,
        grad_fc1,
        grad_fc1_shift,
        grad_fc2,
        grad_fc2_shift,
        grad_mlp_scale,
    )


def solution(mesh):
    rows = P("fsdp", None)
    vec = P("fsdp")
    tok = P("rep", "fsdp", None)
    return jax.shard_map(
        on_device,
        mesh=mesh,
        in_specs=(
            tok, P("rep", "fsdp"), vec, vec, rows, vec, vec, rows, vec, vec, vec, vec, rows, vec,
            rows, vec, vec, tok,
        ),
        out_specs=(
            tok, tok, vec, vec, rows, vec, vec, rows, vec, vec, vec, vec, rows, vec, rows, vec, vec,
        ),
        check_vma=False,
    )
```

```python
import functools
import math

import jax
import jax.numpy as jnp
from jax import lax
from jax.experimental import pallas as pl
from jax.experimental.pallas import tpu as pltpu
from jax.sharding import PartitionSpec as P

D = 1024
HEADS = 16
HEAD_DIM = 64
LANES = 128

EPSILON = 1e-06
MASKED = -1e30
BLOCK = 256

SHORT = pl.CostEstimate(flops=1, transcendentals=0, bytes_accessed=1)

f32 = jnp.float32
bf16 = jnp.bfloat16


def normalize(features):
    row_mean = jnp.mean(features, axis=-1, keepdims=True)
    centred = features - row_mean
    variance = jnp.mean(centred * centred, axis=-1, keepdims=True)
    inverse = lax.rsqrt(variance + EPSILON)
    return centred * inverse, inverse


def norm_back(gradient, normal, inverse, gain_vec):
    scaled = gradient * gain_vec
    mean_first = jnp.mean(scaled, axis=-1, keepdims=True)
    mean_second = jnp.mean(scaled * normal, axis=-1, keepdims=True)
    return inverse * (scaled - mean_first - normal * mean_second)


def gelu_pair(values):
    cumulative = 0.5 * (1.0 + lax.erf(values * 2.0 ** (-0.5)))
    density = jnp.exp(-0.5 * values * values) * (2.0 * math.pi) ** (-0.5)
    return (values * cumulative, cumulative + values * density)


def dot(a, b):
    return jnp.dot(a, b, preferred_element_type=f32)


def dot_nt(a, b):
    return lax.dot_general(a, b, (((1,), (1,)), ((), ())), preferred_element_type=f32)


def dot_tn(a, b):
    return lax.dot_general(a, b, (((0,), (0,)), ((), ())), preferred_element_type=f32)


def swap_cores(value):
    size = lax.axis_size("fsdp")
    return lax.ppermute(value, "fsdp", [(i, i ^ 1) for i in range(size)])


def along_z(value, by):
    size = lax.axis_size("fsdp")
    return lax.ppermute(value, "fsdp", [(i, (i + 2 * by) % size) for i in range(size)])


def from_chip(value, by):
    size = lax.axis_size("fsdp")
    pairs = [(i, i + 2 * by) for i in range(size) if 0 <= i + 2 * by < size]
    return lax.ppermute(value, "fsdp", pairs)


def across_rep(value, bit):
    size = lax.axis_size("rep")
    return lax.ppermute(value, "rep", [(i, i ^ (1 << bit)) for i in range(size)])


def pick(value, index, axis):
    return lax.dynamic_index_in_dim(value, index, axis, keepdims=False)


def rep_bits():
    return lax.axis_size("rep").bit_length() - 1


def tie(*values):
    return lax.optimization_barrier(values)


def settle(value, *fields):
    held = [getattr(o, name) for o, name in fields]
    value, held = lax.optimization_barrier((value, held))
    for (o, name), new in zip(fields, held):
        setattr(o, name, new)
    return value


def fetch_z(own):
    return [own] + [along_z(own, k) for k in range(1, lax.axis_size("fsdp") // 2)]


class Gather:
    def __init__(self, pieces, rows, name):
        self.rows, self.cols, self.name = rows, pieces[0].shape[1], name
        half = rows // 2
        bits = list(range(rep_bits()))
        self.orders = [bits, bits[::-1]]
        self.parts = [
            [(jnp.stack([p[:half] for p in pieces])[None], [0])],
            [(jnp.stack([p[half:rows] for p in pieces])[None], [0])],
        ]
        self.at = 0

    def send(self, *values):
        whole = [
            (ps[0][0] if len(ps) == 1 else jnp.concatenate([a for a, _ in ps]), [o for _, os in ps for o in os])
            for ps in self.parts
        ]
        values, arrays = lax.optimization_barrier((values, [a for a, _ in whole]))
        self.parts = []
        for array, (_, offsets), order in zip(arrays, whole, self.orders):
            flip = 1 << order[self.at]
            received = across_rep(array, order[self.at])
            self.parts.append([(array, offsets), (received, [o ^ flip for o in offsets])])
        self.at += 1
        return values[0] if len(values) == 1 else values

    def arrive(self, value):
        value, arrays = lax.optimization_barrier((value, [a for ps in self.parts for a, _ in ps]))
        self.parts = [[(arrays.pop(0), o) for _, o in ps] for ps in self.parts]
        return value

    def assemble(self, here, rank, tail_rows=0):
        depth, ranks = lax.axis_size("fsdp") // 2, lax.axis_size("rep")
        sources, plan = [], []
        for number, parts in enumerate(self.parts):
            for array, offsets in parts:
                sources.append(array)
                plan.append((number, offsets))
        dtype = sources[0].dtype
        shape = (depth * self.rows, ranks * self.cols)
        shapes = [jax.ShapeDtypeStruct(shape, dtype)]
        if tail_rows:
            tail = shape[1] // 4
            shapes = [
                jax.ShapeDtypeStruct((shape[0], shape[1] - tail), dtype),
                jax.ShapeDtypeStruct((depth * tail_rows, 2 * tail), dtype),
            ]
        out = pl.pallas_call(
            functools.partial(assemble_kernel, plan, depth, self.rows, self.cols, tail_rows),
            out_shape=shapes,
            grid_spec=pltpu.PrefetchScalarGridSpec(
                num_scalar_prefetch=1,
                grid=(1,),
                in_specs=[pl.BlockSpec(memory_space=pl.ANY)] * len(sources),
                out_specs=[pl.BlockSpec(memory_space=pl.ANY)] * len(shapes),
                scratch_shapes=[
                    pltpu.VMEM(shape, dtype),
                    pltpu.SemaphoreType.DMA((2 * ranks * depth,)),
                    pltpu.SemaphoreType.DMA((3 * depth,)),
                ],
            ),
            compiler_params=pltpu.CompilerParams(vmem_limit_bytes=16 << 20),
            cost_estimate=SHORT,
            name=self.name,
        )(jnp.stack([here, rank]).astype(jnp.int32), *sources)
        return out if tail_rows else out[0]


def assemble_kernel(plan, depth, rows, cols, tail_rows, index_ref, *refs):
    count = len(plan)
    sources = refs[:count]
    targets = refs[count : count + (2 if tail_rows else 1)]
    held, in_sems, out_sems = refs[-3:]
    here, rank = index_ref[0], index_ref[1]
    half = rows // 2
    waits = [[] for _ in range(depth)]
    number = 0
    for k in range(depth):
        place = lax.rem(here - k + depth, depth)
        for which, (colour, offsets) in enumerate(plan):
            for m, offset in enumerate(offsets):
                at_row = pl.multiple_of(place * rows + colour * half, half)
                at_col = pl.multiple_of((rank ^ offset) * cols, cols)
                copy = pltpu.make_async_copy(
                    sources[which].at[m, k],
                    held.at[pl.ds(at_row, half), pl.ds(at_col, cols)],
                    in_sems.at[number],
                )
                copy.start()
                waits[k].append(copy)
                number += 1
    outs = []
    main = targets[0].shape[1]
    for k in range(depth):
        place = lax.rem(here - k + depth, depth)
        for copy in waits[k]:
            copy.wait()
        base = pl.multiple_of(place * rows, rows)
        band = pl.ds(base, rows)
        out = pltpu.make_async_copy(held.at[band, pl.ds(0, main)], targets[0].at[band], out_sems.at[3 * k])
        out.start()
        outs.append(out)
        if tail_rows:
            wide = targets[1].shape[1] // 2
            for side in range(2):
                out = pltpu.make_async_copy(
                    held.at[pl.ds(base + side * tail_rows, tail_rows), pl.ds(main, wide)],
                    targets[1].at[
                        pl.ds(pl.multiple_of(place * tail_rows, tail_rows), tail_rows),
                        pl.ds(side * wide, wide),
                    ],
                    out_sems.at[3 * k + 1 + side],
                )
                out.start()
                outs.append(out)
    for out in outs:
        out.wait()


def halves(ranks, bit, held):
    flip = 1 << bit
    kept = [o for o in held if not o & flip]
    return kept, [o ^ flip for o in kept]


def relative_blocks(grads, rank, orders):
    depth, ranks = lax.axis_size("fsdp") // 2, lax.axis_size("rep")
    width = grads.shape[1] // ranks
    rows = grads.shape[0] // depth
    shaped = grads.reshape(depth, rows, grads.shape[1])
    share = rows // len(orders)
    first = []
    for n, order in enumerate(orders):
        block = lambda o: lax.dynamic_slice(
            shaped, (0, n * share, (rank ^ o) * width), (depth, share, width)
        )
        kept, given = halves(ranks, order[0], list(range(ranks)))
        first.append((jnp.stack([block(o) for o in kept]), jnp.stack([block(o) for o in given])))
    return first


class Reduce:
    def __init__(self, first, here, orders):
        self.here, self.orders, self.at = here, orders, 0
        ranks = lax.axis_size("rep")
        self.held = []
        for (keep, give), order in zip(first, orders):
            kept, given = halves(ranks, order[0], list(range(ranks)))
            self.held.append((kept, keep, give))

    def send(self, *values):
        values, gives = lax.optimization_barrier((values, [give for _, _, give in self.held]))
        self.received = [across_rep(g, order[self.at]) for g, order in zip(gives, self.orders)]
        self.at += 1
        return values[0] if len(values) == 1 else values

    def arrive(self, *values):
        values, received = lax.optimization_barrier((values, self.received))
        held = []
        for (kept, keep, _), got, order in zip(self.held, received, self.orders):
            total = (keep.astype(f32) + got.astype(f32)).astype(bf16)
            if self.at < len(order):
                stay, leave = halves(None, order[self.at], kept)
                take = lambda os: jnp.stack([total[kept.index(o)] for o in os])
                held.append((stay, take(stay), take(leave)))
            else:
                held.append((kept, total[0], None))
        self.held = held
        return values[0] if len(values) == 1 else values

    def send_z(self, *values):
        depth = lax.axis_size("fsdp") // 2
        parts = [keep for _, keep, _ in self.held]
        whole = parts[0] if len(parts) == 1 else jnp.concatenate(parts, axis=1)
        pieces = [pick(whole, lax.rem(self.here + k, depth), 0) for k in range(depth)]
        values, pieces = lax.optimization_barrier((values, pieces))
        self.pieces = [pieces[0]] + [along_z(p, k) for k, p in enumerate(pieces) if k]
        return values[0] if len(values) == 1 else values

    def arrive_z(self, *values):
        values, pieces = lax.optimization_barrier((values, self.pieces))
        total = pieces[0].astype(f32)
        for piece in pieces[1:]:
            total = total + piece.astype(f32)
        self.total = total
        return values[0] if len(values) == 1 else values


class Spread:
    def __init__(self, value):
        bits = list(range(rep_bits()))
        self.orders = [bits, bits[::-1]]
        half = value.shape[0] // 2
        self.arrays = [value[:half][None], value[half:][None]]
        self.offsets = [[0], [0]]
        self.at = 0

    def send(self, *values):
        values, arrays = lax.optimization_barrier((values, self.arrays))
        self.arrays = []
        for n, (array, order) in enumerate(zip(arrays, self.orders)):
            flip = 1 << order[self.at]
            received = across_rep(array, order[self.at])
            self.arrays.append(jnp.concatenate([array, received]))
            self.offsets[n] = self.offsets[n] + [o ^ flip for o in self.offsets[n]]
        self.at += 1
        return values[0] if len(values) == 1 else values

    def blocks(self, rank, start, size):
        return jnp.concatenate(
            [rep_blocks(a[:, :, start : start + size], o, rank) for a, o in zip(self.arrays, self.offsets)]
        )


def rep_blocks(stacked, offsets, rank):
    blocks = []
    for i in range(len(offsets)):
        block = stacked[0]
        for entry, offset in enumerate(offsets):
            block = jnp.where((rank ^ offset) == i, stacked[entry], block)
        blocks.append(block)
    return jnp.concatenate(blocks, axis=1)


def share_kernel(widths, index_ref, qkv_ref, proj_ref, fc1_ref, keep_ref, give_ref, sems):
    rank, core = index_ref[0], index_ref[1]
    wide1, wide2, block, unit, half = widths
    is_proj = rank * wide1 >= 3 * half

    def copies(second):
        made = []
        for out, (ref, which) in enumerate(((keep_ref, core), (give_ref, 1 - core))):
            for c in range(wide1 // block):
                col = rank * wide1 + c * block
                if second:
                    source, at = proj_ref, which * half + col - 3 * half
                else:
                    source, at = qkv_ref, 2 * col + which * block
                made.append((source, at, block, ref, c * block))
        return made

    def run(plan, first):
        started = []
        for n, (source, at, size, ref, to) in enumerate(plan):
            copy = pltpu.make_async_copy(
                source.at[:, pl.ds(pl.multiple_of(at, LANES), size)], ref.at[:, pl.ds(to, size)], sems.at[first + n]
            )
            copy.start()
            started.append(copy)
        return started

    col = rank * wide2
    plan2 = []
    for ref, which in ((keep_ref, core), (give_ref, 1 - core)):
        at = col + (lax.div(col, unit) + which) * unit
        plan2.append((fc1_ref, at, wide2, ref, wide1))
    second = run(plan2, 0)

    @pl.when(is_proj)
    def _():
        for copy in run(copies(True), 2):
            copy.wait()

    @pl.when(jnp.logical_not(is_proj))
    def _():
        for copy in run(copies(False), 2):
            copy.wait()

    for copy in second:
        copy.wait()


def weight_share(rank, core, qkv_weight, proj_weight, fc1_weight, ranks, block, unit):
    rows = qkv_weight.shape[0]
    wide1, wide2 = 2 * D // ranks, fc1_weight.shape[1] // 2 // ranks
    out = jax.ShapeDtypeStruct((rows, wide1 + wide2), bf16)
    return pl.pallas_call(
        functools.partial(share_kernel, (wide1, wide2, block, unit, D // 2)),
        out_shape=[out, out],
        grid_spec=pltpu.PrefetchScalarGridSpec(
            num_scalar_prefetch=1,
            grid=(1,),
            in_specs=[pl.BlockSpec(memory_space=pl.ANY)] * 3,
            out_specs=[pl.BlockSpec(out.shape, lambda i, a: (0, 0))] * 2,
            scratch_shapes=[pltpu.SemaphoreType.DMA((2 + 2 * (wide1 // block),))],
        ),
        cost_estimate=SHORT,
        name="weight_share",
    )(jnp.stack([rank, core]).astype(jnp.int32), qkv_weight, proj_weight, fc1_weight)


def whole_specs(arrays):
    return [pl.BlockSpec(a.shape, lambda *_, n=len(a.shape): (0,) * n) for a in arrays]


def slot_lists(sizes):
    slots = []
    for number, size in enumerate(sizes):
        for start in range(0, size, LANES):
            slots.append((number, start, min(LANES, size - start)))
    return slots


def pack_kernel(slots, *refs):
    *sources, out_ref, held = refs
    per_row = held.shape[1] // LANES
    held[...] = jnp.zeros_like(held)
    for slot, (number, start, size) in enumerate(slots):
        row, at = slot // per_row, slot % per_row * LANES
        held[row : row + 1, at : at + size] = sources[number][:, start : start + size].astype(f32)
    out_ref[...] = held[...].astype(out_ref.dtype)


def pack_small(vectors, width, slots):
    shape = (32 * LANES // width, width)
    vectors = [v.reshape(1, -1) for v in vectors]
    return pl.pallas_call(
        functools.partial(pack_kernel, slots),
        out_shape=jax.ShapeDtypeStruct(shape, bf16),
        scratch_shapes=[pltpu.VMEM(shape, f32)],
        name="pack_small",
    )(*vectors)


def unpack_kernel(slots, depth, index_ref, *refs):
    pieces, (vec_ref, unit_ref, tag_ref) = refs[:depth], refs[depth:]
    here, core = index_ref[0], index_ref[1]
    rows, width = pieces[0].shape
    per_row = width // LANES
    single = sum(1 for number, _, _ in slots if number < 10)
    vec_ref[...] = jnp.zeros_like(vec_ref)
    for k in range(depth):
        place = lax.rem(here - k + depth, depth)
        values = pieces[k][...].astype(f32)

        def part(side, slot, size):
            row, at = side * (rows // 2) + slot // per_row, slot % per_row * LANES
            return values[row : row + 1, at : at + size]

        for slot, (number, start, size) in enumerate(slots):
            own, other = part(0, slot, size), part(1, slot, size)
            first = jnp.where(core == 0, own, other)
            second = jnp.where(core == 0, other, own)
            if number < 10:
                at = pl.multiple_of(place * 2 * size, 2 * size)
                vec_ref[number : number + 1, pl.ds(at, 2 * size)] = jnp.concatenate([first, second], axis=1)
            elif number == 10:
                wide = unit_ref.shape[1] // depth
                unit_ref[0:1, pl.ds(pl.multiple_of(place * wide + start, LANES), LANES)] = own
            else:
                wide = tag_ref.shape[1] // depth
                at = pl.multiple_of(place * wide + start, LANES)
                tag_ref[0:1, pl.ds(at, LANES)] = first
                tag_ref[0:1, pl.ds(pl.multiple_of(at + wide // 2, LANES), LANES)] = second


def unpack_small(pieces, slots, rows, here, core, units, group_tokens):
    depth = len(pieces)
    extra, width = pieces[0].shape[0] - rows, pieces[0].shape[1]
    shapes = [(16, D), (1, units), (1, group_tokens)]
    return pl.pallas_call(
        functools.partial(unpack_kernel, slots, depth),
        out_shape=[jax.ShapeDtypeStruct(s, f32) for s in shapes],
        grid_spec=pltpu.PrefetchScalarGridSpec(
            num_scalar_prefetch=1,
            grid=(1,),
            in_specs=[pl.BlockSpec((extra, width), lambda i, a: (rows // extra, 0))] * depth,
            out_specs=[pl.BlockSpec(s, lambda i, a: (0, 0)) for s in shapes],
        ),
        name="unpack_small",
    )(jnp.stack([here, core]).astype(jnp.int32), *pieces)


def pack_grads_kernel(depth, sizes, index_ref, *refs):
    *sources, out_ref = refs
    core = index_ref[0]
    out_ref[...] = jnp.zeros_like(out_ref)
    for z in range(depth):
        for c in range(2):
            row = 16 * c
            for source, (size, of_core) in zip(sources, sizes):
                for start in range(0, size, LANES):
                    lanes = min(LANES, size - start)
                    at = (z if of_core else 2 * z + c) * size + start
                    value = source[0:1, at : at + lanes]
                    if of_core:
                        value = jnp.where(core == c, value, 0.0)
                    out_ref[z, row : row + 1, 0:lanes] = value
                    row += 1


def pack_grads(vectors, sizes, core, depth):
    return pl.pallas_call(
        functools.partial(pack_grads_kernel, depth, sizes),
        out_shape=jax.ShapeDtypeStruct((depth, 32, LANES), f32),
        grid_spec=pltpu.PrefetchScalarGridSpec(
            num_scalar_prefetch=1,
            grid=(1,),
            in_specs=whole_specs(vectors),
            out_specs=pl.BlockSpec((depth, 32, LANES), lambda i, a: (0, 0, 0)),
        ),
        name="pack_grads",
    )(core.reshape(1).astype(jnp.int32), *vectors)


def grad_blocks_kernel(orders, ranks, index_ref, a_ref, b_ref, *refs):
    outs, held = refs[:-1], refs[-1]
    rank = index_ref[0]
    held[...] = dot_tn(a_ref[...], b_ref[...]).astype(bf16)
    width = held.shape[1] // ranks
    share = held.shape[0] // len(orders)
    for n, order in enumerate(orders):
        for which, offsets in enumerate(halves(ranks, order[0], list(range(ranks)))):
            for i, o in enumerate(offsets):
                cols = pl.ds(pl.multiple_of((rank ^ o) * width, width), width)
                outs[2 * n + which][i, 0] = held[n * share : (n + 1) * share, cols]


def grad_blocks(a, b, rank, orders, name):
    depth, ranks = lax.axis_size("fsdp") // 2, lax.axis_size("rep")
    tokens, rows, cols = a.shape[0], a.shape[1] // depth, b.shape[1]
    if cols // ranks % LANES:
        return relative_blocks(dot_tn(a, b).astype(bf16), rank, orders)
    block = (ranks // 2, depth, rows // len(orders), cols // ranks)
    outs = pl.pallas_call(
        functools.partial(grad_blocks_kernel, orders, ranks),
        out_shape=[jax.ShapeDtypeStruct(block, bf16)] * (2 * len(orders)),
        grid_spec=pltpu.PrefetchScalarGridSpec(
            num_scalar_prefetch=1,
            grid=(depth,),
            in_specs=[
                pl.BlockSpec((tokens, rows), lambda i, s: (0, i)),
                pl.BlockSpec((tokens, cols), lambda i, s: (0, 0)),
            ],
            out_specs=[pl.BlockSpec((block[0], 1) + block[2:], lambda i, s: (0, i, 0, 0))] * (2 * len(orders)),
            scratch_shapes=[pltpu.VMEM((rows, cols), bf16)],
        ),
        compiler_params=pltpu.CompilerParams(vmem_limit_bytes=40 << 20),
        cost_estimate=SHORT,
        name=name,
    )(rank.reshape(1).astype(jnp.int32), a, b)
    return [(outs[2 * n], outs[2 * n + 1]) for n in range(len(orders))]


def pre_grad_kernel(g_ref, w_ref, slope_ref, out_ref, sum_ref):
    grad = dot_nt(g_ref[...], w_ref[...]) * slope_ref[...]
    out_ref[...] = grad.astype(bf16)
    sum_ref[...] = jnp.sum(grad, axis=0, keepdims=True)


def pre_grads(mlp_grad, fc2_matrix, slope):
    tokens, units = slope.shape
    tile = 256
    return pl.pallas_call(
        pre_grad_kernel,
        out_shape=[jax.ShapeDtypeStruct((tokens, units), bf16), jax.ShapeDtypeStruct((1, units), f32)],
        grid=(units // tile,),
        in_specs=[
            pl.BlockSpec((tokens, D), lambda i: (0, 0)),
            pl.BlockSpec((tile, D), lambda i: (i, 0)),
            pl.BlockSpec((tokens, tile), lambda i: (0, i)),
        ],
        out_specs=[pl.BlockSpec((tokens, tile), lambda i: (0, i)), pl.BlockSpec((1, tile), lambda i: (0, i))],
        compiler_params=pltpu.CompilerParams(vmem_limit_bytes=40 << 20),
        cost_estimate=SHORT,
        name="pre_grad",
    )(mlp_grad, fc2_matrix, slope)


def product_kernel(multiply, half_ref, first_ref, second_ref, w_ref, out1_ref, out2_ref):
    out1_ref[...] = multiply(first_ref[...], w_ref[...])
    out2_ref[...] = multiply(second_ref[...], w_ref[...])


def product(a, weight, multiply, half, name):
    rows, tile = a.shape[0] // 2, 128
    count = rows // tile
    out = pl.BlockSpec((tile, D), lambda i, h: (i, 0))
    return pl.pallas_call(
        functools.partial(product_kernel, multiply),
        out_shape=[jax.ShapeDtypeStruct((rows, D), f32)] * 2,
        grid_spec=pltpu.PrefetchScalarGridSpec(
            num_scalar_prefetch=1,
            grid=(count,),
            in_specs=[
                pl.BlockSpec((tile, a.shape[1]), lambda i, h: (i + h[0] * count, 0)),
                pl.BlockSpec((tile, a.shape[1]), lambda i, h: (i + (1 - h[0]) * count, 0)),
                pl.BlockSpec(weight.shape, lambda i, h: (0, 0)),
            ],
            out_specs=[out, out],
        ),
        compiler_params=pltpu.CompilerParams(vmem_limit_bytes=32 << 20),
        cost_estimate=SHORT,
        name=name,
    )(jnp.asarray(half, jnp.int32).reshape(1), a, a, weight)


def finish_kernel(
    own1_ref, sent1_ref, tok_ref, grad_ref, own2_ref, sent2_ref, resid_ref, cot_ref, vec_ref,
    in_grad_ref, out_ref, sum_ref,
):
    grad = own1_ref[...] + sent1_ref[...]
    normal, inverse = normalize(tok_ref[...].astype(f32))
    in_grad_ref[...] = grad_ref[...] + norm_back(grad, normal, inverse, vec_ref[0:1, :])
    mlp = own2_ref[...] + sent2_ref[...] + vec_ref[8:9, :]
    out_ref[...] = (resid_ref[...] + vec_ref[9:10, :] * mlp).astype(bf16)
    out_grad = cot_ref[...].astype(f32)

    @pl.when(pl.program_id(0) == 0)
    def _():
        sum_ref[...] = jnp.zeros_like(sum_ref)

    for row, value in enumerate((grad * normal, grad, out_grad * vec_ref[9:10, :], out_grad * mlp)):
        sum_ref[row : row + 1, :] += jnp.sum(value, axis=0, keepdims=True)


def finish(own1, sent1, tok, resid_grad, own2, sent2, resid, cot, vecs):
    rows, tile = own1.shape[0], 64
    part = pl.BlockSpec((tile, D), lambda i: (i, 0))
    return pl.pallas_call(
        finish_kernel,
        out_shape=[
            jax.ShapeDtypeStruct((rows, D), f32), jax.ShapeDtypeStruct((rows, D), bf16),
            jax.ShapeDtypeStruct((8, D), f32),
        ],
        grid=(rows // tile,),
        in_specs=[part] * 8 + [pl.BlockSpec(vecs.shape, lambda i: (0, 0))],
        out_specs=[part, part, pl.BlockSpec((8, D), lambda i: (0, 0))],
        compiler_params=pltpu.CompilerParams(vmem_limit_bytes=24 << 20),
        cost_estimate=SHORT,
        name="finish",
    )(own1, sent1, tok, resid_grad, own2, sent2, resid, cot, vecs)


def norm_grad_kernel(own_ref, sent_ref, resid_ref, cot_ref, attn_ref, vec_ref, grad_ref, scaled_ref, sum_ref):
    grad = own_ref[...] + sent_ref[...]
    normal, inverse = normalize(resid_ref[...])
    resid_grad = cot_ref[...].astype(f32) + norm_back(grad, normal, inverse, vec_ref[6:7, :])
    scaled = resid_grad * vec_ref[5:6, :]
    grad_ref[...] = resid_grad
    scaled_ref[...] = scaled.astype(bf16)

    @pl.when(pl.program_id(0) == 0)
    def _():
        sum_ref[...] = jnp.zeros_like(sum_ref)

    for row, value in enumerate((grad * normal, grad, scaled, resid_grad * attn_ref[...])):
        sum_ref[row : row + 1, :] += jnp.sum(value, axis=0, keepdims=True)


def norm_grads(own, sent, resid, cot, attn_out, vecs):
    rows, tile = own.shape[0], 64
    part = pl.BlockSpec((tile, D), lambda i: (i, 0))
    return pl.pallas_call(
        norm_grad_kernel,
        out_shape=[
            jax.ShapeDtypeStruct((rows, D), f32), jax.ShapeDtypeStruct((rows, D), bf16),
            jax.ShapeDtypeStruct((8, D), f32),
        ],
        grid=(rows // tile,),
        in_specs=[part] * 5 + [pl.BlockSpec(vecs.shape, lambda i: (0, 0))],
        out_specs=[part, part, pl.BlockSpec((8, D), lambda i: (0, 0))],
        compiler_params=pltpu.CompilerParams(vmem_limit_bytes=24 << 20),
        cost_estimate=SHORT,
        name="norm_grad",
    )(own, sent, resid, cot, attn_out, vecs)


def proj_grad_kernel(head_rows, c_ref, g_ref, out_ref):
    wide = out_ref.shape[1]
    for side in range(2):
        grad = dot_tn(c_ref[...], g_ref[:, side * wide : (side + 1) * wide]).astype(bf16)
        for z in range(grad.shape[0] // head_rows):
            at = (2 * z + side) * head_rows
            out_ref[at : at + head_rows, :] = grad[z * head_rows : (z + 1) * head_rows]


def packed_proj_grad(context, attn_grad, head_rows):
    wide = D // 2
    return pl.pallas_call(
        functools.partial(proj_grad_kernel, head_rows),
        out_shape=jax.ShapeDtypeStruct((D, wide), bf16),
        compiler_params=pltpu.CompilerParams(vmem_limit_bytes=32 << 20),
        cost_estimate=SHORT,
        name="proj_grad",
    )(context, attn_grad)


def qkv_grad_kernel(orders, ranks, depth, per, index_ref, n_ref, *refs):
    grads, p_ref = refs[: 3 * per], refs[3 * per]
    outs, held = refs[3 * per + 1 : -1], refs[-1]
    rank = index_ref[0]
    normed = n_ref[...]
    for number in range(3):
        pieces = [g[...] for g in grads[number * per : (number + 1) * per]]
        wide = per * LANES
        joined = pieces[0] if per == 1 else jnp.concatenate(pieces, axis=1)
        held[:, number * wide : (number + 1) * wide] = dot_tn(normed, joined).astype(bf16)
    held[:, 3 * per * LANES :] = p_ref[...]
    width = held.shape[1] // ranks
    rows = held.shape[0] // depth
    share = rows // len(orders)
    for n, order in enumerate(orders):
        for which, offsets in enumerate(halves(ranks, order[0], list(range(ranks)))):
            for i, o in enumerate(offsets):
                cols = pl.ds(pl.multiple_of((rank ^ o) * width, width), width)
                for z in range(depth):
                    at = z * rows + n * share
                    outs[2 * n + which][i, z] = held[at : at + share, cols]


def qkv_grad_blocks(normed, grads, proj_packed, part, parts, rank, orders):
    depth, ranks = lax.axis_size("fsdp") // 2, lax.axis_size("rep")
    per = len(grads) // 3
    cols = 4 * per * LANES
    block = (ranks // 2, depth, D // depth // len(orders), cols // ranks)
    tokens = normed.shape[0] // 3
    outs = pl.pallas_call(
        functools.partial(qkv_grad_kernel, orders, ranks, depth, per),
        out_shape=[jax.ShapeDtypeStruct(block, bf16)] * (2 * len(orders)),
        grid_spec=pltpu.PrefetchScalarGridSpec(
            num_scalar_prefetch=1,
            grid=(1,),
            in_specs=[pl.BlockSpec((tokens, D), lambda i, a: (1, 0))]
            + whole_specs(grads)
            + [pl.BlockSpec((D, per * LANES), lambda i, a: (0, part))],
            out_specs=[pl.BlockSpec(block, lambda i, a: (0, 0, 0, 0))] * (2 * len(orders)),
            scratch_shapes=[pltpu.VMEM((D, cols), bf16)],
        ),
        compiler_params=pltpu.CompilerParams(vmem_limit_bytes=40 << 20),
        cost_estimate=SHORT,
        name="qkv_grad",
    )(rank.reshape(1).astype(jnp.int32), normed, *grads, proj_packed)
    return [(outs[2 * n], outs[2 * n + 1]) for n in range(len(orders))]


def spread_lanes(tags, width):
    return jnp.concatenate([tags] * (width // LANES), axis=1)


def project_kernel(need_ref, n_ref, w_ref, b_ref, q_ref, k_ref, v_ref):
    row = pl.program_id(0)
    wide = q_ref.shape[1]

    @pl.when(need_ref[row] > 0)
    def _():
        n = n_ref[...]
        for i, ref in enumerate((q_ref, k_ref, v_ref)):
            out = dot(n, w_ref[:, i * wide : (i + 1) * wide]) + b_ref[0:1, i * wide : (i + 1) * wide]
            if i == 0:
                out = out.astype(bf16).astype(f32) * HEAD_DIM ** (-0.5)
            ref[...] = out.astype(bf16)

    @pl.when(need_ref[row] == 0)
    def _():
        for ref in (q_ref, k_ref, v_ref):
            ref[...] = jnp.zeros_like(ref)


def project(need, normed, weight, bias, wide):
    rows = normed.shape[0]
    return pl.pallas_call(
        project_kernel,
        out_shape=[jax.ShapeDtypeStruct((rows, wide), bf16)] * 3,
        grid_spec=pltpu.PrefetchScalarGridSpec(
            num_scalar_prefetch=1,
            grid=(rows // BLOCK,),
            in_specs=[
                pl.BlockSpec((BLOCK, D), lambda i, s: (i, 0)),
                pl.BlockSpec(weight.shape, lambda i, s: (0, 0)),
                pl.BlockSpec((1, 3 * wide), lambda i, s: (0, 0)),
            ],
            out_specs=[pl.BlockSpec((BLOCK, wide), lambda i, s: (i, 0))] * 3,
        ),
        compiler_params=pltpu.CompilerParams(vmem_limit_bytes=32 << 20),
        cost_estimate=SHORT,
        name="project",
    )(need, normed, weight, bias)


def norm_kernel(need_ref, info_ref, *refs):
    *sources, vec_ref, out_ref = refs
    row = pl.program_id(0)
    side = (row // info_ref[1]) % 2
    chip = row // (2 * info_ref[1])

    @pl.when(need_ref[row] > 0)
    def _():
        picked = jnp.where(chip == 0, sources[0][...], jnp.where(chip == 1, sources[2][...], sources[4][...]))
        theirs = jnp.where(chip == 0, sources[1][...], jnp.where(chip == 1, sources[3][...], sources[5][...]))
        picked = jnp.where(side == info_ref[0], picked, theirs)
        normal, _ = normalize(picked.astype(f32))
        out_ref[...] = (normal * vec_ref[0:1, :] + vec_ref[1:2, :]).astype(bf16)

    @pl.when(need_ref[row] == 0)
    def _():
        out_ref[...] = jnp.zeros_like(out_ref)


def norm_window(need, info, sources, vecs, window, count):
    per = count // BLOCK

    def spec(chip):
        def index(i, a, b):
            inside = jnp.clip(i - 2 * per * chip, 0, 2 * per - 1)
            return (inside % per, 0)

        return pl.BlockSpec((BLOCK, D), index)

    return pl.pallas_call(
        norm_kernel,
        out_shape=jax.ShapeDtypeStruct((window, D), bf16),
        grid_spec=pltpu.PrefetchScalarGridSpec(
            num_scalar_prefetch=2,
            grid=(window // BLOCK,),
            in_specs=[spec(i // 2) for i in range(6)] + [pl.BlockSpec(vecs.shape, lambda i, a, b: (0, 0))],
            out_specs=pl.BlockSpec((BLOCK, D), lambda i, a, b: (i, 0)),
        ),
        compiler_params=pltpu.CompilerParams(vmem_limit_bytes=24 << 20),
        cost_estimate=SHORT,
        name="norm_window",
    )(need, info, *sources, vecs)


def attend_kernel(lo_ref, hi_ref, first_ref, last_ref, q_ref, k_ref, v_ref, qt_ref, kt_ref, o_ref, lse_ref, s_ref, m_ref):
    i = pl.program_id(0)
    left = lax.broadcasted_iota(jnp.int32, (1, LANES), 1) < HEAD_DIM
    lo, hi = lo_ref[i], hi_ref[i]
    base = (first_ref.shape[0] - pl.num_programs(0)) // 2
    q = q_ref[...]
    zero = jnp.zeros_like(q)
    heads = (jnp.where(left, q, zero), jnp.where(left, zero, q))
    m_ref[...] = jnp.full_like(m_ref, MASKED)
    one_image = first_ref[base + i] == last_ref[base + i]
    folds = BLOCK // LANES

    def fold(value, combine):
        parts = [value[:, n * LANES : (n + 1) * LANES] for n in range(folds)]
        return functools.reduce(combine, parts)

    def scores(j, carry):
        at = pl.multiple_of(j * BLOCK, BLOCK)
        k = k_ref[pl.ds(at, BLOCK), :]
        inside = one_image & (first_ref[j] == first_ref[base + i]) & (last_ref[j] == first_ref[base + i])

        @pl.when(inside)
        def _():
            for h in range(2):
                s = dot_nt(heads[h], k)
                s_ref[h, j] = s
                m_ref[h] = jnp.maximum(m_ref[h], fold(s, jnp.maximum))

        @pl.when(jnp.logical_not(inside))
        def _():
            same = spread_lanes(qt_ref[...], BLOCK) == kt_ref[:, pl.ds(at, BLOCK)]
            for h in range(2):
                s = jnp.where(same, dot_nt(heads[h], k), MASKED)
                s_ref[h, j] = s
                m_ref[h] = jnp.maximum(m_ref[h], fold(s, jnp.maximum))

        return carry

    lax.fori_loop(lo, hi, scores, 0)
    tops = [jnp.max(m_ref[h], axis=1, keepdims=True) for h in range(2)]
    m_ref[...] = jnp.zeros_like(m_ref)

    def powers(j, carry):
        for h in range(2):
            e = jnp.exp(s_ref[h, j] - tops[h])
            s_ref[h, j] = e
            m_ref[h] += fold(e, jnp.add)
        return carry

    lax.fori_loop(lo, hi, powers, 0)
    sums = [jnp.sum(m_ref[h], axis=1, keepdims=True) for h in range(2)]
    shares = [1.0 / s for s in sums]
    m_ref[...] = jnp.zeros_like(m_ref)

    def mix(j, carry):
        at = pl.multiple_of(j * BLOCK, BLOCK)
        v = v_ref[pl.ds(at, BLOCK), :]
        for h in range(2):
            m_ref[h] += dot((s_ref[h, j] * shares[h]).astype(bf16), v)
        return carry

    lax.fori_loop(lo, hi, mix, 0)
    o_ref[...] = jnp.where(left, m_ref[0], m_ref[1]).astype(bf16)
    for h in range(2):
        lse = jnp.broadcast_to(tops[h] + jnp.log(sums[h]), (BLOCK, LANES))
        lse_ref[0, h : h + 1, :] = lse.T[0:1, :]


def attend(lo, hi, firsts, lasts, q, k, v, tag_cols, tag_row, own_rows, pair):
    window = q.shape[0]
    blocks = own_rows // BLOCK
    skip = (window - own_rows) // 2 // BLOCK
    return pl.pallas_call(
        attend_kernel,
        out_shape=[
            jax.ShapeDtypeStruct((own_rows, LANES), bf16),
            jax.ShapeDtypeStruct((1, 2, own_rows), f32),
        ],
        grid_spec=pltpu.PrefetchScalarGridSpec(
            num_scalar_prefetch=4,
            grid=(blocks,),
            in_specs=[
                pl.BlockSpec((BLOCK, LANES), lambda i, *_: (i + skip, pair)),
                pl.BlockSpec((window, LANES), lambda i, *_: (0, pair)),
                pl.BlockSpec((window, LANES), lambda i, *_: (0, pair)),
                pl.BlockSpec((BLOCK, LANES), lambda i, *_: (i + skip, 0)),
                pl.BlockSpec((1, window), lambda i, *_: (0, 0)),
            ],
            out_specs=[
                pl.BlockSpec((BLOCK, LANES), lambda i, *_: (i, 0)),
                pl.BlockSpec((1, 2, BLOCK), lambda i, *_: (0, 0, i)),
            ],
            scratch_shapes=[
                pltpu.VMEM((2, window // BLOCK, BLOCK, BLOCK), f32),
                pltpu.VMEM((2, BLOCK, LANES), f32),
            ],
        ),
        compiler_params=pltpu.CompilerParams(vmem_limit_bytes=32 << 20),
        cost_estimate=SHORT,
        name="attend",
    )(lo, hi, firsts, lasts, q, k, v, tag_cols, tag_row)


def attend_back_kernel(
    start, stop, lo_ref, hi_ref, q_ref, k_ref, v_ref, g_ref, tc_ref, tr_ref, lse_ref, delta_ref,
    dq_ref, dk_ref, dv_ref, sum_ref, dk_acc, dv_acc, dq_acc,
):
    first = lax.broadcasted_iota(jnp.int32, (1, LANES), 1) < HEAD_DIM
    dk_acc[...] = jnp.zeros_like(dk_acc)
    dv_acc[...] = jnp.zeros_like(dv_acc)
    sum_ref[...] = jnp.zeros_like(sum_ref)

    def split(value):
        zero = jnp.zeros_like(value)
        return jnp.where(first, value, zero), jnp.where(first, zero, value)

    def query_block(i, carry):
        at_q = pl.multiple_of(i * BLOCK, BLOCK)
        own_q = jnp.logical_and(i >= start, i < stop)
        lo = jnp.where(own_q, lo_ref[i], jnp.maximum(lo_ref[i], start))
        hi = jnp.where(own_q, hi_ref[i], jnp.minimum(hi_ref[i], stop))

        @pl.when(own_q)
        def _():
            dq_acc[...] = jnp.zeros_like(dq_acc)

        def key_block(j, carry):
            at_k = pl.multiple_of(j * BLOCK, BLOCK)
            k = k_ref[pl.ds(at_k, BLOCK), :]
            v = v_ref[pl.ds(at_k, BLOCK), :]
            qs = split(q_ref[pl.ds(at_q, BLOCK), :])
            gs = split(g_ref[pl.ds(at_q, BLOCK), :])
            same = spread_lanes(tc_ref[pl.ds(at_k, BLOCK), :], BLOCK) == tr_ref[:, pl.ds(at_q, BLOCK)]
            ps, ds = [], []
            for h in range(2):
                s = dot_nt(k, qs[h])
                p = jnp.where(same, jnp.exp(s - lse_ref[0, h : h + 1, pl.ds(at_q, BLOCK)]), 0.0)
                dp = dot_nt(v, gs[h])
                d = p * (dp - delta_ref[0, h : h + 1, pl.ds(at_q, BLOCK)])
                ps.append(p.astype(bf16))
                ds.append(d.astype(bf16))

            @pl.when(jnp.logical_and(j >= start, j < stop))
            def _():
                at = pl.multiple_of((j - start) * BLOCK, BLOCK)
                dv_acc[pl.ds(at, BLOCK), :] += dot(ps[0], gs[0]) + dot(ps[1], gs[1])
                dk_acc[pl.ds(at, BLOCK), :] += dot(ds[0], qs[0]) + dot(ds[1], qs[1])

            @pl.when(own_q)
            def _():
                ks = split(k)
                dq_acc[...] += dot_tn(ds[0], ks[0]) + dot_tn(ds[1], ks[1])

            return carry

        lax.fori_loop(lo, hi, key_block, 0)

        @pl.when(own_q)
        def _():
            at = pl.multiple_of((i - start) * BLOCK, BLOCK)
            dq = dq_acc[...] * HEAD_DIM ** (-0.5)
            dq_ref[pl.ds(at, BLOCK), :] = dq.astype(bf16)
            sum_ref[0, 0:1, :] += jnp.sum(dq, axis=0, keepdims=True)

        return carry

    lax.fori_loop(0, q_ref.shape[0] // BLOCK, query_block, 0)
    dk_ref[...] = dk_acc[...].astype(bf16)
    dv_ref[...] = dv_acc[...].astype(bf16)
    sum_ref[0, 1:2, :] = jnp.sum(dv_acc[...], axis=0, keepdims=True)


def attend_back(lo, hi, q, k, v, g, tag_cols, tag_row, lse, delta, own_rows, pair):
    window = q.shape[0]
    pairs, wide = 1, LANES
    grad_pair = pair % (g.shape[1] // LANES)
    start = (window - own_rows) // 2 // BLOCK
    stop = start + own_rows // BLOCK
    whole = lambda: pl.BlockSpec((window, LANES), lambda p, a, b: (0, pair))
    own = lambda: pl.BlockSpec((own_rows, LANES), lambda p, a, b: (0, p))
    stat = lambda: pl.BlockSpec((1, 2, window), lambda p, a, b: (pair, 0, 0))
    return pl.pallas_call(
        functools.partial(attend_back_kernel, start, stop),
        out_shape=[jax.ShapeDtypeStruct((own_rows, wide), bf16)] * 3
        + [jax.ShapeDtypeStruct((pairs, 8, LANES), f32)],
        grid_spec=pltpu.PrefetchScalarGridSpec(
            num_scalar_prefetch=2,
            grid=(pairs,),
            in_specs=[
                whole(), whole(), whole(),
                pl.BlockSpec((window, LANES), lambda p, a, b: (0, grad_pair)),
                pl.BlockSpec((window, LANES), lambda p, a, b: (0, 0)),
                pl.BlockSpec((1, window), lambda p, a, b: (0, 0)),
                stat(), stat(),
            ],
            out_specs=[own(), own(), own(), pl.BlockSpec((1, 8, LANES), lambda p, a, b: (p, 0, 0))],
            scratch_shapes=[
                pltpu.VMEM((own_rows, LANES), f32),
                pltpu.VMEM((own_rows, LANES), f32),
                pltpu.VMEM((BLOCK, LANES), f32),
            ],
        ),
        compiler_params=pltpu.CompilerParams(vmem_limit_bytes=40 << 20),
        cost_estimate=SHORT,
        name="attend_back",
    )(lo, hi, q, k, v, g, tag_cols, tag_row, lse, delta)


def on_device(
    tokens, image_ids, ln1_gain, ln1_bias, qkv_weight, query_bias, value_bias, proj_weight,
    proj_bias, scale_attn, ln2_gain, ln2_bias, fc1_weight, fc1_bias, fc2_weight, fc2_bias,
    scale_mlp, cotangent,
):
    devices = lax.axis_size("fsdp")
    depth, ranks = devices // 2, lax.axis_size("rep")
    place = lax.axis_index("fsdp")
    rank = lax.axis_index("rep")
    here, core = place // 2, place % 2
    count = tokens.shape[1]
    chip = 2 * count
    head_rows = D // devices
    ff = fc1_weight.shape[1]
    unit_rows = ff // devices
    half_heads = D // 2
    local_heads = half_heads // HEAD_DIM
    pairs = half_heads // LANES
    bits = list(range(rep_bits()))

    def in_order(own, other, axis=0):
        return jnp.where(
            core == 0,
            jnp.concatenate([own, other], axis=axis),
            jnp.concatenate([other, own], axis=axis),
        )

    def mine(value):
        return lax.dynamic_slice_in_dim(value, core * count, count, 0)

    def others(value):
        return lax.dynamic_slice_in_dim(value, (1 - core) * count, count, 0)

    def every_other(value, width, start):
        cuts = range(start * width, value.shape[1], 2 * width)
        return jnp.concatenate([value[:, c : c + width] for c in cuts], axis=1)

    def all_share(which):
        pick_cols = lambda v, w: jnp.where(which == 0, every_other(v, w, 0), every_other(v, w, 1))
        heads = lax.dynamic_slice_in_dim(
            jnp.concatenate(
                [
                    pick_cols(qkv_weight, head_rows),
                    lax.dynamic_slice_in_dim(proj_weight, which * half_heads, half_heads, 1),
                ],
                axis=1,
            ),
            rank * (2 * D // ranks), 2 * D // ranks, 1,
        )
        units = lax.dynamic_slice_in_dim(
            pick_cols(fc1_weight, unit_rows), rank * (ff // 2 // ranks), ff // 2 // ranks, 1
        )
        return jnp.concatenate([heads, units], axis=1)

    if head_rows % LANES:
        kept, given = all_share(core), all_share(1 - core)
    else:
        kept, given = weight_share(
            rank, core, qkv_weight, proj_weight, fc1_weight, ranks, head_rows, unit_rows
        )
    wide1 = 2 * D // ranks
    got = swap_cores(given)
    is_proj = rank * wide1 >= 3 * half_heads
    own1 = in_order(kept[:, :wide1], jnp.where(is_proj, given[:, :wide1], got[:, :wide1]))
    own2 = in_order(kept[:, wide1:], got[:, wide1:])
    own3 = lax.dynamic_slice_in_dim(fc2_weight, rank * (D // ranks), D // ranks, 1)
    small = (
        ln1_gain, ln1_bias, query_bias, value_bias, proj_bias, scale_attn, ln2_gain, ln2_bias,
        fc2_bias, scale_mlp, fc1_bias, (image_ids[0] + 1).astype(bf16),
    )
    sizes = [v.shape[0] for v in small]
    slots = slot_lists(sizes)
    width = 2 * D // ranks
    small = pack_small(small, width, slots)
    small_other = swap_cores(small)
    rows1, rows3 = own1.shape[0], own3.shape[0]
    tok, cot = tokens[0], cotangent[0]
    tok_other = swap_cores(tok)
    cot_other = swap_cores(cot)
    own1 = jnp.concatenate([own1, small, small_other])
    own1, own2, own3, tok = tie(own1, own2, own3, tok)
    pieces1 = fetch_z(own1)
    tok, pieces1[1] = tie(tok, pieces1[1])
    behind, ahead = from_chip(tok, 1), from_chip(tok, -1)
    gather1 = Gather(pieces1, rows1, "gather1")
    gather1.send()
    behind_other, ahead_other = swap_cores(behind), swap_cores(ahead)
    for _ in bits[1:]:
        gather1.send()

    vec_rows, fc1_shift, all_tags = unpack_small(
        pieces1, slots, rows1, here, core, ff // 2, devices * count
    )
    vector = lambda i: vec_rows[i : i + 1]
    (
        attn_gain, attn_shift, query_shift, value_shift, proj_shift, attn_scale, mlp_gain,
        mlp_shift, fc2_shift, mlp_scale,
    ) = map(vector, range(10))
    core_part = lambda vec: jnp.where(
        core == 0, every_other(vec, head_rows, 0), every_other(vec, head_rows, 1)
    )

    window = 3 * chip
    padded = jnp.concatenate(
        [jnp.zeros((1, chip), f32), all_tags, jnp.full((1, chip), 1e6, f32)], axis=1
    )
    tag_row = lax.dynamic_slice(padded, (0, here * chip), (1, window))
    tags = tag_row.reshape(window)
    firsts, lasts = tags[::BLOCK], tags[BLOCK - 1 :: BLOCK]
    real = firsts * (1e6 - firsts) > 0
    below = jnp.sum((tag_row < firsts[:, None]).astype(jnp.int32), axis=1)
    upto = jnp.sum((tag_row <= lasts[:, None]).astype(jnp.int32), axis=1)
    blocks = window // BLOCK
    block_lo = jnp.where(real, below // BLOCK, 0)
    block_hi = jnp.where(real, (upto + BLOCK - 1) // BLOCK, 0)
    own_lo, own_hi = chip // BLOCK, 2 * chip // BLOCK
    numbers = jnp.arange(blocks)
    need = jnp.logical_and(numbers >= block_lo[own_lo], numbers < block_hi[own_hi - 1]).astype(jnp.int32)
    firsts, lasts = firsts.astype(jnp.int32), lasts.astype(jnp.int32)
    tag_cols = jnp.broadcast_to(tags[:, None], (window, LANES))

    info = jnp.stack([core, jnp.int32(count // BLOCK)]).astype(jnp.int32)
    normed1 = norm_window(
        need, info, (behind, behind_other, tok, tok_other, ahead, ahead_other), vec_rows, window, count
    )

    normed1, own2 = tie(normed1, own2)
    pieces2 = fetch_z(own2)
    normed1 = gather1.arrive(normed1)
    qkv_matrix, proj_matrix = gather1.assemble(here, rank, head_rows)

    shifts = jnp.concatenate(
        [core_part(query_shift), jnp.zeros((1, half_heads), f32), core_part(value_shift)], axis=1
    )
    queries, keys, values = project(need, normed1, qkv_matrix, shifts, half_heads)

    contexts, lses = [], []
    los = block_lo[own_lo:own_hi]
    los, queries = tie(los, queries)
    for pair in range(pairs):
        if pair == 1:
            los, own3, *pieces2 = tie(los, own3, *pieces2)
            gather2 = Gather(pieces2, rows1, "gather2")
            los = gather2.send(los)
            pieces3 = fetch_z(own3)
        if pair == 2:
            los = gather2.arrive(los)
            los = gather2.send(los)
        if pair == 3:
            los = gather2.arrive(los)
            for _ in bits[2:]:
                los = gather2.arrive(gather2.send(los))
            los, *pieces3 = tie(los, *pieces3)
            gather3 = Gather(pieces3, rows3, "gather3")
            los = gather3.send(los)
        context, lse = attend(
            los, block_hi[own_lo:own_hi], firsts, lasts, queries, keys, values, tag_cols,
            tag_row, chip, pair,
        )
        los, context = tie(los, context)
        contexts.append(context)
        lses.append(lse)
    context = jnp.concatenate(contexts, axis=1)
    lse_rows = jnp.concatenate(lses).reshape(local_heads, chip)
    context = gather3.arrive(context)
    context = gather3.send(context)
    fc1_matrix = gather2.assemble(here, rank)

    features = tok.astype(f32)
    sent = swap_cores(dot(others(context), proj_matrix))
    attn_out = dot(mine(context), proj_matrix) + sent + proj_shift
    resid = features + attn_scale * attn_out
    mlp_normal, mlp_inverse = normalize(resid)
    mlp_input = (mlp_normal * mlp_gain + mlp_shift).astype(bf16)
    mlp_input = jnp.concatenate([mlp_input, swap_cores(mlp_input)])
    pre_act = dot(mlp_input, fc1_matrix) + fc1_shift
    activated, slope = gelu_pair(pre_act)
    activated = activated.astype(bf16)

    out_grad = cot.astype(f32)
    mlp_grad_full = out_grad * mlp_scale
    mlp_grad = (jnp.concatenate([cot, cot_other]).astype(f32) * mlp_scale).astype(bf16)

    both = [bits, bits[::-1]]
    activated = gather3.arrive(activated)
    for _ in bits[2:]:
        activated = gather3.arrive(gather3.send(activated))
    reduce3 = Reduce(grad_blocks(activated, mlp_grad, rank, both, "fc2_grad"), here, both)
    mlp_grad = reduce3.send(mlp_grad)
    fc2_matrix = gather3.assemble(here, rank)
    pre_grad, fc1_bias_part = pre_grads(mlp_grad, fc2_matrix, slope)
    reduce2 = Reduce(grad_blocks(mlp_input, pre_grad, rank, both, "fc1_grad"), here, both)
    pre_grad, _ = tie(pre_grad, [give for _, _, give in reduce2.held])
    own, given = product(pre_grad, fc1_matrix, dot_nt, 0, "mlp_in_grad")
    own, given = reduce3.arrive(own, given)
    for _ in bits[2:]:
        own, given = reduce3.arrive(*reduce3.send(own, given))
    own, given = reduce3.send(own, given)
    sent = swap_cores(given)
    resid_grad, attn_grad, norm_sums = norm_grads(own, sent, resid, cot, attn_out, vec_rows)
    attn_grad = in_order(attn_grad, swap_cores(attn_grad))
    context_grad = dot_nt(attn_grad, proj_matrix).astype(bf16)
    head_of = (
        lax.broadcasted_iota(jnp.int32, (local_heads, half_heads), 1) // HEAD_DIM
        == lax.broadcasted_iota(jnp.int32, (local_heads, half_heads), 0)
    ).astype(f32)
    row_delta = lax.dot_general(
        head_of, context_grad.astype(f32) * context.astype(f32), (((1,), (1,)), ((), ())),
        precision=lax.Precision.HIGHEST, preferred_element_type=f32,
    )
    stats = jnp.concatenate([lse_rows, row_delta])
    context_grad, activated, attn_grad = tie(context_grad, activated, attn_grad)
    chunk = half_heads // 2
    chunks = [context_grad[:, :chunk], context_grad[:, chunk:]]
    grads_behind, grads_ahead = zip(*[(from_chip(c, 1), from_chip(c, -1)) for c in chunks])
    stats_behind, stats_ahead = from_chip(stats, 1), from_chip(stats, -1)
    proj_grad = packed_proj_grad(context, attn_grad, head_rows)
    stat_window = jnp.concatenate([stats_behind, stats, stats_ahead], axis=1)
    by_pair = lambda s: s.reshape(pairs, 2, window)
    lse_window, delta_window = by_pair(stat_window[:local_heads]), by_pair(stat_window[local_heads:])

    half_pairs = pairs // 2
    half_width = half_heads // 2

    def first_group(parts, number):
        grads = [g for kind in zip(*parts) for g in kind]
        return Reduce(
            qkv_grad_blocks(normed1, grads, proj_grad, number, 2, rank, both), here, both
        )

    parts, sums = [], []
    first, delta_window, lo = settle(
        ((grads_behind[0], grads_ahead[0]), delta_window, block_lo), (reduce3, "received")
    )
    sides = [first, *list(zip(grads_behind, grads_ahead))[1:]]
    grad_windows = [jnp.concatenate([b, c, a]) for c, (b, a) in zip(chunks, sides)]
    for pair in range(pairs):
        if pair == 0:
            lo = reduce3.arrive(lo)
            lo = reduce2.send(lo)
        if pair == 1:
            lo = reduce2.arrive(lo)
            lo = reduce3.send_z(lo)
            for _ in bits[2:]:
                lo = reduce2.arrive(reduce2.send(lo))
            lo = reduce2.send(lo)
        if pair == 2:
            lo = settle(lo, (reduce2, "received"), (reduce3, "pieces"))
            lo = reduce2.arrive(lo)
            lo = reduce2.send_z(lo)
            reduce1a = first_group(parts, 0)
            lo = reduce1a.send(lo)
        if pair == 3:
            lo = settle(lo, (reduce2, "pieces"), (reduce1a, "received"))
            lo = reduce3.arrive_z(lo)
            lo = reduce2.arrive_z(lo)
            fc2_part = reduce3.total.astype(bf16)
            fc1_part = reduce2.total.astype(bf16)
            split = fc2_part.shape[0] // fc1_part.shape[0]
            mlp_spread = Spread(jnp.concatenate([fc1_part, *jnp.split(fc2_part, split)], axis=1))
            lo = mlp_spread.send(lo)
            lo = reduce1a.arrive(lo)
            for _ in bits[2:]:
                lo = reduce1a.arrive(reduce1a.send(lo))
            lo = reduce1a.send(lo)
        *grads, total = attend_back(
            lo, block_hi, queries, keys, values, grad_windows[pair * 2 // pairs], tag_cols, tag_row, lse_window,
            delta_window, chip, pair,
        )
        lo, *grads = tie(lo, *grads)
        parts.append(grads)
        sums.append(total[0])

    parts[-1], activated = settle((parts[-1], activated), (mlp_spread, "arrays"))
    parts[-1] = reduce1a.arrive(parts[-1])
    parts[-1] = reduce1a.send_z(parts[-1])
    reduce1b = first_group(parts[half_pairs:], 1)
    parts[-1], activated = reduce1b.send(parts[-1], activated)
    every = [jnp.concatenate(p, axis=1) for p in zip(*parts)]

    factor = 1.0 / math.sqrt(count * devices * ranks)
    in_own, in_given = product(
        jnp.concatenate(every, axis=1), qkv_matrix, dot_nt, core, "attn_in_grad"
    )
    out_own, out_given = product(activated, fc2_matrix, dot, 0, "mlp_out")
    tail = (in_own, in_given, out_own, out_given)
    tail = settle(tail, (reduce1b, "received"), (reduce1a, "pieces"))
    for _ in bits[1:]:
        tail = reduce1b.arrive(tail)
        tail = reduce1b.send(tail)
        tail = mlp_spread.send(tail)
    in_own, in_given, out_own, out_given = tail
    input_rows, output_rows, end_sums = finish(
        in_own, swap_cores(in_given), tok, resid_grad, out_own, swap_cores(out_given), resid, cot, vec_rows
    )

    vectors = (
        end_sums[0:1], end_sums[1:2],
        jnp.concatenate([s[0:1] for s in sums], axis=1), jnp.concatenate([s[1:2] for s in sums], axis=1),
        norm_sums[2:3], norm_sums[3:4], norm_sums[0:1], norm_sums[1:2],
        end_sums[2:3], end_sums[3:4], fc1_bias_part,
    )
    of_core = [number in (2, 3, 10) for number in range(11)]
    partial = pack_grads(vectors, list(zip(sizes, of_core)), core, depth)
    partial = reduce1b.arrive(partial)
    partial = reduce1b.send_z(partial)

    vec_total = pick(partial, here, 0)
    for k in range(1, depth):
        vec_total = vec_total + along_z(pick(partial, lax.rem(here + k, depth), 0), k)
    reduce1a.arrive_z()
    vec_total = reduce1b.arrive_z(vec_total)
    vec_total = settle(vec_total, (mlp_spread, "arrays"))
    first_spread = Spread(jnp.concatenate([reduce1a.total, reduce1b.total], axis=1).astype(bf16))
    for bit in bits:
        first_spread.send()
        vec_total = vec_total + across_rep(vec_total, bit)
    vec_half = vec_total.reshape(2, 16, LANES)
    totals = (pick(vec_half, core, 0) + swap_cores(pick(vec_half, 1 - core, 0))) * factor

    mlp_cols = fc1_part.shape[1]
    fc1_full = mlp_spread.blocks(rank, 0, mlp_cols)
    fc2_width = fc2_part.shape[1]
    grad_fc2 = jnp.concatenate(
        [mlp_spread.blocks(rank, mlp_cols + n * fc2_width, fc2_width) for n in range(split)]
    ).astype(f32) * factor
    vec_width = D // ranks
    first_a = first_spread.blocks(rank, 0, vec_width)
    first_b = first_spread.blocks(rank, vec_width, vec_width)

    def rows_of(value, index):
        return lax.dynamic_slice_in_dim(value, index * head_rows, head_rows, 0)

    def interleave(own, other, width):
        cuts = range(0, own.shape[1], width)
        zipped = lambda a, b: jnp.concatenate(
            [v[:, c : c + width] for c in cuts for v in (a, b)], axis=1
        )
        return jnp.where(core == 0, zipped(own, other), zipped(other, own)).astype(f32) * factor

    fc1_other = swap_cores(rows_of(fc1_full, 1 - core))
    grad_fc1 = interleave(rows_of(fc1_full, core), fc1_other, unit_rows)
    qkv_full = jnp.concatenate(
        [
            part[:, n * half_width : (n + 1) * half_width]
            for n in range(3)
            for part in (first_a, first_b)
        ],
        axis=1,
    )
    grad_qkv = interleave(rows_of(qkv_full, core), swap_cores(rows_of(qkv_full, 1 - core)), head_rows)
    proj_part = jnp.concatenate([first_a[:, 3 * half_width :], first_b[:, 3 * half_width :]], axis=1)
    grad_proj = jnp.concatenate([proj_part[:head_rows], proj_part[head_rows:]], axis=1).astype(f32) * factor

    small_grads = [totals[i, : sizes[i]] for i in range(10)]
    lines = -(-sizes[10] // LANES)
    small_grads.append(totals[10 : 10 + lines].reshape(-1))
    (
        grad_attn_gain, grad_attn_shift, grad_query_shift, grad_value_shift, grad_proj_shift,
        grad_attn_scale, grad_mlp_gain, grad_mlp_shift, grad_fc2_shift, grad_mlp_scale, grad_fc1_shift,
    ) = small_grads

    return (
        output_rows[None],
        input_rows[None],
        grad_attn_gain,
        grad_attn_shift,
        grad_qkv,
        grad_query_shift,
        grad_value_shift,
        grad_proj,
        grad_proj_shift,
        grad_attn_scale,
        grad_mlp_gain,
        grad_mlp_shift,
        grad_fc1,
        grad_fc1_shift,
        grad_fc2,
        grad_fc2_shift,
        grad_mlp_scale,
    )


def solution(mesh):
    rows = P("fsdp", None)
    vec = P("fsdp")
    tok = P("rep", "fsdp", None)
    return jax.shard_map(
        on_device,
        mesh=mesh,
        in_specs=(
            tok, P("rep", "fsdp"), vec, vec, rows, vec, vec, rows, vec, vec, vec, vec, rows, vec,
            rows, vec, vec, tok,
        ),
        out_specs=(
            tok, tok, vec, vec, rows, vec, vec, rows, vec, vec, vec, vec, rows, vec, rows, vec, vec,
        ),
        check_vma=False,
    )
```

```python
import functools
import math

import jax
import jax.numpy as jnp
from jax import lax
from jax.experimental import pallas as pl
from jax.experimental.pallas import tpu as pltpu
from jax.sharding import PartitionSpec as P

D = 1024
HEADS = 16
HEAD_DIM = 64
LANES = 128

EPSILON = 1e-06
MASKED = -1e30
BLOCK = 256

SHORT = pl.CostEstimate(flops=1, transcendentals=0, bytes_accessed=1)

f32 = jnp.float32
bf16 = jnp.bfloat16


def normalize(features):
    row_mean = jnp.mean(features, axis=-1, keepdims=True)
    centred = features - row_mean
    variance = jnp.mean(centred * centred, axis=-1, keepdims=True)
    inverse = lax.rsqrt(variance + EPSILON)
    return centred * inverse, inverse


def norm_back(gradient, normal, inverse, gain_vec):
    scaled = gradient * gain_vec
    mean_first = jnp.mean(scaled, axis=-1, keepdims=True)
    mean_second = jnp.mean(scaled * normal, axis=-1, keepdims=True)
    return inverse * (scaled - mean_first - normal * mean_second)


def gelu_pair(values):
    cumulative = 0.5 * (1.0 + lax.erf(values * 2.0 ** (-0.5)))
    density = jnp.exp(-0.5 * values * values) * (2.0 * math.pi) ** (-0.5)
    return (values * cumulative, cumulative + values * density)


def dot(a, b):
    return jnp.dot(a, b, preferred_element_type=f32)


def dot_nt(a, b):
    return lax.dot_general(a, b, (((1,), (1,)), ((), ())), preferred_element_type=f32)


def dot_tn(a, b):
    return lax.dot_general(a, b, (((0,), (0,)), ((), ())), preferred_element_type=f32)


def swap_cores(value):
    size = lax.axis_size("fsdp")
    return lax.ppermute(value, "fsdp", [(i, i ^ 1) for i in range(size)])


def along_z(value, by):
    size = lax.axis_size("fsdp")
    return lax.ppermute(value, "fsdp", [(i, (i + 2 * by) % size) for i in range(size)])


def from_chip(value, by):
    size = lax.axis_size("fsdp")
    pairs = [(i, i + 2 * by) for i in range(size) if 0 <= i + 2 * by < size]
    return lax.ppermute(value, "fsdp", pairs)


def across_rep(value, bit):
    size = lax.axis_size("rep")
    return lax.ppermute(value, "rep", [(i, i ^ (1 << bit)) for i in range(size)])


def pick(value, index, axis):
    return lax.dynamic_index_in_dim(value, index, axis, keepdims=False)


def rep_bits():
    return lax.axis_size("rep").bit_length() - 1


def tie(*values):
    return lax.optimization_barrier(values)


def settle(value, *fields):
    held = [getattr(o, name) for o, name in fields]
    value, held = lax.optimization_barrier((value, held))
    for (o, name), new in zip(fields, held):
        setattr(o, name, new)
    return value


def fetch_z(own):
    return [own] + [along_z(own, k) for k in range(1, lax.axis_size("fsdp") // 2)]


class Gather:
    def __init__(self, pieces, rows, name):
        self.rows, self.cols, self.name = rows, pieces[0].shape[1], name
        half = rows // 2
        bits = list(range(rep_bits()))
        self.orders = [bits, bits[::-1]]
        self.parts = [
            [(jnp.stack([p[:half] for p in pieces])[None], [0])],
            [(jnp.stack([p[half:rows] for p in pieces])[None], [0])],
        ]
        self.at = 0

    def send(self, *values):
        whole = [
            (ps[0][0] if len(ps) == 1 else jnp.concatenate([a for a, _ in ps]), [o for _, os in ps for o in os])
            for ps in self.parts
        ]
        values, arrays = lax.optimization_barrier((values, [a for a, _ in whole]))
        self.parts = []
        for array, (_, offsets), order in zip(arrays, whole, self.orders):
            flip = 1 << order[self.at]
            received = across_rep(array, order[self.at])
            self.parts.append([(array, offsets), (received, [o ^ flip for o in offsets])])
        self.at += 1
        return values[0] if len(values) == 1 else values

    def arrive(self, value):
        value, arrays = lax.optimization_barrier((value, [a for ps in self.parts for a, _ in ps]))
        self.parts = [[(arrays.pop(0), o) for _, o in ps] for ps in self.parts]
        return value

    def assemble(self, here, rank, tail_rows=0):
        depth, ranks = lax.axis_size("fsdp") // 2, lax.axis_size("rep")
        sources, plan = [], []
        for number, parts in enumerate(self.parts):
            for array, offsets in parts:
                sources.append(array)
                plan.append((number, offsets))
        dtype = sources[0].dtype
        shape = (depth * self.rows, ranks * self.cols)
        shapes = [jax.ShapeDtypeStruct(shape, dtype)]
        if tail_rows:
            tail = shape[1] // 4
            shapes = [
                jax.ShapeDtypeStruct((shape[0], shape[1] - tail), dtype),
                jax.ShapeDtypeStruct((depth * tail_rows, 2 * tail), dtype),
            ]
        out = pl.pallas_call(
            functools.partial(assemble_kernel, plan, depth, self.rows, self.cols, tail_rows),
            out_shape=shapes,
            grid_spec=pltpu.PrefetchScalarGridSpec(
                num_scalar_prefetch=1,
                grid=(1,),
                in_specs=[pl.BlockSpec(memory_space=pl.ANY)] * len(sources),
                out_specs=[pl.BlockSpec(memory_space=pl.ANY)] * len(shapes),
                scratch_shapes=[
                    pltpu.VMEM(shape, dtype),
                    pltpu.SemaphoreType.DMA((2 * ranks * depth,)),
                    pltpu.SemaphoreType.DMA((3 * depth,)),
                ],
            ),
            compiler_params=pltpu.CompilerParams(vmem_limit_bytes=16 << 20),
            cost_estimate=SHORT,
            name=self.name,
        )(jnp.stack([here, rank]).astype(jnp.int32), *sources)
        return out if tail_rows else out[0]


def assemble_kernel(plan, depth, rows, cols, tail_rows, index_ref, *refs):
    count = len(plan)
    sources = refs[:count]
    targets = refs[count : count + (2 if tail_rows else 1)]
    held, in_sems, out_sems = refs[-3:]
    here, rank = index_ref[0], index_ref[1]
    half = rows // 2
    waits = [[] for _ in range(depth)]
    number = 0
    for k in range(depth):
        place = lax.rem(here - k + depth, depth)
        for which, (colour, offsets) in enumerate(plan):
            for m, offset in enumerate(offsets):
                at_row = pl.multiple_of(place * rows + colour * half, half)
                at_col = pl.multiple_of((rank ^ offset) * cols, cols)
                copy = pltpu.make_async_copy(
                    sources[which].at[m, k],
                    held.at[pl.ds(at_row, half), pl.ds(at_col, cols)],
                    in_sems.at[number],
                )
                copy.start()
                waits[k].append(copy)
                number += 1
    outs = []
    main = targets[0].shape[1]
    for k in range(depth):
        place = lax.rem(here - k + depth, depth)
        for copy in waits[k]:
            copy.wait()
        base = pl.multiple_of(place * rows, rows)
        band = pl.ds(base, rows)
        out = pltpu.make_async_copy(held.at[band, pl.ds(0, main)], targets[0].at[band], out_sems.at[3 * k])
        out.start()
        outs.append(out)
        if tail_rows:
            wide = targets[1].shape[1] // 2
            for side in range(2):
                out = pltpu.make_async_copy(
                    held.at[pl.ds(base + side * tail_rows, tail_rows), pl.ds(main, wide)],
                    targets[1].at[
                        pl.ds(pl.multiple_of(place * tail_rows, tail_rows), tail_rows),
                        pl.ds(side * wide, wide),
                    ],
                    out_sems.at[3 * k + 1 + side],
                )
                out.start()
                outs.append(out)
    for out in outs:
        out.wait()


def halves(ranks, bit, held):
    flip = 1 << bit
    kept = [o for o in held if not o & flip]
    return kept, [o ^ flip for o in kept]


def relative_blocks(grads, rank, orders):
    depth, ranks = lax.axis_size("fsdp") // 2, lax.axis_size("rep")
    width = grads.shape[1] // ranks
    rows = grads.shape[0] // depth
    shaped = grads.reshape(depth, rows, grads.shape[1])
    share = rows // len(orders)
    first = []
    for n, order in enumerate(orders):
        block = lambda o: lax.dynamic_slice(
            shaped, (0, n * share, (rank ^ o) * width), (depth, share, width)
        )
        kept, given = halves(ranks, order[0], list(range(ranks)))
        first.append((jnp.stack([block(o) for o in kept]), jnp.stack([block(o) for o in given])))
    return first


class Reduce:
    def __init__(self, first, here, orders):
        self.here, self.orders, self.at = here, orders, 0
        ranks = lax.axis_size("rep")
        self.held = []
        for (keep, give), order in zip(first, orders):
            kept, given = halves(ranks, order[0], list(range(ranks)))
            self.held.append((kept, keep, give))

    def send(self, *values):
        values, gives = lax.optimization_barrier((values, [give for _, _, give in self.held]))
        self.received = [across_rep(g, order[self.at]) for g, order in zip(gives, self.orders)]
        self.at += 1
        return values[0] if len(values) == 1 else values

    def arrive(self, *values):
        values, received = lax.optimization_barrier((values, self.received))
        held = []
        for (kept, keep, _), got, order in zip(self.held, received, self.orders):
            total = (keep.astype(f32) + got.astype(f32)).astype(bf16)
            if self.at < len(order):
                stay, leave = halves(None, order[self.at], kept)
                take = lambda os: jnp.stack([total[kept.index(o)] for o in os])
                held.append((stay, take(stay), take(leave)))
            else:
                held.append((kept, total[0], None))
        self.held = held
        return values[0] if len(values) == 1 else values

    def send_z(self, *values):
        depth = lax.axis_size("fsdp") // 2
        parts = [keep for _, keep, _ in self.held]
        whole = parts[0] if len(parts) == 1 else jnp.concatenate(parts, axis=1)
        pieces = [pick(whole, lax.rem(self.here + k, depth), 0) for k in range(depth)]
        values, pieces = lax.optimization_barrier((values, pieces))
        self.pieces = [pieces[0]] + [along_z(p, k) for k, p in enumerate(pieces) if k]
        return values[0] if len(values) == 1 else values

    def arrive_z(self, *values):
        values, pieces = lax.optimization_barrier((values, self.pieces))
        total = pieces[0].astype(f32)
        for piece in pieces[1:]:
            total = total + piece.astype(f32)
        self.total = total
        return values[0] if len(values) == 1 else values


class Spread:
    def __init__(self, value):
        bits = list(range(rep_bits()))
        self.orders = [bits, bits[::-1]]
        half = value.shape[0] // 2
        self.arrays = [value[:half][None], value[half:][None]]
        self.offsets = [[0], [0]]
        self.at = 0

    def send(self, *values):
        values, arrays = lax.optimization_barrier((values, self.arrays))
        self.arrays = []
        for n, (array, order) in enumerate(zip(arrays, self.orders)):
            flip = 1 << order[self.at]
            received = across_rep(array, order[self.at])
            self.arrays.append(jnp.concatenate([array, received]))
            self.offsets[n] = self.offsets[n] + [o ^ flip for o in self.offsets[n]]
        self.at += 1
        return values[0] if len(values) == 1 else values

    def blocks(self, rank, start, size):
        return jnp.concatenate(
            [rep_blocks(a[:, :, start : start + size], o, rank) for a, o in zip(self.arrays, self.offsets)]
        )


def rep_blocks(stacked, offsets, rank):
    blocks = []
    for i in range(len(offsets)):
        block = stacked[0]
        for entry, offset in enumerate(offsets):
            block = jnp.where((rank ^ offset) == i, stacked[entry], block)
        blocks.append(block)
    return jnp.concatenate(blocks, axis=1)


def share_kernel(widths, index_ref, qkv_ref, proj_ref, fc1_ref, keep_ref, give_ref, sems):
    rank, core = index_ref[0], index_ref[1]
    wide1, wide2, block, unit, half = widths
    is_proj = rank * wide1 >= 3 * half

    def copies(second):
        made = []
        for out, (ref, which) in enumerate(((keep_ref, core), (give_ref, 1 - core))):
            for c in range(wide1 // block):
                col = rank * wide1 + c * block
                if second:
                    source, at = proj_ref, which * half + col - 3 * half
                else:
                    source, at = qkv_ref, 2 * col + which * block
                made.append((source, at, block, ref, c * block))
        return made

    def run(plan, first):
        started = []
        for n, (source, at, size, ref, to) in enumerate(plan):
            copy = pltpu.make_async_copy(
                source.at[:, pl.ds(pl.multiple_of(at, LANES), size)], ref.at[:, pl.ds(to, size)], sems.at[first + n]
            )
            copy.start()
            started.append(copy)
        return started

    col = rank * wide2
    plan2 = []
    for ref, which in ((keep_ref, core), (give_ref, 1 - core)):
        at = col + (lax.div(col, unit) + which) * unit
        plan2.append((fc1_ref, at, wide2, ref, wide1))
    second = run(plan2, 0)

    @pl.when(is_proj)
    def _():
        for copy in run(copies(True), 2):
            copy.wait()

    @pl.when(jnp.logical_not(is_proj))
    def _():
        for copy in run(copies(False), 2):
            copy.wait()

    for copy in second:
        copy.wait()


def weight_share(rank, core, qkv_weight, proj_weight, fc1_weight, ranks, block, unit):
    rows = qkv_weight.shape[0]
    wide1, wide2 = 2 * D // ranks, fc1_weight.shape[1] // 2 // ranks
    out = jax.ShapeDtypeStruct((rows, wide1 + wide2), bf16)
    return pl.pallas_call(
        functools.partial(share_kernel, (wide1, wide2, block, unit, D // 2)),
        out_shape=[out, out],
        grid_spec=pltpu.PrefetchScalarGridSpec(
            num_scalar_prefetch=1,
            grid=(1,),
            in_specs=[pl.BlockSpec(memory_space=pl.ANY)] * 3,
            out_specs=[pl.BlockSpec(out.shape, lambda i, a: (0, 0))] * 2,
            scratch_shapes=[pltpu.SemaphoreType.DMA((2 + 2 * (wide1 // block),))],
        ),
        cost_estimate=SHORT,
        name="weight_share",
    )(jnp.stack([rank, core]).astype(jnp.int32), qkv_weight, proj_weight, fc1_weight)


def whole_specs(arrays):
    return [pl.BlockSpec(a.shape, lambda *_, n=len(a.shape): (0,) * n) for a in arrays]


def slot_lists(sizes):
    slots = []
    for number, size in enumerate(sizes):
        for start in range(0, size, LANES):
            slots.append((number, start, min(LANES, size - start)))
    return slots


def pack_kernel(slots, *refs):
    *sources, out_ref, held = refs
    per_row = held.shape[1] // LANES
    held[...] = jnp.zeros_like(held)
    for slot, (number, start, size) in enumerate(slots):
        row, at = slot // per_row, slot % per_row * LANES
        held[row : row + 1, at : at + size] = sources[number][:, start : start + size].astype(f32)
    out_ref[...] = held[...].astype(out_ref.dtype)


def pack_small(vectors, width, slots):
    shape = (32 * LANES // width, width)
    vectors = [v.reshape(1, -1) for v in vectors]
    return pl.pallas_call(
        functools.partial(pack_kernel, slots),
        out_shape=jax.ShapeDtypeStruct(shape, bf16),
        scratch_shapes=[pltpu.VMEM(shape, f32)],
        name="pack_small",
    )(*vectors)


def unpack_kernel(slots, depth, index_ref, *refs):
    pieces, (vec_ref, unit_ref, tag_ref) = refs[:depth], refs[depth:]
    here, core = index_ref[0], index_ref[1]
    rows, width = pieces[0].shape
    per_row = width // LANES
    single = sum(1 for number, _, _ in slots if number < 10)
    vec_ref[...] = jnp.zeros_like(vec_ref)
    for k in range(depth):
        place = lax.rem(here - k + depth, depth)
        values = pieces[k][...].astype(f32)

        def part(side, slot, size):
            row, at = side * (rows // 2) + slot // per_row, slot % per_row * LANES
            return values[row : row + 1, at : at + size]

        for slot, (number, start, size) in enumerate(slots):
            own, other = part(0, slot, size), part(1, slot, size)
            first = jnp.where(core == 0, own, other)
            second = jnp.where(core == 0, other, own)
            if number < 10:
                at = pl.multiple_of(place * 2 * size, 2 * size)
                vec_ref[number : number + 1, pl.ds(at, 2 * size)] = jnp.concatenate([first, second], axis=1)
            elif number == 10:
                wide = unit_ref.shape[1] // depth
                unit_ref[0:1, pl.ds(pl.multiple_of(place * wide + start, LANES), LANES)] = own
            else:
                wide = tag_ref.shape[1] // depth
                at = pl.multiple_of(place * wide + start, LANES)
                tag_ref[0:1, pl.ds(at, LANES)] = first
                tag_ref[0:1, pl.ds(pl.multiple_of(at + wide // 2, LANES), LANES)] = second


def unpack_small(pieces, slots, rows, here, core, units, group_tokens):
    depth = len(pieces)
    extra, width = pieces[0].shape[0] - rows, pieces[0].shape[1]
    shapes = [(16, D), (1, units), (1, group_tokens)]
    return pl.pallas_call(
        functools.partial(unpack_kernel, slots, depth),
        out_shape=[jax.ShapeDtypeStruct(s, f32) for s in shapes],
        grid_spec=pltpu.PrefetchScalarGridSpec(
            num_scalar_prefetch=1,
            grid=(1,),
            in_specs=[pl.BlockSpec((extra, width), lambda i, a: (rows // extra, 0))] * depth,
            out_specs=[pl.BlockSpec(s, lambda i, a: (0, 0)) for s in shapes],
        ),
        name="unpack_small",
    )(jnp.stack([here, core]).astype(jnp.int32), *pieces)


def pack_grads_kernel(depth, sizes, index_ref, *refs):
    *sources, out_ref = refs
    core = index_ref[0]
    out_ref[...] = jnp.zeros_like(out_ref)
    for z in range(depth):
        for c in range(2):
            row = 16 * c
            for source, (size, of_core) in zip(sources, sizes):
                for start in range(0, size, LANES):
                    lanes = min(LANES, size - start)
                    at = (z if of_core else 2 * z + c) * size + start
                    value = source[0:1, at : at + lanes]
                    if of_core:
                        value = jnp.where(core == c, value, 0.0)
                    out_ref[z, row : row + 1, 0:lanes] = value
                    row += 1


def pack_grads(vectors, sizes, core, depth):
    return pl.pallas_call(
        functools.partial(pack_grads_kernel, depth, sizes),
        out_shape=jax.ShapeDtypeStruct((depth, 32, LANES), f32),
        grid_spec=pltpu.PrefetchScalarGridSpec(
            num_scalar_prefetch=1,
            grid=(1,),
            in_specs=whole_specs(vectors),
            out_specs=pl.BlockSpec((depth, 32, LANES), lambda i, a: (0, 0, 0)),
        ),
        name="pack_grads",
    )(core.reshape(1).astype(jnp.int32), *vectors)


def grad_blocks_kernel(orders, ranks, index_ref, a_ref, b_ref, *refs):
    outs, held = refs[:-1], refs[-1]
    rank = index_ref[0]
    held[...] = dot_tn(a_ref[...], b_ref[...]).astype(bf16)
    width = held.shape[1] // ranks
    share = held.shape[0] // len(orders)
    for n, order in enumerate(orders):
        for which, offsets in enumerate(halves(ranks, order[0], list(range(ranks)))):
            for i, o in enumerate(offsets):
                cols = pl.ds(pl.multiple_of((rank ^ o) * width, width), width)
                outs[2 * n + which][i, 0] = held[n * share : (n + 1) * share, cols]


def grad_blocks(a, b, rank, orders, name):
    depth, ranks = lax.axis_size("fsdp") // 2, lax.axis_size("rep")
    tokens, rows, cols = a.shape[0], a.shape[1] // depth, b.shape[1]
    if cols // ranks % LANES:
        return relative_blocks(dot_tn(a, b).astype(bf16), rank, orders)
    block = (ranks // 2, depth, rows // len(orders), cols // ranks)
    outs = pl.pallas_call(
        functools.partial(grad_blocks_kernel, orders, ranks),
        out_shape=[jax.ShapeDtypeStruct(block, bf16)] * (2 * len(orders)),
        grid_spec=pltpu.PrefetchScalarGridSpec(
            num_scalar_prefetch=1,
            grid=(depth,),
            in_specs=[
                pl.BlockSpec((tokens, rows), lambda i, s: (0, i)),
                pl.BlockSpec((tokens, cols), lambda i, s: (0, 0)),
            ],
            out_specs=[pl.BlockSpec((block[0], 1) + block[2:], lambda i, s: (0, i, 0, 0))] * (2 * len(orders)),
            scratch_shapes=[pltpu.VMEM((rows, cols), bf16)],
        ),
        compiler_params=pltpu.CompilerParams(vmem_limit_bytes=40 << 20),
        cost_estimate=SHORT,
        name=name,
    )(rank.reshape(1).astype(jnp.int32), a, b)
    return [(outs[2 * n], outs[2 * n + 1]) for n in range(len(orders))]


def pre_grad_kernel(g_ref, w_ref, slope_ref, out_ref, sum_ref):
    grad = dot_nt(g_ref[...], w_ref[...]) * slope_ref[...]
    out_ref[...] = grad.astype(bf16)
    sum_ref[...] = jnp.sum(grad, axis=0, keepdims=True)


def pre_grads(mlp_grad, fc2_matrix, slope):
    tokens, units = slope.shape
    tile = 256
    return pl.pallas_call(
        pre_grad_kernel,
        out_shape=[jax.ShapeDtypeStruct((tokens, units), bf16), jax.ShapeDtypeStruct((1, units), f32)],
        grid=(units // tile,),
        in_specs=[
            pl.BlockSpec((tokens, D), lambda i: (0, 0)),
            pl.BlockSpec((tile, D), lambda i: (i, 0)),
            pl.BlockSpec((tokens, tile), lambda i: (0, i)),
        ],
        out_specs=[pl.BlockSpec((tokens, tile), lambda i: (0, i)), pl.BlockSpec((1, tile), lambda i: (0, i))],
        compiler_params=pltpu.CompilerParams(vmem_limit_bytes=40 << 20),
        cost_estimate=SHORT,
        name="pre_grad",
    )(mlp_grad, fc2_matrix, slope)


def product_kernel(half_ref, first_ref, second_ref, w_ref, out1_ref, out2_ref):
    out1_ref[...] = dot(first_ref[...], w_ref[...])
    out2_ref[...] = dot(second_ref[...], w_ref[...])


def product_nt_kernel(half_ref, first_ref, second_ref, w_ref, out1_ref, out2_ref, held):
    @pl.when(pl.program_id(0) == 0)
    def _():
        held[...] = w_ref[...].T

    out1_ref[...] = dot(first_ref[...], held[...])
    out2_ref[...] = dot(second_ref[...], held[...])


def product(a, weight, flipped, half, name):
    rows, tile = a.shape[0] // 2, 128
    count = rows // tile
    out = pl.BlockSpec((tile, D), lambda i, h: (i, 0))
    return pl.pallas_call(
        product_nt_kernel if flipped else product_kernel,
        out_shape=[jax.ShapeDtypeStruct((rows, D), f32)] * 2,
        grid_spec=pltpu.PrefetchScalarGridSpec(
            num_scalar_prefetch=1,
            grid=(count,),
            in_specs=[
                pl.BlockSpec((tile, a.shape[1]), lambda i, h: (i + h[0] * count, 0)),
                pl.BlockSpec((tile, a.shape[1]), lambda i, h: (i + (1 - h[0]) * count, 0)),
                pl.BlockSpec(weight.shape, lambda i, h: (0, 0)),
            ],
            out_specs=[out, out],
            scratch_shapes=[pltpu.VMEM(weight.shape[::-1], bf16)] if flipped else [],
        ),
        compiler_params=pltpu.CompilerParams(vmem_limit_bytes=32 << 20),
        cost_estimate=SHORT,
        name=name,
    )(jnp.asarray(half, jnp.int32).reshape(1), a, a, weight)


def finish_kernel(
    own1_ref, sent1_ref, tok_ref, grad_ref, own2_ref, sent2_ref, resid_ref, cot_ref, vec_ref,
    in_grad_ref, out_ref, sum_ref,
):
    grad = own1_ref[...] + sent1_ref[...]
    normal, inverse = normalize(tok_ref[...].astype(f32))
    in_grad_ref[...] = grad_ref[...] + norm_back(grad, normal, inverse, vec_ref[0:1, :])
    mlp = own2_ref[...] + sent2_ref[...] + vec_ref[8:9, :]
    out_ref[...] = (resid_ref[...] + vec_ref[9:10, :] * mlp).astype(bf16)
    out_grad = cot_ref[...].astype(f32)

    @pl.when(pl.program_id(0) == 0)
    def _():
        sum_ref[...] = jnp.zeros_like(sum_ref)

    for row, value in enumerate((grad * normal, grad, out_grad * vec_ref[9:10, :], out_grad * mlp)):
        sum_ref[row : row + 1, :] += jnp.sum(value, axis=0, keepdims=True)


def finish(own1, sent1, tok, resid_grad, own2, sent2, resid, cot, vecs):
    rows, tile = own1.shape[0], 64
    part = pl.BlockSpec((tile, D), lambda i: (i, 0))
    return pl.pallas_call(
        finish_kernel,
        out_shape=[
            jax.ShapeDtypeStruct((rows, D), f32), jax.ShapeDtypeStruct((rows, D), bf16),
            jax.ShapeDtypeStruct((8, D), f32),
        ],
        grid=(rows // tile,),
        in_specs=[part] * 8 + [pl.BlockSpec(vecs.shape, lambda i: (0, 0))],
        out_specs=[part, part, pl.BlockSpec((8, D), lambda i: (0, 0))],
        compiler_params=pltpu.CompilerParams(vmem_limit_bytes=24 << 20),
        cost_estimate=SHORT,
        name="finish",
    )(own1, sent1, tok, resid_grad, own2, sent2, resid, cot, vecs)


def norm_grad_kernel(own_ref, sent_ref, resid_ref, cot_ref, attn_ref, vec_ref, grad_ref, scaled_ref, sum_ref):
    grad = own_ref[...] + sent_ref[...]
    normal, inverse = normalize(resid_ref[...])
    resid_grad = cot_ref[...].astype(f32) + norm_back(grad, normal, inverse, vec_ref[6:7, :])
    scaled = resid_grad * vec_ref[5:6, :]
    grad_ref[...] = resid_grad
    scaled_ref[...] = scaled.astype(bf16)

    @pl.when(pl.program_id(0) == 0)
    def _():
        sum_ref[...] = jnp.zeros_like(sum_ref)

    for row, value in enumerate((grad * normal, grad, scaled, resid_grad * attn_ref[...])):
        sum_ref[row : row + 1, :] += jnp.sum(value, axis=0, keepdims=True)


def norm_grads(own, sent, resid, cot, attn_out, vecs):
    rows, tile = own.shape[0], 64
    part = pl.BlockSpec((tile, D), lambda i: (i, 0))
    return pl.pallas_call(
        norm_grad_kernel,
        out_shape=[
            jax.ShapeDtypeStruct((rows, D), f32), jax.ShapeDtypeStruct((rows, D), bf16),
            jax.ShapeDtypeStruct((8, D), f32),
        ],
        grid=(rows // tile,),
        in_specs=[part] * 5 + [pl.BlockSpec(vecs.shape, lambda i: (0, 0))],
        out_specs=[part, part, pl.BlockSpec((8, D), lambda i: (0, 0))],
        compiler_params=pltpu.CompilerParams(vmem_limit_bytes=24 << 20),
        cost_estimate=SHORT,
        name="norm_grad",
    )(own, sent, resid, cot, attn_out, vecs)


def proj_grad_kernel(head_rows, c_ref, g_ref, out_ref):
    wide = out_ref.shape[1]
    for side in range(2):
        grad = dot_tn(c_ref[...], g_ref[:, side * wide : (side + 1) * wide]).astype(bf16)
        for z in range(grad.shape[0] // head_rows):
            at = (2 * z + side) * head_rows
            out_ref[at : at + head_rows, :] = grad[z * head_rows : (z + 1) * head_rows]


def packed_proj_grad(context, attn_grad, head_rows):
    wide = D // 2
    return pl.pallas_call(
        functools.partial(proj_grad_kernel, head_rows),
        out_shape=jax.ShapeDtypeStruct((D, wide), bf16),
        compiler_params=pltpu.CompilerParams(vmem_limit_bytes=32 << 20),
        cost_estimate=SHORT,
        name="proj_grad",
    )(context, attn_grad)


def qkv_grad_kernel(orders, ranks, depth, per, index_ref, n_ref, *refs):
    grads, p_ref = refs[: 3 * per], refs[3 * per]
    outs, held = refs[3 * per + 1 : -1], refs[-1]
    rank = index_ref[0]
    normed = n_ref[...]
    for number in range(3):
        pieces = [g[...] for g in grads[number * per : (number + 1) * per]]
        wide = per * LANES
        joined = pieces[0] if per == 1 else jnp.concatenate(pieces, axis=1)
        held[:, number * wide : (number + 1) * wide] = dot_tn(normed, joined).astype(bf16)
    held[:, 3 * per * LANES :] = p_ref[...]
    width = held.shape[1] // ranks
    rows = held.shape[0] // depth
    share = rows // len(orders)
    for n, order in enumerate(orders):
        for which, offsets in enumerate(halves(ranks, order[0], list(range(ranks)))):
            for i, o in enumerate(offsets):
                cols = pl.ds(pl.multiple_of((rank ^ o) * width, width), width)
                for z in range(depth):
                    at = z * rows + n * share
                    outs[2 * n + which][i, z] = held[at : at + share, cols]


def qkv_grad_blocks(normed, grads, proj_packed, part, parts, rank, orders):
    depth, ranks = lax.axis_size("fsdp") // 2, lax.axis_size("rep")
    per = len(grads) // 3
    cols = 4 * per * LANES
    block = (ranks // 2, depth, D // depth // len(orders), cols // ranks)
    tokens = normed.shape[0] // 3
    outs = pl.pallas_call(
        functools.partial(qkv_grad_kernel, orders, ranks, depth, per),
        out_shape=[jax.ShapeDtypeStruct(block, bf16)] * (2 * len(orders)),
        grid_spec=pltpu.PrefetchScalarGridSpec(
            num_scalar_prefetch=1,
            grid=(1,),
            in_specs=[pl.BlockSpec((tokens, D), lambda i, a: (1, 0))]
            + whole_specs(grads)
            + [pl.BlockSpec((D, per * LANES), lambda i, a: (0, part))],
            out_specs=[pl.BlockSpec(block, lambda i, a: (0, 0, 0, 0))] * (2 * len(orders)),
            scratch_shapes=[pltpu.VMEM((D, cols), bf16)],
        ),
        compiler_params=pltpu.CompilerParams(vmem_limit_bytes=40 << 20),
        cost_estimate=SHORT,
        name="qkv_grad",
    )(rank.reshape(1).astype(jnp.int32), normed, *grads, proj_packed)
    return [(outs[2 * n], outs[2 * n + 1]) for n in range(len(orders))]


def spread_lanes(tags, width):
    return jnp.concatenate([tags] * (width // LANES), axis=1)


def project_kernel(need_ref, n_ref, w_ref, b_ref, q_ref, k_ref, v_ref):
    row = pl.program_id(0)
    wide = q_ref.shape[1]

    @pl.when(need_ref[row] > 0)
    def _():
        n = n_ref[...]
        for i, ref in enumerate((q_ref, k_ref, v_ref)):
            out = dot(n, w_ref[:, i * wide : (i + 1) * wide]) + b_ref[0:1, i * wide : (i + 1) * wide]
            if i == 0:
                out = out.astype(bf16).astype(f32) * HEAD_DIM ** (-0.5)
            ref[...] = out.astype(bf16)

    @pl.when(need_ref[row] == 0)
    def _():
        for ref in (q_ref, k_ref, v_ref):
            ref[...] = jnp.zeros_like(ref)


def project(need, normed, weight, bias, wide):
    rows = normed.shape[0]
    return pl.pallas_call(
        project_kernel,
        out_shape=[jax.ShapeDtypeStruct((rows, wide), bf16)] * 3,
        grid_spec=pltpu.PrefetchScalarGridSpec(
            num_scalar_prefetch=1,
            grid=(rows // BLOCK,),
            in_specs=[
                pl.BlockSpec((BLOCK, D), lambda i, s: (i, 0)),
                pl.BlockSpec(weight.shape, lambda i, s: (0, 0)),
                pl.BlockSpec((1, 3 * wide), lambda i, s: (0, 0)),
            ],
            out_specs=[pl.BlockSpec((BLOCK, wide), lambda i, s: (i, 0))] * 3,
        ),
        compiler_params=pltpu.CompilerParams(vmem_limit_bytes=32 << 20),
        cost_estimate=SHORT,
        name="project",
    )(need, normed, weight, bias)


def norm_kernel(need_ref, info_ref, *refs):
    *sources, vec_ref, out_ref = refs
    row = pl.program_id(0)
    side = (row // info_ref[1]) % 2
    chip = row // (2 * info_ref[1])

    @pl.when(need_ref[row] > 0)
    def _():
        picked = jnp.where(chip == 0, sources[0][...], jnp.where(chip == 1, sources[2][...], sources[4][...]))
        theirs = jnp.where(chip == 0, sources[1][...], jnp.where(chip == 1, sources[3][...], sources[5][...]))
        picked = jnp.where(side == info_ref[0], picked, theirs)
        normal, _ = normalize(picked.astype(f32))
        out_ref[...] = (normal * vec_ref[0:1, :] + vec_ref[1:2, :]).astype(bf16)

    @pl.when(need_ref[row] == 0)
    def _():
        out_ref[...] = jnp.zeros_like(out_ref)


def norm_window(need, info, sources, vecs, window, count):
    per = count // BLOCK

    def spec(chip):
        def index(i, a, b):
            inside = jnp.clip(i - 2 * per * chip, 0, 2 * per - 1)
            return (inside % per, 0)

        return pl.BlockSpec((BLOCK, D), index)

    return pl.pallas_call(
        norm_kernel,
        out_shape=jax.ShapeDtypeStruct((window, D), bf16),
        grid_spec=pltpu.PrefetchScalarGridSpec(
            num_scalar_prefetch=2,
            grid=(window // BLOCK,),
            in_specs=[spec(i // 2) for i in range(6)] + [pl.BlockSpec(vecs.shape, lambda i, a, b: (0, 0))],
            out_specs=pl.BlockSpec((BLOCK, D), lambda i, a, b: (i, 0)),
        ),
        compiler_params=pltpu.CompilerParams(vmem_limit_bytes=24 << 20),
        cost_estimate=SHORT,
        name="norm_window",
    )(need, info, *sources, vecs)


def attend_kernel(lo_ref, hi_ref, first_ref, last_ref, q_ref, k_ref, v_ref, qt_ref, kt_ref, o_ref, lse_ref, s_ref, m_ref, acc_ref):
    i = pl.program_id(0)
    left = lax.broadcasted_iota(jnp.int32, (1, LANES), 1) < HEAD_DIM
    lo, hi = lo_ref[i], hi_ref[i]
    base = (first_ref.shape[0] - pl.num_programs(0)) // 2
    q = q_ref[...]
    zero = jnp.zeros_like(q)
    heads = (jnp.where(left, q, zero), jnp.where(left, zero, q))
    m_ref[...] = jnp.full_like(m_ref, MASKED)
    one_image = first_ref[base + i] == last_ref[base + i]
    folds = BLOCK // LANES

    def fold(value, combine):
        parts = [value[:, n * LANES : (n + 1) * LANES] for n in range(folds)]
        return functools.reduce(combine, parts)

    def scores(j, carry):
        at = pl.multiple_of(j * BLOCK, BLOCK)
        k = k_ref[pl.ds(at, BLOCK), :]
        inside = one_image & (first_ref[j] == first_ref[base + i]) & (last_ref[j] == first_ref[base + i])

        @pl.when(inside)
        def _():
            for h in range(2):
                s = dot_nt(heads[h], k)
                s_ref[h, j] = s
                m_ref[h] = jnp.maximum(m_ref[h], fold(s, jnp.maximum))

        @pl.when(jnp.logical_not(inside))
        def _():
            same = spread_lanes(qt_ref[...], BLOCK) == kt_ref[:, pl.ds(at, BLOCK)]
            for h in range(2):
                s = jnp.where(same, dot_nt(heads[h], k), MASKED)
                s_ref[h, j] = s
                m_ref[h] = jnp.maximum(m_ref[h], fold(s, jnp.maximum))

        return carry

    lax.fori_loop(lo, hi, scores, 0)
    tops = [jnp.max(m_ref[h], axis=1, keepdims=True) for h in range(2)]
    m_ref[...] = jnp.zeros_like(m_ref)
    acc_ref[...] = jnp.zeros_like(acc_ref)

    def mix(j, carry):
        at = pl.multiple_of(j * BLOCK, BLOCK)
        v = v_ref[pl.ds(at, BLOCK), :]
        for h in range(2):
            e = jnp.exp(s_ref[h, j] - tops[h])
            m_ref[h] += fold(e, jnp.add)
            acc_ref[h] += dot(e.astype(bf16), v)
        return carry

    lax.fori_loop(lo, hi, mix, 0)
    sums = [jnp.sum(m_ref[h], axis=1, keepdims=True) for h in range(2)]
    o_ref[...] = jnp.where(left, acc_ref[0] / sums[0], acc_ref[1] / sums[1]).astype(bf16)
    for h in range(2):
        lse = jnp.broadcast_to(tops[h] + jnp.log(sums[h]), (BLOCK, LANES))
        lse_ref[0, h : h + 1, :] = lse.T[0:1, :]


def attend(lo, hi, firsts, lasts, q, k, v, tag_cols, tag_row, own_rows, pair):
    window = q.shape[0]
    blocks = own_rows // BLOCK
    skip = (window - own_rows) // 2 // BLOCK
    return pl.pallas_call(
        attend_kernel,
        out_shape=[
            jax.ShapeDtypeStruct((own_rows, LANES), bf16),
            jax.ShapeDtypeStruct((1, 2, own_rows), f32),
        ],
        grid_spec=pltpu.PrefetchScalarGridSpec(
            num_scalar_prefetch=4,
            grid=(blocks,),
            in_specs=[
                pl.BlockSpec((BLOCK, LANES), lambda i, *_: (i + skip, pair)),
                pl.BlockSpec((window, LANES), lambda i, *_: (0, pair)),
                pl.BlockSpec((window, LANES), lambda i, *_: (0, pair)),
                pl.BlockSpec((BLOCK, LANES), lambda i, *_: (i + skip, 0)),
                pl.BlockSpec((1, window), lambda i, *_: (0, 0)),
            ],
            out_specs=[
                pl.BlockSpec((BLOCK, LANES), lambda i, *_: (i, 0)),
                pl.BlockSpec((1, 2, BLOCK), lambda i, *_: (0, 0, i)),
            ],
            scratch_shapes=[
                pltpu.VMEM((2, window // BLOCK, BLOCK, BLOCK), f32),
                pltpu.VMEM((2, BLOCK, LANES), f32),
                pltpu.VMEM((2, BLOCK, LANES), f32),
            ],
        ),
        compiler_params=pltpu.CompilerParams(vmem_limit_bytes=32 << 20),
        cost_estimate=SHORT,
        name="attend",
    )(lo, hi, firsts, lasts, q, k, v, tag_cols, tag_row)


def attend_back_kernel(
    start, stop, lo_ref, hi_ref, q_ref, k_ref, v_ref, g_ref, tc_ref, tr_ref, lse_ref, delta_ref,
    dq_ref, dk_ref, dv_ref, sum_ref, dk_acc, dv_acc, dq_acc,
):
    first = lax.broadcasted_iota(jnp.int32, (1, LANES), 1) < HEAD_DIM
    dk_acc[...] = jnp.zeros_like(dk_acc)
    dv_acc[...] = jnp.zeros_like(dv_acc)
    sum_ref[...] = jnp.zeros_like(sum_ref)

    def split(value):
        zero = jnp.zeros_like(value)
        return jnp.where(first, value, zero), jnp.where(first, zero, value)

    def visit(i, j, qs, gs, of_key, of_query):
        at_q, at_k = pl.multiple_of(i * BLOCK, BLOCK), pl.multiple_of(j * BLOCK, BLOCK)
        k = k_ref[pl.ds(at_k, BLOCK), :]
        v = v_ref[pl.ds(at_k, BLOCK), :]
        same = spread_lanes(tc_ref[pl.ds(at_k, BLOCK), :], BLOCK) == tr_ref[:, pl.ds(at_q, BLOCK)]
        ps, ds = [], []
        for h in range(2):
            s = dot_nt(k, qs[h])
            dp = dot_nt(v, gs[h])
            p = jnp.where(same, jnp.exp(s - lse_ref[0, h : h + 1, pl.ds(at_q, BLOCK)]), 0.0)
            d = p * (dp - delta_ref[0, h : h + 1, pl.ds(at_q, BLOCK)])
            ps.append(p.astype(bf16))
            ds.append(d.astype(bf16))
        if of_key:
            at = pl.multiple_of((j - start) * BLOCK, BLOCK)
            dv_acc[pl.ds(at, BLOCK), :] += dot(ps[0], gs[0]) + dot(ps[1], gs[1])
            dk_acc[pl.ds(at, BLOCK), :] += dot(ds[0], qs[0]) + dot(ds[1], qs[1])
        if of_query:
            ks = split(k)
            dq_acc[...] += dot_tn(ds[0], ks[0]) + dot_tn(ds[1], ks[1])

    def query_block(own_q, i, carry):
        at_q = pl.multiple_of(i * BLOCK, BLOCK)
        qs = split(q_ref[pl.ds(at_q, BLOCK), :])
        gs = split(g_ref[pl.ds(at_q, BLOCK), :])
        lo, hi = lo_ref[i], hi_ref[i]

        def keys(first_key, last_key, of_key):
            def body(j, carry):
                visit(i, j, qs, gs, of_key, own_q)
                return carry

            lax.fori_loop(first_key, last_key, body, 0)

        if own_q:
            dq_acc[...] = jnp.zeros_like(dq_acc)
            keys(lo, jnp.minimum(hi, start), False)
            keys(jnp.maximum(lo, stop), hi, False)
        keys(jnp.maximum(lo, start), jnp.minimum(hi, stop), True)
        if own_q:
            at = pl.multiple_of((i - start) * BLOCK, BLOCK)
            dq = dq_acc[...] * HEAD_DIM ** (-0.5)
            dq_ref[pl.ds(at, BLOCK), :] = dq.astype(bf16)
            sum_ref[0, 0:1, :] += jnp.sum(dq, axis=0, keepdims=True)
        return carry

    before = jnp.where(lo_ref[start] < start, lo_ref[start], start)
    after = jnp.maximum(hi_ref[stop - 1], stop)
    lax.fori_loop(before, start, functools.partial(query_block, False), 0)
    lax.fori_loop(start, stop, functools.partial(query_block, True), 0)
    lax.fori_loop(stop, after, functools.partial(query_block, False), 0)
    dk_ref[...] = dk_acc[...].astype(bf16)
    dv_ref[...] = dv_acc[...].astype(bf16)
    sum_ref[0, 1:2, :] = jnp.sum(dv_acc[...], axis=0, keepdims=True)


def attend_back(lo, hi, q, k, v, g, tag_cols, tag_row, lse, delta, own_rows, pair):
    window = q.shape[0]
    pairs, wide = 1, LANES
    grad_pair = pair % (g.shape[1] // LANES)
    start = (window - own_rows) // 2 // BLOCK
    stop = start + own_rows // BLOCK
    whole = lambda: pl.BlockSpec((window, LANES), lambda p, a, b: (0, pair))
    own = lambda: pl.BlockSpec((own_rows, LANES), lambda p, a, b: (0, p))
    stat = lambda: pl.BlockSpec((1, 2, window), lambda p, a, b: (pair, 0, 0))
    return pl.pallas_call(
        functools.partial(attend_back_kernel, start, stop),
        out_shape=[jax.ShapeDtypeStruct((own_rows, wide), bf16)] * 3
        + [jax.ShapeDtypeStruct((pairs, 8, LANES), f32)],
        grid_spec=pltpu.PrefetchScalarGridSpec(
            num_scalar_prefetch=2,
            grid=(pairs,),
            in_specs=[
                whole(), whole(), whole(),
                pl.BlockSpec((window, LANES), lambda p, a, b: (0, grad_pair)),
                pl.BlockSpec((window, LANES), lambda p, a, b: (0, 0)),
                pl.BlockSpec((1, window), lambda p, a, b: (0, 0)),
                stat(), stat(),
            ],
            out_specs=[own(), own(), own(), pl.BlockSpec((1, 8, LANES), lambda p, a, b: (p, 0, 0))],
            scratch_shapes=[
                pltpu.VMEM((own_rows, LANES), f32),
                pltpu.VMEM((own_rows, LANES), f32),
                pltpu.VMEM((BLOCK, LANES), f32),
            ],
        ),
        compiler_params=pltpu.CompilerParams(vmem_limit_bytes=40 << 20),
        cost_estimate=SHORT,
        name="attend_back",
    )(lo, hi, q, k, v, g, tag_cols, tag_row, lse, delta)


def on_device(
    tokens, image_ids, ln1_gain, ln1_bias, qkv_weight, query_bias, value_bias, proj_weight,
    proj_bias, scale_attn, ln2_gain, ln2_bias, fc1_weight, fc1_bias, fc2_weight, fc2_bias,
    scale_mlp, cotangent,
):
    devices = lax.axis_size("fsdp")
    depth, ranks = devices // 2, lax.axis_size("rep")
    place = lax.axis_index("fsdp")
    rank = lax.axis_index("rep")
    here, core = place // 2, place % 2
    count = tokens.shape[1]
    chip = 2 * count
    head_rows = D // devices
    ff = fc1_weight.shape[1]
    unit_rows = ff // devices
    half_heads = D // 2
    local_heads = half_heads // HEAD_DIM
    pairs = half_heads // LANES
    bits = list(range(rep_bits()))

    def in_order(own, other, axis=0):
        return jnp.where(
            core == 0,
            jnp.concatenate([own, other], axis=axis),
            jnp.concatenate([other, own], axis=axis),
        )

    def mine(value):
        return lax.dynamic_slice_in_dim(value, core * count, count, 0)

    def others(value):
        return lax.dynamic_slice_in_dim(value, (1 - core) * count, count, 0)

    def every_other(value, width, start):
        cuts = range(start * width, value.shape[1], 2 * width)
        return jnp.concatenate([value[:, c : c + width] for c in cuts], axis=1)

    def all_share(which):
        pick_cols = lambda v, w: jnp.where(which == 0, every_other(v, w, 0), every_other(v, w, 1))
        heads = lax.dynamic_slice_in_dim(
            jnp.concatenate(
                [
                    pick_cols(qkv_weight, head_rows),
                    lax.dynamic_slice_in_dim(proj_weight, which * half_heads, half_heads, 1),
                ],
                axis=1,
            ),
            rank * (2 * D // ranks), 2 * D // ranks, 1,
        )
        units = lax.dynamic_slice_in_dim(
            pick_cols(fc1_weight, unit_rows), rank * (ff // 2 // ranks), ff // 2 // ranks, 1
        )
        return jnp.concatenate([heads, units], axis=1)

    if head_rows % LANES:
        kept, given = all_share(core), all_share(1 - core)
    else:
        kept, given = weight_share(
            rank, core, qkv_weight, proj_weight, fc1_weight, ranks, head_rows, unit_rows
        )
    wide1 = 2 * D // ranks
    got = swap_cores(given)
    is_proj = rank * wide1 >= 3 * half_heads
    own1 = in_order(kept[:, :wide1], jnp.where(is_proj, given[:, :wide1], got[:, :wide1]))
    own2 = in_order(kept[:, wide1:], got[:, wide1:])
    own3 = lax.dynamic_slice_in_dim(fc2_weight, rank * (D // ranks), D // ranks, 1)
    small = (
        ln1_gain, ln1_bias, query_bias, value_bias, proj_bias, scale_attn, ln2_gain, ln2_bias,
        fc2_bias, scale_mlp, fc1_bias, (image_ids[0] + 1).astype(bf16),
    )
    sizes = [v.shape[0] for v in small]
    slots = slot_lists(sizes)
    width = 2 * D // ranks
    small = pack_small(small, width, slots)
    small_other = swap_cores(small)
    rows1, rows3 = own1.shape[0], own3.shape[0]
    tok, cot = tokens[0], cotangent[0]
    tok_other = swap_cores(tok)
    cot_other = swap_cores(cot)
    own1 = jnp.concatenate([own1, small, small_other])
    own1, own2, own3, tok = tie(own1, own2, own3, tok)
    pieces1 = fetch_z(own1)
    tok, pieces1[1] = tie(tok, pieces1[1])
    behind, ahead = from_chip(tok, 1), from_chip(tok, -1)
    gather1 = Gather(pieces1, rows1, "gather1")
    gather1.send()
    behind_other, ahead_other = swap_cores(behind), swap_cores(ahead)
    for _ in bits[1:]:
        gather1.send()

    vec_rows, fc1_shift, all_tags = unpack_small(
        pieces1, slots, rows1, here, core, ff // 2, devices * count
    )
    vector = lambda i: vec_rows[i : i + 1]
    (
        attn_gain, attn_shift, query_shift, value_shift, proj_shift, attn_scale, mlp_gain,
        mlp_shift, fc2_shift, mlp_scale,
    ) = map(vector, range(10))
    core_part = lambda vec: jnp.where(
        core == 0, every_other(vec, head_rows, 0), every_other(vec, head_rows, 1)
    )

    window = 3 * chip
    padded = jnp.concatenate(
        [jnp.zeros((1, chip), f32), all_tags, jnp.full((1, chip), 1e6, f32)], axis=1
    )
    tag_row = lax.dynamic_slice(padded, (0, here * chip), (1, window))
    tags = tag_row.reshape(window)
    firsts, lasts = tags[::BLOCK], tags[BLOCK - 1 :: BLOCK]
    real = firsts * (1e6 - firsts) > 0
    below = jnp.sum((tag_row < firsts[:, None]).astype(jnp.int32), axis=1)
    upto = jnp.sum((tag_row <= lasts[:, None]).astype(jnp.int32), axis=1)
    blocks = window // BLOCK
    block_lo = jnp.where(real, below // BLOCK, 0)
    block_hi = jnp.where(real, (upto + BLOCK - 1) // BLOCK, 0)
    own_lo, own_hi = chip // BLOCK, 2 * chip // BLOCK
    numbers = jnp.arange(blocks)
    need = jnp.logical_and(numbers >= block_lo[own_lo], numbers < block_hi[own_hi - 1]).astype(jnp.int32)
    firsts, lasts = firsts.astype(jnp.int32), lasts.astype(jnp.int32)
    tag_cols = jnp.broadcast_to(tags[:, None], (window, LANES))

    info = jnp.stack([core, jnp.int32(count // BLOCK)]).astype(jnp.int32)
    normed1 = norm_window(
        need, info, (behind, behind_other, tok, tok_other, ahead, ahead_other), vec_rows, window, count
    )

    normed1, own2 = tie(normed1, own2)
    pieces2 = fetch_z(own2)
    normed1 = gather1.arrive(normed1)
    qkv_matrix, proj_matrix = gather1.assemble(here, rank, head_rows)

    shifts = jnp.concatenate(
        [core_part(query_shift), jnp.zeros((1, half_heads), f32), core_part(value_shift)], axis=1
    )
    queries, keys, values = project(need, normed1, qkv_matrix, shifts, half_heads)

    contexts, lses = [], []
    los = block_lo[own_lo:own_hi]
    los, queries = tie(los, queries)
    for pair in range(pairs):
        if pair == 1:
            los, own3, *pieces2 = tie(los, own3, *pieces2)
            gather2 = Gather(pieces2, rows1, "gather2")
            los = gather2.send(los)
            pieces3 = fetch_z(own3)
        if pair == 2:
            los = gather2.arrive(los)
            los = gather2.send(los)
        if pair == 3:
            los = gather2.arrive(los)
            for _ in bits[2:]:
                los = gather2.arrive(gather2.send(los))
            los, *pieces3 = tie(los, *pieces3)
            gather3 = Gather(pieces3, rows3, "gather3")
            los = gather3.send(los)
        context, lse = attend(
            los, block_hi[own_lo:own_hi], firsts, lasts, queries, keys, values, tag_cols,
            tag_row, chip, pair,
        )
        los, context = tie(los, context)
        contexts.append(context)
        lses.append(lse)
    context = jnp.concatenate(contexts, axis=1)
    lse_rows = jnp.concatenate(lses).reshape(local_heads, chip)
    context = gather3.arrive(context)
    context = gather3.send(context)
    fc1_matrix = gather2.assemble(here, rank)

    features = tok.astype(f32)
    sent = swap_cores(dot(others(context), proj_matrix))
    attn_out = dot(mine(context), proj_matrix) + sent + proj_shift
    resid = features + attn_scale * attn_out
    mlp_normal, mlp_inverse = normalize(resid)
    mlp_input = (mlp_normal * mlp_gain + mlp_shift).astype(bf16)
    mlp_input = jnp.concatenate([mlp_input, swap_cores(mlp_input)])
    pre_act = dot(mlp_input, fc1_matrix) + fc1_shift
    activated, slope = gelu_pair(pre_act)
    activated = activated.astype(bf16)

    out_grad = cot.astype(f32)
    mlp_grad_full = out_grad * mlp_scale
    mlp_grad = (jnp.concatenate([cot, cot_other]).astype(f32) * mlp_scale).astype(bf16)

    both = [bits, bits[::-1]]
    activated = gather3.arrive(activated)
    for _ in bits[2:]:
        activated = gather3.arrive(gather3.send(activated))
    reduce3 = Reduce(grad_blocks(activated, mlp_grad, rank, both, "fc2_grad"), here, both)
    mlp_grad = reduce3.send(mlp_grad)
    fc2_matrix = gather3.assemble(here, rank)
    pre_grad, fc1_bias_part = pre_grads(mlp_grad, fc2_matrix, slope)
    reduce2 = Reduce(grad_blocks(mlp_input, pre_grad, rank, both, "fc1_grad"), here, both)
    pre_grad, _ = tie(pre_grad, [give for _, _, give in reduce2.held])
    own, given = product(pre_grad, fc1_matrix, True, 0, "mlp_in_grad")
    own, given = reduce3.arrive(own, given)
    for _ in bits[2:]:
        own, given = reduce3.arrive(*reduce3.send(own, given))
    own, given = reduce3.send(own, given)
    sent = swap_cores(given)
    resid_grad, attn_grad, norm_sums = norm_grads(own, sent, resid, cot, attn_out, vec_rows)
    attn_grad = in_order(attn_grad, swap_cores(attn_grad))
    context_grad = dot_nt(attn_grad, proj_matrix).astype(bf16)
    head_of = (
        lax.broadcasted_iota(jnp.int32, (local_heads, half_heads), 1) // HEAD_DIM
        == lax.broadcasted_iota(jnp.int32, (local_heads, half_heads), 0)
    ).astype(f32)
    row_delta = lax.dot_general(
        head_of, context_grad.astype(f32) * context.astype(f32), (((1,), (1,)), ((), ())),
        precision=lax.Precision.HIGHEST, preferred_element_type=f32,
    )
    stats = jnp.concatenate([lse_rows, row_delta])
    context_grad, activated, attn_grad = tie(context_grad, activated, attn_grad)
    chunk = half_heads // 2
    chunks = [context_grad[:, :chunk], context_grad[:, chunk:]]
    grads_behind, grads_ahead = zip(*[(from_chip(c, 1), from_chip(c, -1)) for c in chunks])
    stats_behind, stats_ahead = from_chip(stats, 1), from_chip(stats, -1)
    proj_grad = packed_proj_grad(context, attn_grad, head_rows)
    stat_window = jnp.concatenate([stats_behind, stats, stats_ahead], axis=1)
    by_pair = lambda s: s.reshape(pairs, 2, window)
    lse_window, delta_window = by_pair(stat_window[:local_heads]), by_pair(stat_window[local_heads:])

    half_pairs = pairs // 2
    half_width = half_heads // 2

    def first_group(parts, number):
        grads = [g for kind in zip(*parts) for g in kind]
        return Reduce(
            qkv_grad_blocks(normed1, grads, proj_grad, number, 2, rank, both), here, both
        )

    parts, sums = [], []
    first, delta_window, lo = settle(
        ((grads_behind[0], grads_ahead[0]), delta_window, block_lo), (reduce3, "received")
    )
    sides = [first, *list(zip(grads_behind, grads_ahead))[1:]]
    grad_windows = [jnp.concatenate([b, c, a]) for c, (b, a) in zip(chunks, sides)]
    for pair in range(pairs):
        if pair == 0:
            lo = reduce3.arrive(lo)
            lo = reduce2.send(lo)
        if pair == 1:
            lo = reduce2.arrive(lo)
            lo = reduce3.send_z(lo)
            for _ in bits[2:]:
                lo = reduce2.arrive(reduce2.send(lo))
            lo = reduce2.send(lo)
        if pair == 2:
            lo = settle(lo, (reduce2, "received"), (reduce3, "pieces"))
            lo = reduce2.arrive(lo)
            lo = reduce2.send_z(lo)
            reduce1a = first_group(parts, 0)
            lo = reduce1a.send(lo)
        if pair == 3:
            lo = settle(lo, (reduce2, "pieces"), (reduce1a, "received"))
            lo = reduce3.arrive_z(lo)
            lo = reduce2.arrive_z(lo)
            fc2_part = reduce3.total.astype(bf16)
            fc1_part = reduce2.total.astype(bf16)
            split = fc2_part.shape[0] // fc1_part.shape[0]
            mlp_spread = Spread(jnp.concatenate([fc1_part, *jnp.split(fc2_part, split)], axis=1))
            lo = mlp_spread.send(lo)
            lo = reduce1a.arrive(lo)
            for _ in bits[2:]:
                lo = reduce1a.arrive(reduce1a.send(lo))
            lo = reduce1a.send(lo)
        *grads, total = attend_back(
            lo, block_hi, queries, keys, values, grad_windows[pair * 2 // pairs], tag_cols, tag_row, lse_window,
            delta_window, chip, pair,
        )
        lo, *grads = tie(lo, *grads)
        parts.append(grads)
        sums.append(total[0])

    parts[-1], activated = settle((parts[-1], activated), (mlp_spread, "arrays"))
    parts[-1] = reduce1a.arrive(parts[-1])
    parts[-1] = reduce1a.send_z(parts[-1])
    reduce1b = first_group(parts[half_pairs:], 1)
    parts[-1], activated = reduce1b.send(parts[-1], activated)
    every = [jnp.concatenate(p, axis=1) for p in zip(*parts)]

    factor = 1.0 / math.sqrt(count * devices * ranks)
    in_own, in_given = product(
        jnp.concatenate(every, axis=1), qkv_matrix, True, core, "attn_in_grad"
    )
    out_own, out_given = product(activated, fc2_matrix, False, 0, "mlp_out")
    tail = (in_own, in_given, out_own, out_given)
    tail = settle(tail, (reduce1b, "received"), (reduce1a, "pieces"))
    for _ in bits[1:]:
        tail = reduce1b.arrive(tail)
        tail = reduce1b.send(tail)
    in_own, in_given, out_own, out_given = tail
    input_rows, output_rows, end_sums = finish(
        in_own, swap_cores(in_given), tok, resid_grad, out_own, swap_cores(out_given), resid, cot, vec_rows
    )

    vectors = (
        end_sums[0:1], end_sums[1:2],
        jnp.concatenate([s[0:1] for s in sums], axis=1), jnp.concatenate([s[1:2] for s in sums], axis=1),
        norm_sums[2:3], norm_sums[3:4], norm_sums[0:1], norm_sums[1:2],
        end_sums[2:3], end_sums[3:4], fc1_bias_part,
    )
    of_core = [number in (2, 3, 10) for number in range(11)]
    partial = pack_grads(vectors, list(zip(sizes, of_core)), core, depth)
    partial = reduce1b.arrive(partial)
    partial = reduce1b.send_z(partial)
    for _ in bits[1:]:
        partial = mlp_spread.send(partial)

    vec_total = pick(partial, here, 0)
    for k in range(1, depth):
        vec_total = vec_total + along_z(pick(partial, lax.rem(here + k, depth), 0), k)
    reduce1a.arrive_z()
    vec_total = reduce1b.arrive_z(vec_total)
    vec_total = settle(vec_total, (mlp_spread, "arrays"))
    first_spread = Spread(jnp.concatenate([reduce1a.total, reduce1b.total], axis=1).astype(bf16))
    for bit in bits:
        first_spread.send()
        vec_total = vec_total + across_rep(vec_total, bit)
    vec_half = vec_total.reshape(2, 16, LANES)
    totals = (pick(vec_half, core, 0) + swap_cores(pick(vec_half, 1 - core, 0))) * factor

    mlp_cols = fc1_part.shape[1]
    fc1_full = mlp_spread.blocks(rank, 0, mlp_cols)
    fc2_width = fc2_part.shape[1]
    fc2_full = tie(*[mlp_spread.blocks(rank, mlp_cols + n * fc2_width, fc2_width) for n in range(split)])
    grad_fc2 = jnp.concatenate(fc2_full).astype(f32) * factor
    vec_width = D // ranks
    first_a = first_spread.blocks(rank, 0, vec_width)
    first_b = first_spread.blocks(rank, vec_width, vec_width)

    def rows_of(value, index):
        return lax.dynamic_slice_in_dim(value, index * head_rows, head_rows, 0)

    def interleave(own, other, width):
        cuts = range(0, own.shape[1], width)
        zipped = lambda a, b: jnp.concatenate(
            [v[:, c : c + width] for c in cuts for v in (a, b)], axis=1
        )
        return jnp.where(core == 0, zipped(own, other), zipped(other, own)).astype(f32) * factor

    fc1_other = swap_cores(rows_of(fc1_full, 1 - core))
    grad_fc1 = interleave(rows_of(fc1_full, core), fc1_other, unit_rows)
    qkv_full = jnp.concatenate(
        [
            part[:, n * half_width : (n + 1) * half_width]
            for n in range(3)
            for part in (first_a, first_b)
        ],
        axis=1,
    )
    grad_qkv = interleave(rows_of(qkv_full, core), swap_cores(rows_of(qkv_full, 1 - core)), head_rows)
    proj_part = jnp.concatenate([first_a[:, 3 * half_width :], first_b[:, 3 * half_width :]], axis=1)
    grad_proj = jnp.concatenate([proj_part[:head_rows], proj_part[head_rows:]], axis=1).astype(f32) * factor

    small_grads = [totals[i, : sizes[i]] for i in range(10)]
    lines = -(-sizes[10] // LANES)
    small_grads.append(totals[10 : 10 + lines].reshape(-1))
    (
        grad_attn_gain, grad_attn_shift, grad_query_shift, grad_value_shift, grad_proj_shift,
        grad_attn_scale, grad_mlp_gain, grad_mlp_shift, grad_fc2_shift, grad_mlp_scale, grad_fc1_shift,
    ) = small_grads

    return (
        output_rows[None],
        input_rows[None],
        grad_attn_gain,
        grad_attn_shift,
        grad_qkv,
        grad_query_shift,
        grad_value_shift,
        grad_proj,
        grad_proj_shift,
        grad_attn_scale,
        grad_mlp_gain,
        grad_mlp_shift,
        grad_fc1,
        grad_fc1_shift,
        grad_fc2,
        grad_fc2_shift,
        grad_mlp_scale,
    )


def solution(mesh):
    rows = P("fsdp", None)
    vec = P("fsdp")
    tok = P("rep", "fsdp", None)
    return jax.shard_map(
        on_device,
        mesh=mesh,
        in_specs=(
            tok, P("rep", "fsdp"), vec, vec, rows, vec, vec, rows, vec, vec, vec, vec, rows, vec,
            rows, vec, vec, tok,
        ),
        out_specs=(
            tok, tok, vec, vec, rows, vec, vec, rows, vec, vec, vec, vec, rows, vec, rows, vec, vec,
        ),
        check_vma=False,
    )
```

```python
import functools
import math

import jax
import jax.numpy as jnp
from jax import lax
from jax.experimental import pallas as pl
from jax.experimental.pallas import tpu as pltpu
from jax.sharding import PartitionSpec as P

D = 1024
HEADS = 16
HEAD_DIM = 64
LANES = 128

EPSILON = 1e-06
MASKED = -1e30
BLOCK = 256

SHORT = pl.CostEstimate(flops=1, transcendentals=0, bytes_accessed=1)

f32 = jnp.float32
bf16 = jnp.bfloat16


def normalize(features):
    row_mean = jnp.mean(features, axis=-1, keepdims=True)
    centred = features - row_mean
    variance = jnp.mean(centred * centred, axis=-1, keepdims=True)
    inverse = lax.rsqrt(variance + EPSILON)
    return centred * inverse, inverse


def norm_back(gradient, normal, inverse, gain_vec):
    scaled = gradient * gain_vec
    mean_first = jnp.mean(scaled, axis=-1, keepdims=True)
    mean_second = jnp.mean(scaled * normal, axis=-1, keepdims=True)
    return inverse * (scaled - mean_first - normal * mean_second)


def gelu_pair(values):
    cumulative = 0.5 * (1.0 + lax.erf(values * 2.0 ** (-0.5)))
    density = jnp.exp(-0.5 * values * values) * (2.0 * math.pi) ** (-0.5)
    return (values * cumulative, cumulative + values * density)


def dot(a, b):
    return jnp.dot(a, b, preferred_element_type=f32)


def dot_nt(a, b):
    return lax.dot_general(a, b, (((1,), (1,)), ((), ())), preferred_element_type=f32)


def dot_tn(a, b):
    return lax.dot_general(a, b, (((0,), (0,)), ((), ())), preferred_element_type=f32)


def swap_cores(value):
    size = lax.axis_size("fsdp")
    return lax.ppermute(value, "fsdp", [(i, i ^ 1) for i in range(size)])


def along_z(value, by):
    size = lax.axis_size("fsdp")
    return lax.ppermute(value, "fsdp", [(i, (i + 2 * by) % size) for i in range(size)])


def from_chip(value, by):
    size = lax.axis_size("fsdp")
    pairs = [(i, i + 2 * by) for i in range(size) if 0 <= i + 2 * by < size]
    return lax.ppermute(value, "fsdp", pairs)


def across_rep(value, bit):
    size = lax.axis_size("rep")
    return lax.ppermute(value, "rep", [(i, i ^ (1 << bit)) for i in range(size)])


def pick(value, index, axis):
    return lax.dynamic_index_in_dim(value, index, axis, keepdims=False)


def rep_bits():
    return lax.axis_size("rep").bit_length() - 1


def tie(*values):
    return lax.optimization_barrier(values)


def settle(value, *fields):
    held = [getattr(o, name) for o, name in fields]
    value, held = lax.optimization_barrier((value, held))
    for (o, name), new in zip(fields, held):
        setattr(o, name, new)
    return value


def fetch_z(own):
    return [own] + [along_z(own, k) for k in range(1, lax.axis_size("fsdp") // 2)]


class Gather:
    def __init__(self, pieces, rows, name):
        self.rows, self.cols, self.name = rows, pieces[0].shape[1], name
        half = rows // 2
        bits = list(range(rep_bits()))
        self.orders = [bits, bits[::-1]]
        self.parts = [
            [(jnp.stack([p[:half] for p in pieces])[None], [0])],
            [(jnp.stack([p[half:rows] for p in pieces])[None], [0])],
        ]
        self.at = 0

    def send(self, *values):
        whole = [
            (ps[0][0] if len(ps) == 1 else jnp.concatenate([a for a, _ in ps]), [o for _, os in ps for o in os])
            for ps in self.parts
        ]
        values, arrays = lax.optimization_barrier((values, [a for a, _ in whole]))
        self.parts = []
        for array, (_, offsets), order in zip(arrays, whole, self.orders):
            flip = 1 << order[self.at]
            received = across_rep(array, order[self.at])
            self.parts.append([(array, offsets), (received, [o ^ flip for o in offsets])])
        self.at += 1
        return values[0] if len(values) == 1 else values

    def arrive(self, value):
        value, arrays = lax.optimization_barrier((value, [a for ps in self.parts for a, _ in ps]))
        self.parts = [[(arrays.pop(0), o) for _, o in ps] for ps in self.parts]
        return value

    def assemble(self, here, rank, tail_rows=0):
        depth, ranks = lax.axis_size("fsdp") // 2, lax.axis_size("rep")
        sources, plan = [], []
        for number, parts in enumerate(self.parts):
            for array, offsets in parts:
                sources.append(array)
                plan.append((number, offsets))
        dtype = sources[0].dtype
        shape = (depth * self.rows, ranks * self.cols)
        shapes = [jax.ShapeDtypeStruct(shape, dtype)]
        if tail_rows:
            tail = shape[1] // 4
            shapes = [
                jax.ShapeDtypeStruct((shape[0], shape[1] - tail), dtype),
                jax.ShapeDtypeStruct((depth * tail_rows, 2 * tail), dtype),
            ]
        out = pl.pallas_call(
            functools.partial(assemble_kernel, plan, depth, self.rows, self.cols, tail_rows),
            out_shape=shapes,
            grid_spec=pltpu.PrefetchScalarGridSpec(
                num_scalar_prefetch=1,
                grid=(1,),
                in_specs=[pl.BlockSpec(memory_space=pl.ANY)] * len(sources),
                out_specs=[pl.BlockSpec(memory_space=pl.ANY)] * len(shapes),
                scratch_shapes=[
                    pltpu.VMEM(shape, dtype),
                    pltpu.SemaphoreType.DMA((2 * ranks * depth,)),
                    pltpu.SemaphoreType.DMA((3 * depth,)),
                ],
            ),
            compiler_params=pltpu.CompilerParams(vmem_limit_bytes=16 << 20),
            cost_estimate=SHORT,
            name=self.name,
        )(jnp.stack([here, rank]).astype(jnp.int32), *sources)
        return out if tail_rows else out[0]


def assemble_kernel(plan, depth, rows, cols, tail_rows, index_ref, *refs):
    count = len(plan)
    sources = refs[:count]
    targets = refs[count : count + (2 if tail_rows else 1)]
    held, in_sems, out_sems = refs[-3:]
    here, rank = index_ref[0], index_ref[1]
    half = rows // 2
    waits = [[] for _ in range(depth)]
    number = 0
    for k in range(depth):
        place = lax.rem(here - k + depth, depth)
        for which, (colour, offsets) in enumerate(plan):
            for m, offset in enumerate(offsets):
                at_row = pl.multiple_of(place * rows + colour * half, half)
                at_col = pl.multiple_of((rank ^ offset) * cols, cols)
                copy = pltpu.make_async_copy(
                    sources[which].at[m, k],
                    held.at[pl.ds(at_row, half), pl.ds(at_col, cols)],
                    in_sems.at[number],
                )
                copy.start()
                waits[k].append(copy)
                number += 1
    outs = []
    main = targets[0].shape[1]
    for k in range(depth):
        place = lax.rem(here - k + depth, depth)
        for copy in waits[k]:
            copy.wait()
        base = pl.multiple_of(place * rows, rows)
        band = pl.ds(base, rows)
        out = pltpu.make_async_copy(held.at[band, pl.ds(0, main)], targets[0].at[band], out_sems.at[3 * k])
        out.start()
        outs.append(out)
        if tail_rows:
            wide = targets[1].shape[1] // 2
            for side in range(2):
                out = pltpu.make_async_copy(
                    held.at[pl.ds(base + side * tail_rows, tail_rows), pl.ds(main, wide)],
                    targets[1].at[
                        pl.ds(pl.multiple_of(place * tail_rows, tail_rows), tail_rows),
                        pl.ds(side * wide, wide),
                    ],
                    out_sems.at[3 * k + 1 + side],
                )
                out.start()
                outs.append(out)
    for out in outs:
        out.wait()


def halves(ranks, bit, held):
    flip = 1 << bit
    kept = [o for o in held if not o & flip]
    return kept, [o ^ flip for o in kept]


def relative_blocks(grads, rank, orders):
    depth, ranks = lax.axis_size("fsdp") // 2, lax.axis_size("rep")
    width = grads.shape[1] // ranks
    rows = grads.shape[0] // depth
    shaped = grads.reshape(depth, rows, grads.shape[1])
    share = rows // len(orders)
    first = []
    for n, order in enumerate(orders):
        block = lambda o: lax.dynamic_slice(
            shaped, (0, n * share, (rank ^ o) * width), (depth, share, width)
        )
        kept, given = halves(ranks, order[0], list(range(ranks)))
        first.append((jnp.stack([block(o) for o in kept]), jnp.stack([block(o) for o in given])))
    return first


class Reduce:
    def __init__(self, first, here, orders):
        self.here, self.orders, self.at = here, orders, 0
        ranks = lax.axis_size("rep")
        self.held = []
        for (keep, give), order in zip(first, orders):
            kept, given = halves(ranks, order[0], list(range(ranks)))
            self.held.append((kept, keep, give))

    def send(self, *values):
        values, gives = lax.optimization_barrier((values, [give for _, _, give in self.held]))
        self.received = [across_rep(g, order[self.at]) for g, order in zip(gives, self.orders)]
        self.at += 1
        return values[0] if len(values) == 1 else values

    def arrive(self, *values):
        values, received = lax.optimization_barrier((values, self.received))
        held = []
        for (kept, keep, _), got, order in zip(self.held, received, self.orders):
            total = (keep.astype(f32) + got.astype(f32)).astype(bf16)
            if self.at < len(order):
                stay, leave = halves(None, order[self.at], kept)
                take = lambda os: jnp.stack([total[kept.index(o)] for o in os])
                held.append((stay, take(stay), take(leave)))
            else:
                held.append((kept, total[0], None))
        self.held = held
        return values[0] if len(values) == 1 else values

    def send_z(self, *values, extra=None):
        depth = lax.axis_size("fsdp") // 2
        parts = [keep for _, keep, _ in self.held]
        whole = parts[0] if len(parts) == 1 else jnp.concatenate(parts, axis=1)
        if extra is not None:
            whole = jnp.concatenate([whole, extra], axis=1)
        pieces = [pick(whole, lax.rem(self.here + k, depth), 0) for k in range(depth)]
        values, pieces = lax.optimization_barrier((values, pieces))
        self.pieces = [pieces[0]] + [along_z(p, k) for k, p in enumerate(pieces) if k]
        return values[0] if len(values) == 1 else values

    def arrive_z(self, *values):
        values, pieces = lax.optimization_barrier((values, self.pieces))
        total = pieces[0].astype(f32)
        for piece in pieces[1:]:
            total = total + piece.astype(f32)
        self.total = total
        return values[0] if len(values) == 1 else values


class Spread:
    def __init__(self, value):
        bits = list(range(rep_bits()))
        self.orders = [bits, bits[::-1]]
        half = value.shape[0] // 2
        self.arrays = [value[:half][None], value[half:][None]]
        self.offsets = [[0], [0]]
        self.at = 0

    def send(self, *values):
        values, arrays = lax.optimization_barrier((values, self.arrays))
        self.arrays = []
        for n, (array, order) in enumerate(zip(arrays, self.orders)):
            flip = 1 << order[self.at]
            received = across_rep(array, order[self.at])
            self.arrays.append(jnp.concatenate([array, received]))
            self.offsets[n] = self.offsets[n] + [o ^ flip for o in self.offsets[n]]
        self.at += 1
        return values[0] if len(values) == 1 else values

    def blocks(self, rank, start, size):
        return jnp.concatenate(
            [rep_blocks(a[:, :, start : start + size], o, rank) for a, o in zip(self.arrays, self.offsets)]
        )


def rep_blocks(stacked, offsets, rank):
    blocks = []
    for i in range(len(offsets)):
        block = stacked[0]
        for entry, offset in enumerate(offsets):
            block = jnp.where((rank ^ offset) == i, stacked[entry], block)
        blocks.append(block)
    return jnp.concatenate(blocks, axis=1)


def share_kernel(widths, index_ref, qkv_ref, proj_ref, fc1_ref, keep_ref, give_ref, sems):
    rank, core = index_ref[0], index_ref[1]
    wide1, wide2, block, unit, half = widths
    is_proj = rank * wide1 >= 3 * half

    def copies(second):
        made = []
        for out, (ref, which) in enumerate(((keep_ref, core), (give_ref, 1 - core))):
            for c in range(wide1 // block):
                col = rank * wide1 + c * block
                if second:
                    source, at = proj_ref, which * half + col - 3 * half
                else:
                    source, at = qkv_ref, 2 * col + which * block
                made.append((source, at, block, ref, c * block))
        return made

    def run(plan, first):
        started = []
        for n, (source, at, size, ref, to) in enumerate(plan):
            copy = pltpu.make_async_copy(
                source.at[:, pl.ds(pl.multiple_of(at, LANES), size)], ref.at[:, pl.ds(to, size)], sems.at[first + n]
            )
            copy.start()
            started.append(copy)
        return started

    col = rank * wide2
    plan2 = []
    for ref, which in ((keep_ref, core), (give_ref, 1 - core)):
        at = col + (lax.div(col, unit) + which) * unit
        plan2.append((fc1_ref, at, wide2, ref, wide1))
    second = run(plan2, 0)

    @pl.when(is_proj)
    def _():
        for copy in run(copies(True), 2):
            copy.wait()

    @pl.when(jnp.logical_not(is_proj))
    def _():
        for copy in run(copies(False), 2):
            copy.wait()

    for copy in second:
        copy.wait()


def weight_share(rank, core, qkv_weight, proj_weight, fc1_weight, ranks, block, unit):
    rows = qkv_weight.shape[0]
    wide1, wide2 = 2 * D // ranks, fc1_weight.shape[1] // 2 // ranks
    out = jax.ShapeDtypeStruct((rows, wide1 + wide2), bf16)
    return pl.pallas_call(
        functools.partial(share_kernel, (wide1, wide2, block, unit, D // 2)),
        out_shape=[out, out],
        grid_spec=pltpu.PrefetchScalarGridSpec(
            num_scalar_prefetch=1,
            grid=(1,),
            in_specs=[pl.BlockSpec(memory_space=pl.ANY)] * 3,
            out_specs=[pl.BlockSpec(out.shape, lambda i, a: (0, 0))] * 2,
            scratch_shapes=[pltpu.SemaphoreType.DMA((2 + 2 * (wide1 // block),))],
        ),
        cost_estimate=SHORT,
        name="weight_share",
    )(jnp.stack([rank, core]).astype(jnp.int32), qkv_weight, proj_weight, fc1_weight)


def whole_specs(arrays):
    return [pl.BlockSpec(a.shape, lambda *_, n=len(a.shape): (0,) * n) for a in arrays]


def slot_lists(sizes):
    slots = []
    for number, size in enumerate(sizes):
        for start in range(0, size, LANES):
            slots.append((number, start, min(LANES, size - start)))
    return slots


def pack_kernel(slots, *refs):
    *sources, out_ref, held = refs
    per_row = held.shape[1] // LANES
    held[...] = jnp.zeros_like(held)
    for slot, (number, start, size) in enumerate(slots):
        row, at = slot // per_row, slot % per_row * LANES
        held[row : row + 1, at : at + size] = sources[number][:, start : start + size].astype(f32)
    out_ref[...] = held[...].astype(out_ref.dtype)


def pack_small(vectors, width, slots):
    shape = (32 * LANES // width, width)
    vectors = [v.reshape(1, -1) for v in vectors]
    return pl.pallas_call(
        functools.partial(pack_kernel, slots),
        out_shape=jax.ShapeDtypeStruct(shape, bf16),
        scratch_shapes=[pltpu.VMEM(shape, f32)],
        name="pack_small",
    )(*vectors)


def unpack_kernel(slots, depth, index_ref, *refs):
    pieces, (vec_ref, unit_ref, tag_ref) = refs[:depth], refs[depth:]
    here, core = index_ref[0], index_ref[1]
    rows, width = pieces[0].shape
    per_row = width // LANES
    single = sum(1 for number, _, _ in slots if number < 10)
    vec_ref[...] = jnp.zeros_like(vec_ref)
    for k in range(depth):
        place = lax.rem(here - k + depth, depth)
        values = pieces[k][...].astype(f32)

        def part(side, slot, size):
            row, at = side * (rows // 2) + slot // per_row, slot % per_row * LANES
            return values[row : row + 1, at : at + size]

        for slot, (number, start, size) in enumerate(slots):
            own, other = part(0, slot, size), part(1, slot, size)
            first = jnp.where(core == 0, own, other)
            second = jnp.where(core == 0, other, own)
            if number < 10:
                at = pl.multiple_of(place * 2 * size, 2 * size)
                vec_ref[number : number + 1, pl.ds(at, 2 * size)] = jnp.concatenate([first, second], axis=1)
            elif number == 10:
                wide = unit_ref.shape[1] // depth
                unit_ref[0:1, pl.ds(pl.multiple_of(place * wide + start, LANES), LANES)] = own
            else:
                wide = tag_ref.shape[1] // depth
                at = pl.multiple_of(place * wide + start, LANES)
                tag_ref[0:1, pl.ds(at, LANES)] = first
                tag_ref[0:1, pl.ds(pl.multiple_of(at + wide // 2, LANES), LANES)] = second


def unpack_small(pieces, slots, rows, here, core, units, group_tokens):
    depth = len(pieces)
    extra, width = pieces[0].shape[0] - rows, pieces[0].shape[1]
    shapes = [(16, D), (1, units), (1, group_tokens)]
    return pl.pallas_call(
        functools.partial(unpack_kernel, slots, depth),
        out_shape=[jax.ShapeDtypeStruct(s, f32) for s in shapes],
        grid_spec=pltpu.PrefetchScalarGridSpec(
            num_scalar_prefetch=1,
            grid=(1,),
            in_specs=[pl.BlockSpec((extra, width), lambda i, a: (rows // extra, 0))] * depth,
            out_specs=[pl.BlockSpec(s, lambda i, a: (0, 0)) for s in shapes],
        ),
        name="unpack_small",
    )(jnp.stack([here, core]).astype(jnp.int32), *pieces)


def pack_grads_kernel(depth, sizes, index_ref, *refs):
    *sources, out_ref = refs
    core = index_ref[0]
    out_ref[...] = jnp.zeros_like(out_ref)
    for z in range(depth):
        for c in range(2):
            row = 16 * c
            for source, (size, of_core) in zip(sources, sizes):
                for start in range(0, size, LANES):
                    lanes = min(LANES, size - start)
                    at = (z if of_core else 2 * z + c) * size + start
                    value = source[0:1, at : at + lanes]
                    if of_core:
                        value = jnp.where(core == c, value, 0.0)
                    out_ref[z, row : row + 1, 0:lanes] = value
                    row += 1


def pack_grads(vectors, sizes, core, depth):
    return pl.pallas_call(
        functools.partial(pack_grads_kernel, depth, sizes),
        out_shape=jax.ShapeDtypeStruct((depth, 32, LANES), f32),
        grid_spec=pltpu.PrefetchScalarGridSpec(
            num_scalar_prefetch=1,
            grid=(1,),
            in_specs=whole_specs(vectors),
            out_specs=pl.BlockSpec((depth, 32, LANES), lambda i, a: (0, 0, 0)),
        ),
        name="pack_grads",
    )(core.reshape(1).astype(jnp.int32), *vectors)


def grad_blocks_kernel(orders, ranks, index_ref, a_ref, b_ref, *refs):
    outs, held = refs[:-1], refs[-1]
    rank = index_ref[0]
    held[...] = dot_tn(a_ref[...], b_ref[...]).astype(bf16)
    width = held.shape[1] // ranks
    share = held.shape[0] // len(orders)
    for n, order in enumerate(orders):
        for which, offsets in enumerate(halves(ranks, order[0], list(range(ranks)))):
            for i, o in enumerate(offsets):
                cols = pl.ds(pl.multiple_of((rank ^ o) * width, width), width)
                outs[2 * n + which][i, 0] = held[n * share : (n + 1) * share, cols]


def grad_blocks(a, b, rank, orders, name):
    depth, ranks = lax.axis_size("fsdp") // 2, lax.axis_size("rep")
    tokens, rows, cols = a.shape[0], a.shape[1] // depth, b.shape[1]
    if cols // ranks % LANES:
        return relative_blocks(dot_tn(a, b).astype(bf16), rank, orders)
    block = (ranks // 2, depth, rows // len(orders), cols // ranks)
    outs = pl.pallas_call(
        functools.partial(grad_blocks_kernel, orders, ranks),
        out_shape=[jax.ShapeDtypeStruct(block, bf16)] * (2 * len(orders)),
        grid_spec=pltpu.PrefetchScalarGridSpec(
            num_scalar_prefetch=1,
            grid=(depth,),
            in_specs=[
                pl.BlockSpec((tokens, rows), lambda i, s: (0, i)),
                pl.BlockSpec((tokens, cols), lambda i, s: (0, 0)),
            ],
            out_specs=[pl.BlockSpec((block[0], 1) + block[2:], lambda i, s: (0, i, 0, 0))] * (2 * len(orders)),
            scratch_shapes=[pltpu.VMEM((rows, cols), bf16)],
        ),
        compiler_params=pltpu.CompilerParams(vmem_limit_bytes=40 << 20),
        cost_estimate=SHORT,
        name=name,
    )(rank.reshape(1).astype(jnp.int32), a, b)
    return [(outs[2 * n], outs[2 * n + 1]) for n in range(len(orders))]


def pre_grad_kernel(g_ref, w_ref, slope_ref, out_ref, sum_ref):
    grad = dot_nt(g_ref[...], w_ref[...]) * slope_ref[...]
    out_ref[...] = grad.astype(bf16)
    sum_ref[...] = jnp.sum(grad, axis=0, keepdims=True)


def pre_grads(mlp_grad, fc2_matrix, slope):
    tokens, units = slope.shape
    tile = 256
    return pl.pallas_call(
        pre_grad_kernel,
        out_shape=[jax.ShapeDtypeStruct((tokens, units), bf16), jax.ShapeDtypeStruct((1, units), f32)],
        grid=(units // tile,),
        in_specs=[
            pl.BlockSpec((tokens, D), lambda i: (0, 0)),
            pl.BlockSpec((tile, D), lambda i: (i, 0)),
            pl.BlockSpec((tokens, tile), lambda i: (0, i)),
        ],
        out_specs=[pl.BlockSpec((tokens, tile), lambda i: (0, i)), pl.BlockSpec((1, tile), lambda i: (0, i))],
        compiler_params=pltpu.CompilerParams(vmem_limit_bytes=40 << 20),
        cost_estimate=SHORT,
        name="pre_grad",
    )(mlp_grad, fc2_matrix, slope)


def product_kernel(half_ref, first_ref, second_ref, w_ref, out1_ref, out2_ref):
    out1_ref[...] = dot(first_ref[...], w_ref[...])
    out2_ref[...] = dot(second_ref[...], w_ref[...])


def product_nt_kernel(half_ref, first_ref, second_ref, w_ref, out1_ref, out2_ref, held):
    @pl.when(pl.program_id(0) == 0)
    def _():
        held[...] = w_ref[...].T

    out1_ref[...] = dot(first_ref[...], held[...])
    out2_ref[...] = dot(second_ref[...], held[...])


def product(a, weight, flipped, half, name):
    rows, tile = a.shape[0] // 2, 128
    count = rows // tile
    out = pl.BlockSpec((tile, D), lambda i, h: (i, 0))
    return pl.pallas_call(
        product_nt_kernel if flipped else product_kernel,
        out_shape=[jax.ShapeDtypeStruct((rows, D), f32)] * 2,
        grid_spec=pltpu.PrefetchScalarGridSpec(
            num_scalar_prefetch=1,
            grid=(count,),
            in_specs=[
                pl.BlockSpec((tile, a.shape[1]), lambda i, h: (i + h[0] * count, 0)),
                pl.BlockSpec((tile, a.shape[1]), lambda i, h: (i + (1 - h[0]) * count, 0)),
                pl.BlockSpec(weight.shape, lambda i, h: (0, 0)),
            ],
            out_specs=[out, out],
            scratch_shapes=[pltpu.VMEM(weight.shape[::-1], bf16)] if flipped else [],
        ),
        compiler_params=pltpu.CompilerParams(vmem_limit_bytes=32 << 20),
        cost_estimate=SHORT,
        name=name,
    )(jnp.asarray(half, jnp.int32).reshape(1), a, a, weight)


def finish_kernel(
    own1_ref, sent1_ref, tok_ref, grad_ref, own2_ref, sent2_ref, resid_ref, cot_ref, vec_ref,
    in_grad_ref, out_ref, sum_ref,
):
    grad = own1_ref[...] + sent1_ref[...]
    normal, inverse = normalize(tok_ref[...].astype(f32))
    in_grad_ref[...] = grad_ref[...] + norm_back(grad, normal, inverse, vec_ref[0:1, :])
    mlp = own2_ref[...] + sent2_ref[...] + vec_ref[8:9, :]
    out_ref[...] = (resid_ref[...] + vec_ref[9:10, :] * mlp).astype(bf16)
    out_grad = cot_ref[...].astype(f32)

    @pl.when(pl.program_id(0) == 0)
    def _():
        sum_ref[...] = jnp.zeros_like(sum_ref)

    for row, value in enumerate((grad * normal, grad, out_grad * vec_ref[9:10, :], out_grad * mlp)):
        sum_ref[row : row + 1, :] += jnp.sum(value, axis=0, keepdims=True)


def finish(own1, sent1, tok, resid_grad, own2, sent2, resid, cot, vecs):
    rows, tile = own1.shape[0], 64
    part = pl.BlockSpec((tile, D), lambda i: (i, 0))
    return pl.pallas_call(
        finish_kernel,
        out_shape=[
            jax.ShapeDtypeStruct((rows, D), f32), jax.ShapeDtypeStruct((rows, D), bf16),
            jax.ShapeDtypeStruct((8, D), f32),
        ],
        grid=(rows // tile,),
        in_specs=[part] * 8 + [pl.BlockSpec(vecs.shape, lambda i: (0, 0))],
        out_specs=[part, part, pl.BlockSpec((8, D), lambda i: (0, 0))],
        compiler_params=pltpu.CompilerParams(vmem_limit_bytes=24 << 20),
        cost_estimate=SHORT,
        name="finish",
    )(own1, sent1, tok, resid_grad, own2, sent2, resid, cot, vecs)


def residual_kernel(own_ref, sent_ref, tok_ref, vec_ref, attn_ref, resid_ref, input_ref):
    attn = own_ref[...] + sent_ref[...] + vec_ref[4:5, :]
    resid = tok_ref[...].astype(f32) + vec_ref[5:6, :] * attn
    attn_ref[...] = attn
    resid_ref[...] = resid
    normal, _ = normalize(resid)
    input_ref[...] = (normal * vec_ref[6:7, :] + vec_ref[7:8, :]).astype(bf16)


def residual(own, sent, tok, vecs):
    rows, tile = own.shape[0], 64
    part = pl.BlockSpec((tile, D), lambda i: (i, 0))
    return pl.pallas_call(
        residual_kernel,
        out_shape=[jax.ShapeDtypeStruct((rows, D), t) for t in (f32, f32, bf16)],
        grid=(rows // tile,),
        in_specs=[part] * 3 + [pl.BlockSpec(vecs.shape, lambda i: (0, 0))],
        out_specs=[part] * 3,
        compiler_params=pltpu.CompilerParams(vmem_limit_bytes=24 << 20),
        cost_estimate=SHORT,
        name="residual",
    )(own, sent, tok, vecs)


def scaled_kernel(own_ref, other_ref, vec_ref, out_ref):
    rows = own_ref.shape[0]
    for n, ref in enumerate((own_ref, other_ref)):
        out_ref[n * rows : (n + 1) * rows, :] = (ref[...].astype(f32) * vec_ref[9:10, :]).astype(bf16)


def scaled(own, other, vecs):
    return pl.pallas_call(
        scaled_kernel,
        out_shape=jax.ShapeDtypeStruct((2 * own.shape[0], D), bf16),
        compiler_params=pltpu.CompilerParams(vmem_limit_bytes=24 << 20),
        cost_estimate=SHORT,
        name="scaled",
    )(own, other, vecs)


def units_kernel(n_ref, w_ref, b_ref, act_ref, slope_ref):
    act, slope = gelu_pair(dot(n_ref[...], w_ref[...]) + b_ref[...])
    act_ref[...] = act.astype(bf16)
    slope_ref[...] = slope


def hidden_units(normed, weight, bias):
    tokens, units = normed.shape[0], weight.shape[1]
    tile = 256
    part = pl.BlockSpec((tokens, tile), lambda i: (0, i))
    return pl.pallas_call(
        units_kernel,
        out_shape=[jax.ShapeDtypeStruct((tokens, units), t) for t in (bf16, f32)],
        grid=(units // tile,),
        in_specs=[
            pl.BlockSpec((tokens, D), lambda i: (0, 0)),
            pl.BlockSpec((D, tile), lambda i: (0, i)),
            pl.BlockSpec((1, tile), lambda i: (0, i)),
        ],
        out_specs=[part, part],
        compiler_params=pltpu.CompilerParams(vmem_limit_bytes=32 << 20),
        cost_estimate=SHORT,
        name="units",
    )(normed, weight, bias)


def norm_grad_kernel(own_ref, sent_ref, resid_ref, cot_ref, attn_ref, vec_ref, grad_ref, scaled_ref, sum_ref):
    grad = own_ref[...] + sent_ref[...]
    normal, inverse = normalize(resid_ref[...])
    resid_grad = cot_ref[...].astype(f32) + norm_back(grad, normal, inverse, vec_ref[6:7, :])
    scaled = resid_grad * vec_ref[5:6, :]
    grad_ref[...] = resid_grad
    scaled_ref[...] = scaled.astype(bf16)

    @pl.when(pl.program_id(0) == 0)
    def _():
        sum_ref[...] = jnp.zeros_like(sum_ref)

    for row, value in enumerate((grad * normal, grad, scaled, resid_grad * attn_ref[...])):
        sum_ref[row : row + 1, :] += jnp.sum(value, axis=0, keepdims=True)


def norm_grads(own, sent, resid, cot, attn_out, vecs):
    rows, tile = own.shape[0], 64
    part = pl.BlockSpec((tile, D), lambda i: (i, 0))
    return pl.pallas_call(
        norm_grad_kernel,
        out_shape=[
            jax.ShapeDtypeStruct((rows, D), f32), jax.ShapeDtypeStruct((rows, D), bf16),
            jax.ShapeDtypeStruct((8, D), f32),
        ],
        grid=(rows // tile,),
        in_specs=[part] * 5 + [pl.BlockSpec(vecs.shape, lambda i: (0, 0))],
        out_specs=[part, part, pl.BlockSpec((8, D), lambda i: (0, 0))],
        compiler_params=pltpu.CompilerParams(vmem_limit_bytes=24 << 20),
        cost_estimate=SHORT,
        name="norm_grad",
    )(own, sent, resid, cot, attn_out, vecs)


def proj_grad_kernel(head_rows, c_ref, g_ref, out_ref):
    wide = out_ref.shape[1]
    for side in range(2):
        grad = dot_tn(c_ref[...], g_ref[:, side * wide : (side + 1) * wide]).astype(bf16)
        for z in range(grad.shape[0] // head_rows):
            at = (2 * z + side) * head_rows
            out_ref[at : at + head_rows, :] = grad[z * head_rows : (z + 1) * head_rows]


def packed_proj_grad(context, attn_grad, head_rows):
    wide = D // 2
    return pl.pallas_call(
        functools.partial(proj_grad_kernel, head_rows),
        out_shape=jax.ShapeDtypeStruct((D, wide), bf16),
        compiler_params=pltpu.CompilerParams(vmem_limit_bytes=32 << 20),
        cost_estimate=SHORT,
        name="proj_grad",
    )(context, attn_grad)


def qkv_grad_kernel(orders, ranks, depth, per, index_ref, n_ref, *refs):
    grads, p_ref = refs[: 3 * per], refs[3 * per]
    outs, held = refs[3 * per + 1 : -1], refs[-1]
    rank = index_ref[0]
    normed = n_ref[...]
    for number in range(3):
        pieces = [g[...] for g in grads[number * per : (number + 1) * per]]
        wide = per * LANES
        joined = pieces[0] if per == 1 else jnp.concatenate(pieces, axis=1)
        held[:, number * wide : (number + 1) * wide] = dot_tn(normed, joined).astype(bf16)
    held[:, 3 * per * LANES :] = p_ref[...]
    width = held.shape[1] // ranks
    rows = held.shape[0] // depth
    share = rows // len(orders)
    for n, order in enumerate(orders):
        for which, offsets in enumerate(halves(ranks, order[0], list(range(ranks)))):
            for i, o in enumerate(offsets):
                cols = pl.ds(pl.multiple_of((rank ^ o) * width, width), width)
                for z in range(depth):
                    at = z * rows + n * share
                    outs[2 * n + which][i, z] = held[at : at + share, cols]


def qkv_grad_blocks(normed, grads, proj_packed, part, parts, rank, orders):
    depth, ranks = lax.axis_size("fsdp") // 2, lax.axis_size("rep")
    per = len(grads) // 3
    cols = 4 * per * LANES
    block = (ranks // 2, depth, D // depth // len(orders), cols // ranks)
    tokens = normed.shape[0] // 3
    outs = pl.pallas_call(
        functools.partial(qkv_grad_kernel, orders, ranks, depth, per),
        out_shape=[jax.ShapeDtypeStruct(block, bf16)] * (2 * len(orders)),
        grid_spec=pltpu.PrefetchScalarGridSpec(
            num_scalar_prefetch=1,
            grid=(1,),
            in_specs=[pl.BlockSpec((tokens, D), lambda i, a: (1, 0))]
            + whole_specs(grads)
            + [pl.BlockSpec((D, per * LANES), lambda i, a: (0, part))],
            out_specs=[pl.BlockSpec(block, lambda i, a: (0, 0, 0, 0))] * (2 * len(orders)),
            scratch_shapes=[pltpu.VMEM((D, cols), bf16)],
        ),
        compiler_params=pltpu.CompilerParams(vmem_limit_bytes=40 << 20),
        cost_estimate=SHORT,
        name="qkv_grad",
    )(rank.reshape(1).astype(jnp.int32), normed, *grads, proj_packed)
    return [(outs[2 * n], outs[2 * n + 1]) for n in range(len(orders))]


def spread_lanes(tags, width):
    return jnp.concatenate([tags] * (width // LANES), axis=1)


def project_kernel(need_ref, n_ref, w_ref, b_ref, q_ref, k_ref, v_ref):
    row = pl.program_id(0)
    wide = q_ref.shape[1]

    @pl.when(need_ref[row] > 0)
    def _():
        n = n_ref[...]
        for i, ref in enumerate((q_ref, k_ref, v_ref)):
            out = dot(n, w_ref[:, i * wide : (i + 1) * wide]) + b_ref[0:1, i * wide : (i + 1) * wide]
            if i == 0:
                out = out.astype(bf16).astype(f32) * HEAD_DIM ** (-0.5)
            ref[...] = out.astype(bf16)

    @pl.when(need_ref[row] == 0)
    def _():
        for ref in (q_ref, k_ref, v_ref):
            ref[...] = jnp.zeros_like(ref)


def project(need, normed, weight, bias, wide):
    rows = normed.shape[0]
    return pl.pallas_call(
        project_kernel,
        out_shape=[jax.ShapeDtypeStruct((rows, wide), bf16)] * 3,
        grid_spec=pltpu.PrefetchScalarGridSpec(
            num_scalar_prefetch=1,
            grid=(rows // BLOCK,),
            in_specs=[
                pl.BlockSpec((BLOCK, D), lambda i, s: (i, 0)),
                pl.BlockSpec(weight.shape, lambda i, s: (0, 0)),
                pl.BlockSpec((1, 3 * wide), lambda i, s: (0, 0)),
            ],
            out_specs=[pl.BlockSpec((BLOCK, wide), lambda i, s: (i, 0))] * 3,
        ),
        compiler_params=pltpu.CompilerParams(vmem_limit_bytes=32 << 20),
        cost_estimate=SHORT,
        name="project",
    )(need, normed, weight, bias)


def norm_kernel(need_ref, info_ref, *refs):
    *sources, vec_ref, out_ref = refs
    row = pl.program_id(0)
    side = (row // info_ref[1]) % 2
    chip = row // (2 * info_ref[1])

    @pl.when(need_ref[row] > 0)
    def _():
        picked = jnp.where(chip == 0, sources[0][...], jnp.where(chip == 1, sources[2][...], sources[4][...]))
        theirs = jnp.where(chip == 0, sources[1][...], jnp.where(chip == 1, sources[3][...], sources[5][...]))
        picked = jnp.where(side == info_ref[0], picked, theirs)
        normal, _ = normalize(picked.astype(f32))
        out_ref[...] = (normal * vec_ref[0:1, :] + vec_ref[1:2, :]).astype(bf16)

    @pl.when(need_ref[row] == 0)
    def _():
        out_ref[...] = jnp.zeros_like(out_ref)


def norm_window(need, info, sources, vecs, window, count):
    per = count // BLOCK

    def spec(chip):
        def index(i, a, b):
            inside = jnp.clip(i - 2 * per * chip, 0, 2 * per - 1)
            return (inside % per, 0)

        return pl.BlockSpec((BLOCK, D), index)

    return pl.pallas_call(
        norm_kernel,
        out_shape=jax.ShapeDtypeStruct((window, D), bf16),
        grid_spec=pltpu.PrefetchScalarGridSpec(
            num_scalar_prefetch=2,
            grid=(window // BLOCK,),
            in_specs=[spec(i // 2) for i in range(6)] + [pl.BlockSpec(vecs.shape, lambda i, a, b: (0, 0))],
            out_specs=pl.BlockSpec((BLOCK, D), lambda i, a, b: (i, 0)),
        ),
        compiler_params=pltpu.CompilerParams(vmem_limit_bytes=24 << 20),
        cost_estimate=SHORT,
        name="norm_window",
    )(need, info, *sources, vecs)


def attend_kernel(lo_ref, hi_ref, first_ref, last_ref, q_ref, k_ref, v_ref, qt_ref, kt_ref, o_ref, lse_ref, s_ref, m_ref, acc_ref):
    i = pl.program_id(0)
    left = lax.broadcasted_iota(jnp.int32, (1, LANES), 1) < HEAD_DIM
    lo, hi = lo_ref[i], hi_ref[i]
    base = (first_ref.shape[0] - pl.num_programs(0)) // 2
    q = q_ref[...]
    zero = jnp.zeros_like(q)
    heads = (jnp.where(left, q, zero), jnp.where(left, zero, q))
    m_ref[...] = jnp.full_like(m_ref, MASKED)
    one_image = first_ref[base + i] == last_ref[base + i]
    folds = BLOCK // LANES

    def fold(value, combine):
        parts = [value[:, n * LANES : (n + 1) * LANES] for n in range(folds)]
        return functools.reduce(combine, parts)

    def scores(j, carry):
        at = pl.multiple_of(j * BLOCK, BLOCK)
        k = k_ref[pl.ds(at, BLOCK), :]
        inside = one_image & (first_ref[j] == first_ref[base + i]) & (last_ref[j] == first_ref[base + i])

        @pl.when(inside)
        def _():
            for h in range(2):
                s = dot_nt(heads[h], k)
                s_ref[h, j] = s
                m_ref[h] = jnp.maximum(m_ref[h], fold(s, jnp.maximum))

        @pl.when(jnp.logical_not(inside))
        def _():
            same = spread_lanes(qt_ref[...], BLOCK) == kt_ref[:, pl.ds(at, BLOCK)]
            for h in range(2):
                s = jnp.where(same, dot_nt(heads[h], k), MASKED)
                s_ref[h, j] = s
                m_ref[h] = jnp.maximum(m_ref[h], fold(s, jnp.maximum))

        return carry

    lax.fori_loop(lo, hi, scores, 0)
    tops = [jnp.max(m_ref[h], axis=1, keepdims=True) for h in range(2)]
    m_ref[...] = jnp.zeros_like(m_ref)
    acc_ref[...] = jnp.zeros_like(acc_ref)

    def mix(j, carry):
        at = pl.multiple_of(j * BLOCK, BLOCK)
        v = v_ref[pl.ds(at, BLOCK), :]
        for h in range(2):
            e = jnp.exp(s_ref[h, j] - tops[h])
            m_ref[h] += fold(e, jnp.add)
            acc_ref[h] += dot(e.astype(bf16), v)
        return carry

    lax.fori_loop(lo, hi, mix, 0)
    sums = [jnp.sum(m_ref[h], axis=1, keepdims=True) for h in range(2)]
    o_ref[...] = jnp.where(left, acc_ref[0] / sums[0], acc_ref[1] / sums[1]).astype(bf16)
    for h in range(2):
        lse = jnp.broadcast_to(tops[h] + jnp.log(sums[h]), (BLOCK, LANES))
        lse_ref[0, h : h + 1, :] = lse.T[0:1, :]


def attend(lo, hi, firsts, lasts, q, k, v, tag_cols, tag_row, own_rows, pair):
    window = q.shape[0]
    blocks = own_rows // BLOCK
    skip = (window - own_rows) // 2 // BLOCK
    return pl.pallas_call(
        attend_kernel,
        out_shape=[
            jax.ShapeDtypeStruct((own_rows, LANES), bf16),
            jax.ShapeDtypeStruct((1, 2, own_rows), f32),
        ],
        grid_spec=pltpu.PrefetchScalarGridSpec(
            num_scalar_prefetch=4,
            grid=(blocks,),
            in_specs=[
                pl.BlockSpec((BLOCK, LANES), lambda i, *_: (i + skip, pair)),
                pl.BlockSpec((window, LANES), lambda i, *_: (0, pair)),
                pl.BlockSpec((window, LANES), lambda i, *_: (0, pair)),
                pl.BlockSpec((BLOCK, LANES), lambda i, *_: (i + skip, 0)),
                pl.BlockSpec((1, window), lambda i, *_: (0, 0)),
            ],
            out_specs=[
                pl.BlockSpec((BLOCK, LANES), lambda i, *_: (i, 0)),
                pl.BlockSpec((1, 2, BLOCK), lambda i, *_: (0, 0, i)),
            ],
            scratch_shapes=[
                pltpu.VMEM((2, window // BLOCK, BLOCK, BLOCK), f32),
                pltpu.VMEM((2, BLOCK, LANES), f32),
                pltpu.VMEM((2, BLOCK, LANES), f32),
            ],
        ),
        compiler_params=pltpu.CompilerParams(vmem_limit_bytes=32 << 20),
        cost_estimate=SHORT,
        name="attend",
    )(lo, hi, firsts, lasts, q, k, v, tag_cols, tag_row)


def attend_back_kernel(
    start, stop, lo_ref, hi_ref, q_ref, k_ref, v_ref, g_ref, tc_ref, tr_ref, lse_ref, delta_ref,
    dq_ref, dk_ref, dv_ref, sum_ref, dk_acc, dv_acc, dq_acc,
):
    first = lax.broadcasted_iota(jnp.int32, (1, LANES), 1) < HEAD_DIM
    dk_acc[...] = jnp.zeros_like(dk_acc)
    dv_acc[...] = jnp.zeros_like(dv_acc)
    sum_ref[...] = jnp.zeros_like(sum_ref)

    def split(value):
        zero = jnp.zeros_like(value)
        return jnp.where(first, value, zero), jnp.where(first, zero, value)

    def visit(i, j, qs, gs, of_key, of_query):
        at_q, at_k = pl.multiple_of(i * BLOCK, BLOCK), pl.multiple_of(j * BLOCK, BLOCK)
        k = k_ref[pl.ds(at_k, BLOCK), :]
        v = v_ref[pl.ds(at_k, BLOCK), :]
        same = spread_lanes(tc_ref[pl.ds(at_k, BLOCK), :], BLOCK) == tr_ref[:, pl.ds(at_q, BLOCK)]
        ps, ds = [], []
        for h in range(2):
            s = dot_nt(k, qs[h])
            dp = dot_nt(v, gs[h])
            p = jnp.where(same, jnp.exp(s - lse_ref[0, h : h + 1, pl.ds(at_q, BLOCK)]), 0.0)
            d = p * (dp - delta_ref[0, h : h + 1, pl.ds(at_q, BLOCK)])
            ps.append(p.astype(bf16))
            ds.append(d.astype(bf16))
        if of_key:
            at = pl.multiple_of((j - start) * BLOCK, BLOCK)
            dv_acc[pl.ds(at, BLOCK), :] += dot(ps[0], gs[0]) + dot(ps[1], gs[1])
            dk_acc[pl.ds(at, BLOCK), :] += dot(ds[0], qs[0]) + dot(ds[1], qs[1])
        if of_query:
            ks = split(k)
            dq_acc[...] += dot_tn(ds[0], ks[0]) + dot_tn(ds[1], ks[1])

    def query_block(own_q, i, carry):
        at_q = pl.multiple_of(i * BLOCK, BLOCK)
        qs = split(q_ref[pl.ds(at_q, BLOCK), :])
        gs = split(g_ref[pl.ds(at_q, BLOCK), :])
        lo, hi = lo_ref[i], hi_ref[i]

        def keys(first_key, last_key, of_key):
            def body(j, carry):
                visit(i, j, qs, gs, of_key, own_q)
                return carry

            lax.fori_loop(first_key, last_key, body, 0)

        if own_q:
            dq_acc[...] = jnp.zeros_like(dq_acc)
            keys(lo, jnp.minimum(hi, start), False)
            keys(jnp.maximum(lo, stop), hi, False)
        keys(jnp.maximum(lo, start), jnp.minimum(hi, stop), True)
        if own_q:
            at = pl.multiple_of((i - start) * BLOCK, BLOCK)
            dq = dq_acc[...] * HEAD_DIM ** (-0.5)
            dq_ref[pl.ds(at, BLOCK), :] = dq.astype(bf16)
            sum_ref[0, 0:1, :] += jnp.sum(dq, axis=0, keepdims=True)
        return carry

    before = jnp.where(lo_ref[start] < start, lo_ref[start], start)
    after = jnp.maximum(hi_ref[stop - 1], stop)
    lax.fori_loop(before, start, functools.partial(query_block, False), 0)
    lax.fori_loop(start, stop, functools.partial(query_block, True), 0)
    lax.fori_loop(stop, after, functools.partial(query_block, False), 0)
    dk_ref[...] = dk_acc[...].astype(bf16)
    dv_ref[...] = dv_acc[...].astype(bf16)
    sum_ref[0, 1:2, :] = jnp.sum(dv_acc[...], axis=0, keepdims=True)


def attend_back(lo, hi, q, k, v, g, tag_cols, tag_row, lse, delta, own_rows, pair):
    window = q.shape[0]
    pairs, wide = 1, LANES
    grad_pair = pair % (g.shape[1] // LANES)
    start = (window - own_rows) // 2 // BLOCK
    stop = start + own_rows // BLOCK
    whole = lambda: pl.BlockSpec((window, LANES), lambda p, a, b: (0, pair))
    own = lambda: pl.BlockSpec((own_rows, LANES), lambda p, a, b: (0, p))
    stat = lambda: pl.BlockSpec((1, 2, window), lambda p, a, b: (pair, 0, 0))
    return pl.pallas_call(
        functools.partial(attend_back_kernel, start, stop),
        out_shape=[jax.ShapeDtypeStruct((own_rows, wide), bf16)] * 3
        + [jax.ShapeDtypeStruct((pairs, 8, LANES), f32)],
        grid_spec=pltpu.PrefetchScalarGridSpec(
            num_scalar_prefetch=2,
            grid=(pairs,),
            in_specs=[
                whole(), whole(), whole(),
                pl.BlockSpec((window, LANES), lambda p, a, b: (0, grad_pair)),
                pl.BlockSpec((window, LANES), lambda p, a, b: (0, 0)),
                pl.BlockSpec((1, window), lambda p, a, b: (0, 0)),
                stat(), stat(),
            ],
            out_specs=[own(), own(), own(), pl.BlockSpec((1, 8, LANES), lambda p, a, b: (p, 0, 0))],
            scratch_shapes=[
                pltpu.VMEM((own_rows, LANES), f32),
                pltpu.VMEM((own_rows, LANES), f32),
                pltpu.VMEM((BLOCK, LANES), f32),
            ],
        ),
        compiler_params=pltpu.CompilerParams(vmem_limit_bytes=40 << 20),
        cost_estimate=SHORT,
        name="attend_back",
    )(lo, hi, q, k, v, g, tag_cols, tag_row, lse, delta)


def on_device(
    tokens, image_ids, ln1_gain, ln1_bias, qkv_weight, query_bias, value_bias, proj_weight,
    proj_bias, scale_attn, ln2_gain, ln2_bias, fc1_weight, fc1_bias, fc2_weight, fc2_bias,
    scale_mlp, cotangent,
):
    devices = lax.axis_size("fsdp")
    depth, ranks = devices // 2, lax.axis_size("rep")
    place = lax.axis_index("fsdp")
    rank = lax.axis_index("rep")
    here, core = place // 2, place % 2
    count = tokens.shape[1]
    chip = 2 * count
    head_rows = D // devices
    ff = fc1_weight.shape[1]
    unit_rows = ff // devices
    half_heads = D // 2
    local_heads = half_heads // HEAD_DIM
    pairs = half_heads // LANES
    bits = list(range(rep_bits()))

    def in_order(own, other, axis=0):
        return jnp.where(
            core == 0,
            jnp.concatenate([own, other], axis=axis),
            jnp.concatenate([other, own], axis=axis),
        )

    def mine(value):
        return lax.dynamic_slice_in_dim(value, core * count, count, 0)

    def others(value):
        return lax.dynamic_slice_in_dim(value, (1 - core) * count, count, 0)

    def every_other(value, width, start):
        cuts = range(start * width, value.shape[1], 2 * width)
        return jnp.concatenate([value[:, c : c + width] for c in cuts], axis=1)

    def all_share(which):
        pick_cols = lambda v, w: jnp.where(which == 0, every_other(v, w, 0), every_other(v, w, 1))
        heads = lax.dynamic_slice_in_dim(
            jnp.concatenate(
                [
                    pick_cols(qkv_weight, head_rows),
                    lax.dynamic_slice_in_dim(proj_weight, which * half_heads, half_heads, 1),
                ],
                axis=1,
            ),
            rank * (2 * D // ranks), 2 * D // ranks, 1,
        )
        units = lax.dynamic_slice_in_dim(
            pick_cols(fc1_weight, unit_rows), rank * (ff // 2 // ranks), ff // 2 // ranks, 1
        )
        return jnp.concatenate([heads, units], axis=1)

    if head_rows % LANES:
        kept, given = all_share(core), all_share(1 - core)
    else:
        kept, given = weight_share(
            rank, core, qkv_weight, proj_weight, fc1_weight, ranks, head_rows, unit_rows
        )
    wide1 = 2 * D // ranks
    got = swap_cores(given)
    is_proj = rank * wide1 >= 3 * half_heads
    own1 = in_order(kept[:, :wide1], jnp.where(is_proj, given[:, :wide1], got[:, :wide1]))
    own2 = in_order(kept[:, wide1:], got[:, wide1:])
    own3 = lax.dynamic_slice_in_dim(fc2_weight, rank * (D // ranks), D // ranks, 1)
    small = (
        ln1_gain, ln1_bias, query_bias, value_bias, proj_bias, scale_attn, ln2_gain, ln2_bias,
        fc2_bias, scale_mlp, fc1_bias, (image_ids[0] + 1).astype(bf16),
    )
    sizes = [v.shape[0] for v in small]
    slots = slot_lists(sizes)
    width = 2 * D // ranks
    small = pack_small(small, width, slots)
    small_other = swap_cores(small)
    rows1, rows3 = own1.shape[0], own3.shape[0]
    tok, cot = tokens[0], cotangent[0]
    tok_other = swap_cores(tok)
    cot_other = swap_cores(cot)
    own1 = jnp.concatenate([own1, small, small_other])
    own1, own2, own3, tok = tie(own1, own2, own3, tok)
    pieces1 = fetch_z(own1)
    tok, pieces1[1] = tie(tok, pieces1[1])
    behind, ahead = from_chip(tok, 1), from_chip(tok, -1)
    gather1 = Gather(pieces1, rows1, "gather1")
    gather1.send()
    behind_other, ahead_other = swap_cores(behind), swap_cores(ahead)
    for _ in bits[1:]:
        gather1.send()

    vec_rows, fc1_shift, all_tags = unpack_small(
        pieces1, slots, rows1, here, core, ff // 2, devices * count
    )
    vector = lambda i: vec_rows[i : i + 1]
    (
        attn_gain, attn_shift, query_shift, value_shift, proj_shift, attn_scale, mlp_gain,
        mlp_shift, fc2_shift, mlp_scale,
    ) = map(vector, range(10))
    core_part = lambda vec: jnp.where(
        core == 0, every_other(vec, head_rows, 0), every_other(vec, head_rows, 1)
    )

    window = 3 * chip
    padded = jnp.concatenate(
        [jnp.zeros((1, chip), f32), all_tags, jnp.full((1, chip), 1e6, f32)], axis=1
    )
    tag_row = lax.dynamic_slice(padded, (0, here * chip), (1, window))
    tags = tag_row.reshape(window)
    firsts, lasts = tags[::BLOCK], tags[BLOCK - 1 :: BLOCK]
    real = firsts * (1e6 - firsts) > 0
    below = jnp.sum((tag_row < firsts[:, None]).astype(jnp.int32), axis=1)
    upto = jnp.sum((tag_row <= lasts[:, None]).astype(jnp.int32), axis=1)
    blocks = window // BLOCK
    block_lo = jnp.where(real, below // BLOCK, 0)
    block_hi = jnp.where(real, (upto + BLOCK - 1) // BLOCK, 0)
    own_lo, own_hi = chip // BLOCK, 2 * chip // BLOCK
    numbers = jnp.arange(blocks)
    need = jnp.logical_and(numbers >= block_lo[own_lo], numbers < block_hi[own_hi - 1]).astype(jnp.int32)
    firsts, lasts = firsts.astype(jnp.int32), lasts.astype(jnp.int32)
    tag_cols = jnp.broadcast_to(tags[:, None], (window, LANES))

    info = jnp.stack([core, jnp.int32(count // BLOCK)]).astype(jnp.int32)
    normed1 = norm_window(
        need, info, (behind, behind_other, tok, tok_other, ahead, ahead_other), vec_rows, window, count
    )

    normed1, own2 = tie(normed1, own2)
    pieces2 = fetch_z(own2)
    normed1 = gather1.arrive(normed1)
    qkv_matrix, proj_matrix = gather1.assemble(here, rank, head_rows)

    shifts = jnp.concatenate(
        [core_part(query_shift), jnp.zeros((1, half_heads), f32), core_part(value_shift)], axis=1
    )
    queries, keys, values = project(need, normed1, qkv_matrix, shifts, half_heads)

    contexts, lses = [], []
    los = block_lo[own_lo:own_hi]
    los, queries = tie(los, queries)
    for pair in range(pairs):
        if pair == 1:
            los, own3, *pieces2 = tie(los, own3, *pieces2)
            gather2 = Gather(pieces2, rows1, "gather2")
            los = gather2.send(los)
            pieces3 = fetch_z(own3)
        if pair == 2:
            los = gather2.arrive(los)
            los = gather2.send(los)
        if pair == 3:
            los = gather2.arrive(los)
            for _ in bits[2:]:
                los = gather2.arrive(gather2.send(los))
            los, *pieces3 = tie(los, *pieces3)
            gather3 = Gather(pieces3, rows3, "gather3")
            los = gather3.send(los)
        context, lse = attend(
            los, block_hi[own_lo:own_hi], firsts, lasts, queries, keys, values, tag_cols,
            tag_row, chip, pair,
        )
        los, context = tie(los, context)
        contexts.append(context)
        lses.append(lse)
    context = jnp.concatenate(contexts, axis=1)
    lse_rows = jnp.concatenate(lses).reshape(local_heads, chip)
    context = gather3.arrive(context)
    context = gather3.send(context)
    own, given = product(context, proj_matrix, False, core, "attn_out")
    attn_out, resid, mlp_input = residual(own, swap_cores(given), tok, vec_rows)
    mlp_input = jnp.concatenate([mlp_input, swap_cores(mlp_input)])
    fc1_matrix = gather2.assemble(here, rank)
    activated, slope = hidden_units(mlp_input, fc1_matrix, fc1_shift)
    mlp_grad = scaled(cot, cot_other, vec_rows)
    both = [bits, bits[::-1]]
    activated = gather3.arrive(activated)
    for _ in bits[2:]:
        activated = gather3.arrive(gather3.send(activated))
    reduce3 = Reduce(grad_blocks(activated, mlp_grad, rank, both, "fc2_grad"), here, both)
    mlp_grad = reduce3.send(mlp_grad)
    fc2_matrix = gather3.assemble(here, rank)
    pre_grad, fc1_bias_part = pre_grads(mlp_grad, fc2_matrix, slope)
    reduce2 = Reduce(grad_blocks(mlp_input, pre_grad, rank, both, "fc1_grad"), here, both)
    pre_grad, _ = tie(pre_grad, [give for _, _, give in reduce2.held])
    own, given = product(pre_grad, fc1_matrix, True, 0, "mlp_in_grad")
    own, given = reduce3.arrive(own, given)
    for _ in bits[2:]:
        own, given = reduce3.arrive(*reduce3.send(own, given))
    own, given = reduce3.send(own, given)
    sent = swap_cores(given)
    resid_grad, attn_grad, norm_sums = norm_grads(own, sent, resid, cot, attn_out, vec_rows)
    attn_grad = in_order(attn_grad, swap_cores(attn_grad))
    context_grad = dot_nt(attn_grad, proj_matrix).astype(bf16)
    head_of = (
        lax.broadcasted_iota(jnp.int32, (local_heads, half_heads), 1) // HEAD_DIM
        == lax.broadcasted_iota(jnp.int32, (local_heads, half_heads), 0)
    ).astype(f32)
    row_delta = lax.dot_general(
        head_of, context_grad.astype(f32) * context.astype(f32), (((1,), (1,)), ((), ())),
        precision=lax.Precision.HIGHEST, preferred_element_type=f32,
    )
    stats = jnp.concatenate([lse_rows, row_delta])
    context_grad, activated, attn_grad = tie(context_grad, activated, attn_grad)
    chunk = half_heads // 2
    chunks = [context_grad[:, :chunk], context_grad[:, chunk:]]
    grads_behind, grads_ahead = zip(*[(from_chip(c, 1), from_chip(c, -1)) for c in chunks])
    stats_behind, stats_ahead = from_chip(stats, 1), from_chip(stats, -1)
    proj_grad = packed_proj_grad(context, attn_grad, head_rows)
    stat_window = jnp.concatenate([stats_behind, stats, stats_ahead], axis=1)
    by_pair = lambda s: s.reshape(pairs, 2, window)
    lse_window, delta_window = by_pair(stat_window[:local_heads]), by_pair(stat_window[local_heads:])

    half_pairs = pairs // 2
    half_width = half_heads // 2

    def first_group(parts, number):
        grads = [g for kind in zip(*parts) for g in kind]
        return Reduce(
            qkv_grad_blocks(normed1, grads, proj_grad, number, 2, rank, both), here, both
        )

    parts, sums = [], []
    out_own, out_given = product(activated, fc2_matrix, False, 0, "mlp_out")
    first, delta_window, lo, out_own, out_given = settle(
        ((grads_behind[0], grads_ahead[0]), delta_window, block_lo, out_own, out_given),
        (reduce3, "received"),
    )
    sides = [first, *list(zip(grads_behind, grads_ahead))[1:]]
    grad_windows = [jnp.concatenate([b, c, a]) for c, (b, a) in zip(chunks, sides)]
    for pair in range(pairs):
        if pair == 0:
            lo = reduce3.arrive(lo)
            lo = reduce2.send(lo)
        if pair == 1:
            lo = reduce2.arrive(lo)
            lo = reduce3.send_z(lo)
            for _ in bits[2:]:
                lo = reduce2.arrive(reduce2.send(lo))
            lo = reduce2.send(lo)
        if pair == 2:
            lo = settle(lo, (reduce2, "received"), (reduce3, "pieces"))
            lo = reduce2.arrive(lo)
            lo = reduce2.send_z(lo)
            reduce1a = first_group(parts, 0)
            lo = reduce1a.send(lo)
        if pair == 3:
            lo = settle(lo, (reduce2, "pieces"), (reduce1a, "received"))
            lo = reduce3.arrive_z(lo)
            lo = reduce2.arrive_z(lo)
            fc2_part = reduce3.total.astype(bf16)
            fc1_part = reduce2.total.astype(bf16)
            split = fc2_part.shape[0] // fc1_part.shape[0]
            mlp_spread = Spread(jnp.concatenate([fc1_part, *jnp.split(fc2_part, split)], axis=1))
            lo = mlp_spread.send(lo)
            lo = reduce1a.arrive(lo)
            for _ in bits[2:]:
                lo = reduce1a.arrive(reduce1a.send(lo))
            lo = reduce1a.send(lo)
        *grads, total = attend_back(
            lo, block_hi, queries, keys, values, grad_windows[pair * 2 // pairs], tag_cols, tag_row, lse_window,
            delta_window, chip, pair,
        )
        lo, *grads = tie(lo, *grads)
        parts.append(grads)
        sums.append(total[0])

    parts[-1] = settle(parts[-1], (mlp_spread, "arrays"))
    parts[-1] = reduce1a.arrive(parts[-1])
    parts[-1] = reduce1a.send_z(parts[-1])
    reduce1b = first_group(parts[half_pairs:], 1)
    parts[-1] = reduce1b.send(parts[-1])
    every = [jnp.concatenate(p, axis=1) for p in zip(*parts)]

    factor = 1.0 / math.sqrt(count * devices * ranks)
    in_own, in_given = product(
        jnp.concatenate(every, axis=1), qkv_matrix, True, core, "attn_in_grad"
    )
    tail = (in_own, in_given)
    tail = settle(tail, (reduce1b, "received"), (reduce1a, "pieces"))
    for _ in bits[1:]:
        tail = reduce1b.arrive(tail)
        tail = reduce1b.send(tail)
    in_own, in_given = tail
    input_rows, output_rows, end_sums = finish(
        in_own, swap_cores(in_given), tok, resid_grad, out_own, swap_cores(out_given), resid, cot, vec_rows
    )

    vectors = (
        end_sums[0:1], end_sums[1:2],
        jnp.concatenate([s[0:1] for s in sums], axis=1), jnp.concatenate([s[1:2] for s in sums], axis=1),
        norm_sums[2:3], norm_sums[3:4], norm_sums[0:1], norm_sums[1:2],
        end_sums[2:3], end_sums[3:4], fc1_bias_part,
    )
    of_core = [number in (2, 3, 10) for number in range(11)]
    partial = pack_grads(vectors, list(zip(sizes, of_core)), core, depth)
    vec_width = D // ranks
    half_of = lambda which: lax.dynamic_slice_in_dim(partial, which * 16, 16, 1)
    partial = half_of(core) + swap_cores(half_of(1 - core))
    vec_high = lax.reduce_precision(partial, 8, 7)
    side_by_side = 2 if vec_width >= 2 * LANES else 1
    extra = jnp.concatenate([vec_high, partial - vec_high], axis=side_by_side).astype(bf16)
    extra = jnp.pad(extra, ((0, 0), (0, 0), (0, vec_width - extra.shape[2])))
    extra = reduce1b.arrive(extra)
    extra = reduce1b.send_z(extra, extra=extra)
    for _ in bits[1:]:
        mlp_spread.send(extra)

    reduce1a.arrive_z()
    reduce1b.arrive_z()
    rows = reduce1a.total.shape[0]
    vec_total = reduce1b.total[rows:]
    if side_by_side == 2:
        vec_total = vec_total[:, :LANES] + vec_total[:, LANES : 2 * LANES]
    else:
        vec_total = vec_total[:16] + vec_total[16:]
    vec_high = lax.reduce_precision(vec_total, 8, 7)
    sides = [jnp.pad(v, ((0, 16), (0, vec_width - LANES))) for v in (vec_high, vec_total - vec_high)]
    payload = jnp.concatenate(
        [
            jnp.concatenate([reduce1a.total, reduce1b.total[:rows]], axis=1),
            jnp.concatenate(sides, axis=1),
        ]
    ).astype(bf16)
    payload = settle(payload, (mlp_spread, "arrays"))
    first_spread = Spread(payload)
    for bit in bits:
        first_spread.send()

    mlp_cols = fc1_part.shape[1]
    fc1_full = mlp_spread.blocks(rank, 0, mlp_cols)
    fc2_width = fc2_part.shape[1]
    fc2_full = tie(*[mlp_spread.blocks(rank, mlp_cols + n * fc2_width, fc2_width) for n in range(split)])
    grad_fc2 = jnp.concatenate(fc2_full).astype(f32) * factor
    first_a = first_spread.blocks(rank, 0, vec_width)
    first_b = first_spread.blocks(rank, vec_width, vec_width)
    totals = sum(
        part[rows : rows + 16, r * vec_width : r * vec_width + LANES].astype(f32)
        for part in (first_a, first_b)
        for r in range(ranks)
    ) * factor
    first_a, first_b = first_a[:rows], first_b[:rows]

    def rows_of(value, index):
        return lax.dynamic_slice_in_dim(value, index * head_rows, head_rows, 0)

    def interleave(own, other, width):
        cuts = range(0, own.shape[1], width)
        zipped = lambda a, b: jnp.concatenate(
            [v[:, c : c + width] for c in cuts for v in (a, b)], axis=1
        )
        return jnp.where(core == 0, zipped(own, other), zipped(other, own)).astype(f32) * factor

    fc1_other = swap_cores(rows_of(fc1_full, 1 - core))
    grad_fc1 = interleave(rows_of(fc1_full, core), fc1_other, unit_rows)
    qkv_full = jnp.concatenate(
        [
            part[:, n * half_width : (n + 1) * half_width]
            for n in range(3)
            for part in (first_a, first_b)
        ],
        axis=1,
    )
    grad_qkv = interleave(rows_of(qkv_full, core), swap_cores(rows_of(qkv_full, 1 - core)), head_rows)
    proj_part = jnp.concatenate([first_a[:, 3 * half_width :], first_b[:, 3 * half_width :]], axis=1)
    grad_proj = jnp.concatenate([proj_part[:head_rows], proj_part[head_rows:]], axis=1).astype(f32) * factor

    small_grads = [totals[i, : sizes[i]] for i in range(10)]
    lines = -(-sizes[10] // LANES)
    small_grads.append(totals[10 : 10 + lines].reshape(-1))
    (
        grad_attn_gain, grad_attn_shift, grad_query_shift, grad_value_shift, grad_proj_shift,
        grad_attn_scale, grad_mlp_gain, grad_mlp_shift, grad_fc2_shift, grad_mlp_scale, grad_fc1_shift,
    ) = small_grads

    return (
        output_rows[None],
        input_rows[None],
        grad_attn_gain,
        grad_attn_shift,
        grad_qkv,
        grad_query_shift,
        grad_value_shift,
        grad_proj,
        grad_proj_shift,
        grad_attn_scale,
        grad_mlp_gain,
        grad_mlp_shift,
        grad_fc1,
        grad_fc1_shift,
        grad_fc2,
        grad_fc2_shift,
        grad_mlp_scale,
    )


def solution(mesh):
    rows = P("fsdp", None)
    vec = P("fsdp")
    tok = P("rep", "fsdp", None)
    return jax.shard_map(
        on_device,
        mesh=mesh,
        in_specs=(
            tok, P("rep", "fsdp"), vec, vec, rows, vec, vec, rows, vec, vec, vec, vec, rows, vec,
            rows, vec, vec, tok,
        ),
        out_specs=(
            tok, tok, vec, vec, rows, vec, vec, rows, vec, vec, vec, vec, rows, vec, rows, vec, vec,
        ),
        check_vma=False,
    )
```

```python
import functools
import math

import jax
import jax.numpy as jnp
from jax import lax
from jax.experimental import pallas as pl
from jax.experimental.pallas import tpu as pltpu
from jax.sharding import PartitionSpec as P

D = 1024
HEADS = 16
HEAD_DIM = 64
LANES = 128

EPSILON = 1e-06
MASKED = -1e30
BLOCK = 256

SHORT = pl.CostEstimate(flops=1, transcendentals=0, bytes_accessed=1)

f32 = jnp.float32
bf16 = jnp.bfloat16


def normalize(features):
    row_mean = jnp.mean(features, axis=-1, keepdims=True)
    centred = features - row_mean
    variance = jnp.mean(centred * centred, axis=-1, keepdims=True)
    inverse = lax.rsqrt(variance + EPSILON)
    return centred * inverse, inverse


def norm_back(gradient, normal, inverse, gain_vec):
    scaled = gradient * gain_vec
    mean_first = jnp.mean(scaled, axis=-1, keepdims=True)
    mean_second = jnp.mean(scaled * normal, axis=-1, keepdims=True)
    return inverse * (scaled - mean_first - normal * mean_second)


def gelu_pair(values):
    cumulative = 0.5 * (1.0 + lax.erf(values * 2.0 ** (-0.5)))
    density = jnp.exp(-0.5 * values * values) * (2.0 * math.pi) ** (-0.5)
    return (values * cumulative, cumulative + values * density)


def dot(a, b):
    return jnp.dot(a, b, preferred_element_type=f32)


def dot_nt(a, b):
    return lax.dot_general(a, b, (((1,), (1,)), ((), ())), preferred_element_type=f32)


def dot_tn(a, b):
    return lax.dot_general(a, b, (((0,), (0,)), ((), ())), preferred_element_type=f32)


def swap_cores(value):
    size = lax.axis_size("fsdp")
    return lax.ppermute(value, "fsdp", [(i, i ^ 1) for i in range(size)])


def along_z(value, by):
    size = lax.axis_size("fsdp")
    return lax.ppermute(value, "fsdp", [(i, (i + 2 * by) % size) for i in range(size)])


def from_chip(value, by):
    size = lax.axis_size("fsdp")
    pairs = [(i, i + 2 * by) for i in range(size) if 0 <= i + 2 * by < size]
    return lax.ppermute(value, "fsdp", pairs)


def across_rep(value, bit):
    size = lax.axis_size("rep")
    return lax.ppermute(value, "rep", [(i, i ^ (1 << bit)) for i in range(size)])


def pick(value, index, axis):
    return lax.dynamic_index_in_dim(value, index, axis, keepdims=False)


def rep_bits():
    return lax.axis_size("rep").bit_length() - 1


def tie(*values):
    return lax.optimization_barrier(values)


def settle(value, *fields):
    held = [getattr(o, name) for o, name in fields]
    value, held = lax.optimization_barrier((value, held))
    for (o, name), new in zip(fields, held):
        setattr(o, name, new)
    return value


def fetch_z(own):
    return [own] + [along_z(own, k) for k in range(1, lax.axis_size("fsdp") // 2)]


class Gather:
    def __init__(self, pieces, rows, name):
        self.rows, self.cols, self.name = rows, pieces[0].shape[1], name
        half = rows // 2
        bits = list(range(rep_bits()))
        self.orders = [bits, bits[::-1]]
        self.parts = [
            [(jnp.stack([p[:half] for p in pieces])[None], [0])],
            [(jnp.stack([p[half:rows] for p in pieces])[None], [0])],
        ]
        self.at = 0

    def send(self, *values):
        whole = [
            (ps[0][0] if len(ps) == 1 else jnp.concatenate([a for a, _ in ps]), [o for _, os in ps for o in os])
            for ps in self.parts
        ]
        values, arrays = lax.optimization_barrier((values, [a for a, _ in whole]))
        self.parts = []
        for array, (_, offsets), order in zip(arrays, whole, self.orders):
            flip = 1 << order[self.at]
            received = across_rep(array, order[self.at])
            self.parts.append([(array, offsets), (received, [o ^ flip for o in offsets])])
        self.at += 1
        return values[0] if len(values) == 1 else values

    def arrive(self, value):
        value, arrays = lax.optimization_barrier((value, [a for ps in self.parts for a, _ in ps]))
        self.parts = [[(arrays.pop(0), o) for _, o in ps] for ps in self.parts]
        return value

    def assemble(self, here, rank, tail_rows=0):
        depth, ranks = lax.axis_size("fsdp") // 2, lax.axis_size("rep")
        sources, plan = [], []
        for number, parts in enumerate(self.parts):
            for array, offsets in parts:
                sources.append(array)
                plan.append((number, offsets))
        dtype = sources[0].dtype
        shape = (depth * self.rows, ranks * self.cols)
        shapes = [jax.ShapeDtypeStruct(shape, dtype)]
        if tail_rows:
            tail = shape[1] // 4
            shapes = [
                jax.ShapeDtypeStruct((shape[0], shape[1] - tail), dtype),
                jax.ShapeDtypeStruct((depth * tail_rows, 2 * tail), dtype),
            ]
        out = pl.pallas_call(
            functools.partial(assemble_kernel, plan, depth, self.rows, self.cols, tail_rows),
            out_shape=shapes,
            grid_spec=pltpu.PrefetchScalarGridSpec(
                num_scalar_prefetch=1,
                grid=(1,),
                in_specs=[pl.BlockSpec(memory_space=pl.ANY)] * len(sources),
                out_specs=[pl.BlockSpec(memory_space=pl.ANY)] * len(shapes),
                scratch_shapes=[
                    pltpu.VMEM(shape, dtype),
                    pltpu.SemaphoreType.DMA((2 * ranks * depth,)),
                    pltpu.SemaphoreType.DMA((3 * depth,)),
                ],
            ),
            compiler_params=pltpu.CompilerParams(vmem_limit_bytes=16 << 20),
            cost_estimate=SHORT,
            name=self.name,
        )(jnp.stack([here, rank]).astype(jnp.int32), *sources)
        return out if tail_rows else out[0]


def assemble_kernel(plan, depth, rows, cols, tail_rows, index_ref, *refs):
    count = len(plan)
    sources = refs[:count]
    targets = refs[count : count + (2 if tail_rows else 1)]
    held, in_sems, out_sems = refs[-3:]
    here, rank = index_ref[0], index_ref[1]
    half = rows // 2
    waits = [[] for _ in range(depth)]
    number = 0
    for k in range(depth):
        place = lax.rem(here - k + depth, depth)
        for which, (colour, offsets) in enumerate(plan):
            for m, offset in enumerate(offsets):
                at_row = pl.multiple_of(place * rows + colour * half, half)
                at_col = pl.multiple_of((rank ^ offset) * cols, cols)
                copy = pltpu.make_async_copy(
                    sources[which].at[m, k],
                    held.at[pl.ds(at_row, half), pl.ds(at_col, cols)],
                    in_sems.at[number],
                )
                copy.start()
                waits[k].append(copy)
                number += 1
    outs = []
    main = targets[0].shape[1]
    for k in range(depth):
        place = lax.rem(here - k + depth, depth)
        for copy in waits[k]:
            copy.wait()
        base = pl.multiple_of(place * rows, rows)
        band = pl.ds(base, rows)
        out = pltpu.make_async_copy(held.at[band, pl.ds(0, main)], targets[0].at[band], out_sems.at[3 * k])
        out.start()
        outs.append(out)
        if tail_rows:
            wide = targets[1].shape[1] // 2
            for side in range(2):
                out = pltpu.make_async_copy(
                    held.at[pl.ds(base + side * tail_rows, tail_rows), pl.ds(main, wide)],
                    targets[1].at[
                        pl.ds(pl.multiple_of(place * tail_rows, tail_rows), tail_rows),
                        pl.ds(side * wide, wide),
                    ],
                    out_sems.at[3 * k + 1 + side],
                )
                out.start()
                outs.append(out)
    for out in outs:
        out.wait()


def halves(ranks, bit, held):
    flip = 1 << bit
    kept = [o for o in held if not o & flip]
    return kept, [o ^ flip for o in kept]


def relative_blocks(grads, rank, orders):
    depth, ranks = lax.axis_size("fsdp") // 2, lax.axis_size("rep")
    width = grads.shape[1] // ranks
    rows = grads.shape[0] // depth
    shaped = grads.reshape(depth, rows, grads.shape[1])
    share = rows // len(orders)
    first = []
    for n, order in enumerate(orders):
        block = lambda o: lax.dynamic_slice(
            shaped, (0, n * share, (rank ^ o) * width), (depth, share, width)
        )
        kept, given = halves(ranks, order[0], list(range(ranks)))
        first.append((jnp.stack([block(o) for o in kept]), jnp.stack([block(o) for o in given])))
    return first


class Reduce:
    def __init__(self, first, here, orders):
        self.here, self.orders, self.at = here, orders, 0
        ranks = lax.axis_size("rep")
        self.held = []
        for (keep, give), order in zip(first, orders):
            kept, given = halves(ranks, order[0], list(range(ranks)))
            self.held.append((kept, keep, give))

    def send(self, *values):
        values, gives = lax.optimization_barrier((values, [give for _, _, give in self.held]))
        self.received = [across_rep(g, order[self.at]) for g, order in zip(gives, self.orders)]
        self.at += 1
        return values[0] if len(values) == 1 else values

    def arrive(self, *values):
        values, received = lax.optimization_barrier((values, self.received))
        held = []
        for (kept, keep, _), got, order in zip(self.held, received, self.orders):
            total = (keep.astype(f32) + got.astype(f32)).astype(bf16)
            if self.at < len(order):
                stay, leave = halves(None, order[self.at], kept)
                take = lambda os: jnp.stack([total[kept.index(o)] for o in os])
                held.append((stay, take(stay), take(leave)))
            else:
                held.append((kept, total[0], None))
        self.held = held
        return values[0] if len(values) == 1 else values

    def send_z(self, *values, extra=None):
        depth = lax.axis_size("fsdp") // 2
        parts = [keep for _, keep, _ in self.held]
        whole = parts[0] if len(parts) == 1 else jnp.concatenate(parts, axis=1)
        if extra is not None:
            whole = jnp.concatenate([whole, extra], axis=1)
        pieces = [pick(whole, lax.rem(self.here + k, depth), 0) for k in range(depth)]
        values, pieces = lax.optimization_barrier((values, pieces))
        self.pieces = [pieces[0]] + [along_z(p, k) for k, p in enumerate(pieces) if k]
        return values[0] if len(values) == 1 else values

    def arrive_z(self, *values):
        values, pieces = lax.optimization_barrier((values, self.pieces))
        total = pieces[0].astype(f32)
        for piece in pieces[1:]:
            total = total + piece.astype(f32)
        self.total = total
        return values[0] if len(values) == 1 else values


class Spread:
    def __init__(self, value):
        bits = list(range(rep_bits()))
        self.orders = [bits, bits[::-1]]
        half = value.shape[0] // 2
        self.arrays = [value[:half][None], value[half:][None]]
        self.offsets = [[0], [0]]
        self.at = 0

    def send(self, *values):
        values, arrays = lax.optimization_barrier((values, self.arrays))
        self.arrays = []
        for n, (array, order) in enumerate(zip(arrays, self.orders)):
            flip = 1 << order[self.at]
            received = across_rep(array, order[self.at])
            self.arrays.append(jnp.concatenate([array, received]))
            self.offsets[n] = self.offsets[n] + [o ^ flip for o in self.offsets[n]]
        self.at += 1
        return values[0] if len(values) == 1 else values

    def blocks(self, rank, start, size):
        return jnp.concatenate(
            [rep_blocks(a[:, :, start : start + size], o, rank) for a, o in zip(self.arrays, self.offsets)]
        )


def rep_blocks(stacked, offsets, rank):
    blocks = []
    for i in range(len(offsets)):
        block = stacked[0]
        for entry, offset in enumerate(offsets):
            block = jnp.where((rank ^ offset) == i, stacked[entry], block)
        blocks.append(block)
    return jnp.concatenate(blocks, axis=1)


def share_kernel(widths, index_ref, qkv_ref, proj_ref, fc1_ref, keep_ref, give_ref, sems):
    rank, core = index_ref[0], index_ref[1]
    wide1, wide2, block, unit, half = widths
    is_proj = rank * wide1 >= 3 * half

    def copies(second):
        made = []
        for out, (ref, which) in enumerate(((keep_ref, core), (give_ref, 1 - core))):
            for c in range(wide1 // block):
                col = rank * wide1 + c * block
                if second:
                    source, at = proj_ref, which * half + col - 3 * half
                else:
                    source, at = qkv_ref, 2 * col + which * block
                made.append((source, at, block, ref, c * block))
        return made

    def run(plan, first):
        started = []
        for n, (source, at, size, ref, to) in enumerate(plan):
            copy = pltpu.make_async_copy(
                source.at[:, pl.ds(pl.multiple_of(at, LANES), size)], ref.at[:, pl.ds(to, size)], sems.at[first + n]
            )
            copy.start()
            started.append(copy)
        return started

    col = rank * wide2
    plan2 = []
    for ref, which in ((keep_ref, core), (give_ref, 1 - core)):
        at = col + (lax.div(col, unit) + which) * unit
        plan2.append((fc1_ref, at, wide2, ref, wide1))
    second = run(plan2, 0)

    @pl.when(is_proj)
    def _():
        for copy in run(copies(True), 2):
            copy.wait()

    @pl.when(jnp.logical_not(is_proj))
    def _():
        for copy in run(copies(False), 2):
            copy.wait()

    for copy in second:
        copy.wait()


def weight_share(rank, core, qkv_weight, proj_weight, fc1_weight, ranks, block, unit):
    rows = qkv_weight.shape[0]
    wide1, wide2 = 2 * D // ranks, fc1_weight.shape[1] // 2 // ranks
    out = jax.ShapeDtypeStruct((rows, wide1 + wide2), bf16)
    return pl.pallas_call(
        functools.partial(share_kernel, (wide1, wide2, block, unit, D // 2)),
        out_shape=[out, out],
        grid_spec=pltpu.PrefetchScalarGridSpec(
            num_scalar_prefetch=1,
            grid=(1,),
            in_specs=[pl.BlockSpec(memory_space=pl.ANY)] * 3,
            out_specs=[pl.BlockSpec(out.shape, lambda i, a: (0, 0))] * 2,
            scratch_shapes=[pltpu.SemaphoreType.DMA((2 + 2 * (wide1 // block),))],
        ),
        cost_estimate=SHORT,
        name="weight_share",
    )(jnp.stack([rank, core]).astype(jnp.int32), qkv_weight, proj_weight, fc1_weight)


def whole_specs(arrays):
    return [pl.BlockSpec(a.shape, lambda *_, n=len(a.shape): (0,) * n) for a in arrays]


def slot_lists(sizes):
    slots = []
    for number, size in enumerate(sizes):
        for start in range(0, size, LANES):
            slots.append((number, start, min(LANES, size - start)))
    return slots


def pack_kernel(slots, *refs):
    *sources, out_ref, held = refs
    per_row = held.shape[1] // LANES
    held[...] = jnp.zeros_like(held)
    for slot, (number, start, size) in enumerate(slots):
        row, at = slot // per_row, slot % per_row * LANES
        held[row : row + 1, at : at + size] = sources[number][:, start : start + size].astype(f32)
    out_ref[...] = held[...].astype(out_ref.dtype)


def pack_small(vectors, width, slots):
    shape = (32 * LANES // width, width)
    vectors = [v.reshape(1, -1) for v in vectors]
    return pl.pallas_call(
        functools.partial(pack_kernel, slots),
        out_shape=jax.ShapeDtypeStruct(shape, bf16),
        scratch_shapes=[pltpu.VMEM(shape, f32)],
        name="pack_small",
    )(*vectors)


def unpack_kernel(slots, depth, index_ref, *refs):
    pieces, (vec_ref, unit_ref, tag_ref) = refs[:depth], refs[depth:]
    here, core = index_ref[0], index_ref[1]
    rows, width = pieces[0].shape
    per_row = width // LANES
    single = sum(1 for number, _, _ in slots if number < 10)
    vec_ref[...] = jnp.zeros_like(vec_ref)
    for k in range(depth):
        place = lax.rem(here - k + depth, depth)
        values = pieces[k][...].astype(f32)

        def part(side, slot, size):
            row, at = side * (rows // 2) + slot // per_row, slot % per_row * LANES
            return values[row : row + 1, at : at + size]

        for slot, (number, start, size) in enumerate(slots):
            own, other = part(0, slot, size), part(1, slot, size)
            first = jnp.where(core == 0, own, other)
            second = jnp.where(core == 0, other, own)
            if number < 10:
                at = pl.multiple_of(place * 2 * size, 2 * size)
                vec_ref[number : number + 1, pl.ds(at, 2 * size)] = jnp.concatenate([first, second], axis=1)
            elif number == 10:
                wide = unit_ref.shape[1] // depth
                unit_ref[0:1, pl.ds(pl.multiple_of(place * wide + start, LANES), LANES)] = own
            else:
                wide = tag_ref.shape[1] // depth
                at = pl.multiple_of(place * wide + start, LANES)
                tag_ref[0:1, pl.ds(at, LANES)] = first
                tag_ref[0:1, pl.ds(pl.multiple_of(at + wide // 2, LANES), LANES)] = second


def unpack_small(pieces, slots, rows, here, core, units, group_tokens):
    depth = len(pieces)
    extra, width = pieces[0].shape[0] - rows, pieces[0].shape[1]
    shapes = [(16, D), (1, units), (1, group_tokens)]
    return pl.pallas_call(
        functools.partial(unpack_kernel, slots, depth),
        out_shape=[jax.ShapeDtypeStruct(s, f32) for s in shapes],
        grid_spec=pltpu.PrefetchScalarGridSpec(
            num_scalar_prefetch=1,
            grid=(1,),
            in_specs=[pl.BlockSpec((extra, width), lambda i, a: (rows // extra, 0))] * depth,
            out_specs=[pl.BlockSpec(s, lambda i, a: (0, 0)) for s in shapes],
        ),
        name="unpack_small",
    )(jnp.stack([here, core]).astype(jnp.int32), *pieces)


def pack_grads_kernel(depth, sizes, index_ref, *refs):
    *sources, out_ref = refs
    core = index_ref[0]
    out_ref[...] = jnp.zeros_like(out_ref)
    for z in range(depth):
        for c in range(2):
            row = 16 * c
            for source, (size, of_core) in zip(sources, sizes):
                for start in range(0, size, LANES):
                    lanes = min(LANES, size - start)
                    at = (z if of_core else 2 * z + c) * size + start
                    value = source[0:1, at : at + lanes]
                    if of_core:
                        value = jnp.where(core == c, value, 0.0)
                    out_ref[z, row : row + 1, 0:lanes] = value
                    row += 1


def pack_grads(vectors, sizes, core, depth):
    return pl.pallas_call(
        functools.partial(pack_grads_kernel, depth, sizes),
        out_shape=jax.ShapeDtypeStruct((depth, 32, LANES), f32),
        grid_spec=pltpu.PrefetchScalarGridSpec(
            num_scalar_prefetch=1,
            grid=(1,),
            in_specs=whole_specs(vectors),
            out_specs=pl.BlockSpec((depth, 32, LANES), lambda i, a: (0, 0, 0)),
        ),
        name="pack_grads",
    )(core.reshape(1).astype(jnp.int32), *vectors)


def grad_blocks_kernel(orders, ranks, index_ref, a_ref, b_ref, *refs):
    outs, held = refs[:-1], refs[-1]
    rank = index_ref[0]
    held[...] = dot_tn(a_ref[...], b_ref[...]).astype(bf16)
    width = held.shape[1] // ranks
    share = held.shape[0] // len(orders)
    for n, order in enumerate(orders):
        for which, offsets in enumerate(halves(ranks, order[0], list(range(ranks)))):
            for i, o in enumerate(offsets):
                cols = pl.ds(pl.multiple_of((rank ^ o) * width, width), width)
                outs[2 * n + which][i, 0] = held[n * share : (n + 1) * share, cols]


def grad_blocks(a, b, rank, orders, name):
    depth, ranks = lax.axis_size("fsdp") // 2, lax.axis_size("rep")
    tokens, rows, cols = a.shape[0], a.shape[1] // depth, b.shape[1]
    if cols // ranks % LANES:
        return relative_blocks(dot_tn(a, b).astype(bf16), rank, orders)
    block = (ranks // 2, depth, rows // len(orders), cols // ranks)
    outs = pl.pallas_call(
        functools.partial(grad_blocks_kernel, orders, ranks),
        out_shape=[jax.ShapeDtypeStruct(block, bf16)] * (2 * len(orders)),
        grid_spec=pltpu.PrefetchScalarGridSpec(
            num_scalar_prefetch=1,
            grid=(depth,),
            in_specs=[
                pl.BlockSpec((tokens, rows), lambda i, s: (0, i)),
                pl.BlockSpec((tokens, cols), lambda i, s: (0, 0)),
            ],
            out_specs=[pl.BlockSpec((block[0], 1) + block[2:], lambda i, s: (0, i, 0, 0))] * (2 * len(orders)),
            scratch_shapes=[pltpu.VMEM((rows, cols), bf16)],
        ),
        compiler_params=pltpu.CompilerParams(vmem_limit_bytes=40 << 20),
        cost_estimate=SHORT,
        name=name,
    )(rank.reshape(1).astype(jnp.int32), a, b)
    return [(outs[2 * n], outs[2 * n + 1]) for n in range(len(orders))]


def pre_grad_kernel(g_ref, w_ref, slope_ref, out_ref, sum_ref):
    grad = dot_nt(g_ref[...], w_ref[...]) * slope_ref[...].astype(f32)
    out_ref[...] = grad.astype(bf16)
    sum_ref[...] = jnp.sum(grad, axis=0, keepdims=True)


def pre_grads(mlp_grad, fc2_matrix, slope):
    tokens, units = slope.shape
    tile = 256
    return pl.pallas_call(
        pre_grad_kernel,
        out_shape=[jax.ShapeDtypeStruct((tokens, units), bf16), jax.ShapeDtypeStruct((1, units), f32)],
        grid=(units // tile,),
        in_specs=[
            pl.BlockSpec((tokens, D), lambda i: (0, 0)),
            pl.BlockSpec((tile, D), lambda i: (i, 0)),
            pl.BlockSpec((tokens, tile), lambda i: (0, i)),
        ],
        out_specs=[pl.BlockSpec((tokens, tile), lambda i: (0, i)), pl.BlockSpec((1, tile), lambda i: (0, i))],
        compiler_params=pltpu.CompilerParams(vmem_limit_bytes=40 << 20),
        cost_estimate=SHORT,
        name="pre_grad",
    )(mlp_grad, fc2_matrix, slope)


def product_kernel(half_ref, first_ref, second_ref, w_ref, out1_ref, out2_ref):
    out1_ref[...] = dot(first_ref[...], w_ref[...])
    out2_ref[...] = dot(second_ref[...], w_ref[...])


def product_nt_kernel(half_ref, first_ref, second_ref, w_ref, out1_ref, out2_ref, held):
    @pl.when(pl.program_id(0) == 0)
    def _():
        held[...] = w_ref[...].T

    out1_ref[...] = dot(first_ref[...], held[...])
    out2_ref[...] = dot(second_ref[...], held[...])


def product(a, weight, flipped, half, name):
    rows, tile = a.shape[0] // 2, 128
    count = rows // tile
    out = pl.BlockSpec((tile, D), lambda i, h: (i, 0))
    return pl.pallas_call(
        product_nt_kernel if flipped else product_kernel,
        out_shape=[jax.ShapeDtypeStruct((rows, D), f32)] * 2,
        grid_spec=pltpu.PrefetchScalarGridSpec(
            num_scalar_prefetch=1,
            grid=(count,),
            in_specs=[
                pl.BlockSpec((tile, a.shape[1]), lambda i, h: (i + h[0] * count, 0)),
                pl.BlockSpec((tile, a.shape[1]), lambda i, h: (i + (1 - h[0]) * count, 0)),
                pl.BlockSpec(weight.shape, lambda i, h: (0, 0)),
            ],
            out_specs=[out, out],
            scratch_shapes=[pltpu.VMEM(weight.shape[::-1], bf16)] if flipped else [],
        ),
        compiler_params=pltpu.CompilerParams(vmem_limit_bytes=32 << 20),
        cost_estimate=SHORT,
        name=name,
    )(jnp.asarray(half, jnp.int32).reshape(1), a, a, weight)


def finish_kernel(
    own1_ref, sent1_ref, tok_ref, grad_ref, own2_ref, sent2_ref, resid_ref, cot_ref, vec_ref,
    in_grad_ref, out_ref, sum_ref,
):
    grad = own1_ref[...] + sent1_ref[...]
    normal, inverse = normalize(tok_ref[...].astype(f32))
    in_grad_ref[...] = grad_ref[...] + norm_back(grad, normal, inverse, vec_ref[0:1, :])
    mlp = own2_ref[...] + sent2_ref[...] + vec_ref[8:9, :]
    out_ref[...] = (resid_ref[...] + vec_ref[9:10, :] * mlp).astype(bf16)
    out_grad = cot_ref[...].astype(f32)

    @pl.when(pl.program_id(0) == 0)
    def _():
        sum_ref[...] = jnp.zeros_like(sum_ref)

    for row, value in enumerate((grad * normal, grad, out_grad * vec_ref[9:10, :], out_grad * mlp)):
        sum_ref[row : row + 1, :] += jnp.sum(value, axis=0, keepdims=True)


def finish(own1, sent1, tok, resid_grad, own2, sent2, resid, cot, vecs):
    rows, tile = own1.shape[0], 64
    part = pl.BlockSpec((tile, D), lambda i: (i, 0))
    return pl.pallas_call(
        finish_kernel,
        out_shape=[
            jax.ShapeDtypeStruct((rows, D), f32), jax.ShapeDtypeStruct((rows, D), bf16),
            jax.ShapeDtypeStruct((8, D), f32),
        ],
        grid=(rows // tile,),
        in_specs=[part] * 8 + [pl.BlockSpec(vecs.shape, lambda i: (0, 0))],
        out_specs=[part, part, pl.BlockSpec((8, D), lambda i: (0, 0))],
        compiler_params=pltpu.CompilerParams(vmem_limit_bytes=24 << 20),
        cost_estimate=SHORT,
        name="finish",
    )(own1, sent1, tok, resid_grad, own2, sent2, resid, cot, vecs)


def residual_kernel(own_ref, sent_ref, tok_ref, vec_ref, attn_ref, resid_ref, input_ref):
    attn = own_ref[...] + sent_ref[...] + vec_ref[4:5, :]
    resid = tok_ref[...].astype(f32) + vec_ref[5:6, :] * attn
    attn_ref[...] = attn
    resid_ref[...] = resid
    normal, _ = normalize(resid)
    input_ref[...] = (normal * vec_ref[6:7, :] + vec_ref[7:8, :]).astype(bf16)


def residual(own, sent, tok, vecs):
    rows, tile = own.shape[0], 64
    part = pl.BlockSpec((tile, D), lambda i: (i, 0))
    return pl.pallas_call(
        residual_kernel,
        out_shape=[jax.ShapeDtypeStruct((rows, D), t) for t in (f32, f32, bf16)],
        grid=(rows // tile,),
        in_specs=[part] * 3 + [pl.BlockSpec(vecs.shape, lambda i: (0, 0))],
        out_specs=[part] * 3,
        compiler_params=pltpu.CompilerParams(vmem_limit_bytes=24 << 20),
        cost_estimate=SHORT,
        name="residual",
    )(own, sent, tok, vecs)


def scaled_kernel(own_ref, other_ref, vec_ref, out_ref):
    rows = own_ref.shape[0]
    for n, ref in enumerate((own_ref, other_ref)):
        out_ref[n * rows : (n + 1) * rows, :] = (ref[...].astype(f32) * vec_ref[9:10, :]).astype(bf16)


def scaled(own, other, vecs):
    return pl.pallas_call(
        scaled_kernel,
        out_shape=jax.ShapeDtypeStruct((2 * own.shape[0], D), bf16),
        compiler_params=pltpu.CompilerParams(vmem_limit_bytes=24 << 20),
        cost_estimate=SHORT,
        name="scaled",
    )(own, other, vecs)


def units_kernel(n_ref, w_ref, b_ref, act_ref, slope_ref):
    act, slope = gelu_pair(dot(n_ref[...], w_ref[...]) + b_ref[...])
    act_ref[...] = act.astype(bf16)
    slope_ref[...] = slope.astype(bf16)


def hidden_units(normed, weight, bias):
    tokens, units = normed.shape[0], weight.shape[1]
    tile = 256
    part = pl.BlockSpec((tokens, tile), lambda i: (0, i))
    return pl.pallas_call(
        units_kernel,
        out_shape=[jax.ShapeDtypeStruct((tokens, units), bf16)] * 2,
        grid=(units // tile,),
        in_specs=[
            pl.BlockSpec((tokens, D), lambda i: (0, 0)),
            pl.BlockSpec((D, tile), lambda i: (0, i)),
            pl.BlockSpec((1, tile), lambda i: (0, i)),
        ],
        out_specs=[part, part],
        compiler_params=pltpu.CompilerParams(vmem_limit_bytes=32 << 20),
        cost_estimate=SHORT,
        name="units",
    )(normed, weight, bias)


def norm_grad_kernel(own_ref, sent_ref, resid_ref, cot_ref, attn_ref, vec_ref, grad_ref, scaled_ref, sum_ref):
    grad = own_ref[...] + sent_ref[...]
    normal, inverse = normalize(resid_ref[...])
    resid_grad = cot_ref[...].astype(f32) + norm_back(grad, normal, inverse, vec_ref[6:7, :])
    scaled = resid_grad * vec_ref[5:6, :]
    grad_ref[...] = resid_grad
    scaled_ref[...] = scaled.astype(bf16)

    @pl.when(pl.program_id(0) == 0)
    def _():
        sum_ref[...] = jnp.zeros_like(sum_ref)

    for row, value in enumerate((grad * normal, grad, scaled, resid_grad * attn_ref[...])):
        sum_ref[row : row + 1, :] += jnp.sum(value, axis=0, keepdims=True)


def norm_grads(own, sent, resid, cot, attn_out, vecs):
    rows, tile = own.shape[0], 64
    part = pl.BlockSpec((tile, D), lambda i: (i, 0))
    return pl.pallas_call(
        norm_grad_kernel,
        out_shape=[
            jax.ShapeDtypeStruct((rows, D), f32), jax.ShapeDtypeStruct((rows, D), bf16),
            jax.ShapeDtypeStruct((8, D), f32),
        ],
        grid=(rows // tile,),
        in_specs=[part] * 5 + [pl.BlockSpec(vecs.shape, lambda i: (0, 0))],
        out_specs=[part, part, pl.BlockSpec((8, D), lambda i: (0, 0))],
        compiler_params=pltpu.CompilerParams(vmem_limit_bytes=24 << 20),
        cost_estimate=SHORT,
        name="norm_grad",
    )(own, sent, resid, cot, attn_out, vecs)


def proj_grad_kernel(head_rows, c_ref, g_ref, out_ref):
    wide = out_ref.shape[1]
    for side in range(2):
        grad = dot_tn(c_ref[...], g_ref[:, side * wide : (side + 1) * wide]).astype(bf16)
        for z in range(grad.shape[0] // head_rows):
            at = (2 * z + side) * head_rows
            out_ref[at : at + head_rows, :] = grad[z * head_rows : (z + 1) * head_rows]


def packed_proj_grad(context, attn_grad, head_rows):
    wide = D // 2
    return pl.pallas_call(
        functools.partial(proj_grad_kernel, head_rows),
        out_shape=jax.ShapeDtypeStruct((D, wide), bf16),
        compiler_params=pltpu.CompilerParams(vmem_limit_bytes=32 << 20),
        cost_estimate=SHORT,
        name="proj_grad",
    )(context, attn_grad)


def qkv_grad_kernel(orders, ranks, depth, per, index_ref, n_ref, *refs):
    grads, p_ref = refs[: 3 * per], refs[3 * per]
    outs, held = refs[3 * per + 1 : -1], refs[-1]
    rank = index_ref[0]
    normed = n_ref[...]
    for number in range(3):
        pieces = [g[...] for g in grads[number * per : (number + 1) * per]]
        wide = per * LANES
        joined = pieces[0] if per == 1 else jnp.concatenate(pieces, axis=1)
        held[:, number * wide : (number + 1) * wide] = dot_tn(normed, joined).astype(bf16)
    held[:, 3 * per * LANES :] = p_ref[...]
    width = held.shape[1] // ranks
    rows = held.shape[0] // depth
    share = rows // len(orders)
    for n, order in enumerate(orders):
        for which, offsets in enumerate(halves(ranks, order[0], list(range(ranks)))):
            for i, o in enumerate(offsets):
                cols = pl.ds(pl.multiple_of((rank ^ o) * width, width), width)
                for z in range(depth):
                    at = z * rows + n * share
                    outs[2 * n + which][i, z] = held[at : at + share, cols]


def qkv_grad_blocks(normed, grads, proj_packed, part, parts, rank, orders):
    depth, ranks = lax.axis_size("fsdp") // 2, lax.axis_size("rep")
    per = len(grads) // 3
    cols = 4 * per * LANES
    block = (ranks // 2, depth, D // depth // len(orders), cols // ranks)
    tokens = normed.shape[0] // 3
    outs = pl.pallas_call(
        functools.partial(qkv_grad_kernel, orders, ranks, depth, per),
        out_shape=[jax.ShapeDtypeStruct(block, bf16)] * (2 * len(orders)),
        grid_spec=pltpu.PrefetchScalarGridSpec(
            num_scalar_prefetch=1,
            grid=(1,),
            in_specs=[pl.BlockSpec((tokens, D), lambda i, a: (1, 0))]
            + whole_specs(grads)
            + [pl.BlockSpec((D, per * LANES), lambda i, a: (0, part))],
            out_specs=[pl.BlockSpec(block, lambda i, a: (0, 0, 0, 0))] * (2 * len(orders)),
            scratch_shapes=[pltpu.VMEM((D, cols), bf16)],
        ),
        compiler_params=pltpu.CompilerParams(vmem_limit_bytes=40 << 20),
        cost_estimate=SHORT,
        name="qkv_grad",
    )(rank.reshape(1).astype(jnp.int32), normed, *grads, proj_packed)
    return [(outs[2 * n], outs[2 * n + 1]) for n in range(len(orders))]


def spread_lanes(tags, width):
    return jnp.concatenate([tags] * (width // LANES), axis=1)


def project_kernel(need_ref, n_ref, w_ref, b_ref, q_ref, k_ref, v_ref):
    row = pl.program_id(0)
    wide = q_ref.shape[1]

    @pl.when(need_ref[row] > 0)
    def _():
        n = n_ref[...]
        for i, ref in enumerate((q_ref, k_ref, v_ref)):
            out = dot(n, w_ref[:, i * wide : (i + 1) * wide]) + b_ref[0:1, i * wide : (i + 1) * wide]
            if i == 0:
                out = out.astype(bf16).astype(f32) * HEAD_DIM ** (-0.5)
            ref[...] = out.astype(bf16)

    @pl.when(need_ref[row] == 0)
    def _():
        for ref in (q_ref, k_ref, v_ref):
            ref[...] = jnp.zeros_like(ref)


def project(need, normed, weight, bias, wide):
    rows = normed.shape[0]
    return pl.pallas_call(
        project_kernel,
        out_shape=[jax.ShapeDtypeStruct((rows, wide), bf16)] * 3,
        grid_spec=pltpu.PrefetchScalarGridSpec(
            num_scalar_prefetch=1,
            grid=(rows // BLOCK,),
            in_specs=[
                pl.BlockSpec((BLOCK, D), lambda i, s: (i, 0)),
                pl.BlockSpec(weight.shape, lambda i, s: (0, 0)),
                pl.BlockSpec((1, 3 * wide), lambda i, s: (0, 0)),
            ],
            out_specs=[pl.BlockSpec((BLOCK, wide), lambda i, s: (i, 0))] * 3,
        ),
        compiler_params=pltpu.CompilerParams(vmem_limit_bytes=32 << 20),
        cost_estimate=SHORT,
        name="project",
    )(need, normed, weight, bias)


def norm_kernel(need_ref, info_ref, *refs):
    *sources, vec_ref, out_ref = refs
    row = pl.program_id(0)
    side = (row // info_ref[1]) % 2
    chip = row // (2 * info_ref[1])

    @pl.when(need_ref[row] > 0)
    def _():
        picked = jnp.where(chip == 0, sources[0][...], jnp.where(chip == 1, sources[2][...], sources[4][...]))
        theirs = jnp.where(chip == 0, sources[1][...], jnp.where(chip == 1, sources[3][...], sources[5][...]))
        picked = jnp.where(side == info_ref[0], picked, theirs)
        normal, _ = normalize(picked.astype(f32))
        out_ref[...] = (normal * vec_ref[0:1, :] + vec_ref[1:2, :]).astype(bf16)

    @pl.when(need_ref[row] == 0)
    def _():
        out_ref[...] = jnp.zeros_like(out_ref)


def norm_window(need, info, sources, vecs, window, count):
    per = count // BLOCK

    def spec(chip):
        def index(i, a, b):
            inside = jnp.clip(i - 2 * per * chip, 0, 2 * per - 1)
            return (inside % per, 0)

        return pl.BlockSpec((BLOCK, D), index)

    return pl.pallas_call(
        norm_kernel,
        out_shape=jax.ShapeDtypeStruct((window, D), bf16),
        grid_spec=pltpu.PrefetchScalarGridSpec(
            num_scalar_prefetch=2,
            grid=(window // BLOCK,),
            in_specs=[spec(i // 2) for i in range(6)] + [pl.BlockSpec(vecs.shape, lambda i, a, b: (0, 0))],
            out_specs=pl.BlockSpec((BLOCK, D), lambda i, a, b: (i, 0)),
        ),
        compiler_params=pltpu.CompilerParams(vmem_limit_bytes=24 << 20),
        cost_estimate=SHORT,
        name="norm_window",
    )(need, info, *sources, vecs)


def attend_kernel(lo_ref, hi_ref, first_ref, last_ref, q_ref, k_ref, v_ref, qt_ref, kt_ref, o_ref, lse_ref, s_ref, m_ref, acc_ref):
    i = pl.program_id(0)
    left = lax.broadcasted_iota(jnp.int32, (1, LANES), 1) < HEAD_DIM
    lo, hi = lo_ref[i], hi_ref[i]
    base = (first_ref.shape[0] - pl.num_programs(0)) // 2
    q = q_ref[...]
    zero = jnp.zeros_like(q)
    heads = (jnp.where(left, q, zero), jnp.where(left, zero, q))
    m_ref[...] = jnp.full_like(m_ref, MASKED)
    one_image = first_ref[base + i] == last_ref[base + i]
    folds = BLOCK // LANES

    def fold(value, combine):
        parts = [value[:, n * LANES : (n + 1) * LANES] for n in range(folds)]
        return functools.reduce(combine, parts)

    def scores(j, carry):
        at = pl.multiple_of(j * BLOCK, BLOCK)
        k = k_ref[pl.ds(at, BLOCK), :]
        inside = one_image & (first_ref[j] == first_ref[base + i]) & (last_ref[j] == first_ref[base + i])

        @pl.when(inside)
        def _():
            for h in range(2):
                s = dot_nt(heads[h], k)
                s_ref[h, j] = s
                m_ref[h] = jnp.maximum(m_ref[h], fold(s, jnp.maximum))

        @pl.when(jnp.logical_not(inside))
        def _():
            same = spread_lanes(qt_ref[...], BLOCK) == kt_ref[:, pl.ds(at, BLOCK)]
            for h in range(2):
                s = jnp.where(same, dot_nt(heads[h], k), MASKED)
                s_ref[h, j] = s
                m_ref[h] = jnp.maximum(m_ref[h], fold(s, jnp.maximum))

        return carry

    lax.fori_loop(lo, hi, scores, 0)
    tops = [jnp.max(m_ref[h], axis=1, keepdims=True) for h in range(2)]
    m_ref[...] = jnp.zeros_like(m_ref)
    acc_ref[...] = jnp.zeros_like(acc_ref)

    def mix(j, carry):
        at = pl.multiple_of(j * BLOCK, BLOCK)
        v = v_ref[pl.ds(at, BLOCK), :]
        for h in range(2):
            e = jnp.exp(s_ref[h, j] - tops[h])
            m_ref[h] += fold(e, jnp.add)
            acc_ref[h] += dot(e.astype(bf16), v)
        return carry

    lax.fori_loop(lo, hi, mix, 0)
    sums = [jnp.sum(m_ref[h], axis=1, keepdims=True) for h in range(2)]
    o_ref[...] = jnp.where(left, acc_ref[0] / sums[0], acc_ref[1] / sums[1]).astype(bf16)
    for h in range(2):
        lse = jnp.broadcast_to(tops[h] + jnp.log(sums[h]), (BLOCK, LANES))
        lse_ref[0, h : h + 1, :] = lse.T[0:1, :]


def attend(lo, hi, firsts, lasts, q, k, v, tag_cols, tag_row, own_rows, pair):
    window = q.shape[0]
    blocks = own_rows // BLOCK
    skip = (window - own_rows) // 2 // BLOCK
    return pl.pallas_call(
        attend_kernel,
        out_shape=[
            jax.ShapeDtypeStruct((own_rows, LANES), bf16),
            jax.ShapeDtypeStruct((1, 2, own_rows), f32),
        ],
        grid_spec=pltpu.PrefetchScalarGridSpec(
            num_scalar_prefetch=4,
            grid=(blocks,),
            in_specs=[
                pl.BlockSpec((BLOCK, LANES), lambda i, *_: (i + skip, pair)),
                pl.BlockSpec((window, LANES), lambda i, *_: (0, pair)),
                pl.BlockSpec((window, LANES), lambda i, *_: (0, pair)),
                pl.BlockSpec((BLOCK, LANES), lambda i, *_: (i + skip, 0)),
                pl.BlockSpec((1, window), lambda i, *_: (0, 0)),
            ],
            out_specs=[
                pl.BlockSpec((BLOCK, LANES), lambda i, *_: (i, 0)),
                pl.BlockSpec((1, 2, BLOCK), lambda i, *_: (0, 0, i)),
            ],
            scratch_shapes=[
                pltpu.VMEM((2, window // BLOCK, BLOCK, BLOCK), f32),
                pltpu.VMEM((2, BLOCK, LANES), f32),
                pltpu.VMEM((2, BLOCK, LANES), f32),
            ],
        ),
        compiler_params=pltpu.CompilerParams(vmem_limit_bytes=32 << 20),
        cost_estimate=SHORT,
        name="attend",
    )(lo, hi, firsts, lasts, q, k, v, tag_cols, tag_row)


def attend_back_kernel(
    start, stop, lo_ref, hi_ref, q_ref, k_ref, v_ref, g_ref, tc_ref, tr_ref, lse_ref, delta_ref,
    dq_ref, dk_ref, dv_ref, sum_ref, dk_acc, dv_acc, dq_acc,
):
    first = lax.broadcasted_iota(jnp.int32, (1, LANES), 1) < HEAD_DIM
    dk_acc[...] = jnp.zeros_like(dk_acc)
    dv_acc[...] = jnp.zeros_like(dv_acc)
    sum_ref[...] = jnp.zeros_like(sum_ref)

    def split(value):
        zero = jnp.zeros_like(value)
        return jnp.where(first, value, zero), jnp.where(first, zero, value)

    def visit(i, j, qs, gs, of_key, of_query):
        at_q, at_k = pl.multiple_of(i * BLOCK, BLOCK), pl.multiple_of(j * BLOCK, BLOCK)
        k = k_ref[pl.ds(at_k, BLOCK), :]
        v = v_ref[pl.ds(at_k, BLOCK), :]
        same = spread_lanes(tc_ref[pl.ds(at_k, BLOCK), :], BLOCK) == tr_ref[:, pl.ds(at_q, BLOCK)]
        ps, ds = [], []
        for h in range(2):
            s = dot_nt(k, qs[h])
            dp = dot_nt(v, gs[h])
            p = jnp.where(same, jnp.exp(s - lse_ref[0, h : h + 1, pl.ds(at_q, BLOCK)]), 0.0)
            d = p * (dp - delta_ref[0, h : h + 1, pl.ds(at_q, BLOCK)])
            ps.append(p.astype(bf16))
            ds.append(d.astype(bf16))
        if of_key:
            at = pl.multiple_of((j - start) * BLOCK, BLOCK)
            dv_acc[pl.ds(at, BLOCK), :] += dot(ps[0], gs[0]) + dot(ps[1], gs[1])
            dk_acc[pl.ds(at, BLOCK), :] += dot(ds[0], qs[0]) + dot(ds[1], qs[1])
        if of_query:
            ks = split(k)
            dq_acc[...] += dot_tn(ds[0], ks[0]) + dot_tn(ds[1], ks[1])

    def query_block(own_q, i, carry):
        at_q = pl.multiple_of(i * BLOCK, BLOCK)
        qs = split(q_ref[pl.ds(at_q, BLOCK), :])
        gs = split(g_ref[pl.ds(at_q, BLOCK), :])
        lo, hi = lo_ref[i], hi_ref[i]

        def keys(first_key, last_key, of_key):
            def body(j, carry):
                visit(i, j, qs, gs, of_key, own_q)
                return carry

            lax.fori_loop(first_key, last_key, body, 0)

        if own_q:
            dq_acc[...] = jnp.zeros_like(dq_acc)
            keys(lo, jnp.minimum(hi, start), False)
            keys(jnp.maximum(lo, stop), hi, False)
        keys(jnp.maximum(lo, start), jnp.minimum(hi, stop), True)
        if own_q:
            at = pl.multiple_of((i - start) * BLOCK, BLOCK)
            dq = dq_acc[...] * HEAD_DIM ** (-0.5)
            dq_ref[pl.ds(at, BLOCK), :] = dq.astype(bf16)
            sum_ref[0, 0:1, :] += jnp.sum(dq, axis=0, keepdims=True)
        return carry

    before = jnp.where(lo_ref[start] < start, lo_ref[start], start)
    after = jnp.maximum(hi_ref[stop - 1], stop)
    lax.fori_loop(before, start, functools.partial(query_block, False), 0)
    lax.fori_loop(start, stop, functools.partial(query_block, True), 0)
    lax.fori_loop(stop, after, functools.partial(query_block, False), 0)
    dk_ref[...] = dk_acc[...].astype(bf16)
    dv_ref[...] = dv_acc[...].astype(bf16)
    sum_ref[0, 1:2, :] = jnp.sum(dv_acc[...], axis=0, keepdims=True)


def attend_back(lo, hi, q, k, v, g, tag_cols, tag_row, lse, delta, own_rows, pair):
    window = q.shape[0]
    pairs, wide = 1, LANES
    grad_pair = pair % (g.shape[1] // LANES)
    start = (window - own_rows) // 2 // BLOCK
    stop = start + own_rows // BLOCK
    whole = lambda: pl.BlockSpec((window, LANES), lambda p, a, b: (0, pair))
    own = lambda: pl.BlockSpec((own_rows, LANES), lambda p, a, b: (0, p))
    stat = lambda: pl.BlockSpec((1, 2, window), lambda p, a, b: (pair, 0, 0))
    return pl.pallas_call(
        functools.partial(attend_back_kernel, start, stop),
        out_shape=[jax.ShapeDtypeStruct((own_rows, wide), bf16)] * 3
        + [jax.ShapeDtypeStruct((pairs, 8, LANES), f32)],
        grid_spec=pltpu.PrefetchScalarGridSpec(
            num_scalar_prefetch=2,
            grid=(pairs,),
            in_specs=[
                whole(), whole(), whole(),
                pl.BlockSpec((window, LANES), lambda p, a, b: (0, grad_pair)),
                pl.BlockSpec((window, LANES), lambda p, a, b: (0, 0)),
                pl.BlockSpec((1, window), lambda p, a, b: (0, 0)),
                stat(), stat(),
            ],
            out_specs=[own(), own(), own(), pl.BlockSpec((1, 8, LANES), lambda p, a, b: (p, 0, 0))],
            scratch_shapes=[
                pltpu.VMEM((own_rows, LANES), f32),
                pltpu.VMEM((own_rows, LANES), f32),
                pltpu.VMEM((BLOCK, LANES), f32),
            ],
        ),
        compiler_params=pltpu.CompilerParams(vmem_limit_bytes=40 << 20),
        cost_estimate=SHORT,
        name="attend_back",
    )(lo, hi, q, k, v, g, tag_cols, tag_row, lse, delta)


def on_device(
    tokens, image_ids, ln1_gain, ln1_bias, qkv_weight, query_bias, value_bias, proj_weight,
    proj_bias, scale_attn, ln2_gain, ln2_bias, fc1_weight, fc1_bias, fc2_weight, fc2_bias,
    scale_mlp, cotangent,
):
    devices = lax.axis_size("fsdp")
    depth, ranks = devices // 2, lax.axis_size("rep")
    place = lax.axis_index("fsdp")
    rank = lax.axis_index("rep")
    here, core = place // 2, place % 2
    count = tokens.shape[1]
    chip = 2 * count
    head_rows = D // devices
    ff = fc1_weight.shape[1]
    unit_rows = ff // devices
    half_heads = D // 2
    local_heads = half_heads // HEAD_DIM
    pairs = half_heads // LANES
    bits = list(range(rep_bits()))

    def in_order(own, other, axis=0):
        return jnp.where(
            core == 0,
            jnp.concatenate([own, other], axis=axis),
            jnp.concatenate([other, own], axis=axis),
        )

    def mine(value):
        return lax.dynamic_slice_in_dim(value, core * count, count, 0)

    def others(value):
        return lax.dynamic_slice_in_dim(value, (1 - core) * count, count, 0)

    def every_other(value, width, start):
        cuts = range(start * width, value.shape[1], 2 * width)
        return jnp.concatenate([value[:, c : c + width] for c in cuts], axis=1)

    def all_share(which):
        pick_cols = lambda v, w: jnp.where(which == 0, every_other(v, w, 0), every_other(v, w, 1))
        heads = lax.dynamic_slice_in_dim(
            jnp.concatenate(
                [
                    pick_cols(qkv_weight, head_rows),
                    lax.dynamic_slice_in_dim(proj_weight, which * half_heads, half_heads, 1),
                ],
                axis=1,
            ),
            rank * (2 * D // ranks), 2 * D // ranks, 1,
        )
        units = lax.dynamic_slice_in_dim(
            pick_cols(fc1_weight, unit_rows), rank * (ff // 2 // ranks), ff // 2 // ranks, 1
        )
        return jnp.concatenate([heads, units], axis=1)

    if head_rows % LANES:
        kept, given = all_share(core), all_share(1 - core)
    else:
        kept, given = weight_share(
            rank, core, qkv_weight, proj_weight, fc1_weight, ranks, head_rows, unit_rows
        )
    wide1 = 2 * D // ranks
    got = swap_cores(given)
    is_proj = rank * wide1 >= 3 * half_heads
    own1 = in_order(kept[:, :wide1], jnp.where(is_proj, given[:, :wide1], got[:, :wide1]))
    own2 = in_order(kept[:, wide1:], got[:, wide1:])
    own3 = lax.dynamic_slice_in_dim(fc2_weight, rank * (D // ranks), D // ranks, 1)
    small = (
        ln1_gain, ln1_bias, query_bias, value_bias, proj_bias, scale_attn, ln2_gain, ln2_bias,
        fc2_bias, scale_mlp, fc1_bias, (image_ids[0] + 1).astype(bf16),
    )
    sizes = [v.shape[0] for v in small]
    slots = slot_lists(sizes)
    width = 2 * D // ranks
    small = pack_small(small, width, slots)
    small_other = swap_cores(small)
    rows1, rows3 = own1.shape[0], own3.shape[0]
    tok, cot = tokens[0], cotangent[0]
    tok_other = swap_cores(tok)
    cot_other = swap_cores(cot)
    own1 = jnp.concatenate([own1, small, small_other])
    own1, own2, own3, tok = tie(own1, own2, own3, tok)
    pieces1 = fetch_z(own1)
    tok, pieces1[1] = tie(tok, pieces1[1])
    behind, ahead = from_chip(tok, 1), from_chip(tok, -1)
    gather1 = Gather(pieces1, rows1, "gather1")
    gather1.send()
    behind_other, ahead_other = swap_cores(behind), swap_cores(ahead)
    for _ in bits[1:]:
        gather1.send()

    vec_rows, fc1_shift, all_tags = unpack_small(
        pieces1, slots, rows1, here, core, ff // 2, devices * count
    )
    vector = lambda i: vec_rows[i : i + 1]
    (
        attn_gain, attn_shift, query_shift, value_shift, proj_shift, attn_scale, mlp_gain,
        mlp_shift, fc2_shift, mlp_scale,
    ) = map(vector, range(10))
    core_part = lambda vec: jnp.where(
        core == 0, every_other(vec, head_rows, 0), every_other(vec, head_rows, 1)
    )

    window = 3 * chip
    padded = jnp.concatenate(
        [jnp.zeros((1, chip), f32), all_tags, jnp.full((1, chip), 1e6, f32)], axis=1
    )
    tag_row = lax.dynamic_slice(padded, (0, here * chip), (1, window))
    tags = tag_row.reshape(window)
    firsts, lasts = tags[::BLOCK], tags[BLOCK - 1 :: BLOCK]
    real = firsts * (1e6 - firsts) > 0
    below = jnp.sum((tag_row < firsts[:, None]).astype(jnp.int32), axis=1)
    upto = jnp.sum((tag_row <= lasts[:, None]).astype(jnp.int32), axis=1)
    blocks = window // BLOCK
    block_lo = jnp.where(real, below // BLOCK, 0)
    block_hi = jnp.where(real, (upto + BLOCK - 1) // BLOCK, 0)
    own_lo, own_hi = chip // BLOCK, 2 * chip // BLOCK
    numbers = jnp.arange(blocks)
    need = jnp.logical_and(numbers >= block_lo[own_lo], numbers < block_hi[own_hi - 1]).astype(jnp.int32)
    firsts, lasts = firsts.astype(jnp.int32), lasts.astype(jnp.int32)
    tag_cols = jnp.broadcast_to(tags[:, None], (window, LANES))

    info = jnp.stack([core, jnp.int32(count // BLOCK)]).astype(jnp.int32)
    normed1 = norm_window(
        need, info, (behind, behind_other, tok, tok_other, ahead, ahead_other), vec_rows, window, count
    )

    normed1, own2 = tie(normed1, own2)
    pieces2 = fetch_z(own2)
    normed1 = gather1.arrive(normed1)
    qkv_matrix, proj_matrix = gather1.assemble(here, rank, head_rows)

    shifts = jnp.concatenate(
        [core_part(query_shift), jnp.zeros((1, half_heads), f32), core_part(value_shift)], axis=1
    )
    queries, keys, values = project(need, normed1, qkv_matrix, shifts, half_heads)

    contexts, lses = [], []
    los = block_lo[own_lo:own_hi]
    los, queries = tie(los, queries)
    for pair in range(pairs):
        if pair == 1:
            los, own3, *pieces2 = tie(los, own3, *pieces2)
            gather2 = Gather(pieces2, rows1, "gather2")
            los = gather2.send(los)
            pieces3 = fetch_z(own3)
        if pair == 2:
            los = gather2.arrive(los)
            los = gather2.send(los)
        if pair == 3:
            los = gather2.arrive(los)
            for _ in bits[2:]:
                los = gather2.arrive(gather2.send(los))
            los, *pieces3 = tie(los, *pieces3)
            gather3 = Gather(pieces3, rows3, "gather3")
            los = gather3.send(los)
        context, lse = attend(
            los, block_hi[own_lo:own_hi], firsts, lasts, queries, keys, values, tag_cols,
            tag_row, chip, pair,
        )
        los, context = tie(los, context)
        contexts.append(context)
        lses.append(lse)
    context = jnp.concatenate(contexts, axis=1)
    lse_rows = jnp.concatenate(lses).reshape(local_heads, chip)
    context = gather3.arrive(context)
    context = gather3.send(context)
    own, given = product(context, proj_matrix, False, core, "attn_out")
    attn_out, resid, mlp_input = residual(own, swap_cores(given), tok, vec_rows)
    mlp_input = jnp.concatenate([mlp_input, swap_cores(mlp_input)])
    fc1_matrix = gather2.assemble(here, rank)
    activated, slope = hidden_units(mlp_input, fc1_matrix, fc1_shift)
    mlp_grad = scaled(cot, cot_other, vec_rows)
    both = [bits, bits[::-1]]
    activated = gather3.arrive(activated)
    for _ in bits[2:]:
        activated = gather3.arrive(gather3.send(activated))
    reduce3 = Reduce(grad_blocks(activated, mlp_grad, rank, both, "fc2_grad"), here, both)
    mlp_grad = reduce3.send(mlp_grad)
    fc2_matrix = gather3.assemble(here, rank)
    pre_grad, fc1_bias_part = pre_grads(mlp_grad, fc2_matrix, slope)
    reduce2 = Reduce(grad_blocks(mlp_input, pre_grad, rank, both, "fc1_grad"), here, both)
    pre_grad, _ = tie(pre_grad, [give for _, _, give in reduce2.held])
    own, given = product(pre_grad, fc1_matrix, True, 0, "mlp_in_grad")
    own, given = reduce3.arrive(own, given)
    for _ in bits[2:]:
        own, given = reduce3.arrive(*reduce3.send(own, given))
    own, given = reduce3.send(own, given)
    sent = swap_cores(given)
    resid_grad, attn_grad, norm_sums = norm_grads(own, sent, resid, cot, attn_out, vec_rows)
    both_grads = jnp.zeros((chip, D), bf16)
    for part, which in ((attn_grad, core), (swap_cores(attn_grad), 1 - core)):
        both_grads = lax.dynamic_update_slice_in_dim(both_grads, part, which * count, 0)
    attn_grad = both_grads
    context_grad = dot_nt(attn_grad, proj_matrix).astype(bf16)
    head_of = (
        lax.broadcasted_iota(jnp.int32, (local_heads, half_heads), 1) // HEAD_DIM
        == lax.broadcasted_iota(jnp.int32, (local_heads, half_heads), 0)
    ).astype(f32)
    row_delta = lax.dot_general(
        head_of, context_grad.astype(f32) * context.astype(f32), (((1,), (1,)), ((), ())),
        precision=lax.Precision.HIGHEST, preferred_element_type=f32,
    )
    stats = jnp.concatenate([lse_rows, row_delta])
    context_grad, activated, attn_grad = tie(context_grad, activated, attn_grad)
    chunk = half_heads // 2
    chunks = [context_grad[:, :chunk], context_grad[:, chunk:]]
    grads_behind, grads_ahead = zip(*[(from_chip(c, 1), from_chip(c, -1)) for c in chunks])
    stats_behind, stats_ahead = from_chip(stats, 1), from_chip(stats, -1)
    proj_grad = packed_proj_grad(context, attn_grad, head_rows)
    stat_window = jnp.concatenate([stats_behind, stats, stats_ahead], axis=1)
    by_pair = lambda s: s.reshape(pairs, 2, window)
    lse_window, delta_window = by_pair(stat_window[:local_heads]), by_pair(stat_window[local_heads:])

    half_pairs = pairs // 2
    half_width = half_heads // 2

    def first_group(parts, number):
        grads = [g for kind in zip(*parts) for g in kind]
        return Reduce(
            qkv_grad_blocks(normed1, grads, proj_grad, number, 2, rank, both), here, both
        )

    parts, sums = [], []
    out_own, out_given = product(activated, fc2_matrix, False, 0, "mlp_out")
    first, delta_window, lo, out_own, out_given = settle(
        ((grads_behind[0], grads_ahead[0]), delta_window, block_lo, out_own, out_given),
        (reduce3, "received"),
    )
    grad_windows = [jnp.concatenate([first[0], chunks[0], first[1]])]
    for pair in range(pairs):
        if pair == 0:
            lo = reduce3.arrive(lo)
            lo = reduce2.send(lo)
        if pair == 1:
            lo, second = settle((lo, (grads_behind[1], grads_ahead[1])), (reduce2, "received"))
            grad_windows.append(jnp.concatenate([second[0], chunks[1], second[1]]))
            lo = reduce2.arrive(lo)
            lo = reduce3.send_z(lo)
            for _ in bits[2:]:
                lo = reduce2.arrive(reduce2.send(lo))
            lo = reduce2.send(lo)
        if pair == 2:
            lo = settle(lo, (reduce2, "received"), (reduce3, "pieces"))
            lo = reduce2.arrive(lo)
            lo = reduce2.send_z(lo)
            reduce1a = first_group(parts, 0)
            lo = reduce1a.send(lo)
        if pair == 3:
            lo = settle(lo, (reduce2, "pieces"), (reduce1a, "received"))
            lo = reduce3.arrive_z(lo)
            lo = reduce2.arrive_z(lo)
            fc2_part = reduce3.total.astype(bf16)
            fc1_part = reduce2.total.astype(bf16)
            split = fc2_part.shape[0] // fc1_part.shape[0]
            mlp_spread = Spread(jnp.concatenate([fc1_part, *jnp.split(fc2_part, split)], axis=1))
            lo = mlp_spread.send(lo)
            lo = reduce1a.arrive(lo)
            for _ in bits[2:]:
                lo = reduce1a.arrive(reduce1a.send(lo))
            lo = reduce1a.send(lo)
        *grads, total = attend_back(
            lo, block_hi, queries, keys, values, grad_windows[pair * 2 // pairs], tag_cols, tag_row, lse_window,
            delta_window, chip, pair,
        )
        lo, *grads = tie(lo, *grads)
        parts.append(grads)
        sums.append(total[0])

    parts[-1] = settle(parts[-1], (mlp_spread, "arrays"))
    parts[-1] = reduce1a.arrive(parts[-1])
    parts[-1] = reduce1a.send_z(parts[-1])
    reduce1b = first_group(parts[half_pairs:], 1)
    parts[-1] = reduce1b.send(parts[-1])
    every = [jnp.concatenate(p, axis=1) for p in zip(*parts)]

    factor = 1.0 / math.sqrt(count * devices * ranks)
    in_own, in_given = product(
        jnp.concatenate(every, axis=1), qkv_matrix, True, core, "attn_in_grad"
    )
    tail = (in_own, in_given)
    tail = settle(tail, (reduce1b, "received"), (reduce1a, "pieces"))
    for _ in bits[1:]:
        tail = reduce1b.arrive(tail)
        tail = reduce1b.send(tail)
    in_own, in_given = tail
    input_rows, output_rows, end_sums = finish(
        in_own, swap_cores(in_given), tok, resid_grad, out_own, swap_cores(out_given), resid, cot, vec_rows
    )

    vectors = (
        end_sums[0:1], end_sums[1:2],
        jnp.concatenate([s[0:1] for s in sums], axis=1), jnp.concatenate([s[1:2] for s in sums], axis=1),
        norm_sums[2:3], norm_sums[3:4], norm_sums[0:1], norm_sums[1:2],
        end_sums[2:3], end_sums[3:4], fc1_bias_part,
    )
    of_core = [number in (2, 3, 10) for number in range(11)]
    partial = pack_grads(vectors, list(zip(sizes, of_core)), core, depth)
    vec_width = D // ranks
    half_of = lambda which: lax.dynamic_slice_in_dim(partial, which * 16, 16, 1)
    partial = half_of(core) + swap_cores(half_of(1 - core))
    vec_high = lax.reduce_precision(partial, 8, 7)
    side_by_side = 2 if vec_width >= 2 * LANES else 1
    extra = jnp.concatenate([vec_high, partial - vec_high], axis=side_by_side).astype(bf16)
    extra = jnp.pad(extra, ((0, 0), (0, 0), (0, vec_width - extra.shape[2])))
    extra = reduce1b.arrive(extra)
    extra = reduce1b.send_z(extra, extra=extra)
    for _ in bits[1:]:
        mlp_spread.send(extra)

    reduce1a.arrive_z()
    reduce1b.arrive_z()
    rows = reduce1a.total.shape[0]
    vec_total = reduce1b.total[rows:]
    if side_by_side == 2:
        vec_total = vec_total[:, :LANES] + vec_total[:, LANES : 2 * LANES]
    else:
        vec_total = vec_total[:16] + vec_total[16:]
    vec_high = lax.reduce_precision(vec_total, 8, 7)
    sides = [jnp.pad(v, ((0, 16), (0, vec_width - LANES))) for v in (vec_high, vec_total - vec_high)]
    payload = jnp.concatenate(
        [
            jnp.concatenate([reduce1a.total, reduce1b.total[:rows]], axis=1),
            jnp.concatenate(sides, axis=1),
        ]
    ).astype(bf16)
    payload = settle(payload, (mlp_spread, "arrays"))
    first_spread = Spread(payload)
    for bit in bits:
        first_spread.send()

    mlp_cols = fc1_part.shape[1]
    fc1_full = mlp_spread.blocks(rank, 0, mlp_cols)
    fc2_width = fc2_part.shape[1]
    fc2_full = tie(*[mlp_spread.blocks(rank, mlp_cols + n * fc2_width, fc2_width) for n in range(split)])
    grad_fc2 = jnp.concatenate(fc2_full).astype(f32) * factor
    first_a = first_spread.blocks(rank, 0, vec_width)
    first_b = first_spread.blocks(rank, vec_width, vec_width)
    totals = sum(
        part[rows : rows + 16, r * vec_width : r * vec_width + LANES].astype(f32)
        for part in (first_a, first_b)
        for r in range(ranks)
    ) * factor
    first_a, first_b = first_a[:rows], first_b[:rows]

    def rows_of(value, index):
        return lax.dynamic_slice_in_dim(value, index * head_rows, head_rows, 0)

    def interleave(own, other, width):
        cuts = range(0, own.shape[1], width)
        zipped = lambda a, b: jnp.concatenate(
            [v[:, c : c + width] for c in cuts for v in (a, b)], axis=1
        )
        return jnp.where(core == 0, zipped(own, other), zipped(other, own)).astype(f32) * factor

    fc1_other = swap_cores(rows_of(fc1_full, 1 - core))
    grad_fc1 = interleave(rows_of(fc1_full, core), fc1_other, unit_rows)
    qkv_full = jnp.concatenate(
        [
            part[:, n * half_width : (n + 1) * half_width]
            for n in range(3)
            for part in (first_a, first_b)
        ],
        axis=1,
    )
    grad_qkv = interleave(rows_of(qkv_full, core), swap_cores(rows_of(qkv_full, 1 - core)), head_rows)
    proj_part = jnp.concatenate([first_a[:, 3 * half_width :], first_b[:, 3 * half_width :]], axis=1)
    grad_proj = jnp.concatenate([proj_part[:head_rows], proj_part[head_rows:]], axis=1).astype(f32) * factor

    small_grads = [totals[i, : sizes[i]] for i in range(10)]
    lines = -(-sizes[10] // LANES)
    small_grads.append(totals[10 : 10 + lines].reshape(-1))
    (
        grad_attn_gain, grad_attn_shift, grad_query_shift, grad_value_shift, grad_proj_shift,
        grad_attn_scale, grad_mlp_gain, grad_mlp_shift, grad_fc2_shift, grad_mlp_scale, grad_fc1_shift,
    ) = small_grads

    return (
        output_rows[None],
        input_rows[None],
        grad_attn_gain,
        grad_attn_shift,
        grad_qkv,
        grad_query_shift,
        grad_value_shift,
        grad_proj,
        grad_proj_shift,
        grad_attn_scale,
        grad_mlp_gain,
        grad_mlp_shift,
        grad_fc1,
        grad_fc1_shift,
        grad_fc2,
        grad_fc2_shift,
        grad_mlp_scale,
    )


def solution(mesh):
    rows = P("fsdp", None)
    vec = P("fsdp")
    tok = P("rep", "fsdp", None)
    return jax.shard_map(
        on_device,
        mesh=mesh,
        in_specs=(
            tok, P("rep", "fsdp"), vec, vec, rows, vec, vec, rows, vec, vec, vec, vec, rows, vec,
            rows, vec, vec, tok,
        ),
        out_specs=(
            tok, tok, vec, vec, rows, vec, vec, rows, vec, vec, vec, vec, rows, vec, rows, vec, vec,
        ),
        check_vma=False,
    )
```

```python
import functools
import math

import jax
import jax.numpy as jnp
from jax import lax
from jax.experimental import pallas as pl
from jax.experimental.pallas import tpu as pltpu
from jax.sharding import PartitionSpec as P

D = 1024
HEADS = 16
HEAD_DIM = 64
LANES = 128

EPSILON = 1e-06
MASKED = -1e30
BLOCK = 256

SHORT = pl.CostEstimate(flops=1, transcendentals=0, bytes_accessed=1)
FILLER = pl.CostEstimate(flops=1 << 33, transcendentals=0, bytes_accessed=1 << 23)

f32 = jnp.float32
bf16 = jnp.bfloat16


def normalize(features):
    row_mean = jnp.mean(features, axis=-1, keepdims=True)
    centred = features - row_mean
    variance = jnp.mean(centred * centred, axis=-1, keepdims=True)
    inverse = lax.rsqrt(variance + EPSILON)
    return centred * inverse, inverse


def norm_back(gradient, normal, inverse, gain_vec):
    scaled = gradient * gain_vec
    mean_first = jnp.mean(scaled, axis=-1, keepdims=True)
    mean_second = jnp.mean(scaled * normal, axis=-1, keepdims=True)
    return inverse * (scaled - mean_first - normal * mean_second)


def gelu_pair(values):
    cumulative = 0.5 * (1.0 + lax.erf(values * 2.0 ** (-0.5)))
    density = jnp.exp(-0.5 * values * values) * (2.0 * math.pi) ** (-0.5)
    return (values * cumulative, cumulative + values * density)


def dot(a, b):
    return jnp.dot(a, b, preferred_element_type=f32)


def dot_nt(a, b):
    return lax.dot_general(a, b, (((1,), (1,)), ((), ())), preferred_element_type=f32)


def dot_tn(a, b):
    return lax.dot_general(a, b, (((0,), (0,)), ((), ())), preferred_element_type=f32)


def swap_cores(value):
    size = lax.axis_size("fsdp")
    return lax.ppermute(value, "fsdp", [(i, i ^ 1) for i in range(size)])


def along_z(value, by):
    size = lax.axis_size("fsdp")
    return lax.ppermute(value, "fsdp", [(i, (i + 2 * by) % size) for i in range(size)])


def from_chip(value, by):
    size = lax.axis_size("fsdp")
    pairs = [(i, i + 2 * by) for i in range(size) if 0 <= i + 2 * by < size]
    return lax.ppermute(value, "fsdp", pairs)


def across_rep(value, bit):
    size = lax.axis_size("rep")
    return lax.ppermute(value, "rep", [(i, i ^ (1 << bit)) for i in range(size)])


def pick(value, index, axis):
    return lax.dynamic_index_in_dim(value, index, axis, keepdims=False)


def rep_bits():
    return lax.axis_size("rep").bit_length() - 1


def tie(*values):
    return lax.optimization_barrier(values)


def settle(value, *fields):
    held = [getattr(o, name) for o, name in fields]
    value, held = lax.optimization_barrier((value, held))
    for (o, name), new in zip(fields, held):
        setattr(o, name, new)
    return value


def fetch_z(own):
    return [own] + [along_z(own, k) for k in range(1, lax.axis_size("fsdp") // 2)]


class Gather:
    def __init__(self, pieces, rows, name):
        self.rows, self.cols, self.name = rows, pieces[0].shape[1], name
        half = rows // 2
        bits = list(range(rep_bits()))
        self.orders = [bits, bits[::-1]]
        self.parts = [
            [(jnp.stack([p[:half] for p in pieces])[None], [0])],
            [(jnp.stack([p[half:rows] for p in pieces])[None], [0])],
        ]
        self.at = 0

    def send(self, *values):
        whole = [
            (ps[0][0] if len(ps) == 1 else jnp.concatenate([a for a, _ in ps]), [o for _, os in ps for o in os])
            for ps in self.parts
        ]
        values, arrays = lax.optimization_barrier((values, [a for a, _ in whole]))
        self.parts = []
        for array, (_, offsets), order in zip(arrays, whole, self.orders):
            flip = 1 << order[self.at]
            received = across_rep(array, order[self.at])
            self.parts.append([(array, offsets), (received, [o ^ flip for o in offsets])])
        self.at += 1
        return values[0] if len(values) == 1 else values

    def arrive(self, value):
        value, arrays = lax.optimization_barrier((value, [a for ps in self.parts for a, _ in ps]))
        self.parts = [[(arrays.pop(0), o) for _, o in ps] for ps in self.parts]
        return value

    def assemble(self, here, rank, tail_rows=0):
        depth, ranks = lax.axis_size("fsdp") // 2, lax.axis_size("rep")
        sources, plan = [], []
        for number, parts in enumerate(self.parts):
            for array, offsets in parts:
                sources.append(array)
                plan.append((number, offsets))
        dtype = sources[0].dtype
        shape = (depth * self.rows, ranks * self.cols)
        shapes = [jax.ShapeDtypeStruct(shape, dtype)]
        if tail_rows:
            tail = shape[1] // 4
            shapes = [
                jax.ShapeDtypeStruct((shape[0], shape[1] - tail), dtype),
                jax.ShapeDtypeStruct((depth * tail_rows, 2 * tail), dtype),
            ]
        out = pl.pallas_call(
            functools.partial(assemble_kernel, plan, depth, self.rows, self.cols, tail_rows),
            out_shape=shapes,
            grid_spec=pltpu.PrefetchScalarGridSpec(
                num_scalar_prefetch=1,
                grid=(1,),
                in_specs=[pl.BlockSpec(memory_space=pl.ANY)] * len(sources),
                out_specs=[pl.BlockSpec(memory_space=pl.ANY)] * len(shapes),
                scratch_shapes=[
                    pltpu.VMEM(shape, dtype),
                    pltpu.SemaphoreType.DMA((2 * ranks * depth,)),
                    pltpu.SemaphoreType.DMA((3 * depth,)),
                ],
            ),
            compiler_params=pltpu.CompilerParams(vmem_limit_bytes=16 << 20),
            cost_estimate=SHORT,
            name=self.name,
        )(jnp.stack([here, rank]).astype(jnp.int32), *sources)
        return out if tail_rows else out[0]


def assemble_kernel(plan, depth, rows, cols, tail_rows, index_ref, *refs):
    count = len(plan)
    sources = refs[:count]
    targets = refs[count : count + (2 if tail_rows else 1)]
    held, in_sems, out_sems = refs[-3:]
    here, rank = index_ref[0], index_ref[1]
    half = rows // 2
    waits = [[] for _ in range(depth)]
    number = 0
    for k in range(depth):
        place = lax.rem(here - k + depth, depth)
        for which, (colour, offsets) in enumerate(plan):
            for m, offset in enumerate(offsets):
                at_row = pl.multiple_of(place * rows + colour * half, half)
                at_col = pl.multiple_of((rank ^ offset) * cols, cols)
                copy = pltpu.make_async_copy(
                    sources[which].at[m, k],
                    held.at[pl.ds(at_row, half), pl.ds(at_col, cols)],
                    in_sems.at[number],
                )
                copy.start()
                waits[k].append(copy)
                number += 1
    outs = []
    main = targets[0].shape[1]
    for k in range(depth):
        place = lax.rem(here - k + depth, depth)
        for copy in waits[k]:
            copy.wait()
        base = pl.multiple_of(place * rows, rows)
        band = pl.ds(base, rows)
        out = pltpu.make_async_copy(held.at[band, pl.ds(0, main)], targets[0].at[band], out_sems.at[3 * k])
        out.start()
        outs.append(out)
        if tail_rows:
            wide = targets[1].shape[1] // 2
            for side in range(2):
                out = pltpu.make_async_copy(
                    held.at[pl.ds(base + side * tail_rows, tail_rows), pl.ds(main, wide)],
                    targets[1].at[
                        pl.ds(pl.multiple_of(place * tail_rows, tail_rows), tail_rows),
                        pl.ds(side * wide, wide),
                    ],
                    out_sems.at[3 * k + 1 + side],
                )
                out.start()
                outs.append(out)
    for out in outs:
        out.wait()


def halves(ranks, bit, held):
    flip = 1 << bit
    kept = [o for o in held if not o & flip]
    return kept, [o ^ flip for o in kept]


def relative_blocks(grads, rank, orders):
    depth, ranks = lax.axis_size("fsdp") // 2, lax.axis_size("rep")
    width = grads.shape[1] // ranks
    rows = grads.shape[0] // depth
    shaped = grads.reshape(depth, rows, grads.shape[1])
    share = rows // len(orders)
    first = []
    for n, order in enumerate(orders):
        block = lambda o: lax.dynamic_slice(
            shaped, (0, n * share, (rank ^ o) * width), (depth, share, width)
        )
        kept, given = halves(ranks, order[0], list(range(ranks)))
        first.append((jnp.stack([block(o) for o in kept]), jnp.stack([block(o) for o in given])))
    return first


class Reduce:
    def __init__(self, first, here, orders):
        self.here, self.orders, self.at = here, orders, 0
        ranks = lax.axis_size("rep")
        self.held = []
        for (keep, give), order in zip(first, orders):
            kept, given = halves(ranks, order[0], list(range(ranks)))
            self.held.append((kept, keep, give))

    def send(self, *values):
        values, gives = lax.optimization_barrier((values, [give for _, _, give in self.held]))
        self.received = [across_rep(g, order[self.at]) for g, order in zip(gives, self.orders)]
        self.at += 1
        return values[0] if len(values) == 1 else values

    def arrive(self, *values):
        values, received = lax.optimization_barrier((values, self.received))
        held = []
        for (kept, keep, _), got, order in zip(self.held, received, self.orders):
            total = (keep.astype(f32) + got.astype(f32)).astype(bf16)
            if self.at < len(order):
                stay, leave = halves(None, order[self.at], kept)
                take = lambda os: jnp.stack([total[kept.index(o)] for o in os])
                held.append((stay, take(stay), take(leave)))
            else:
                held.append((kept, total[0], None))
        self.held = held
        return values[0] if len(values) == 1 else values

    def send_z(self, *values, extra=None):
        depth = lax.axis_size("fsdp") // 2
        parts = [keep for _, keep, _ in self.held]
        whole = parts[0] if len(parts) == 1 else jnp.concatenate(parts, axis=1)
        if extra is not None:
            whole = jnp.concatenate([whole, extra], axis=1)
        pieces = [pick(whole, lax.rem(self.here + k, depth), 0) for k in range(depth)]
        values, pieces = lax.optimization_barrier((values, pieces))
        self.pieces = [pieces[0]] + [along_z(p, k) for k, p in enumerate(pieces) if k]
        return values[0] if len(values) == 1 else values

    def arrive_z(self, *values):
        values, pieces = lax.optimization_barrier((values, self.pieces))
        total = pieces[0].astype(f32)
        for piece in pieces[1:]:
            total = total + piece.astype(f32)
        self.total = total
        return values[0] if len(values) == 1 else values


class Spread:
    def __init__(self, value):
        bits = list(range(rep_bits()))
        self.orders = [bits, bits[::-1]]
        half = value.shape[0] // 2
        self.arrays = [value[:half][None], value[half:][None]]
        self.offsets = [[0], [0]]
        self.at = 0

    def send(self, *values):
        values, arrays = lax.optimization_barrier((values, self.arrays))
        self.arrays = []
        for n, (array, order) in enumerate(zip(arrays, self.orders)):
            flip = 1 << order[self.at]
            received = across_rep(array, order[self.at])
            self.arrays.append(jnp.concatenate([array, received]))
            self.offsets[n] = self.offsets[n] + [o ^ flip for o in self.offsets[n]]
        self.at += 1
        return values[0] if len(values) == 1 else values

    def blocks(self, rank, start, size):
        return jnp.concatenate(
            [rep_blocks(a[:, :, start : start + size], o, rank) for a, o in zip(self.arrays, self.offsets)]
        )


def rep_blocks(stacked, offsets, rank):
    blocks = []
    for i in range(len(offsets)):
        block = stacked[0]
        for entry, offset in enumerate(offsets):
            block = jnp.where((rank ^ offset) == i, stacked[entry], block)
        blocks.append(block)
    return jnp.concatenate(blocks, axis=1)


def share_kernel(widths, index_ref, qkv_ref, proj_ref, fc1_ref, keep_ref, give_ref, sems):
    rank, core = index_ref[0], index_ref[1]
    wide1, wide2, block, unit, half = widths
    is_proj = rank * wide1 >= 3 * half

    def copies(second):
        made = []
        for out, (ref, which) in enumerate(((keep_ref, core), (give_ref, 1 - core))):
            for c in range(wide1 // block):
                col = rank * wide1 + c * block
                if second:
                    source, at = proj_ref, which * half + col - 3 * half
                else:
                    source, at = qkv_ref, 2 * col + which * block
                made.append((source, at, block, ref, c * block))
        return made

    def run(plan, first):
        started = []
        for n, (source, at, size, ref, to) in enumerate(plan):
            copy = pltpu.make_async_copy(
                source.at[:, pl.ds(pl.multiple_of(at, LANES), size)], ref.at[:, pl.ds(to, size)], sems.at[first + n]
            )
            copy.start()
            started.append(copy)
        return started

    col = rank * wide2
    plan2 = []
    for ref, which in ((keep_ref, core), (give_ref, 1 - core)):
        at = col + (lax.div(col, unit) + which) * unit
        plan2.append((fc1_ref, at, wide2, ref, wide1))
    second = run(plan2, 0)

    @pl.when(is_proj)
    def _():
        for copy in run(copies(True), 2):
            copy.wait()

    @pl.when(jnp.logical_not(is_proj))
    def _():
        for copy in run(copies(False), 2):
            copy.wait()

    for copy in second:
        copy.wait()


def weight_share(rank, core, qkv_weight, proj_weight, fc1_weight, ranks, block, unit):
    rows = qkv_weight.shape[0]
    wide1, wide2 = 2 * D // ranks, fc1_weight.shape[1] // 2 // ranks
    out = jax.ShapeDtypeStruct((rows, wide1 + wide2), bf16)
    return pl.pallas_call(
        functools.partial(share_kernel, (wide1, wide2, block, unit, D // 2)),
        out_shape=[out, out],
        grid_spec=pltpu.PrefetchScalarGridSpec(
            num_scalar_prefetch=1,
            grid=(1,),
            in_specs=[pl.BlockSpec(memory_space=pl.ANY)] * 3,
            out_specs=[pl.BlockSpec(out.shape, lambda i, a: (0, 0))] * 2,
            scratch_shapes=[pltpu.SemaphoreType.DMA((2 + 2 * (wide1 // block),))],
        ),
        cost_estimate=SHORT,
        name="weight_share",
    )(jnp.stack([rank, core]).astype(jnp.int32), qkv_weight, proj_weight, fc1_weight)


def whole_specs(arrays):
    return [pl.BlockSpec(a.shape, lambda *_, n=len(a.shape): (0,) * n) for a in arrays]


def slot_lists(sizes):
    slots = []
    for number, size in enumerate(sizes):
        for start in range(0, size, LANES):
            slots.append((number, start, min(LANES, size - start)))
    return slots


def pack_kernel(slots, *refs):
    *sources, out_ref, held = refs
    per_row = held.shape[1] // LANES
    held[...] = jnp.zeros_like(held)
    for slot, (number, start, size) in enumerate(slots):
        row, at = slot // per_row, slot % per_row * LANES
        held[row : row + 1, at : at + size] = sources[number][:, start : start + size].astype(f32)
    out_ref[...] = held[...].astype(out_ref.dtype)


def pack_small(vectors, width, slots):
    shape = (32 * LANES // width, width)
    vectors = [v.reshape(1, -1) for v in vectors]
    return pl.pallas_call(
        functools.partial(pack_kernel, slots),
        out_shape=jax.ShapeDtypeStruct(shape, bf16),
        scratch_shapes=[pltpu.VMEM(shape, f32)],
        name="pack_small",
    )(*vectors)


def unpack_kernel(slots, depth, index_ref, *refs):
    pieces, (vec_ref, unit_ref, tag_ref) = refs[:depth], refs[depth:]
    here, core = index_ref[0], index_ref[1]
    rows, width = pieces[0].shape
    per_row = width // LANES
    single = sum(1 for number, _, _ in slots if number < 10)
    vec_ref[...] = jnp.zeros_like(vec_ref)
    for k in range(depth):
        place = lax.rem(here - k + depth, depth)
        values = pieces[k][...].astype(f32)

        def part(side, slot, size):
            row, at = side * (rows // 2) + slot // per_row, slot % per_row * LANES
            return values[row : row + 1, at : at + size]

        for slot, (number, start, size) in enumerate(slots):
            own, other = part(0, slot, size), part(1, slot, size)
            first = jnp.where(core == 0, own, other)
            second = jnp.where(core == 0, other, own)
            if number < 10:
                at = pl.multiple_of(place * 2 * size, 2 * size)
                vec_ref[number : number + 1, pl.ds(at, 2 * size)] = jnp.concatenate([first, second], axis=1)
            elif number == 10:
                wide = unit_ref.shape[1] // depth
                unit_ref[0:1, pl.ds(pl.multiple_of(place * wide + start, LANES), LANES)] = own
            else:
                wide = tag_ref.shape[1] // depth
                at = pl.multiple_of(place * wide + start, LANES)
                tag_ref[0:1, pl.ds(at, LANES)] = first
                tag_ref[0:1, pl.ds(pl.multiple_of(at + wide // 2, LANES), LANES)] = second


def unpack_small(pieces, slots, rows, here, core, units, group_tokens):
    depth = len(pieces)
    extra, width = pieces[0].shape[0] - rows, pieces[0].shape[1]
    shapes = [(16, D), (1, units), (1, group_tokens)]
    return pl.pallas_call(
        functools.partial(unpack_kernel, slots, depth),
        out_shape=[jax.ShapeDtypeStruct(s, f32) for s in shapes],
        grid_spec=pltpu.PrefetchScalarGridSpec(
            num_scalar_prefetch=1,
            grid=(1,),
            in_specs=[pl.BlockSpec((extra, width), lambda i, a: (rows // extra, 0))] * depth,
            out_specs=[pl.BlockSpec(s, lambda i, a: (0, 0)) for s in shapes],
        ),
        name="unpack_small",
    )(jnp.stack([here, core]).astype(jnp.int32), *pieces)


def pack_grads_kernel(depth, sizes, index_ref, *refs):
    *sources, out_ref = refs
    core = index_ref[0]
    out_ref[...] = jnp.zeros_like(out_ref)
    for z in range(depth):
        for c in range(2):
            row = 16 * c
            for source, (size, of_core) in zip(sources, sizes):
                for start in range(0, size, LANES):
                    lanes = min(LANES, size - start)
                    at = (z if of_core else 2 * z + c) * size + start
                    value = source[0:1, at : at + lanes]
                    if of_core:
                        value = jnp.where(core == c, value, 0.0)
                    out_ref[z, row : row + 1, 0:lanes] = value
                    row += 1


def pack_grads(vectors, sizes, core, depth):
    return pl.pallas_call(
        functools.partial(pack_grads_kernel, depth, sizes),
        out_shape=jax.ShapeDtypeStruct((depth, 32, LANES), f32),
        grid_spec=pltpu.PrefetchScalarGridSpec(
            num_scalar_prefetch=1,
            grid=(1,),
            in_specs=whole_specs(vectors),
            out_specs=pl.BlockSpec((depth, 32, LANES), lambda i, a: (0, 0, 0)),
        ),
        name="pack_grads",
    )(core.reshape(1).astype(jnp.int32), *vectors)


def grad_blocks_kernel(orders, ranks, index_ref, a_ref, b_ref, *refs):
    outs, held = refs[:-1], refs[-1]
    rank = index_ref[0]
    held[...] = dot_tn(a_ref[...], b_ref[...]).astype(bf16)
    width = held.shape[1] // ranks
    share = held.shape[0] // len(orders)
    for n, order in enumerate(orders):
        for which, offsets in enumerate(halves(ranks, order[0], list(range(ranks)))):
            for i, o in enumerate(offsets):
                cols = pl.ds(pl.multiple_of((rank ^ o) * width, width), width)
                outs[2 * n + which][i, 0] = held[n * share : (n + 1) * share, cols]


def grad_blocks(a, b, rank, orders, name):
    depth, ranks = lax.axis_size("fsdp") // 2, lax.axis_size("rep")
    tokens, rows, cols = a.shape[0], a.shape[1] // depth, b.shape[1]
    if cols // ranks % LANES:
        return relative_blocks(dot_tn(a, b).astype(bf16), rank, orders)
    block = (ranks // 2, depth, rows // len(orders), cols // ranks)
    outs = pl.pallas_call(
        functools.partial(grad_blocks_kernel, orders, ranks),
        out_shape=[jax.ShapeDtypeStruct(block, bf16)] * (2 * len(orders)),
        grid_spec=pltpu.PrefetchScalarGridSpec(
            num_scalar_prefetch=1,
            grid=(depth,),
            in_specs=[
                pl.BlockSpec((tokens, rows), lambda i, s: (0, i)),
                pl.BlockSpec((tokens, cols), lambda i, s: (0, 0)),
            ],
            out_specs=[pl.BlockSpec((block[0], 1) + block[2:], lambda i, s: (0, i, 0, 0))] * (2 * len(orders)),
            scratch_shapes=[pltpu.VMEM((rows, cols), bf16)],
        ),
        compiler_params=pltpu.CompilerParams(vmem_limit_bytes=40 << 20),
        cost_estimate=SHORT,
        name=name,
    )(rank.reshape(1).astype(jnp.int32), a, b)
    return [(outs[2 * n], outs[2 * n + 1]) for n in range(len(orders))]


def pre_grad_kernel(g_ref, w_ref, slope_ref, out_ref, sum_ref):
    grad = dot_nt(g_ref[...], w_ref[...]) * slope_ref[...].astype(f32)
    out_ref[...] = grad.astype(bf16)
    sum_ref[...] = jnp.sum(grad, axis=0, keepdims=True)


def pre_grads(mlp_grad, fc2_matrix, slope):
    tokens, units = slope.shape
    tile = 256
    return pl.pallas_call(
        pre_grad_kernel,
        out_shape=[jax.ShapeDtypeStruct((tokens, units), bf16), jax.ShapeDtypeStruct((1, units), f32)],
        grid=(units // tile,),
        in_specs=[
            pl.BlockSpec((tokens, D), lambda i: (0, 0)),
            pl.BlockSpec((tile, D), lambda i: (i, 0)),
            pl.BlockSpec((tokens, tile), lambda i: (0, i)),
        ],
        out_specs=[pl.BlockSpec((tokens, tile), lambda i: (0, i)), pl.BlockSpec((1, tile), lambda i: (0, i))],
        compiler_params=pltpu.CompilerParams(vmem_limit_bytes=40 << 20),
        cost_estimate=SHORT,
        name="pre_grad",
    )(mlp_grad, fc2_matrix, slope)


def product_kernel(half_ref, first_ref, second_ref, w_ref, out1_ref, out2_ref):
    out1_ref[...] = dot(first_ref[...], w_ref[...])
    out2_ref[...] = dot(second_ref[...], w_ref[...])


def product_nt_kernel(half_ref, first_ref, second_ref, w_ref, out1_ref, out2_ref, held):
    @pl.when(pl.program_id(0) == 0)
    def _():
        held[...] = w_ref[...].T

    out1_ref[...] = dot(first_ref[...], held[...])
    out2_ref[...] = dot(second_ref[...], held[...])


def product(a, weight, flipped, half, name, cost=SHORT):
    rows, tile = a.shape[0] // 2, 128
    count = rows // tile
    out = pl.BlockSpec((tile, D), lambda i, h: (i, 0))
    return pl.pallas_call(
        product_nt_kernel if flipped else product_kernel,
        out_shape=[jax.ShapeDtypeStruct((rows, D), f32)] * 2,
        grid_spec=pltpu.PrefetchScalarGridSpec(
            num_scalar_prefetch=1,
            grid=(count,),
            in_specs=[
                pl.BlockSpec((tile, a.shape[1]), lambda i, h: (i + h[0] * count, 0)),
                pl.BlockSpec((tile, a.shape[1]), lambda i, h: (i + (1 - h[0]) * count, 0)),
                pl.BlockSpec(weight.shape, lambda i, h: (0, 0)),
            ],
            out_specs=[out, out],
            scratch_shapes=[pltpu.VMEM(weight.shape[::-1], bf16)] if flipped else [],
        ),
        compiler_params=pltpu.CompilerParams(vmem_limit_bytes=32 << 20),
        cost_estimate=cost,
        name=name,
    )(jnp.asarray(half, jnp.int32).reshape(1), a, a, weight)


def add_sums(sum_ref, values):
    @pl.when(pl.program_id(0) == 0)
    def _():
        sum_ref[...] = jnp.zeros_like(sum_ref)

    for row, value in enumerate(values):
        sum_ref[row : row + 1, :] += jnp.sum(value, axis=0, keepdims=True)


def input_kernel(own_ref, sent_ref, tok_ref, grad_ref, vec_ref, out_ref, sum_ref):
    grad = own_ref[...] + sent_ref[...]
    normal, inverse = normalize(tok_ref[...].astype(f32))
    out_ref[...] = grad_ref[...] + norm_back(grad, normal, inverse, vec_ref[0:1, :])
    add_sums(sum_ref, (grad * normal, grad))


def output_kernel(own_ref, sent_ref, cot_ref, resid_ref, vec_ref, out_ref, sum_ref):
    mlp = own_ref[...] + sent_ref[...] + vec_ref[8:9, :]
    out_ref[...] = (resid_ref[...] + vec_ref[9:10, :] * mlp).astype(bf16)
    out_grad = cot_ref[...].astype(f32)
    add_sums(sum_ref, (out_grad * vec_ref[9:10, :], out_grad * mlp))


def finish(kernel, dtype, parts, vecs, name):
    rows, tile = parts[0].shape[0], 64
    part = pl.BlockSpec((tile, D), lambda i: (i, 0))
    return pl.pallas_call(
        kernel,
        out_shape=[jax.ShapeDtypeStruct((rows, D), dtype), jax.ShapeDtypeStruct((8, D), f32)],
        grid=(rows // tile,),
        in_specs=[part] * len(parts) + [pl.BlockSpec(vecs.shape, lambda i: (0, 0))],
        out_specs=[part, pl.BlockSpec((8, D), lambda i: (0, 0))],
        compiler_params=pltpu.CompilerParams(vmem_limit_bytes=24 << 20),
        cost_estimate=SHORT,
        name=name,
    )(*parts, vecs)


def residual_kernel(own_ref, sent_ref, tok_ref, vec_ref, attn_ref, resid_ref, input_ref):
    attn = own_ref[...] + sent_ref[...] + vec_ref[4:5, :]
    resid = tok_ref[...].astype(f32) + vec_ref[5:6, :] * attn
    attn_ref[...] = attn
    resid_ref[...] = resid
    normal, _ = normalize(resid)
    input_ref[...] = (normal * vec_ref[6:7, :] + vec_ref[7:8, :]).astype(bf16)


def residual(own, sent, tok, vecs):
    rows, tile = own.shape[0], 64
    part = pl.BlockSpec((tile, D), lambda i: (i, 0))
    return pl.pallas_call(
        residual_kernel,
        out_shape=[jax.ShapeDtypeStruct((rows, D), t) for t in (f32, f32, bf16)],
        grid=(rows // tile,),
        in_specs=[part] * 3 + [pl.BlockSpec(vecs.shape, lambda i: (0, 0))],
        out_specs=[part] * 3,
        compiler_params=pltpu.CompilerParams(vmem_limit_bytes=24 << 20),
        cost_estimate=SHORT,
        name="residual",
    )(own, sent, tok, vecs)


def scaled_kernel(own_ref, other_ref, vec_ref, out_ref):
    rows = own_ref.shape[0]
    for n, ref in enumerate((own_ref, other_ref)):
        out_ref[n * rows : (n + 1) * rows, :] = (ref[...].astype(f32) * vec_ref[9:10, :]).astype(bf16)


def scaled(own, other, vecs):
    return pl.pallas_call(
        scaled_kernel,
        out_shape=jax.ShapeDtypeStruct((2 * own.shape[0], D), bf16),
        compiler_params=pltpu.CompilerParams(vmem_limit_bytes=24 << 20),
        cost_estimate=SHORT,
        name="scaled",
    )(own, other, vecs)


def units_kernel(n_ref, w_ref, b_ref, act_ref, slope_ref):
    act, slope = gelu_pair(dot(n_ref[...], w_ref[...]) + b_ref[...])
    act_ref[...] = act.astype(bf16)
    slope_ref[...] = slope.astype(bf16)


def hidden_units(normed, weight, bias):
    tokens, units = normed.shape[0], weight.shape[1]
    tile = 256
    part = pl.BlockSpec((tokens, tile), lambda i: (0, i))
    return pl.pallas_call(
        units_kernel,
        out_shape=[jax.ShapeDtypeStruct((tokens, units), bf16)] * 2,
        grid=(units // tile,),
        in_specs=[
            pl.BlockSpec((tokens, D), lambda i: (0, 0)),
            pl.BlockSpec((D, tile), lambda i: (0, i)),
            pl.BlockSpec((1, tile), lambda i: (0, i)),
        ],
        out_specs=[part, part],
        compiler_params=pltpu.CompilerParams(vmem_limit_bytes=32 << 20),
        cost_estimate=SHORT,
        name="units",
    )(normed, weight, bias)


def norm_grad_kernel(own_ref, sent_ref, resid_ref, cot_ref, attn_ref, vec_ref, grad_ref, scaled_ref, sum_ref):
    grad = own_ref[...] + sent_ref[...]
    normal, inverse = normalize(resid_ref[...])
    resid_grad = cot_ref[...].astype(f32) + norm_back(grad, normal, inverse, vec_ref[6:7, :])
    scaled = resid_grad * vec_ref[5:6, :]
    grad_ref[...] = resid_grad
    scaled_ref[...] = scaled.astype(bf16)

    @pl.when(pl.program_id(0) == 0)
    def _():
        sum_ref[...] = jnp.zeros_like(sum_ref)

    for row, value in enumerate((grad * normal, grad, scaled, resid_grad * attn_ref[...])):
        sum_ref[row : row + 1, :] += jnp.sum(value, axis=0, keepdims=True)


def norm_grads(own, sent, resid, cot, attn_out, vecs):
    rows, tile = own.shape[0], 64
    part = pl.BlockSpec((tile, D), lambda i: (i, 0))
    return pl.pallas_call(
        norm_grad_kernel,
        out_shape=[
            jax.ShapeDtypeStruct((rows, D), f32), jax.ShapeDtypeStruct((rows, D), bf16),
            jax.ShapeDtypeStruct((8, D), f32),
        ],
        grid=(rows // tile,),
        in_specs=[part] * 5 + [pl.BlockSpec(vecs.shape, lambda i: (0, 0))],
        out_specs=[part, part, pl.BlockSpec((8, D), lambda i: (0, 0))],
        compiler_params=pltpu.CompilerParams(vmem_limit_bytes=24 << 20),
        cost_estimate=SHORT,
        name="norm_grad",
    )(own, sent, resid, cot, attn_out, vecs)


def proj_grad_kernel(head_rows, c_ref, g_ref, out_ref):
    wide = out_ref.shape[1]
    for side in range(2):
        grad = dot_tn(c_ref[...], g_ref[:, side * wide : (side + 1) * wide]).astype(bf16)
        for z in range(grad.shape[0] // head_rows):
            at = (2 * z + side) * head_rows
            out_ref[at : at + head_rows, :] = grad[z * head_rows : (z + 1) * head_rows]


def packed_proj_grad(context, attn_grad, head_rows):
    wide = D // 2
    return pl.pallas_call(
        functools.partial(proj_grad_kernel, head_rows),
        out_shape=jax.ShapeDtypeStruct((D, wide), bf16),
        compiler_params=pltpu.CompilerParams(vmem_limit_bytes=32 << 20),
        cost_estimate=SHORT,
        name="proj_grad",
    )(context, attn_grad)


def qkv_grad_kernel(orders, ranks, depth, per, index_ref, n_ref, *refs):
    grads, p_ref = refs[: 3 * per], refs[3 * per]
    outs, held = refs[3 * per + 1 : -1], refs[-1]
    rank = index_ref[0]
    normed = n_ref[...]
    for number in range(3):
        pieces = [g[...] for g in grads[number * per : (number + 1) * per]]
        wide = per * LANES
        joined = pieces[0] if per == 1 else jnp.concatenate(pieces, axis=1)
        held[:, number * wide : (number + 1) * wide] = dot_tn(normed, joined).astype(bf16)
    held[:, 3 * per * LANES :] = p_ref[...]
    width = held.shape[1] // ranks
    rows = held.shape[0] // depth
    share = rows // len(orders)
    for n, order in enumerate(orders):
        for which, offsets in enumerate(halves(ranks, order[0], list(range(ranks)))):
            for i, o in enumerate(offsets):
                cols = pl.ds(pl.multiple_of((rank ^ o) * width, width), width)
                for z in range(depth):
                    at = z * rows + n * share
                    outs[2 * n + which][i, z] = held[at : at + share, cols]


def qkv_grad_blocks(normed, grads, proj_packed, part, parts, rank, orders):
    depth, ranks = lax.axis_size("fsdp") // 2, lax.axis_size("rep")
    per = len(grads) // 3
    cols = 4 * per * LANES
    block = (ranks // 2, depth, D // depth // len(orders), cols // ranks)
    tokens = normed.shape[0] // 3
    outs = pl.pallas_call(
        functools.partial(qkv_grad_kernel, orders, ranks, depth, per),
        out_shape=[jax.ShapeDtypeStruct(block, bf16)] * (2 * len(orders)),
        grid_spec=pltpu.PrefetchScalarGridSpec(
            num_scalar_prefetch=1,
            grid=(1,),
            in_specs=[pl.BlockSpec((tokens, D), lambda i, a: (1, 0))]
            + whole_specs(grads)
            + [pl.BlockSpec((D, per * LANES), lambda i, a: (0, part))],
            out_specs=[pl.BlockSpec(block, lambda i, a: (0, 0, 0, 0))] * (2 * len(orders)),
            scratch_shapes=[pltpu.VMEM((D, cols), bf16)],
        ),
        compiler_params=pltpu.CompilerParams(vmem_limit_bytes=40 << 20),
        cost_estimate=SHORT,
        name="qkv_grad",
    )(rank.reshape(1).astype(jnp.int32), normed, *grads, proj_packed)
    return [(outs[2 * n], outs[2 * n + 1]) for n in range(len(orders))]


def spread_lanes(tags, width):
    return jnp.concatenate([tags] * (width // LANES), axis=1)


def project_kernel(need_ref, n_ref, w_ref, b_ref, q_ref, k_ref, v_ref):
    row = pl.program_id(0)
    wide = q_ref.shape[1]

    @pl.when(need_ref[row] > 0)
    def _():
        n = n_ref[...]
        for i, ref in enumerate((q_ref, k_ref, v_ref)):
            out = dot(n, w_ref[:, i * wide : (i + 1) * wide]) + b_ref[0:1, i * wide : (i + 1) * wide]
            if i == 0:
                out = out.astype(bf16).astype(f32) * HEAD_DIM ** (-0.5)
            ref[...] = out.astype(bf16)

    @pl.when(need_ref[row] == 0)
    def _():
        for ref in (q_ref, k_ref, v_ref):
            ref[...] = jnp.zeros_like(ref)


def project(need, normed, weight, bias, wide):
    rows = normed.shape[0]
    return pl.pallas_call(
        project_kernel,
        out_shape=[jax.ShapeDtypeStruct((rows, wide), bf16)] * 3,
        grid_spec=pltpu.PrefetchScalarGridSpec(
            num_scalar_prefetch=1,
            grid=(rows // BLOCK,),
            in_specs=[
                pl.BlockSpec((BLOCK, D), lambda i, s: (i, 0)),
                pl.BlockSpec(weight.shape, lambda i, s: (0, 0)),
                pl.BlockSpec((1, 3 * wide), lambda i, s: (0, 0)),
            ],
            out_specs=[pl.BlockSpec((BLOCK, wide), lambda i, s: (i, 0))] * 3,
        ),
        compiler_params=pltpu.CompilerParams(vmem_limit_bytes=32 << 20),
        cost_estimate=SHORT,
        name="project",
    )(need, normed, weight, bias)


def norm_kernel(need_ref, info_ref, *refs):
    *sources, vec_ref, out_ref = refs
    row = pl.program_id(0)
    side = (row // info_ref[1]) % 2
    chip = row // (2 * info_ref[1])

    @pl.when(need_ref[row] > 0)
    def _():
        picked = jnp.where(chip == 0, sources[0][...], jnp.where(chip == 1, sources[2][...], sources[4][...]))
        theirs = jnp.where(chip == 0, sources[1][...], jnp.where(chip == 1, sources[3][...], sources[5][...]))
        picked = jnp.where(side == info_ref[0], picked, theirs)
        normal, _ = normalize(picked.astype(f32))
        out_ref[...] = (normal * vec_ref[0:1, :] + vec_ref[1:2, :]).astype(bf16)

    @pl.when(need_ref[row] == 0)
    def _():
        out_ref[...] = jnp.zeros_like(out_ref)


def norm_window(need, info, sources, vecs, window, count):
    per = count // BLOCK

    def spec(chip):
        def index(i, a, b):
            inside = jnp.clip(i - 2 * per * chip, 0, 2 * per - 1)
            return (inside % per, 0)

        return pl.BlockSpec((BLOCK, D), index)

    return pl.pallas_call(
        norm_kernel,
        out_shape=jax.ShapeDtypeStruct((window, D), bf16),
        grid_spec=pltpu.PrefetchScalarGridSpec(
            num_scalar_prefetch=2,
            grid=(window // BLOCK,),
            in_specs=[spec(i // 2) for i in range(6)] + [pl.BlockSpec(vecs.shape, lambda i, a, b: (0, 0))],
            out_specs=pl.BlockSpec((BLOCK, D), lambda i, a, b: (i, 0)),
        ),
        compiler_params=pltpu.CompilerParams(vmem_limit_bytes=24 << 20),
        cost_estimate=SHORT,
        name="norm_window",
    )(need, info, *sources, vecs)


def attend_kernel(lo_ref, hi_ref, first_ref, last_ref, q_ref, k_ref, v_ref, qt_ref, kt_ref, o_ref, lse_ref, s_ref, m_ref, acc_ref):
    i = pl.program_id(0)
    left = lax.broadcasted_iota(jnp.int32, (1, LANES), 1) < HEAD_DIM
    lo, hi = lo_ref[i], hi_ref[i]
    base = (first_ref.shape[0] - pl.num_programs(0)) // 2
    q = q_ref[...]
    zero = jnp.zeros_like(q)
    heads = (jnp.where(left, q, zero), jnp.where(left, zero, q))
    m_ref[...] = jnp.full_like(m_ref, MASKED)
    one_image = first_ref[base + i] == last_ref[base + i]
    folds = BLOCK // LANES

    def fold(value, combine):
        parts = [value[:, n * LANES : (n + 1) * LANES] for n in range(folds)]
        return functools.reduce(combine, parts)

    def scores(j, carry):
        at = pl.multiple_of(j * BLOCK, BLOCK)
        k = k_ref[pl.ds(at, BLOCK), :]
        inside = one_image & (first_ref[j] == first_ref[base + i]) & (last_ref[j] == first_ref[base + i])

        @pl.when(inside)
        def _():
            for h in range(2):
                s = dot_nt(heads[h], k)
                s_ref[h, j] = s
                m_ref[h] = jnp.maximum(m_ref[h], fold(s, jnp.maximum))

        @pl.when(jnp.logical_not(inside))
        def _():
            same = spread_lanes(qt_ref[...], BLOCK) == kt_ref[:, pl.ds(at, BLOCK)]
            for h in range(2):
                s = jnp.where(same, dot_nt(heads[h], k), MASKED)
                s_ref[h, j] = s
                m_ref[h] = jnp.maximum(m_ref[h], fold(s, jnp.maximum))

        return carry

    lax.fori_loop(lo, hi, scores, 0)
    tops = [jnp.max(m_ref[h], axis=1, keepdims=True) for h in range(2)]
    m_ref[...] = jnp.zeros_like(m_ref)
    acc_ref[...] = jnp.zeros_like(acc_ref)

    def mix(j, carry):
        at = pl.multiple_of(j * BLOCK, BLOCK)
        v = v_ref[pl.ds(at, BLOCK), :]
        for h in range(2):
            e = jnp.exp(s_ref[h, j] - tops[h])
            m_ref[h] += fold(e, jnp.add)
            acc_ref[h] += dot(e.astype(bf16), v)
        return carry

    lax.fori_loop(lo, hi, mix, 0)
    sums = [jnp.sum(m_ref[h], axis=1, keepdims=True) for h in range(2)]
    o_ref[...] = jnp.where(left, acc_ref[0] / sums[0], acc_ref[1] / sums[1]).astype(bf16)
    for h in range(2):
        lse = jnp.broadcast_to(tops[h] + jnp.log(sums[h]), (BLOCK, LANES))
        lse_ref[0, h : h + 1, :] = lse.T[0:1, :]


def attend(lo, hi, firsts, lasts, q, k, v, tag_cols, tag_row, own_rows, pair):
    window = q.shape[0]
    blocks = own_rows // BLOCK
    skip = (window - own_rows) // 2 // BLOCK
    return pl.pallas_call(
        attend_kernel,
        out_shape=[
            jax.ShapeDtypeStruct((own_rows, LANES), bf16),
            jax.ShapeDtypeStruct((1, 2, own_rows), f32),
        ],
        grid_spec=pltpu.PrefetchScalarGridSpec(
            num_scalar_prefetch=4,
            grid=(blocks,),
            in_specs=[
                pl.BlockSpec((BLOCK, LANES), lambda i, *_: (i + skip, pair)),
                pl.BlockSpec((window, LANES), lambda i, *_: (0, pair)),
                pl.BlockSpec((window, LANES), lambda i, *_: (0, pair)),
                pl.BlockSpec((BLOCK, LANES), lambda i, *_: (i + skip, 0)),
                pl.BlockSpec((1, window), lambda i, *_: (0, 0)),
            ],
            out_specs=[
                pl.BlockSpec((BLOCK, LANES), lambda i, *_: (i, 0)),
                pl.BlockSpec((1, 2, BLOCK), lambda i, *_: (0, 0, i)),
            ],
            scratch_shapes=[
                pltpu.VMEM((2, window // BLOCK, BLOCK, BLOCK), f32),
                pltpu.VMEM((2, BLOCK, LANES), f32),
                pltpu.VMEM((2, BLOCK, LANES), f32),
            ],
        ),
        compiler_params=pltpu.CompilerParams(vmem_limit_bytes=32 << 20),
        cost_estimate=SHORT,
        name="attend",
    )(lo, hi, firsts, lasts, q, k, v, tag_cols, tag_row)


def attend_back_kernel(
    start, stop, lo_ref, hi_ref, q_ref, k_ref, v_ref, g_ref, tc_ref, tr_ref, lse_ref, delta_ref,
    dq_ref, dk_ref, dv_ref, sum_ref, dk_acc, dv_acc, dq_acc,
):
    first = lax.broadcasted_iota(jnp.int32, (1, LANES), 1) < HEAD_DIM
    dk_acc[...] = jnp.zeros_like(dk_acc)
    dv_acc[...] = jnp.zeros_like(dv_acc)
    sum_ref[...] = jnp.zeros_like(sum_ref)

    def split(value):
        zero = jnp.zeros_like(value)
        return jnp.where(first, value, zero), jnp.where(first, zero, value)

    def visit(i, j, qs, gs, of_key, of_query):
        at_q, at_k = pl.multiple_of(i * BLOCK, BLOCK), pl.multiple_of(j * BLOCK, BLOCK)
        k = k_ref[pl.ds(at_k, BLOCK), :]
        v = v_ref[pl.ds(at_k, BLOCK), :]
        same = spread_lanes(tc_ref[pl.ds(at_k, BLOCK), :], BLOCK) == tr_ref[:, pl.ds(at_q, BLOCK)]
        ps, ds = [], []
        for h in range(2):
            s = dot_nt(k, qs[h])
            dp = dot_nt(v, gs[h])
            p = jnp.where(same, jnp.exp(s - lse_ref[0, h : h + 1, pl.ds(at_q, BLOCK)]), 0.0)
            d = p * (dp - delta_ref[0, h : h + 1, pl.ds(at_q, BLOCK)])
            ps.append(p.astype(bf16))
            ds.append(d.astype(bf16))
        if of_key:
            at = pl.multiple_of((j - start) * BLOCK, BLOCK)
            dv_acc[pl.ds(at, BLOCK), :] += dot(ps[0], gs[0]) + dot(ps[1], gs[1])
            dk_acc[pl.ds(at, BLOCK), :] += dot(ds[0], qs[0]) + dot(ds[1], qs[1])
        if of_query:
            ks = split(k)
            dq_acc[...] += dot_tn(ds[0], ks[0]) + dot_tn(ds[1], ks[1])

    def query_block(own_q, i, carry):
        at_q = pl.multiple_of(i * BLOCK, BLOCK)
        qs = split(q_ref[pl.ds(at_q, BLOCK), :])
        gs = split(g_ref[pl.ds(at_q, BLOCK), :])
        lo, hi = lo_ref[i], hi_ref[i]

        def keys(first_key, last_key, of_key):
            def body(j, carry):
                visit(i, j, qs, gs, of_key, own_q)
                return carry

            lax.fori_loop(first_key, last_key, body, 0)

        if own_q:
            dq_acc[...] = jnp.zeros_like(dq_acc)
            keys(lo, jnp.minimum(hi, start), False)
            keys(jnp.maximum(lo, stop), hi, False)
        keys(jnp.maximum(lo, start), jnp.minimum(hi, stop), True)
        if own_q:
            at = pl.multiple_of((i - start) * BLOCK, BLOCK)
            dq = dq_acc[...] * HEAD_DIM ** (-0.5)
            dq_ref[pl.ds(at, BLOCK), :] = dq.astype(bf16)
            sum_ref[0, 0:1, :] += jnp.sum(dq, axis=0, keepdims=True)
        return carry

    before = jnp.where(lo_ref[start] < start, lo_ref[start], start)
    after = jnp.maximum(hi_ref[stop - 1], stop)
    lax.fori_loop(before, start, functools.partial(query_block, False), 0)
    lax.fori_loop(start, stop, functools.partial(query_block, True), 0)
    lax.fori_loop(stop, after, functools.partial(query_block, False), 0)
    dk_ref[...] = dk_acc[...].astype(bf16)
    dv_ref[...] = dv_acc[...].astype(bf16)
    sum_ref[0, 1:2, :] = jnp.sum(dv_acc[...], axis=0, keepdims=True)


def attend_back(lo, hi, q, k, v, g, tag_cols, tag_row, lse, delta, own_rows, pair):
    window = q.shape[0]
    pairs, wide = 1, LANES
    grad_pair = pair % (g.shape[1] // LANES)
    start = (window - own_rows) // 2 // BLOCK
    stop = start + own_rows // BLOCK
    whole = lambda: pl.BlockSpec((window, LANES), lambda p, a, b: (0, pair))
    own = lambda: pl.BlockSpec((own_rows, LANES), lambda p, a, b: (0, p))
    stat = lambda: pl.BlockSpec((1, 2, window), lambda p, a, b: (pair, 0, 0))
    return pl.pallas_call(
        functools.partial(attend_back_kernel, start, stop),
        out_shape=[jax.ShapeDtypeStruct((own_rows, wide), bf16)] * 3
        + [jax.ShapeDtypeStruct((pairs, 8, LANES), f32)],
        grid_spec=pltpu.PrefetchScalarGridSpec(
            num_scalar_prefetch=2,
            grid=(pairs,),
            in_specs=[
                whole(), whole(), whole(),
                pl.BlockSpec((window, LANES), lambda p, a, b: (0, grad_pair)),
                pl.BlockSpec((window, LANES), lambda p, a, b: (0, 0)),
                pl.BlockSpec((1, window), lambda p, a, b: (0, 0)),
                stat(), stat(),
            ],
            out_specs=[own(), own(), own(), pl.BlockSpec((1, 8, LANES), lambda p, a, b: (p, 0, 0))],
            scratch_shapes=[
                pltpu.VMEM((own_rows, LANES), f32),
                pltpu.VMEM((own_rows, LANES), f32),
                pltpu.VMEM((BLOCK, LANES), f32),
            ],
        ),
        compiler_params=pltpu.CompilerParams(vmem_limit_bytes=40 << 20),
        cost_estimate=SHORT,
        name="attend_back",
    )(lo, hi, q, k, v, g, tag_cols, tag_row, lse, delta)


def on_device(
    tokens, image_ids, ln1_gain, ln1_bias, qkv_weight, query_bias, value_bias, proj_weight,
    proj_bias, scale_attn, ln2_gain, ln2_bias, fc1_weight, fc1_bias, fc2_weight, fc2_bias,
    scale_mlp, cotangent,
):
    devices = lax.axis_size("fsdp")
    depth, ranks = devices // 2, lax.axis_size("rep")
    place = lax.axis_index("fsdp")
    rank = lax.axis_index("rep")
    here, core = place // 2, place % 2
    count = tokens.shape[1]
    chip = 2 * count
    head_rows = D // devices
    ff = fc1_weight.shape[1]
    unit_rows = ff // devices
    half_heads = D // 2
    local_heads = half_heads // HEAD_DIM
    pairs = half_heads // LANES
    bits = list(range(rep_bits()))

    def in_order(own, other, axis=0):
        return jnp.where(
            core == 0,
            jnp.concatenate([own, other], axis=axis),
            jnp.concatenate([other, own], axis=axis),
        )

    def mine(value):
        return lax.dynamic_slice_in_dim(value, core * count, count, 0)

    def others(value):
        return lax.dynamic_slice_in_dim(value, (1 - core) * count, count, 0)

    def every_other(value, width, start):
        cuts = range(start * width, value.shape[1], 2 * width)
        return jnp.concatenate([value[:, c : c + width] for c in cuts], axis=1)

    def all_share(which):
        pick_cols = lambda v, w: jnp.where(which == 0, every_other(v, w, 0), every_other(v, w, 1))
        heads = lax.dynamic_slice_in_dim(
            jnp.concatenate(
                [
                    pick_cols(qkv_weight, head_rows),
                    lax.dynamic_slice_in_dim(proj_weight, which * half_heads, half_heads, 1),
                ],
                axis=1,
            ),
            rank * (2 * D // ranks), 2 * D // ranks, 1,
        )
        units = lax.dynamic_slice_in_dim(
            pick_cols(fc1_weight, unit_rows), rank * (ff // 2 // ranks), ff // 2 // ranks, 1
        )
        return jnp.concatenate([heads, units], axis=1)

    if head_rows % LANES:
        kept, given = all_share(core), all_share(1 - core)
    else:
        kept, given = weight_share(
            rank, core, qkv_weight, proj_weight, fc1_weight, ranks, head_rows, unit_rows
        )
    wide1 = 2 * D // ranks
    got = swap_cores(given)
    is_proj = rank * wide1 >= 3 * half_heads
    own1 = in_order(kept[:, :wide1], jnp.where(is_proj, given[:, :wide1], got[:, :wide1]))
    own2 = in_order(kept[:, wide1:], got[:, wide1:])
    own3 = lax.dynamic_slice_in_dim(fc2_weight, rank * (D // ranks), D // ranks, 1)
    small = (
        ln1_gain, ln1_bias, query_bias, value_bias, proj_bias, scale_attn, ln2_gain, ln2_bias,
        fc2_bias, scale_mlp, fc1_bias, (image_ids[0] + 1).astype(bf16),
    )
    sizes = [v.shape[0] for v in small]
    slots = slot_lists(sizes)
    width = 2 * D // ranks
    small = pack_small(small, width, slots)
    small_other = swap_cores(small)
    rows1, rows3 = own1.shape[0], own3.shape[0]
    tok, cot = tokens[0], cotangent[0]
    tok_other = swap_cores(tok)
    cot_other = swap_cores(cot)
    own1 = jnp.concatenate([own1, small, small_other])
    own1, own2, own3, tok = tie(own1, own2, own3, tok)
    pieces1 = fetch_z(own1)
    tok, pieces1[1] = tie(tok, pieces1[1])
    behind, ahead = from_chip(tok, 1), from_chip(tok, -1)
    gather1 = Gather(pieces1, rows1, "gather1")
    gather1.send()
    behind_other, ahead_other = swap_cores(behind), swap_cores(ahead)
    for _ in bits[1:]:
        gather1.send()

    vec_rows, fc1_shift, all_tags = unpack_small(
        pieces1, slots, rows1, here, core, ff // 2, devices * count
    )
    vector = lambda i: vec_rows[i : i + 1]
    (
        attn_gain, attn_shift, query_shift, value_shift, proj_shift, attn_scale, mlp_gain,
        mlp_shift, fc2_shift, mlp_scale,
    ) = map(vector, range(10))
    core_part = lambda vec: jnp.where(
        core == 0, every_other(vec, head_rows, 0), every_other(vec, head_rows, 1)
    )

    window = 3 * chip
    padded = jnp.concatenate(
        [jnp.zeros((1, chip), f32), all_tags, jnp.full((1, chip), 1e6, f32)], axis=1
    )
    tag_row = lax.dynamic_slice(padded, (0, here * chip), (1, window))
    tags = tag_row.reshape(window)
    firsts, lasts = tags[::BLOCK], tags[BLOCK - 1 :: BLOCK]
    real = firsts * (1e6 - firsts) > 0
    below = jnp.sum((tag_row < firsts[:, None]).astype(jnp.int32), axis=1)
    upto = jnp.sum((tag_row <= lasts[:, None]).astype(jnp.int32), axis=1)
    blocks = window // BLOCK
    block_lo = jnp.where(real, below // BLOCK, 0)
    block_hi = jnp.where(real, (upto + BLOCK - 1) // BLOCK, 0)
    own_lo, own_hi = chip // BLOCK, 2 * chip // BLOCK
    numbers = jnp.arange(blocks)
    need = jnp.logical_and(numbers >= block_lo[own_lo], numbers < block_hi[own_hi - 1]).astype(jnp.int32)
    firsts, lasts = firsts.astype(jnp.int32), lasts.astype(jnp.int32)
    tag_cols = jnp.broadcast_to(tags[:, None], (window, LANES))

    info = jnp.stack([core, jnp.int32(count // BLOCK)]).astype(jnp.int32)
    normed1 = norm_window(
        need, info, (behind, behind_other, tok, tok_other, ahead, ahead_other), vec_rows, window, count
    )

    normed1, own2 = tie(normed1, own2)
    pieces2 = fetch_z(own2)
    normed1 = gather1.arrive(normed1)
    qkv_matrix, proj_matrix = gather1.assemble(here, rank, head_rows)

    shifts = jnp.concatenate(
        [core_part(query_shift), jnp.zeros((1, half_heads), f32), core_part(value_shift)], axis=1
    )
    queries, keys, values = project(need, normed1, qkv_matrix, shifts, half_heads)

    contexts, lses = [], []
    los = block_lo[own_lo:own_hi]
    los, queries = tie(los, queries)
    for pair in range(pairs):
        if pair == 0:
            los, own3, *pieces2 = tie(los, own3, *pieces2)
            gather2 = Gather(pieces2, rows1, "gather2")
            los = gather2.send(los)
            pieces3 = fetch_z(own3)
        if pair == 1:
            los = gather2.arrive(los)
            los = gather2.send(los)
        if pair == 2:
            los, *pieces3 = tie(los, *pieces3)
            gather3 = Gather(pieces3, rows3, "gather3")
            los = gather3.send(los)
        if pair == 3:
            los = gather2.arrive(los)
            for _ in bits[2:]:
                los = gather2.arrive(gather2.send(los))
            los = gather3.arrive(los)
            los = gather3.send(los)
        context, lse = attend(
            los, block_hi[own_lo:own_hi], firsts, lasts, queries, keys, values, tag_cols,
            tag_row, chip, pair,
        )
        los, context = tie(los, context)
        contexts.append(context)
        lses.append(lse)
    context = jnp.concatenate(contexts, axis=1)
    lse_rows = jnp.concatenate(lses).reshape(local_heads, chip)
    own, given = product(context, proj_matrix, False, core, "attn_out")
    attn_out, resid, mlp_input = residual(own, swap_cores(given), tok, vec_rows)
    mlp_input = jnp.concatenate([mlp_input, swap_cores(mlp_input)])
    fc1_matrix = gather2.assemble(here, rank)
    activated, slope = hidden_units(mlp_input, fc1_matrix, fc1_shift)
    mlp_grad = scaled(cot, cot_other, vec_rows)
    both = [bits, bits[::-1]]
    activated = gather3.arrive(activated)
    for _ in bits[2:]:
        activated = gather3.arrive(gather3.send(activated))
    reduce3 = Reduce(grad_blocks(activated, mlp_grad, rank, both, "fc2_grad"), here, both)
    mlp_grad = reduce3.send(mlp_grad)
    fc2_matrix = gather3.assemble(here, rank)
    pre_grad, fc1_bias_part = pre_grads(mlp_grad, fc2_matrix, slope)
    reduce2 = Reduce(grad_blocks(mlp_input, pre_grad, rank, both, "fc1_grad"), here, both)
    pre_grad, _ = tie(pre_grad, [give for _, _, give in reduce2.held])
    own, given = product(pre_grad, fc1_matrix, True, 0, "mlp_in_grad")
    own, given = reduce3.arrive(own, given)
    for _ in bits[2:]:
        own, given = reduce3.arrive(*reduce3.send(own, given))
    own, given = reduce3.send(own, given)
    sent = swap_cores(given)
    resid_grad, attn_grad, norm_sums = norm_grads(own, sent, resid, cot, attn_out, vec_rows)
    both_grads = jnp.zeros((chip, D), bf16)
    for part, which in ((attn_grad, core), (swap_cores(attn_grad), 1 - core)):
        both_grads = lax.dynamic_update_slice_in_dim(both_grads, part, which * count, 0)
    attn_grad = both_grads
    context_grad = dot_nt(attn_grad, proj_matrix).astype(bf16)
    head_of = (
        lax.broadcasted_iota(jnp.int32, (local_heads, half_heads), 1) // HEAD_DIM
        == lax.broadcasted_iota(jnp.int32, (local_heads, half_heads), 0)
    ).astype(f32)
    row_delta = lax.dot_general(
        head_of, context_grad.astype(f32) * context.astype(f32), (((1,), (1,)), ((), ())),
        precision=lax.Precision.HIGHEST, preferred_element_type=f32,
    )
    stats = jnp.concatenate([lse_rows, row_delta])
    context_grad, activated, attn_grad = tie(context_grad, activated, attn_grad)
    chunk = half_heads // 2
    chunks = [context_grad[:, :chunk], context_grad[:, chunk:]]
    grads_behind, grads_ahead = zip(*[(from_chip(c, 1), from_chip(c, -1)) for c in chunks])
    stats_behind, stats_ahead = from_chip(stats, 1), from_chip(stats, -1)
    proj_grad = packed_proj_grad(context, attn_grad, head_rows)
    stat_window = jnp.concatenate([stats_behind, stats, stats_ahead], axis=1)
    by_pair = lambda s: s.reshape(pairs, 2, window)
    lse_window, delta_window = by_pair(stat_window[:local_heads]), by_pair(stat_window[local_heads:])

    half_pairs = pairs // 2
    half_width = half_heads // 2

    def first_group(parts, number):
        grads = [g for kind in zip(*parts) for g in kind]
        return Reduce(
            qkv_grad_blocks(normed1, grads, proj_grad, number, 2, rank, both), here, both
        )

    parts, sums = [], []
    out_own, out_given = product(activated, fc2_matrix, False, 0, "mlp_out", FILLER)
    output_rows, out_sums = finish(
        output_kernel, bf16, (out_own, swap_cores(out_given), cot, resid), vec_rows, "output"
    )
    first, delta_window, lo, out_sums = settle(
        ((grads_behind[0], grads_ahead[0]), delta_window, block_lo, out_sums), (reduce3, "received")
    )
    grad_windows = [jnp.concatenate([first[0], chunks[0], first[1]])]
    for pair in range(pairs):
        if pair == 0:
            lo = reduce3.arrive(lo)
            lo = reduce2.send(lo)
        if pair == 1:
            lo, second = settle((lo, (grads_behind[1], grads_ahead[1])), (reduce2, "received"))
            grad_windows.append(jnp.concatenate([second[0], chunks[1], second[1]]))
            lo = reduce2.arrive(lo)
            lo = reduce3.send_z(lo)
            for _ in bits[2:]:
                lo = reduce2.arrive(reduce2.send(lo))
            lo = reduce2.send(lo)
        if pair == 2:
            lo = settle(lo, (reduce2, "received"), (reduce3, "pieces"))
            lo = reduce2.arrive(lo)
            lo = reduce2.send_z(lo)
            reduce1a = first_group(parts, 0)
            lo = reduce1a.send(lo)
        if pair == 3:
            lo = settle(lo, (reduce2, "pieces"), (reduce1a, "received"))
            lo = reduce3.arrive_z(lo)
            lo = reduce2.arrive_z(lo)
            fc2_part = reduce3.total.astype(bf16)
            fc1_part = reduce2.total.astype(bf16)
            split = fc2_part.shape[0] // fc1_part.shape[0]
            mlp_spread = Spread(jnp.concatenate([fc1_part, *jnp.split(fc2_part, split)], axis=1))
            lo = mlp_spread.send(lo)
            lo = reduce1a.arrive(lo)
            for _ in bits[2:]:
                lo = reduce1a.arrive(reduce1a.send(lo))
            lo = reduce1a.send(lo)
        *grads, total = attend_back(
            lo, block_hi, queries, keys, values, grad_windows[pair * 2 // pairs], tag_cols, tag_row, lse_window,
            delta_window, chip, pair,
        )
        lo, *grads = tie(lo, *grads)
        parts.append(grads)
        sums.append(total[0])

    parts[-1] = settle(parts[-1], (mlp_spread, "arrays"))
    parts[-1] = reduce1a.arrive(parts[-1])
    parts[-1] = reduce1a.send_z(parts[-1])
    reduce1b = first_group(parts[half_pairs:], 1)
    parts[-1] = reduce1b.send(parts[-1])
    every = [jnp.concatenate(p, axis=1) for p in zip(*parts)]

    factor = 1.0 / math.sqrt(count * devices * ranks)
    in_own, in_given = product(
        jnp.concatenate(every, axis=1), qkv_matrix, True, core, "attn_in_grad"
    )
    tail = (in_own, in_given)
    tail = settle(tail, (reduce1b, "received"), (reduce1a, "pieces"))
    for _ in bits[1:]:
        tail = reduce1b.arrive(tail)
        tail = reduce1b.send(tail)
    in_own, in_given = tail
    input_rows, in_sums = finish(
        input_kernel, f32, (in_own, swap_cores(in_given), tok, resid_grad), vec_rows, "input_grad"
    )

    vectors = (
        in_sums[0:1], in_sums[1:2],
        jnp.concatenate([s[0:1] for s in sums], axis=1), jnp.concatenate([s[1:2] for s in sums], axis=1),
        norm_sums[2:3], norm_sums[3:4], norm_sums[0:1], norm_sums[1:2],
        out_sums[0:1], out_sums[1:2], fc1_bias_part,
    )
    of_core = [number in (2, 3, 10) for number in range(11)]
    partial = pack_grads(vectors, list(zip(sizes, of_core)), core, depth)
    vec_width = D // ranks
    half_of = lambda which: lax.dynamic_slice_in_dim(partial, which * 16, 16, 1)
    partial = half_of(core) + swap_cores(half_of(1 - core))
    vec_high = lax.reduce_precision(partial, 8, 7)
    side_by_side = 2 if vec_width >= 2 * LANES else 1
    extra = jnp.concatenate([vec_high, partial - vec_high], axis=side_by_side).astype(bf16)
    extra = jnp.pad(extra, ((0, 0), (0, 0), (0, vec_width - extra.shape[2])))
    extra = reduce1b.arrive(extra)
    extra = reduce1b.send_z(extra, extra=extra)
    for _ in bits[1:]:
        mlp_spread.send(extra)

    reduce1a.arrive_z()
    reduce1b.arrive_z()
    rows = reduce1a.total.shape[0]
    vec_total = reduce1b.total[rows:]
    if side_by_side == 2:
        vec_total = vec_total[:, :LANES] + vec_total[:, LANES : 2 * LANES]
    else:
        vec_total = vec_total[:16] + vec_total[16:]
    vec_high = lax.reduce_precision(vec_total, 8, 7)
    sides = [jnp.pad(v, ((0, 16), (0, vec_width - LANES))) for v in (vec_high, vec_total - vec_high)]
    payload = jnp.concatenate(
        [
            jnp.concatenate([reduce1a.total, reduce1b.total[:rows]], axis=1),
            jnp.concatenate(sides, axis=1),
        ]
    ).astype(bf16)
    payload = settle(payload, (mlp_spread, "arrays"))
    first_spread = Spread(payload)
    for bit in bits:
        first_spread.send()

    mlp_cols = fc1_part.shape[1]
    fc1_full = mlp_spread.blocks(rank, 0, mlp_cols)
    fc2_width = fc2_part.shape[1]
    fc2_full = tie(*[mlp_spread.blocks(rank, mlp_cols + n * fc2_width, fc2_width) for n in range(split)])
    grad_fc2 = jnp.concatenate(fc2_full).astype(f32) * factor
    first_a = first_spread.blocks(rank, 0, vec_width)
    first_b = first_spread.blocks(rank, vec_width, vec_width)
    totals = sum(
        part[rows : rows + 16, r * vec_width : r * vec_width + LANES].astype(f32)
        for part in (first_a, first_b)
        for r in range(ranks)
    ) * factor
    first_a, first_b = first_a[:rows], first_b[:rows]

    def rows_of(value, index):
        return lax.dynamic_slice_in_dim(value, index * head_rows, head_rows, 0)

    def interleave(own, other, width):
        cuts = range(0, own.shape[1], width)
        zipped = lambda a, b: jnp.concatenate(
            [v[:, c : c + width] for c in cuts for v in (a, b)], axis=1
        )
        return jnp.where(core == 0, zipped(own, other), zipped(other, own)).astype(f32) * factor

    fc1_other = swap_cores(rows_of(fc1_full, 1 - core))
    grad_fc1 = interleave(rows_of(fc1_full, core), fc1_other, unit_rows)
    qkv_full = jnp.concatenate(
        [
            part[:, n * half_width : (n + 1) * half_width]
            for n in range(3)
            for part in (first_a, first_b)
        ],
        axis=1,
    )
    grad_qkv = interleave(rows_of(qkv_full, core), swap_cores(rows_of(qkv_full, 1 - core)), head_rows)
    proj_part = jnp.concatenate([first_a[:, 3 * half_width :], first_b[:, 3 * half_width :]], axis=1)
    grad_proj = jnp.concatenate([proj_part[:head_rows], proj_part[head_rows:]], axis=1).astype(f32) * factor

    small_grads = [totals[i, : sizes[i]] for i in range(10)]
    lines = -(-sizes[10] // LANES)
    small_grads.append(totals[10 : 10 + lines].reshape(-1))
    (
        grad_attn_gain, grad_attn_shift, grad_query_shift, grad_value_shift, grad_proj_shift,
        grad_attn_scale, grad_mlp_gain, grad_mlp_shift, grad_fc2_shift, grad_mlp_scale, grad_fc1_shift,
    ) = small_grads

    return (
        output_rows[None],
        input_rows[None],
        grad_attn_gain,
        grad_attn_shift,
        grad_qkv,
        grad_query_shift,
        grad_value_shift,
        grad_proj,
        grad_proj_shift,
        grad_attn_scale,
        grad_mlp_gain,
        grad_mlp_shift,
        grad_fc1,
        grad_fc1_shift,
        grad_fc2,
        grad_fc2_shift,
        grad_mlp_scale,
    )


def solution(mesh):
    rows = P("fsdp", None)
    vec = P("fsdp")
    tok = P("rep", "fsdp", None)
    return jax.shard_map(
        on_device,
        mesh=mesh,
        in_specs=(
            tok, P("rep", "fsdp"), vec, vec, rows, vec, vec, rows, vec, vec, vec, vec, rows, vec,
            rows, vec, vec, tok,
        ),
        out_specs=(
            tok, tok, vec, vec, rows, vec, vec, rows, vec, vec, vec, vec, rows, vec, rows, vec, vec,
        ),
        check_vma=False,
    )
```

```python
import functools
import math

import jax
import jax.numpy as jnp
from jax import lax
from jax.experimental import pallas as pl
from jax.experimental.pallas import tpu as pltpu
from jax.sharding import PartitionSpec as P

D = 1024
HEADS = 16
HEAD_DIM = 64
LANES = 128

EPSILON = 1e-06
MASKED = -1e30
BLOCK = 256

SHORT = pl.CostEstimate(flops=1, transcendentals=0, bytes_accessed=1)
FILLER = pl.CostEstimate(flops=1 << 33, transcendentals=0, bytes_accessed=1 << 23)

f32 = jnp.float32
bf16 = jnp.bfloat16


def normalize(features):
    row_mean = jnp.mean(features, axis=-1, keepdims=True)
    centred = features - row_mean
    variance = jnp.mean(centred * centred, axis=-1, keepdims=True)
    inverse = lax.rsqrt(variance + EPSILON)
    return centred * inverse, inverse


def norm_back(gradient, normal, inverse, gain_vec):
    scaled = gradient * gain_vec
    mean_first = jnp.mean(scaled, axis=-1, keepdims=True)
    mean_second = jnp.mean(scaled * normal, axis=-1, keepdims=True)
    return inverse * (scaled - mean_first - normal * mean_second)


def gelu_pair(values):
    cumulative = 0.5 * (1.0 + lax.erf(values * 2.0 ** (-0.5)))
    density = jnp.exp(-0.5 * values * values) * (2.0 * math.pi) ** (-0.5)
    return (values * cumulative, cumulative + values * density)


def dot(a, b):
    return jnp.dot(a, b, preferred_element_type=f32)


def dot_nt(a, b):
    return lax.dot_general(a, b, (((1,), (1,)), ((), ())), preferred_element_type=f32)


def dot_tn(a, b):
    return lax.dot_general(a, b, (((0,), (0,)), ((), ())), preferred_element_type=f32)


def swap_cores(value):
    size = lax.axis_size("fsdp")
    return lax.ppermute(value, "fsdp", [(i, i ^ 1) for i in range(size)])


def along_z(value, by):
    size = lax.axis_size("fsdp")
    return lax.ppermute(value, "fsdp", [(i, (i + 2 * by) % size) for i in range(size)])


def from_chip(value, by):
    size = lax.axis_size("fsdp")
    pairs = [(i, i + 2 * by) for i in range(size) if 0 <= i + 2 * by < size]
    return lax.ppermute(value, "fsdp", pairs)


def across_rep(value, bit):
    size = lax.axis_size("rep")
    return lax.ppermute(value, "rep", [(i, i ^ (1 << bit)) for i in range(size)])


def pick(value, index, axis):
    return lax.dynamic_index_in_dim(value, index, axis, keepdims=False)


def rep_bits():
    return lax.axis_size("rep").bit_length() - 1


def tie(*values):
    return lax.optimization_barrier(values)


def settle(value, *fields):
    held = [getattr(o, name) for o, name in fields]
    value, held = lax.optimization_barrier((value, held))
    for (o, name), new in zip(fields, held):
        setattr(o, name, new)
    return value


def fetch_z(own):
    return [own] + [along_z(own, k) for k in range(1, lax.axis_size("fsdp") // 2)]


class Gather:
    def __init__(self, pieces, rows, name):
        self.rows, self.cols, self.name = rows, pieces[0].shape[1], name
        half = rows // 2
        bits = list(range(rep_bits()))
        self.orders = [bits, bits[::-1]]
        self.parts = [
            [(jnp.stack([p[:half] for p in pieces])[None], [0])],
            [(jnp.stack([p[half:rows] for p in pieces])[None], [0])],
        ]
        self.at = 0

    def send(self, *values):
        whole = [
            (ps[0][0] if len(ps) == 1 else jnp.concatenate([a for a, _ in ps]), [o for _, os in ps for o in os])
            for ps in self.parts
        ]
        values, arrays = lax.optimization_barrier((values, [a for a, _ in whole]))
        self.parts = []
        for array, (_, offsets), order in zip(arrays, whole, self.orders):
            flip = 1 << order[self.at]
            received = across_rep(array, order[self.at])
            self.parts.append([(array, offsets), (received, [o ^ flip for o in offsets])])
        self.at += 1
        return values[0] if len(values) == 1 else values

    def arrive(self, value):
        value, arrays = lax.optimization_barrier((value, [a for ps in self.parts for a, _ in ps]))
        self.parts = [[(arrays.pop(0), o) for _, o in ps] for ps in self.parts]
        return value

    def assemble(self, here, rank, tail_rows=0):
        depth, ranks = lax.axis_size("fsdp") // 2, lax.axis_size("rep")
        sources, plan = [], []
        for number, parts in enumerate(self.parts):
            for array, offsets in parts:
                sources.append(array)
                plan.append((number, offsets))
        dtype = sources[0].dtype
        shape = (depth * self.rows, ranks * self.cols)
        shapes = [jax.ShapeDtypeStruct(shape, dtype)]
        if tail_rows:
            tail = shape[1] // 4
            shapes = [
                jax.ShapeDtypeStruct((shape[0], shape[1] - tail), dtype),
                jax.ShapeDtypeStruct((depth * tail_rows, 2 * tail), dtype),
            ]
        out = pl.pallas_call(
            functools.partial(assemble_kernel, plan, depth, self.rows, self.cols, tail_rows),
            out_shape=shapes,
            grid_spec=pltpu.PrefetchScalarGridSpec(
                num_scalar_prefetch=1,
                grid=(1,),
                in_specs=[pl.BlockSpec(memory_space=pl.ANY)] * len(sources),
                out_specs=[pl.BlockSpec(memory_space=pl.ANY)] * len(shapes),
                scratch_shapes=[
                    pltpu.VMEM(shape, dtype),
                    pltpu.SemaphoreType.DMA((2 * ranks * depth,)),
                    pltpu.SemaphoreType.DMA((3 * depth,)),
                ],
            ),
            compiler_params=pltpu.CompilerParams(vmem_limit_bytes=16 << 20),
            cost_estimate=SHORT,
            name=self.name,
        )(jnp.stack([here, rank]).astype(jnp.int32), *sources)
        return out if tail_rows else out[0]


def assemble_kernel(plan, depth, rows, cols, tail_rows, index_ref, *refs):
    count = len(plan)
    sources = refs[:count]
    targets = refs[count : count + (2 if tail_rows else 1)]
    held, in_sems, out_sems = refs[-3:]
    here, rank = index_ref[0], index_ref[1]
    half = rows // 2
    waits = [[] for _ in range(depth)]
    number = 0
    for k in range(depth):
        place = lax.rem(here - k + depth, depth)
        for which, (colour, offsets) in enumerate(plan):
            for m, offset in enumerate(offsets):
                at_row = pl.multiple_of(place * rows + colour * half, half)
                at_col = pl.multiple_of((rank ^ offset) * cols, cols)
                copy = pltpu.make_async_copy(
                    sources[which].at[m, k],
                    held.at[pl.ds(at_row, half), pl.ds(at_col, cols)],
                    in_sems.at[number],
                )
                copy.start()
                waits[k].append(copy)
                number += 1
    outs = []
    main = targets[0].shape[1]
    for k in range(depth):
        place = lax.rem(here - k + depth, depth)
        for copy in waits[k]:
            copy.wait()
        base = pl.multiple_of(place * rows, rows)
        band = pl.ds(base, rows)
        out = pltpu.make_async_copy(held.at[band, pl.ds(0, main)], targets[0].at[band], out_sems.at[3 * k])
        out.start()
        outs.append(out)
        if tail_rows:
            wide = targets[1].shape[1] // 2
            for side in range(2):
                out = pltpu.make_async_copy(
                    held.at[pl.ds(base + side * tail_rows, tail_rows), pl.ds(main, wide)],
                    targets[1].at[
                        pl.ds(pl.multiple_of(place * tail_rows, tail_rows), tail_rows),
                        pl.ds(side * wide, wide),
                    ],
                    out_sems.at[3 * k + 1 + side],
                )
                out.start()
                outs.append(out)
    for out in outs:
        out.wait()


def halves(ranks, bit, held):
    flip = 1 << bit
    kept = [o for o in held if not o & flip]
    return kept, [o ^ flip for o in kept]


def relative_blocks(grads, rank, orders):
    depth, ranks = lax.axis_size("fsdp") // 2, lax.axis_size("rep")
    width = grads.shape[1] // ranks
    rows = grads.shape[0] // depth
    shaped = grads.reshape(depth, rows, grads.shape[1])
    share = rows // len(orders)
    first = []
    for n, order in enumerate(orders):
        block = lambda o: lax.dynamic_slice(
            shaped, (0, n * share, (rank ^ o) * width), (depth, share, width)
        )
        kept, given = halves(ranks, order[0], list(range(ranks)))
        first.append((jnp.stack([block(o) for o in kept]), jnp.stack([block(o) for o in given])))
    return first


class Reduce:
    def __init__(self, first, here, orders):
        self.here, self.orders, self.at = here, orders, 0
        ranks = lax.axis_size("rep")
        self.held = []
        for (keep, give), order in zip(first, orders):
            kept, given = halves(ranks, order[0], list(range(ranks)))
            self.held.append((kept, keep, give))

    def send(self, *values):
        values, gives = lax.optimization_barrier((values, [give for _, _, give in self.held]))
        self.received = [across_rep(g, order[self.at]) for g, order in zip(gives, self.orders)]
        self.at += 1
        return values[0] if len(values) == 1 else values

    def arrive(self, *values):
        values, received = lax.optimization_barrier((values, self.received))
        held = []
        for (kept, keep, _), got, order in zip(self.held, received, self.orders):
            total = (keep.astype(f32) + got.astype(f32)).astype(bf16)
            if self.at < len(order):
                stay, leave = halves(None, order[self.at], kept)
                take = lambda os: jnp.stack([total[kept.index(o)] for o in os])
                held.append((stay, take(stay), take(leave)))
            else:
                held.append((kept, total[0], None))
        self.held = held
        return values[0] if len(values) == 1 else values

    def send_z(self, *values, extra=None):
        depth = lax.axis_size("fsdp") // 2
        parts = [keep for _, keep, _ in self.held]
        whole = parts[0] if len(parts) == 1 else jnp.concatenate(parts, axis=1)
        if extra is not None:
            whole = jnp.concatenate([whole, extra], axis=1)
        pieces = [pick(whole, lax.rem(self.here + k, depth), 0) for k in range(depth)]
        values, pieces = lax.optimization_barrier((values, pieces))
        self.pieces = [pieces[0]] + [along_z(p, k) for k, p in enumerate(pieces) if k]
        return values[0] if len(values) == 1 else values

    def arrive_z(self, *values):
        values, pieces = lax.optimization_barrier((values, self.pieces))
        total = pieces[0].astype(f32)
        for piece in pieces[1:]:
            total = total + piece.astype(f32)
        self.total = total
        return values[0] if len(values) == 1 else values


class Spread:
    def __init__(self, value):
        bits = list(range(rep_bits()))
        self.orders = [bits, bits[::-1]]
        half = value.shape[0] // 2
        self.arrays = [value[:half][None], value[half:][None]]
        self.offsets = [[0], [0]]
        self.at = 0

    def send(self, *values):
        values, arrays = lax.optimization_barrier((values, self.arrays))
        self.arrays = []
        for n, (array, order) in enumerate(zip(arrays, self.orders)):
            flip = 1 << order[self.at]
            received = across_rep(array, order[self.at])
            self.arrays.append(jnp.concatenate([array, received]))
            self.offsets[n] = self.offsets[n] + [o ^ flip for o in self.offsets[n]]
        self.at += 1
        return values[0] if len(values) == 1 else values

    def blocks(self, rank, start, size):
        return jnp.concatenate(
            [rep_blocks(a[:, :, start : start + size], o, rank) for a, o in zip(self.arrays, self.offsets)]
        )


def rep_blocks(stacked, offsets, rank):
    blocks = []
    for i in range(len(offsets)):
        block = stacked[0]
        for entry, offset in enumerate(offsets):
            block = jnp.where((rank ^ offset) == i, stacked[entry], block)
        blocks.append(block)
    return jnp.concatenate(blocks, axis=1)


def share_kernel(widths, index_ref, qkv_ref, proj_ref, fc1_ref, keep_ref, give_ref, sems):
    rank, core = index_ref[0], index_ref[1]
    wide1, wide2, block, unit, half = widths
    is_proj = rank * wide1 >= 3 * half

    def copies(second):
        made = []
        for out, (ref, which) in enumerate(((keep_ref, core), (give_ref, 1 - core))):
            for c in range(wide1 // block):
                col = rank * wide1 + c * block
                if second:
                    source, at = proj_ref, which * half + col - 3 * half
                else:
                    source, at = qkv_ref, 2 * col + which * block
                made.append((source, at, block, ref, c * block))
        return made

    def run(plan, first):
        started = []
        for n, (source, at, size, ref, to) in enumerate(plan):
            copy = pltpu.make_async_copy(
                source.at[:, pl.ds(pl.multiple_of(at, LANES), size)], ref.at[:, pl.ds(to, size)], sems.at[first + n]
            )
            copy.start()
            started.append(copy)
        return started

    col = rank * wide2
    plan2 = []
    for ref, which in ((keep_ref, core), (give_ref, 1 - core)):
        at = col + (lax.div(col, unit) + which) * unit
        plan2.append((fc1_ref, at, wide2, ref, wide1))
    second = run(plan2, 0)

    @pl.when(is_proj)
    def _():
        for copy in run(copies(True), 2):
            copy.wait()

    @pl.when(jnp.logical_not(is_proj))
    def _():
        for copy in run(copies(False), 2):
            copy.wait()

    for copy in second:
        copy.wait()


def weight_share(rank, core, qkv_weight, proj_weight, fc1_weight, ranks, block, unit):
    rows = qkv_weight.shape[0]
    wide1, wide2 = 2 * D // ranks, fc1_weight.shape[1] // 2 // ranks
    out = jax.ShapeDtypeStruct((rows, wide1 + wide2), bf16)
    return pl.pallas_call(
        functools.partial(share_kernel, (wide1, wide2, block, unit, D // 2)),
        out_shape=[out, out],
        grid_spec=pltpu.PrefetchScalarGridSpec(
            num_scalar_prefetch=1,
            grid=(1,),
            in_specs=[pl.BlockSpec(memory_space=pl.ANY)] * 3,
            out_specs=[pl.BlockSpec(out.shape, lambda i, a: (0, 0))] * 2,
            scratch_shapes=[pltpu.SemaphoreType.DMA((2 + 2 * (wide1 // block),))],
        ),
        cost_estimate=SHORT,
        name="weight_share",
    )(jnp.stack([rank, core]).astype(jnp.int32), qkv_weight, proj_weight, fc1_weight)


def whole_specs(arrays):
    return [pl.BlockSpec(a.shape, lambda *_, n=len(a.shape): (0,) * n) for a in arrays]


def slot_lists(sizes):
    slots = []
    for number, size in enumerate(sizes):
        for start in range(0, size, LANES):
            slots.append((number, start, min(LANES, size - start)))
    return slots


def pack_kernel(slots, *refs):
    *sources, out_ref, held = refs
    per_row = held.shape[1] // LANES
    held[...] = jnp.zeros_like(held)
    for slot, (number, start, size) in enumerate(slots):
        row, at = slot // per_row, slot % per_row * LANES
        held[row : row + 1, at : at + size] = sources[number][:, start : start + size].astype(f32)
    out_ref[...] = held[...].astype(out_ref.dtype)


def pack_small(vectors, width, slots):
    shape = (32 * LANES // width, width)
    vectors = [v.reshape(1, -1) for v in vectors]
    return pl.pallas_call(
        functools.partial(pack_kernel, slots),
        out_shape=jax.ShapeDtypeStruct(shape, bf16),
        scratch_shapes=[pltpu.VMEM(shape, f32)],
        name="pack_small",
    )(*vectors)


def unpack_kernel(slots, depth, index_ref, *refs):
    pieces, (vec_ref, unit_ref, tag_ref) = refs[:depth], refs[depth:]
    here, core = index_ref[0], index_ref[1]
    rows, width = pieces[0].shape
    per_row = width // LANES
    single = sum(1 for number, _, _ in slots if number < 10)
    vec_ref[...] = jnp.zeros_like(vec_ref)
    for k in range(depth):
        place = lax.rem(here - k + depth, depth)
        values = pieces[k][...].astype(f32)

        def part(side, slot, size):
            row, at = side * (rows // 2) + slot // per_row, slot % per_row * LANES
            return values[row : row + 1, at : at + size]

        for slot, (number, start, size) in enumerate(slots):
            own, other = part(0, slot, size), part(1, slot, size)
            first = jnp.where(core == 0, own, other)
            second = jnp.where(core == 0, other, own)
            if number < 10:
                at = pl.multiple_of(place * 2 * size, 2 * size)
                vec_ref[number : number + 1, pl.ds(at, 2 * size)] = jnp.concatenate([first, second], axis=1)
            elif number == 10:
                wide = unit_ref.shape[1] // depth
                unit_ref[0:1, pl.ds(pl.multiple_of(place * wide + start, LANES), LANES)] = own
            else:
                wide = tag_ref.shape[1] // depth
                at = pl.multiple_of(place * wide + start, LANES)
                tag_ref[0:1, pl.ds(at, LANES)] = first
                tag_ref[0:1, pl.ds(pl.multiple_of(at + wide // 2, LANES), LANES)] = second


def unpack_small(pieces, slots, rows, here, core, units, group_tokens):
    depth = len(pieces)
    extra, width = pieces[0].shape[0] - rows, pieces[0].shape[1]
    shapes = [(16, D), (1, units), (1, group_tokens)]
    return pl.pallas_call(
        functools.partial(unpack_kernel, slots, depth),
        out_shape=[jax.ShapeDtypeStruct(s, f32) for s in shapes],
        grid_spec=pltpu.PrefetchScalarGridSpec(
            num_scalar_prefetch=1,
            grid=(1,),
            in_specs=[pl.BlockSpec((extra, width), lambda i, a: (rows // extra, 0))] * depth,
            out_specs=[pl.BlockSpec(s, lambda i, a: (0, 0)) for s in shapes],
        ),
        name="unpack_small",
    )(jnp.stack([here, core]).astype(jnp.int32), *pieces)


def pack_grads_kernel(depth, sizes, index_ref, *refs):
    *sources, out_ref = refs
    core = index_ref[0]
    out_ref[...] = jnp.zeros_like(out_ref)
    for z in range(depth):
        for c in range(2):
            row = 16 * c
            for source, (size, of_core) in zip(sources, sizes):
                for start in range(0, size, LANES):
                    lanes = min(LANES, size - start)
                    at = (z if of_core else 2 * z + c) * size + start
                    value = source[0:1, at : at + lanes]
                    if of_core:
                        value = jnp.where(core == c, value, 0.0)
                    out_ref[z, row : row + 1, 0:lanes] = value
                    row += 1


def pack_grads(vectors, sizes, core, depth):
    return pl.pallas_call(
        functools.partial(pack_grads_kernel, depth, sizes),
        out_shape=jax.ShapeDtypeStruct((depth, 32, LANES), f32),
        grid_spec=pltpu.PrefetchScalarGridSpec(
            num_scalar_prefetch=1,
            grid=(1,),
            in_specs=whole_specs(vectors),
            out_specs=pl.BlockSpec((depth, 32, LANES), lambda i, a: (0, 0, 0)),
        ),
        name="pack_grads",
    )(core.reshape(1).astype(jnp.int32), *vectors)


def grad_blocks_kernel(orders, ranks, index_ref, a_ref, b_ref, *refs):
    outs, held = refs[:-1], refs[-1]
    rank = index_ref[0]
    held[...] = dot_tn(a_ref[...], b_ref[...]).astype(bf16)
    width = held.shape[1] // ranks
    share = held.shape[0] // len(orders)
    for n, order in enumerate(orders):
        for which, offsets in enumerate(halves(ranks, order[0], list(range(ranks)))):
            for i, o in enumerate(offsets):
                cols = pl.ds(pl.multiple_of((rank ^ o) * width, width), width)
                outs[2 * n + which][i, 0] = held[n * share : (n + 1) * share, cols]


def grad_blocks(a, b, rank, orders, name):
    depth, ranks = lax.axis_size("fsdp") // 2, lax.axis_size("rep")
    tokens, rows, cols = a.shape[0], a.shape[1] // depth, b.shape[1]
    if cols // ranks % LANES:
        return relative_blocks(dot_tn(a, b).astype(bf16), rank, orders)
    block = (ranks // 2, depth, rows // len(orders), cols // ranks)
    outs = pl.pallas_call(
        functools.partial(grad_blocks_kernel, orders, ranks),
        out_shape=[jax.ShapeDtypeStruct(block, bf16)] * (2 * len(orders)),
        grid_spec=pltpu.PrefetchScalarGridSpec(
            num_scalar_prefetch=1,
            grid=(depth,),
            in_specs=[
                pl.BlockSpec((tokens, rows), lambda i, s: (0, i)),
                pl.BlockSpec((tokens, cols), lambda i, s: (0, 0)),
            ],
            out_specs=[pl.BlockSpec((block[0], 1) + block[2:], lambda i, s: (0, i, 0, 0))] * (2 * len(orders)),
            scratch_shapes=[pltpu.VMEM((rows, cols), bf16)],
        ),
        compiler_params=pltpu.CompilerParams(vmem_limit_bytes=40 << 20),
        cost_estimate=SHORT,
        name=name,
    )(rank.reshape(1).astype(jnp.int32), a, b)
    return [(outs[2 * n], outs[2 * n + 1]) for n in range(len(orders))]


def pre_grad_kernel(g_ref, w_ref, slope_ref, out_ref, sum_ref):
    grad = dot_nt(g_ref[...], w_ref[...]) * slope_ref[...].astype(f32)
    out_ref[...] = grad.astype(bf16)
    sum_ref[...] = jnp.sum(grad, axis=0, keepdims=True)


def pre_grads(mlp_grad, fc2_matrix, slope):
    tokens, units = slope.shape
    tile = 256
    return pl.pallas_call(
        pre_grad_kernel,
        out_shape=[jax.ShapeDtypeStruct((tokens, units), bf16), jax.ShapeDtypeStruct((1, units), f32)],
        grid=(units // tile,),
        in_specs=[
            pl.BlockSpec((tokens, D), lambda i: (0, 0)),
            pl.BlockSpec((tile, D), lambda i: (i, 0)),
            pl.BlockSpec((tokens, tile), lambda i: (0, i)),
        ],
        out_specs=[pl.BlockSpec((tokens, tile), lambda i: (0, i)), pl.BlockSpec((1, tile), lambda i: (0, i))],
        compiler_params=pltpu.CompilerParams(vmem_limit_bytes=40 << 20),
        cost_estimate=SHORT,
        name="pre_grad",
    )(mlp_grad, fc2_matrix, slope)


def product_kernel(half_ref, first_ref, second_ref, w_ref, out1_ref, out2_ref):
    out1_ref[...] = dot(first_ref[...], w_ref[...])
    out2_ref[...] = dot(second_ref[...], w_ref[...])


def product_nt_kernel(half_ref, first_ref, second_ref, w_ref, out1_ref, out2_ref, held):
    @pl.when(pl.program_id(0) == 0)
    def _():
        held[...] = w_ref[...].T

    out1_ref[...] = dot(first_ref[...], held[...])
    out2_ref[...] = dot(second_ref[...], held[...])


def product(a, weight, flipped, half, name, cost=SHORT):
    rows, tile = a.shape[0] // 2, 128
    count = rows // tile
    out = pl.BlockSpec((tile, D), lambda i, h: (i, 0))
    return pl.pallas_call(
        product_nt_kernel if flipped else product_kernel,
        out_shape=[jax.ShapeDtypeStruct((rows, D), f32)] * 2,
        grid_spec=pltpu.PrefetchScalarGridSpec(
            num_scalar_prefetch=1,
            grid=(count,),
            in_specs=[
                pl.BlockSpec((tile, a.shape[1]), lambda i, h: (i + h[0] * count, 0)),
                pl.BlockSpec((tile, a.shape[1]), lambda i, h: (i + (1 - h[0]) * count, 0)),
                pl.BlockSpec(weight.shape, lambda i, h: (0, 0)),
            ],
            out_specs=[out, out],
            scratch_shapes=[pltpu.VMEM(weight.shape[::-1], bf16)] if flipped else [],
        ),
        compiler_params=pltpu.CompilerParams(vmem_limit_bytes=32 << 20),
        cost_estimate=cost,
        name=name,
    )(jnp.asarray(half, jnp.int32).reshape(1), a, a, weight)


def add_sums(sum_ref, values):
    @pl.when(pl.program_id(0) == 0)
    def _():
        sum_ref[...] = jnp.zeros_like(sum_ref)

    for row, value in enumerate(values):
        sum_ref[row : row + 1, :] += jnp.sum(value, axis=0, keepdims=True)


def input_kernel(own_ref, sent_ref, tok_ref, grad_ref, vec_ref, out_ref, sum_ref):
    grad = own_ref[...] + sent_ref[...]
    normal, inverse = normalize(tok_ref[...].astype(f32))
    out_ref[...] = grad_ref[...] + norm_back(grad, normal, inverse, vec_ref[0:1, :])
    add_sums(sum_ref, (grad * normal, grad))


def output_kernel(own_ref, sent_ref, cot_ref, resid_ref, vec_ref, out_ref, sum_ref):
    mlp = own_ref[...] + sent_ref[...] + vec_ref[8:9, :]
    out_ref[...] = (resid_ref[...] + vec_ref[9:10, :] * mlp).astype(bf16)
    out_grad = cot_ref[...].astype(f32)
    add_sums(sum_ref, (out_grad * vec_ref[9:10, :], out_grad * mlp))


def finish(kernel, dtype, parts, vecs, name):
    rows, tile = parts[0].shape[0], 64
    part = pl.BlockSpec((tile, D), lambda i: (i, 0))
    return pl.pallas_call(
        kernel,
        out_shape=[jax.ShapeDtypeStruct((rows, D), dtype), jax.ShapeDtypeStruct((8, D), f32)],
        grid=(rows // tile,),
        in_specs=[part] * len(parts) + [pl.BlockSpec(vecs.shape, lambda i: (0, 0))],
        out_specs=[part, pl.BlockSpec((8, D), lambda i: (0, 0))],
        compiler_params=pltpu.CompilerParams(vmem_limit_bytes=24 << 20),
        cost_estimate=SHORT,
        name=name,
    )(*parts, vecs)


def residual_kernel(own_ref, sent_ref, tok_ref, vec_ref, attn_ref, resid_ref, input_ref):
    attn = own_ref[...] + sent_ref[...] + vec_ref[4:5, :]
    resid = tok_ref[...].astype(f32) + vec_ref[5:6, :] * attn
    attn_ref[...] = attn
    resid_ref[...] = resid
    normal, _ = normalize(resid)
    input_ref[...] = (normal * vec_ref[6:7, :] + vec_ref[7:8, :]).astype(bf16)


def residual(own, sent, tok, vecs):
    rows, tile = own.shape[0], 64
    part = pl.BlockSpec((tile, D), lambda i: (i, 0))
    return pl.pallas_call(
        residual_kernel,
        out_shape=[jax.ShapeDtypeStruct((rows, D), t) for t in (f32, f32, bf16)],
        grid=(rows // tile,),
        in_specs=[part] * 3 + [pl.BlockSpec(vecs.shape, lambda i: (0, 0))],
        out_specs=[part] * 3,
        compiler_params=pltpu.CompilerParams(vmem_limit_bytes=24 << 20),
        cost_estimate=SHORT,
        name="residual",
    )(own, sent, tok, vecs)


def scaled_kernel(own_ref, other_ref, vec_ref, out_ref):
    rows = own_ref.shape[0]
    for n, ref in enumerate((own_ref, other_ref)):
        out_ref[n * rows : (n + 1) * rows, :] = (ref[...].astype(f32) * vec_ref[9:10, :]).astype(bf16)


def scaled(own, other, vecs):
    return pl.pallas_call(
        scaled_kernel,
        out_shape=jax.ShapeDtypeStruct((2 * own.shape[0], D), bf16),
        compiler_params=pltpu.CompilerParams(vmem_limit_bytes=24 << 20),
        cost_estimate=SHORT,
        name="scaled",
    )(own, other, vecs)


def units_kernel(n_ref, w_ref, b_ref, act_ref, slope_ref):
    act, slope = gelu_pair(dot(n_ref[...], w_ref[...]) + b_ref[...])
    act_ref[...] = act.astype(bf16)
    slope_ref[...] = slope.astype(bf16)


def hidden_units(normed, weight, bias):
    tokens, units = normed.shape[0], weight.shape[1]
    tile = 256
    part = pl.BlockSpec((tokens, tile), lambda i: (0, i))
    return pl.pallas_call(
        units_kernel,
        out_shape=[jax.ShapeDtypeStruct((tokens, units), bf16)] * 2,
        grid=(units // tile,),
        in_specs=[
            pl.BlockSpec((tokens, D), lambda i: (0, 0)),
            pl.BlockSpec((D, tile), lambda i: (0, i)),
            pl.BlockSpec((1, tile), lambda i: (0, i)),
        ],
        out_specs=[part, part],
        compiler_params=pltpu.CompilerParams(vmem_limit_bytes=32 << 20),
        cost_estimate=SHORT,
        name="units",
    )(normed, weight, bias)


def norm_grad_kernel(own_ref, sent_ref, resid_ref, cot_ref, attn_ref, vec_ref, grad_ref, scaled_ref, sum_ref):
    grad = own_ref[...] + sent_ref[...]
    normal, inverse = normalize(resid_ref[...])
    resid_grad = cot_ref[...].astype(f32) + norm_back(grad, normal, inverse, vec_ref[6:7, :])
    scaled = resid_grad * vec_ref[5:6, :]
    grad_ref[...] = resid_grad
    scaled_ref[...] = scaled.astype(bf16)

    @pl.when(pl.program_id(0) == 0)
    def _():
        sum_ref[...] = jnp.zeros_like(sum_ref)

    for row, value in enumerate((grad * normal, grad, scaled, resid_grad * attn_ref[...])):
        sum_ref[row : row + 1, :] += jnp.sum(value, axis=0, keepdims=True)


def norm_grads(own, sent, resid, cot, attn_out, vecs):
    rows, tile = own.shape[0], 64
    part = pl.BlockSpec((tile, D), lambda i: (i, 0))
    return pl.pallas_call(
        norm_grad_kernel,
        out_shape=[
            jax.ShapeDtypeStruct((rows, D), f32), jax.ShapeDtypeStruct((rows, D), bf16),
            jax.ShapeDtypeStruct((8, D), f32),
        ],
        grid=(rows // tile,),
        in_specs=[part] * 5 + [pl.BlockSpec(vecs.shape, lambda i: (0, 0))],
        out_specs=[part, part, pl.BlockSpec((8, D), lambda i: (0, 0))],
        compiler_params=pltpu.CompilerParams(vmem_limit_bytes=24 << 20),
        cost_estimate=SHORT,
        name="norm_grad",
    )(own, sent, resid, cot, attn_out, vecs)


def proj_grad_kernel(head_rows, c_ref, g_ref, out_ref):
    wide = out_ref.shape[1]
    for side in range(2):
        grad = dot_tn(c_ref[...], g_ref[:, side * wide : (side + 1) * wide]).astype(bf16)
        for z in range(grad.shape[0] // head_rows):
            at = (2 * z + side) * head_rows
            out_ref[at : at + head_rows, :] = grad[z * head_rows : (z + 1) * head_rows]


def packed_proj_grad(context, attn_grad, head_rows):
    wide = D // 2
    return pl.pallas_call(
        functools.partial(proj_grad_kernel, head_rows),
        out_shape=jax.ShapeDtypeStruct((D, wide), bf16),
        compiler_params=pltpu.CompilerParams(vmem_limit_bytes=32 << 20),
        cost_estimate=SHORT,
        name="proj_grad",
    )(context, attn_grad)


def qkv_grad_kernel(orders, ranks, depth, per, index_ref, n_ref, *refs):
    grads, p_ref = refs[: 3 * per], refs[3 * per]
    outs, held = refs[3 * per + 1 : -1], refs[-1]
    rank = index_ref[0]
    normed = n_ref[...]
    for number in range(3):
        pieces = [g[...] for g in grads[number * per : (number + 1) * per]]
        wide = per * LANES
        joined = pieces[0] if per == 1 else jnp.concatenate(pieces, axis=1)
        held[:, number * wide : (number + 1) * wide] = dot_tn(normed, joined).astype(bf16)
    held[:, 3 * per * LANES :] = p_ref[...]
    width = held.shape[1] // ranks
    rows = held.shape[0] // depth
    share = rows // len(orders)
    for n, order in enumerate(orders):
        for which, offsets in enumerate(halves(ranks, order[0], list(range(ranks)))):
            for i, o in enumerate(offsets):
                cols = pl.ds(pl.multiple_of((rank ^ o) * width, width), width)
                for z in range(depth):
                    at = z * rows + n * share
                    outs[2 * n + which][i, z] = held[at : at + share, cols]


def qkv_grad_blocks(normed, grads, proj_packed, part, parts, rank, orders):
    depth, ranks = lax.axis_size("fsdp") // 2, lax.axis_size("rep")
    per = len(grads) // 3
    cols = 4 * per * LANES
    block = (ranks // 2, depth, D // depth // len(orders), cols // ranks)
    tokens = normed.shape[0] // 3
    outs = pl.pallas_call(
        functools.partial(qkv_grad_kernel, orders, ranks, depth, per),
        out_shape=[jax.ShapeDtypeStruct(block, bf16)] * (2 * len(orders)),
        grid_spec=pltpu.PrefetchScalarGridSpec(
            num_scalar_prefetch=1,
            grid=(1,),
            in_specs=[pl.BlockSpec((tokens, D), lambda i, a: (1, 0))]
            + whole_specs(grads)
            + [pl.BlockSpec((D, per * LANES), lambda i, a: (0, part))],
            out_specs=[pl.BlockSpec(block, lambda i, a: (0, 0, 0, 0))] * (2 * len(orders)),
            scratch_shapes=[pltpu.VMEM((D, cols), bf16)],
        ),
        compiler_params=pltpu.CompilerParams(vmem_limit_bytes=40 << 20),
        cost_estimate=SHORT,
        name="qkv_grad",
    )(rank.reshape(1).astype(jnp.int32), normed, *grads, proj_packed)
    return [(outs[2 * n], outs[2 * n + 1]) for n in range(len(orders))]


def spread_lanes(tags, width):
    return jnp.concatenate([tags] * (width // LANES), axis=1)


def project_kernel(need_ref, n_ref, w_ref, b_ref, q_ref, k_ref, v_ref):
    row = pl.program_id(0)
    wide = q_ref.shape[1]

    @pl.when(need_ref[row] > 0)
    def _():
        n = n_ref[...]
        for i, ref in enumerate((q_ref, k_ref, v_ref)):
            out = dot(n, w_ref[:, i * wide : (i + 1) * wide]) + b_ref[0:1, i * wide : (i + 1) * wide]
            if i == 0:
                out = out.astype(bf16).astype(f32) * HEAD_DIM ** (-0.5)
            ref[...] = out.astype(bf16)

    @pl.when(need_ref[row] == 0)
    def _():
        for ref in (q_ref, k_ref, v_ref):
            ref[...] = jnp.zeros_like(ref)


def project(need, normed, weight, bias, wide):
    rows = normed.shape[0]
    return pl.pallas_call(
        project_kernel,
        out_shape=[jax.ShapeDtypeStruct((rows, wide), bf16)] * 3,
        grid_spec=pltpu.PrefetchScalarGridSpec(
            num_scalar_prefetch=1,
            grid=(rows // BLOCK,),
            in_specs=[
                pl.BlockSpec((BLOCK, D), lambda i, s: (i, 0)),
                pl.BlockSpec(weight.shape, lambda i, s: (0, 0)),
                pl.BlockSpec((1, 3 * wide), lambda i, s: (0, 0)),
            ],
            out_specs=[pl.BlockSpec((BLOCK, wide), lambda i, s: (i, 0))] * 3,
        ),
        compiler_params=pltpu.CompilerParams(vmem_limit_bytes=32 << 20),
        cost_estimate=SHORT,
        name="project",
    )(need, normed, weight, bias)


def norm_kernel(need_ref, info_ref, *refs):
    *sources, vec_ref, out_ref = refs
    row = pl.program_id(0)
    side = (row // info_ref[1]) % 2
    chip = row // (2 * info_ref[1])

    @pl.when(need_ref[row] > 0)
    def _():
        picked = jnp.where(chip == 0, sources[0][...], jnp.where(chip == 1, sources[2][...], sources[4][...]))
        theirs = jnp.where(chip == 0, sources[1][...], jnp.where(chip == 1, sources[3][...], sources[5][...]))
        picked = jnp.where(side == info_ref[0], picked, theirs)
        normal, _ = normalize(picked.astype(f32))
        out_ref[...] = (normal * vec_ref[0:1, :] + vec_ref[1:2, :]).astype(bf16)

    @pl.when(need_ref[row] == 0)
    def _():
        out_ref[...] = jnp.zeros_like(out_ref)


def norm_window(need, info, sources, vecs, window, count):
    per = count // BLOCK

    def spec(chip):
        def index(i, a, b):
            inside = jnp.clip(i - 2 * per * chip, 0, 2 * per - 1)
            return (inside % per, 0)

        return pl.BlockSpec((BLOCK, D), index)

    return pl.pallas_call(
        norm_kernel,
        out_shape=jax.ShapeDtypeStruct((window, D), bf16),
        grid_spec=pltpu.PrefetchScalarGridSpec(
            num_scalar_prefetch=2,
            grid=(window // BLOCK,),
            in_specs=[spec(i // 2) for i in range(6)] + [pl.BlockSpec(vecs.shape, lambda i, a, b: (0, 0))],
            out_specs=pl.BlockSpec((BLOCK, D), lambda i, a, b: (i, 0)),
        ),
        compiler_params=pltpu.CompilerParams(vmem_limit_bytes=24 << 20),
        cost_estimate=SHORT,
        name="norm_window",
    )(need, info, *sources, vecs)


def attend_kernel(lo_ref, hi_ref, first_ref, last_ref, q_ref, k_ref, v_ref, qt_ref, kt_ref, o_ref, lse_ref, s_ref, m_ref, acc_ref):
    i = pl.program_id(0)
    left = lax.broadcasted_iota(jnp.int32, (1, LANES), 1) < HEAD_DIM
    lo, hi = lo_ref[i], hi_ref[i]
    base = (first_ref.shape[0] - pl.num_programs(0)) // 2
    q = q_ref[...]
    zero = jnp.zeros_like(q)
    heads = (jnp.where(left, q, zero), jnp.where(left, zero, q))
    m_ref[...] = jnp.full_like(m_ref, MASKED)
    one_image = first_ref[base + i] == last_ref[base + i]
    folds = BLOCK // LANES

    def fold(value, combine):
        parts = [value[:, n * LANES : (n + 1) * LANES] for n in range(folds)]
        return functools.reduce(combine, parts)

    def scores(j, carry):
        at = pl.multiple_of(j * BLOCK, BLOCK)
        k = k_ref[pl.ds(at, BLOCK), :]
        inside = one_image & (first_ref[j] == first_ref[base + i]) & (last_ref[j] == first_ref[base + i])

        @pl.when(inside)
        def _():
            for h in range(2):
                s = dot_nt(heads[h], k)
                s_ref[h, j] = s
                m_ref[h] = jnp.maximum(m_ref[h], fold(s, jnp.maximum))

        @pl.when(jnp.logical_not(inside))
        def _():
            same = spread_lanes(qt_ref[...], BLOCK) == kt_ref[:, pl.ds(at, BLOCK)]
            for h in range(2):
                s = jnp.where(same, dot_nt(heads[h], k), MASKED)
                s_ref[h, j] = s
                m_ref[h] = jnp.maximum(m_ref[h], fold(s, jnp.maximum))

        return carry

    lax.fori_loop(lo, hi, scores, 0)
    tops = [jnp.max(m_ref[h], axis=1, keepdims=True) for h in range(2)]
    m_ref[...] = jnp.zeros_like(m_ref)
    acc_ref[...] = jnp.zeros_like(acc_ref)

    def mix(j, carry):
        at = pl.multiple_of(j * BLOCK, BLOCK)
        v = v_ref[pl.ds(at, BLOCK), :]
        for h in range(2):
            e = jnp.exp(s_ref[h, j] - tops[h])
            m_ref[h] += fold(e, jnp.add)
            acc_ref[h] += dot(e.astype(bf16), v)
        return carry

    lax.fori_loop(lo, hi, mix, 0)
    sums = [jnp.sum(m_ref[h], axis=1, keepdims=True) for h in range(2)]
    o_ref[...] = jnp.where(left, acc_ref[0] / sums[0], acc_ref[1] / sums[1]).astype(bf16)
    for h in range(2):
        lse = jnp.broadcast_to(tops[h] + jnp.log(sums[h]), (BLOCK, LANES))
        lse_ref[0, h : h + 1, :] = lse.T[0:1, :]


def attend(lo, hi, firsts, lasts, q, k, v, tag_cols, tag_row, own_rows, pair):
    window = q.shape[0]
    blocks = own_rows // BLOCK
    skip = (window - own_rows) // 2 // BLOCK
    return pl.pallas_call(
        attend_kernel,
        out_shape=[
            jax.ShapeDtypeStruct((own_rows, LANES), bf16),
            jax.ShapeDtypeStruct((1, 2, own_rows), f32),
        ],
        grid_spec=pltpu.PrefetchScalarGridSpec(
            num_scalar_prefetch=4,
            grid=(blocks,),
            in_specs=[
                pl.BlockSpec((BLOCK, LANES), lambda i, *_: (i + skip, pair)),
                pl.BlockSpec((window, LANES), lambda i, *_: (0, pair)),
                pl.BlockSpec((window, LANES), lambda i, *_: (0, pair)),
                pl.BlockSpec((BLOCK, LANES), lambda i, *_: (i + skip, 0)),
                pl.BlockSpec((1, window), lambda i, *_: (0, 0)),
            ],
            out_specs=[
                pl.BlockSpec((BLOCK, LANES), lambda i, *_: (i, 0)),
                pl.BlockSpec((1, 2, BLOCK), lambda i, *_: (0, 0, i)),
            ],
            scratch_shapes=[
                pltpu.VMEM((2, window // BLOCK, BLOCK, BLOCK), f32),
                pltpu.VMEM((2, BLOCK, LANES), f32),
                pltpu.VMEM((2, BLOCK, LANES), f32),
            ],
        ),
        compiler_params=pltpu.CompilerParams(vmem_limit_bytes=32 << 20),
        cost_estimate=SHORT,
        name="attend",
    )(lo, hi, firsts, lasts, q, k, v, tag_cols, tag_row)


def attend_back_kernel(
    start, stop, lo_ref, hi_ref, q_ref, k_ref, v_ref, g_ref, tc_ref, tr_ref, lse_ref, delta_ref,
    dq_ref, dk_ref, dv_ref, sum_ref, dk_acc, dv_acc, dq_acc,
):
    first = lax.broadcasted_iota(jnp.int32, (1, LANES), 1) < HEAD_DIM
    dk_acc[...] = jnp.zeros_like(dk_acc)
    dv_acc[...] = jnp.zeros_like(dv_acc)
    sum_ref[...] = jnp.zeros_like(sum_ref)

    def split(value):
        zero = jnp.zeros_like(value)
        return jnp.where(first, value, zero), jnp.where(first, zero, value)

    def visit(i, j, qs, gs, of_key, of_query):
        at_q, at_k = pl.multiple_of(i * BLOCK, BLOCK), pl.multiple_of(j * BLOCK, BLOCK)
        k = k_ref[pl.ds(at_k, BLOCK), :]
        v = v_ref[pl.ds(at_k, BLOCK), :]
        same = spread_lanes(tc_ref[pl.ds(at_k, BLOCK), :], BLOCK) == tr_ref[:, pl.ds(at_q, BLOCK)]
        ps, ds = [], []
        for h in range(2):
            s = dot_nt(k, qs[h])
            dp = dot_nt(v, gs[h])
            p = jnp.where(same, jnp.exp(s - lse_ref[0, h : h + 1, pl.ds(at_q, BLOCK)]), 0.0)
            d = p * (dp - delta_ref[0, h : h + 1, pl.ds(at_q, BLOCK)])
            ps.append(p.astype(bf16))
            ds.append(d.astype(bf16))
        if of_key:
            at = pl.multiple_of((j - start) * BLOCK, BLOCK)
            dv_acc[pl.ds(at, BLOCK), :] += dot(ps[0], gs[0]) + dot(ps[1], gs[1])
            dk_acc[pl.ds(at, BLOCK), :] += dot(ds[0], qs[0]) + dot(ds[1], qs[1])
        if of_query:
            ks = split(k)
            dq_acc[...] += dot_tn(ds[0], ks[0]) + dot_tn(ds[1], ks[1])

    def query_block(own_q, i, carry):
        at_q = pl.multiple_of(i * BLOCK, BLOCK)
        qs = split(q_ref[pl.ds(at_q, BLOCK), :])
        gs = split(g_ref[pl.ds(at_q, BLOCK), :])
        lo, hi = lo_ref[i], hi_ref[i]

        def keys(first_key, last_key, of_key):
            def body(j, carry):
                visit(i, j, qs, gs, of_key, own_q)
                return carry

            lax.fori_loop(first_key, last_key, body, 0)

        if own_q:
            dq_acc[...] = jnp.zeros_like(dq_acc)
            keys(lo, jnp.minimum(hi, start), False)
            keys(jnp.maximum(lo, stop), hi, False)
        keys(jnp.maximum(lo, start), jnp.minimum(hi, stop), True)
        if own_q:
            at = pl.multiple_of((i - start) * BLOCK, BLOCK)
            dq = dq_acc[...] * HEAD_DIM ** (-0.5)
            dq_ref[pl.ds(at, BLOCK), :] = dq.astype(bf16)
            sum_ref[0, 0:1, :] += jnp.sum(dq, axis=0, keepdims=True)
        return carry

    before = jnp.where(lo_ref[start] < start, lo_ref[start], start)
    after = jnp.maximum(hi_ref[stop - 1], stop)
    lax.fori_loop(before, start, functools.partial(query_block, False), 0)
    lax.fori_loop(start, stop, functools.partial(query_block, True), 0)
    lax.fori_loop(stop, after, functools.partial(query_block, False), 0)
    dk_ref[...] = dk_acc[...].astype(bf16)
    dv_ref[...] = dv_acc[...].astype(bf16)
    sum_ref[0, 1:2, :] = jnp.sum(dv_acc[...], axis=0, keepdims=True)


def attend_back(lo, hi, q, k, v, g, tag_cols, tag_row, lse, delta, own_rows, pair):
    window = q.shape[0]
    pairs, wide = 1, LANES
    grad_pair = pair % (g.shape[1] // LANES)
    start = (window - own_rows) // 2 // BLOCK
    stop = start + own_rows // BLOCK
    whole = lambda: pl.BlockSpec((window, LANES), lambda p, a, b: (0, pair))
    own = lambda: pl.BlockSpec((own_rows, LANES), lambda p, a, b: (0, p))
    stat = lambda: pl.BlockSpec((1, 2, window), lambda p, a, b: (pair, 0, 0))
    return pl.pallas_call(
        functools.partial(attend_back_kernel, start, stop),
        out_shape=[jax.ShapeDtypeStruct((own_rows, wide), bf16)] * 3
        + [jax.ShapeDtypeStruct((pairs, 8, LANES), f32)],
        grid_spec=pltpu.PrefetchScalarGridSpec(
            num_scalar_prefetch=2,
            grid=(pairs,),
            in_specs=[
                whole(), whole(), whole(),
                pl.BlockSpec((window, LANES), lambda p, a, b: (0, grad_pair)),
                pl.BlockSpec((window, LANES), lambda p, a, b: (0, 0)),
                pl.BlockSpec((1, window), lambda p, a, b: (0, 0)),
                stat(), stat(),
            ],
            out_specs=[own(), own(), own(), pl.BlockSpec((1, 8, LANES), lambda p, a, b: (p, 0, 0))],
            scratch_shapes=[
                pltpu.VMEM((own_rows, LANES), f32),
                pltpu.VMEM((own_rows, LANES), f32),
                pltpu.VMEM((BLOCK, LANES), f32),
            ],
        ),
        compiler_params=pltpu.CompilerParams(vmem_limit_bytes=40 << 20),
        cost_estimate=SHORT,
        name="attend_back",
    )(lo, hi, q, k, v, g, tag_cols, tag_row, lse, delta)


def on_device(
    tokens, image_ids, ln1_gain, ln1_bias, qkv_weight, query_bias, value_bias, proj_weight,
    proj_bias, scale_attn, ln2_gain, ln2_bias, fc1_weight, fc1_bias, fc2_weight, fc2_bias,
    scale_mlp, cotangent,
):
    devices = lax.axis_size("fsdp")
    depth, ranks = devices // 2, lax.axis_size("rep")
    place = lax.axis_index("fsdp")
    rank = lax.axis_index("rep")
    here, core = place // 2, place % 2
    count = tokens.shape[1]
    chip = 2 * count
    head_rows = D // devices
    ff = fc1_weight.shape[1]
    unit_rows = ff // devices
    half_heads = D // 2
    local_heads = half_heads // HEAD_DIM
    pairs = half_heads // LANES
    bits = list(range(rep_bits()))

    def in_order(own, other, axis=0):
        return jnp.where(
            core == 0,
            jnp.concatenate([own, other], axis=axis),
            jnp.concatenate([other, own], axis=axis),
        )

    def mine(value):
        return lax.dynamic_slice_in_dim(value, core * count, count, 0)

    def others(value):
        return lax.dynamic_slice_in_dim(value, (1 - core) * count, count, 0)

    def every_other(value, width, start):
        cuts = range(start * width, value.shape[1], 2 * width)
        return jnp.concatenate([value[:, c : c + width] for c in cuts], axis=1)

    def all_share(which):
        pick_cols = lambda v, w: jnp.where(which == 0, every_other(v, w, 0), every_other(v, w, 1))
        heads = lax.dynamic_slice_in_dim(
            jnp.concatenate(
                [
                    pick_cols(qkv_weight, head_rows),
                    lax.dynamic_slice_in_dim(proj_weight, which * half_heads, half_heads, 1),
                ],
                axis=1,
            ),
            rank * (2 * D // ranks), 2 * D // ranks, 1,
        )
        units = lax.dynamic_slice_in_dim(
            pick_cols(fc1_weight, unit_rows), rank * (ff // 2 // ranks), ff // 2 // ranks, 1
        )
        return jnp.concatenate([heads, units], axis=1)

    if head_rows % LANES:
        kept, given = all_share(core), all_share(1 - core)
    else:
        kept, given = weight_share(
            rank, core, qkv_weight, proj_weight, fc1_weight, ranks, head_rows, unit_rows
        )
    wide1 = 2 * D // ranks
    got = swap_cores(given)
    is_proj = rank * wide1 >= 3 * half_heads
    own1 = in_order(kept[:, :wide1], jnp.where(is_proj, given[:, :wide1], got[:, :wide1]))
    own2 = in_order(kept[:, wide1:], got[:, wide1:])
    own3 = lax.dynamic_slice_in_dim(fc2_weight, rank * (D // ranks), D // ranks, 1)
    small = (
        ln1_gain, ln1_bias, query_bias, value_bias, proj_bias, scale_attn, ln2_gain, ln2_bias,
        fc2_bias, scale_mlp, fc1_bias, (image_ids[0] + 1).astype(bf16),
    )
    sizes = [v.shape[0] for v in small]
    slots = slot_lists(sizes)
    width = 2 * D // ranks
    small = pack_small(small, width, slots)
    small_other = swap_cores(small)
    rows1, rows3 = own1.shape[0], own3.shape[0]
    tok, cot = tokens[0], cotangent[0]
    tok_other = swap_cores(tok)
    cot_other = swap_cores(cot)
    own1 = jnp.concatenate([own1, small, small_other])
    own1, own2, own3, tok = tie(own1, own2, own3, tok)
    pieces1 = fetch_z(own1)
    tok, pieces1[1] = tie(tok, pieces1[1])
    behind, ahead = from_chip(tok, 1), from_chip(tok, -1)
    gather1 = Gather(pieces1, rows1, "gather1")
    gather1.send()
    behind_other, ahead_other = swap_cores(behind), swap_cores(ahead)
    for _ in bits[1:]:
        gather1.send()

    vec_rows, fc1_shift, all_tags = unpack_small(
        pieces1, slots, rows1, here, core, ff // 2, devices * count
    )
    vector = lambda i: vec_rows[i : i + 1]
    (
        attn_gain, attn_shift, query_shift, value_shift, proj_shift, attn_scale, mlp_gain,
        mlp_shift, fc2_shift, mlp_scale,
    ) = map(vector, range(10))
    core_part = lambda vec: jnp.where(
        core == 0, every_other(vec, head_rows, 0), every_other(vec, head_rows, 1)
    )

    window = 3 * chip
    padded = jnp.concatenate(
        [jnp.zeros((1, chip), f32), all_tags, jnp.full((1, chip), 1e6, f32)], axis=1
    )
    tag_row = lax.dynamic_slice(padded, (0, here * chip), (1, window))
    tags = tag_row.reshape(window)
    firsts, lasts = tags[::BLOCK], tags[BLOCK - 1 :: BLOCK]
    real = firsts * (1e6 - firsts) > 0
    below = jnp.sum((tag_row < firsts[:, None]).astype(jnp.int32), axis=1)
    upto = jnp.sum((tag_row <= lasts[:, None]).astype(jnp.int32), axis=1)
    blocks = window // BLOCK
    block_lo = jnp.where(real, below // BLOCK, 0)
    block_hi = jnp.where(real, (upto + BLOCK - 1) // BLOCK, 0)
    own_lo, own_hi = chip // BLOCK, 2 * chip // BLOCK
    numbers = jnp.arange(blocks)
    need = jnp.logical_and(numbers >= block_lo[own_lo], numbers < block_hi[own_hi - 1]).astype(jnp.int32)
    firsts, lasts = firsts.astype(jnp.int32), lasts.astype(jnp.int32)
    tag_cols = jnp.broadcast_to(tags[:, None], (window, LANES))

    info = jnp.stack([core, jnp.int32(count // BLOCK)]).astype(jnp.int32)
    normed1 = norm_window(
        need, info, (behind, behind_other, tok, tok_other, ahead, ahead_other), vec_rows, window, count
    )

    normed1, own2 = tie(normed1, own2)
    pieces2 = fetch_z(own2)
    normed1 = gather1.arrive(normed1)
    qkv_matrix, proj_matrix = gather1.assemble(here, rank, head_rows)

    shifts = jnp.concatenate(
        [core_part(query_shift), jnp.zeros((1, half_heads), f32), core_part(value_shift)], axis=1
    )
    queries, keys, values = project(need, normed1, qkv_matrix, shifts, half_heads)

    contexts, lses = [], []
    los = block_lo[own_lo:own_hi]
    los, queries = tie(los, queries)
    for pair in range(pairs):
        if pair == 1:
            los, own3, *pieces2 = tie(los, own3, *pieces2)
            gather2 = Gather(pieces2, rows1, "gather2")
            los = gather2.send(los)
            pieces3 = fetch_z(own3)
        if pair == 2:
            los = gather2.arrive(los)
            los = gather2.send(los)
        if pair == 3:
            los = gather2.arrive(los)
            for _ in bits[2:]:
                los = gather2.arrive(gather2.send(los))
            los, *pieces3 = tie(los, *pieces3)
            gather3 = Gather(pieces3, rows3, "gather3")
            los = gather3.send(los)
        context, lse = attend(
            los, block_hi[own_lo:own_hi], firsts, lasts, queries, keys, values, tag_cols,
            tag_row, chip, pair,
        )
        los, context = tie(los, context)
        contexts.append(context)
        lses.append(lse)
    context = jnp.concatenate(contexts, axis=1)
    lse_rows = jnp.concatenate(lses).reshape(local_heads, chip)
    context = gather3.arrive(context)
    context = gather3.send(context)
    own, given = product(context, proj_matrix, False, core, "attn_out")
    attn_out, resid, mlp_input = residual(own, swap_cores(given), tok, vec_rows)
    mlp_input = jnp.concatenate([mlp_input, swap_cores(mlp_input)])
    fc1_matrix = gather2.assemble(here, rank)
    activated, slope = hidden_units(mlp_input, fc1_matrix, fc1_shift)
    mlp_grad = scaled(cot, cot_other, vec_rows)
    both = [bits, bits[::-1]]
    for _ in bits[2:]:
        activated = gather3.send(gather3.arrive(activated))
    fc2_blocks = gather3.arrive(grad_blocks(activated, mlp_grad, rank, both, "fc2_grad"))
    reduce3 = Reduce(fc2_blocks, here, both)
    mlp_grad = reduce3.send(mlp_grad)
    fc2_matrix = gather3.assemble(here, rank)
    pre_grad, fc1_bias_part = pre_grads(mlp_grad, fc2_matrix, slope)
    reduce2 = Reduce(grad_blocks(mlp_input, pre_grad, rank, both, "fc1_grad"), here, both)
    pre_grad, _ = tie(pre_grad, [give for _, _, give in reduce2.held])
    own, given = product(pre_grad, fc1_matrix, True, 0, "mlp_in_grad")
    own, given = reduce3.arrive(own, given)
    for _ in bits[2:]:
        own, given = reduce3.arrive(*reduce3.send(own, given))
    own, given = reduce3.send(own, given)
    sent = swap_cores(given)
    resid_grad, attn_grad, norm_sums = norm_grads(own, sent, resid, cot, attn_out, vec_rows)
    both_grads = jnp.zeros((chip, D), bf16)
    for part, which in ((attn_grad, core), (swap_cores(attn_grad), 1 - core)):
        both_grads = lax.dynamic_update_slice_in_dim(both_grads, part, which * count, 0)
    attn_grad = both_grads
    context_grad = dot_nt(attn_grad, proj_matrix).astype(bf16)
    head_of = (
        lax.broadcasted_iota(jnp.int32, (local_heads, half_heads), 1) // HEAD_DIM
        == lax.broadcasted_iota(jnp.int32, (local_heads, half_heads), 0)
    ).astype(f32)
    row_delta = lax.dot_general(
        head_of, context_grad.astype(f32) * context.astype(f32), (((1,), (1,)), ((), ())),
        precision=lax.Precision.HIGHEST, preferred_element_type=f32,
    )
    stats = jnp.concatenate([lse_rows, row_delta])
    context_grad, activated, attn_grad = tie(context_grad, activated, attn_grad)
    chunk = half_heads // 2
    chunks = [context_grad[:, :chunk], context_grad[:, chunk:]]
    grads_behind, grads_ahead = zip(*[(from_chip(c, 1), from_chip(c, -1)) for c in chunks])
    stats_behind, stats_ahead = from_chip(stats, 1), from_chip(stats, -1)
    proj_grad = packed_proj_grad(context, attn_grad, head_rows)
    stat_window = jnp.concatenate([stats_behind, stats, stats_ahead], axis=1)
    by_pair = lambda s: s.reshape(pairs, 2, window)
    lse_window, delta_window = by_pair(stat_window[:local_heads]), by_pair(stat_window[local_heads:])

    half_pairs = pairs // 2
    half_width = half_heads // 2

    def first_group(parts, number):
        grads = [g for kind in zip(*parts) for g in kind]
        return Reduce(
            qkv_grad_blocks(normed1, grads, proj_grad, number, 2, rank, both), here, both
        )

    parts, sums = [], []
    out_own, out_given = product(activated, fc2_matrix, False, 0, "mlp_out", FILLER)
    output_rows, out_sums = finish(
        output_kernel, bf16, (out_own, swap_cores(out_given), cot, resid), vec_rows, "output"
    )
    first, delta_window, lo, out_sums = settle(
        ((grads_behind[0], grads_ahead[0]), delta_window, block_lo, out_sums), (reduce3, "received")
    )
    grad_windows = [jnp.concatenate([first[0], chunks[0], first[1]])]
    for pair in range(pairs):
        if pair == 0:
            lo = reduce3.arrive(lo)
            lo = reduce2.send(lo)
        if pair == 1:
            lo, second = settle((lo, (grads_behind[1], grads_ahead[1])), (reduce2, "received"))
            grad_windows.append(jnp.concatenate([second[0], chunks[1], second[1]]))
            lo = reduce2.arrive(lo)
            lo = reduce3.send_z(lo)
            for _ in bits[2:]:
                lo = reduce2.arrive(reduce2.send(lo))
            lo = reduce2.send(lo)
        if pair == 2:
            lo = settle(lo, (reduce2, "received"), (reduce3, "pieces"))
            lo = reduce2.arrive(lo)
            lo = reduce2.send_z(lo)
            reduce1a = first_group(parts, 0)
            lo = reduce1a.send(lo)
        if pair == 3:
            lo = settle(lo, (reduce2, "pieces"), (reduce1a, "received"))
            lo = reduce3.arrive_z(lo)
            lo = reduce2.arrive_z(lo)
            fc2_part = reduce3.total.astype(bf16)
            fc1_part = reduce2.total.astype(bf16)
            split = fc2_part.shape[0] // fc1_part.shape[0]
            mlp_spread = Spread(jnp.concatenate([fc1_part, *jnp.split(fc2_part, split)], axis=1))
            lo = mlp_spread.send(lo)
            lo = reduce1a.arrive(lo)
            for _ in bits[2:]:
                lo = reduce1a.arrive(reduce1a.send(lo))
            lo = reduce1a.send(lo)
        *grads, total = attend_back(
            lo, block_hi, queries, keys, values, grad_windows[pair * 2 // pairs], tag_cols, tag_row, lse_window,
            delta_window, chip, pair,
        )
        lo, *grads = tie(lo, *grads)
        parts.append(grads)
        sums.append(total[0])

    parts[-1] = settle(parts[-1], (mlp_spread, "arrays"))
    parts[-1] = reduce1a.arrive(parts[-1])
    parts[-1] = reduce1a.send_z(parts[-1])
    reduce1b = first_group(parts[half_pairs:], 1)
    parts[-1] = reduce1b.send(parts[-1])
    every = [jnp.concatenate(p, axis=1) for p in zip(*parts)]

    factor = 1.0 / math.sqrt(count * devices * ranks)
    in_own, in_given = product(
        jnp.concatenate(every, axis=1), qkv_matrix, True, core, "attn_in_grad"
    )
    tail = (in_own, in_given)
    tail = settle(tail, (reduce1b, "received"), (reduce1a, "pieces"))
    for _ in bits[1:]:
        tail = reduce1b.arrive(tail)
        tail = reduce1b.send(tail)
    in_own, in_given = tail
    input_rows, in_sums = finish(
        input_kernel, f32, (in_own, swap_cores(in_given), tok, resid_grad), vec_rows, "input_grad"
    )

    vectors = (
        in_sums[0:1], in_sums[1:2],
        jnp.concatenate([s[0:1] for s in sums], axis=1), jnp.concatenate([s[1:2] for s in sums], axis=1),
        norm_sums[2:3], norm_sums[3:4], norm_sums[0:1], norm_sums[1:2],
        out_sums[0:1], out_sums[1:2], fc1_bias_part,
    )
    of_core = [number in (2, 3, 10) for number in range(11)]
    partial = pack_grads(vectors, list(zip(sizes, of_core)), core, depth)
    vec_width = D // ranks
    half_of = lambda which: lax.dynamic_slice_in_dim(partial, which * 16, 16, 1)
    partial = half_of(core) + swap_cores(half_of(1 - core))
    vec_high = lax.reduce_precision(partial, 8, 7)
    side_by_side = 2 if vec_width >= 2 * LANES else 1
    extra = jnp.concatenate([vec_high, partial - vec_high], axis=side_by_side).astype(bf16)
    extra = jnp.pad(extra, ((0, 0), (0, 0), (0, vec_width - extra.shape[2])))
    extra = reduce1b.arrive(extra)
    extra = reduce1b.send_z(extra, extra=extra)
    for _ in bits[1:]:
        mlp_spread.send(extra)

    reduce1a.arrive_z()
    reduce1b.arrive_z()
    rows = reduce1a.total.shape[0]
    vec_total = reduce1b.total[rows:]
    if side_by_side == 2:
        vec_total = vec_total[:, :LANES] + vec_total[:, LANES : 2 * LANES]
    else:
        vec_total = vec_total[:16] + vec_total[16:]
    vec_high = lax.reduce_precision(vec_total, 8, 7)
    sides = [jnp.pad(v, ((0, 16), (0, vec_width - LANES))) for v in (vec_high, vec_total - vec_high)]
    payload = jnp.concatenate(
        [
            jnp.concatenate([reduce1a.total, reduce1b.total[:rows]], axis=1),
            jnp.concatenate(sides, axis=1),
        ]
    ).astype(bf16)
    payload = settle(payload, (mlp_spread, "arrays"))
    first_spread = Spread(payload)
    for bit in bits:
        first_spread.send()

    mlp_cols = fc1_part.shape[1]
    fc1_full = mlp_spread.blocks(rank, 0, mlp_cols)
    fc2_width = fc2_part.shape[1]
    fc2_full = tie(*[mlp_spread.blocks(rank, mlp_cols + n * fc2_width, fc2_width) for n in range(split)])
    grad_fc2 = jnp.concatenate(fc2_full).astype(f32) * factor
    first_a = first_spread.blocks(rank, 0, vec_width)
    first_b = first_spread.blocks(rank, vec_width, vec_width)
    totals = sum(
        part[rows : rows + 16, r * vec_width : r * vec_width + LANES].astype(f32)
        for part in (first_a, first_b)
        for r in range(ranks)
    ) * factor
    first_a, first_b = first_a[:rows], first_b[:rows]

    def rows_of(value, index):
        return lax.dynamic_slice_in_dim(value, index * head_rows, head_rows, 0)

    def interleave(own, other, width):
        cuts = range(0, own.shape[1], width)
        zipped = lambda a, b: jnp.concatenate(
            [v[:, c : c + width] for c in cuts for v in (a, b)], axis=1
        )
        return jnp.where(core == 0, zipped(own, other), zipped(other, own)).astype(f32) * factor

    fc1_other = swap_cores(rows_of(fc1_full, 1 - core))
    grad_fc1 = interleave(rows_of(fc1_full, core), fc1_other, unit_rows)
    qkv_full = jnp.concatenate(
        [
            part[:, n * half_width : (n + 1) * half_width]
            for n in range(3)
            for part in (first_a, first_b)
        ],
        axis=1,
    )
    grad_qkv = interleave(rows_of(qkv_full, core), swap_cores(rows_of(qkv_full, 1 - core)), head_rows)
    proj_part = jnp.concatenate([first_a[:, 3 * half_width :], first_b[:, 3 * half_width :]], axis=1)
    grad_proj = jnp.concatenate([proj_part[:head_rows], proj_part[head_rows:]], axis=1).astype(f32) * factor

    small_grads = [totals[i, : sizes[i]] for i in range(10)]
    lines = -(-sizes[10] // LANES)
    small_grads.append(totals[10 : 10 + lines].reshape(-1))
    (
        grad_attn_gain, grad_attn_shift, grad_query_shift, grad_value_shift, grad_proj_shift,
        grad_attn_scale, grad_mlp_gain, grad_mlp_shift, grad_fc2_shift, grad_mlp_scale, grad_fc1_shift,
    ) = small_grads

    return (
        output_rows[None],
        input_rows[None],
        grad_attn_gain,
        grad_attn_shift,
        grad_qkv,
        grad_query_shift,
        grad_value_shift,
        grad_proj,
        grad_proj_shift,
        grad_attn_scale,
        grad_mlp_gain,
        grad_mlp_shift,
        grad_fc1,
        grad_fc1_shift,
        grad_fc2,
        grad_fc2_shift,
        grad_mlp_scale,
    )


def solution(mesh):
    rows = P("fsdp", None)
    vec = P("fsdp")
    tok = P("rep", "fsdp", None)
    return jax.shard_map(
        on_device,
        mesh=mesh,
        in_specs=(
            tok, P("rep", "fsdp"), vec, vec, rows, vec, vec, rows, vec, vec, vec, vec, rows, vec,
            rows, vec, vec, tok,
        ),
        out_specs=(
            tok, tok, vec, vec, rows, vec, vec, rows, vec, vec, vec, vec, rows, vec, rows, vec, vec,
        ),
        check_vma=False,
    )
```

```python
import functools
import math

import jax
import jax.numpy as jnp
from jax import lax
from jax.experimental import pallas as pl
from jax.experimental.pallas import tpu as pltpu
from jax.sharding import PartitionSpec as P

D = 1024
HEADS = 16
HEAD_DIM = 64
LANES = 128

EPSILON = 1e-06
MASKED = -1e30
BLOCK = 256

SHORT = pl.CostEstimate(flops=1, transcendentals=0, bytes_accessed=1)
FILLER = pl.CostEstimate(flops=1 << 33, transcendentals=0, bytes_accessed=1 << 23)

f32 = jnp.float32
bf16 = jnp.bfloat16


def normalize(features):
    row_mean = jnp.mean(features, axis=-1, keepdims=True)
    centred = features - row_mean
    variance = jnp.mean(centred * centred, axis=-1, keepdims=True)
    inverse = lax.rsqrt(variance + EPSILON)
    return centred * inverse, inverse


def norm_back(gradient, normal, inverse, gain_vec):
    scaled = gradient * gain_vec
    mean_first = jnp.mean(scaled, axis=-1, keepdims=True)
    mean_second = jnp.mean(scaled * normal, axis=-1, keepdims=True)
    return inverse * (scaled - mean_first - normal * mean_second)


def gelu_pair(values):
    cumulative = 0.5 * (1.0 + lax.erf(values * 2.0 ** (-0.5)))
    density = jnp.exp(-0.5 * values * values) * (2.0 * math.pi) ** (-0.5)
    return (values * cumulative, cumulative + values * density)


def dot(a, b):
    return jnp.dot(a, b, preferred_element_type=f32)


def dot_nt(a, b):
    return lax.dot_general(a, b, (((1,), (1,)), ((), ())), preferred_element_type=f32)


def dot_tn(a, b):
    return lax.dot_general(a, b, (((0,), (0,)), ((), ())), preferred_element_type=f32)


def swap_cores(value):
    size = lax.axis_size("fsdp")
    return lax.ppermute(value, "fsdp", [(i, i ^ 1) for i in range(size)])


def along_z(value, by):
    size = lax.axis_size("fsdp")
    return lax.ppermute(value, "fsdp", [(i, (i + 2 * by) % size) for i in range(size)])


def from_chip(value, by):
    size = lax.axis_size("fsdp")
    pairs = [(i, i + 2 * by) for i in range(size) if 0 <= i + 2 * by < size]
    return lax.ppermute(value, "fsdp", pairs)


def across_rep(value, bit):
    size = lax.axis_size("rep")
    return lax.ppermute(value, "rep", [(i, i ^ (1 << bit)) for i in range(size)])


def pick(value, index, axis):
    return lax.dynamic_index_in_dim(value, index, axis, keepdims=False)


def rep_bits():
    return lax.axis_size("rep").bit_length() - 1


def tie(*values):
    return lax.optimization_barrier(values)


def settle(value, *fields):
    held = [getattr(o, name) for o, name in fields]
    value, held = lax.optimization_barrier((value, held))
    for (o, name), new in zip(fields, held):
        setattr(o, name, new)
    return value


def fetch_z(own):
    return [own] + [along_z(own, k) for k in range(1, lax.axis_size("fsdp") // 2)]


class Gather:
    def __init__(self, pieces, rows, name):
        self.rows, self.cols, self.name = rows, pieces[0].shape[1], name
        half = rows // 2
        bits = list(range(rep_bits()))
        self.orders = [bits, bits[::-1]]
        self.parts = [
            [(jnp.stack([p[:half] for p in pieces])[None], [0])],
            [(jnp.stack([p[half:rows] for p in pieces])[None], [0])],
        ]
        self.at = 0

    def send(self, *values):
        whole = [
            (ps[0][0] if len(ps) == 1 else jnp.concatenate([a for a, _ in ps]), [o for _, os in ps for o in os])
            for ps in self.parts
        ]
        values, arrays = lax.optimization_barrier((values, [a for a, _ in whole]))
        self.parts = []
        for array, (_, offsets), order in zip(arrays, whole, self.orders):
            flip = 1 << order[self.at]
            received = across_rep(array, order[self.at])
            self.parts.append([(array, offsets), (received, [o ^ flip for o in offsets])])
        self.at += 1
        return values[0] if len(values) == 1 else values

    def arrive(self, value):
        value, arrays = lax.optimization_barrier((value, [a for ps in self.parts for a, _ in ps]))
        self.parts = [[(arrays.pop(0), o) for _, o in ps] for ps in self.parts]
        return value

    def assemble(self, here, rank, tail_rows=0):
        depth, ranks = lax.axis_size("fsdp") // 2, lax.axis_size("rep")
        sources, plan = [], []
        for number, parts in enumerate(self.parts):
            for array, offsets in parts:
                sources.append(array)
                plan.append((number, offsets))
        dtype = sources[0].dtype
        shape = (depth * self.rows, ranks * self.cols)
        shapes = [jax.ShapeDtypeStruct(shape, dtype)]
        if tail_rows:
            tail = shape[1] // 4
            shapes = [
                jax.ShapeDtypeStruct((shape[0], shape[1] - tail), dtype),
                jax.ShapeDtypeStruct((depth * tail_rows, 2 * tail), dtype),
            ]
        out = pl.pallas_call(
            functools.partial(assemble_kernel, plan, depth, self.rows, self.cols, tail_rows),
            out_shape=shapes,
            grid_spec=pltpu.PrefetchScalarGridSpec(
                num_scalar_prefetch=1,
                grid=(1,),
                in_specs=[pl.BlockSpec(memory_space=pl.ANY)] * len(sources),
                out_specs=[pl.BlockSpec(memory_space=pl.ANY)] * len(shapes),
                scratch_shapes=[
                    pltpu.VMEM(shape, dtype),
                    pltpu.SemaphoreType.DMA((2 * ranks * depth,)),
                    pltpu.SemaphoreType.DMA((3 * depth,)),
                ],
            ),
            compiler_params=pltpu.CompilerParams(vmem_limit_bytes=16 << 20),
            cost_estimate=SHORT,
            name=self.name,
        )(jnp.stack([here, rank]).astype(jnp.int32), *sources)
        return out if tail_rows else out[0]


def assemble_kernel(plan, depth, rows, cols, tail_rows, index_ref, *refs):
    count = len(plan)
    sources = refs[:count]
    targets = refs[count : count + (2 if tail_rows else 1)]
    held, in_sems, out_sems = refs[-3:]
    here, rank = index_ref[0], index_ref[1]
    half = rows // 2
    waits = [[] for _ in range(depth)]
    number = 0
    for k in range(depth):
        place = lax.rem(here - k + depth, depth)
        for which, (colour, offsets) in enumerate(plan):
            for m, offset in enumerate(offsets):
                at_row = pl.multiple_of(place * rows + colour * half, half)
                at_col = pl.multiple_of((rank ^ offset) * cols, cols)
                copy = pltpu.make_async_copy(
                    sources[which].at[m, k],
                    held.at[pl.ds(at_row, half), pl.ds(at_col, cols)],
                    in_sems.at[number],
                )
                copy.start()
                waits[k].append(copy)
                number += 1
    outs = []
    main = targets[0].shape[1]
    for k in range(depth):
        place = lax.rem(here - k + depth, depth)
        for copy in waits[k]:
            copy.wait()
        base = pl.multiple_of(place * rows, rows)
        band = pl.ds(base, rows)
        out = pltpu.make_async_copy(held.at[band, pl.ds(0, main)], targets[0].at[band], out_sems.at[3 * k])
        out.start()
        outs.append(out)
        if tail_rows:
            wide = targets[1].shape[1] // 2
            for side in range(2):
                out = pltpu.make_async_copy(
                    held.at[pl.ds(base + side * tail_rows, tail_rows), pl.ds(main, wide)],
                    targets[1].at[
                        pl.ds(pl.multiple_of(place * tail_rows, tail_rows), tail_rows),
                        pl.ds(side * wide, wide),
                    ],
                    out_sems.at[3 * k + 1 + side],
                )
                out.start()
                outs.append(out)
    for out in outs:
        out.wait()


def halves(ranks, bit, held):
    flip = 1 << bit
    kept = [o for o in held if not o & flip]
    return kept, [o ^ flip for o in kept]


def relative_blocks(grads, rank, orders):
    depth, ranks = lax.axis_size("fsdp") // 2, lax.axis_size("rep")
    width = grads.shape[1] // ranks
    rows = grads.shape[0] // depth
    shaped = grads.reshape(depth, rows, grads.shape[1])
    share = rows // len(orders)
    first = []
    for n, order in enumerate(orders):
        block = lambda o: lax.dynamic_slice(
            shaped, (0, n * share, (rank ^ o) * width), (depth, share, width)
        )
        kept, given = halves(ranks, order[0], list(range(ranks)))
        first.append((jnp.stack([block(o) for o in kept]), jnp.stack([block(o) for o in given])))
    return first


class Reduce:
    def __init__(self, first, here, orders):
        self.here, self.orders, self.at = here, orders, 0
        ranks = lax.axis_size("rep")
        self.held = []
        for (keep, give), order in zip(first, orders):
            kept, given = halves(ranks, order[0], list(range(ranks)))
            self.held.append((kept, keep, give))

    def send(self, *values):
        values, gives = lax.optimization_barrier((values, [give for _, _, give in self.held]))
        self.received = [across_rep(g, order[self.at]) for g, order in zip(gives, self.orders)]
        self.at += 1
        return values[0] if len(values) == 1 else values

    def arrive(self, *values):
        values, received = lax.optimization_barrier((values, self.received))
        held = []
        for (kept, keep, _), got, order in zip(self.held, received, self.orders):
            total = (keep.astype(f32) + got.astype(f32)).astype(bf16)
            if self.at < len(order):
                stay, leave = halves(None, order[self.at], kept)
                take = lambda os: jnp.stack([total[kept.index(o)] for o in os])
                held.append((stay, take(stay), take(leave)))
            else:
                held.append((kept, total[0], None))
        self.held = held
        return values[0] if len(values) == 1 else values

    def send_z(self, *values, extra=None):
        depth = lax.axis_size("fsdp") // 2
        parts = [keep for _, keep, _ in self.held]
        whole = parts[0] if len(parts) == 1 else jnp.concatenate(parts, axis=1)
        if extra is not None:
            whole = jnp.concatenate([whole, extra], axis=1)
        pieces = [pick(whole, lax.rem(self.here + k, depth), 0) for k in range(depth)]
        values, pieces = lax.optimization_barrier((values, pieces))
        self.pieces = [pieces[0]] + [along_z(p, k) for k, p in enumerate(pieces) if k]
        return values[0] if len(values) == 1 else values

    def arrive_z(self, *values):
        values, pieces = lax.optimization_barrier((values, self.pieces))
        total = pieces[0].astype(f32)
        for piece in pieces[1:]:
            total = total + piece.astype(f32)
        self.total = total
        return values[0] if len(values) == 1 else values


class Spread:
    def __init__(self, value):
        bits = list(range(rep_bits()))
        self.orders = [bits, bits[::-1]]
        half = value.shape[0] // 2
        self.arrays = [value[:half][None], value[half:][None]]
        self.offsets = [[0], [0]]
        self.at = 0

    def send(self, *values):
        values, arrays = lax.optimization_barrier((values, self.arrays))
        self.arrays = []
        for n, (array, order) in enumerate(zip(arrays, self.orders)):
            flip = 1 << order[self.at]
            received = across_rep(array, order[self.at])
            self.arrays.append(jnp.concatenate([array, received]))
            self.offsets[n] = self.offsets[n] + [o ^ flip for o in self.offsets[n]]
        self.at += 1
        return values[0] if len(values) == 1 else values

    def blocks(self, rank, start, size):
        return jnp.concatenate(
            [rep_blocks(a[:, :, start : start + size], o, rank) for a, o in zip(self.arrays, self.offsets)]
        )


def rep_blocks(stacked, offsets, rank):
    blocks = []
    for i in range(len(offsets)):
        block = stacked[0]
        for entry, offset in enumerate(offsets):
            block = jnp.where((rank ^ offset) == i, stacked[entry], block)
        blocks.append(block)
    return jnp.concatenate(blocks, axis=1)


def share_kernel(widths, index_ref, qkv_ref, proj_ref, fc1_ref, keep_ref, give_ref, sems):
    rank, core = index_ref[0], index_ref[1]
    wide1, wide2, block, unit, half = widths
    is_proj = rank * wide1 >= 3 * half

    def copies(second):
        made = []
        for out, (ref, which) in enumerate(((keep_ref, core), (give_ref, 1 - core))):
            for c in range(wide1 // block):
                col = rank * wide1 + c * block
                if second:
                    source, at = proj_ref, which * half + col - 3 * half
                else:
                    source, at = qkv_ref, 2 * col + which * block
                made.append((source, at, block, ref, c * block))
        return made

    def run(plan, first):
        started = []
        for n, (source, at, size, ref, to) in enumerate(plan):
            copy = pltpu.make_async_copy(
                source.at[:, pl.ds(pl.multiple_of(at, LANES), size)], ref.at[:, pl.ds(to, size)], sems.at[first + n]
            )
            copy.start()
            started.append(copy)
        return started

    col = rank * wide2
    plan2 = []
    for ref, which in ((keep_ref, core), (give_ref, 1 - core)):
        at = col + (lax.div(col, unit) + which) * unit
        plan2.append((fc1_ref, at, wide2, ref, wide1))
    second = run(plan2, 0)

    @pl.when(is_proj)
    def _():
        for copy in run(copies(True), 2):
            copy.wait()

    @pl.when(jnp.logical_not(is_proj))
    def _():
        for copy in run(copies(False), 2):
            copy.wait()

    for copy in second:
        copy.wait()


def weight_share(rank, core, qkv_weight, proj_weight, fc1_weight, ranks, block, unit):
    rows = qkv_weight.shape[0]
    wide1, wide2 = 2 * D // ranks, fc1_weight.shape[1] // 2 // ranks
    out = jax.ShapeDtypeStruct((rows, wide1 + wide2), bf16)
    return pl.pallas_call(
        functools.partial(share_kernel, (wide1, wide2, block, unit, D // 2)),
        out_shape=[out, out],
        grid_spec=pltpu.PrefetchScalarGridSpec(
            num_scalar_prefetch=1,
            grid=(1,),
            in_specs=[pl.BlockSpec(memory_space=pl.ANY)] * 3,
            out_specs=[pl.BlockSpec(out.shape, lambda i, a: (0, 0))] * 2,
            scratch_shapes=[pltpu.SemaphoreType.DMA((2 + 2 * (wide1 // block),))],
        ),
        cost_estimate=SHORT,
        name="weight_share",
    )(jnp.stack([rank, core]).astype(jnp.int32), qkv_weight, proj_weight, fc1_weight)


def whole_specs(arrays):
    return [pl.BlockSpec(a.shape, lambda *_, n=len(a.shape): (0,) * n) for a in arrays]


def slot_lists(sizes):
    slots = []
    for number, size in enumerate(sizes):
        for start in range(0, size, LANES):
            slots.append((number, start, min(LANES, size - start)))
    return slots


def pack_kernel(slots, *refs):
    *sources, out_ref, held = refs
    per_row = held.shape[1] // LANES
    held[...] = jnp.zeros_like(held)
    for slot, (number, start, size) in enumerate(slots):
        row, at = slot // per_row, slot % per_row * LANES
        held[row : row + 1, at : at + size] = sources[number][:, start : start + size].astype(f32)
    out_ref[...] = held[...].astype(out_ref.dtype)


def pack_small(vectors, width, slots):
    shape = (32 * LANES // width, width)
    vectors = [v.reshape(1, -1) for v in vectors]
    return pl.pallas_call(
        functools.partial(pack_kernel, slots),
        out_shape=jax.ShapeDtypeStruct(shape, bf16),
        scratch_shapes=[pltpu.VMEM(shape, f32)],
        name="pack_small",
    )(*vectors)


def unpack_kernel(slots, depth, index_ref, *refs):
    pieces, (vec_ref, unit_ref, tag_ref) = refs[:depth], refs[depth:]
    here, core = index_ref[0], index_ref[1]
    rows, width = pieces[0].shape
    per_row = width // LANES
    single = sum(1 for number, _, _ in slots if number < 10)
    vec_ref[...] = jnp.zeros_like(vec_ref)
    for k in range(depth):
        place = lax.rem(here - k + depth, depth)
        values = pieces[k][...].astype(f32)

        def part(side, slot, size):
            row, at = side * (rows // 2) + slot // per_row, slot % per_row * LANES
            return values[row : row + 1, at : at + size]

        for slot, (number, start, size) in enumerate(slots):
            own, other = part(0, slot, size), part(1, slot, size)
            first = jnp.where(core == 0, own, other)
            second = jnp.where(core == 0, other, own)
            if number < 10:
                at = pl.multiple_of(place * 2 * size, 2 * size)
                vec_ref[number : number + 1, pl.ds(at, 2 * size)] = jnp.concatenate([first, second], axis=1)
            elif number == 10:
                wide = unit_ref.shape[1] // depth
                unit_ref[0:1, pl.ds(pl.multiple_of(place * wide + start, LANES), LANES)] = own
            else:
                wide = tag_ref.shape[1] // depth
                at = pl.multiple_of(place * wide + start, LANES)
                tag_ref[0:1, pl.ds(at, LANES)] = first
                tag_ref[0:1, pl.ds(pl.multiple_of(at + wide // 2, LANES), LANES)] = second


def unpack_small(pieces, slots, rows, here, core, units, group_tokens):
    depth = len(pieces)
    extra, width = pieces[0].shape[0] - rows, pieces[0].shape[1]
    shapes = [(16, D), (1, units), (1, group_tokens)]
    return pl.pallas_call(
        functools.partial(unpack_kernel, slots, depth),
        out_shape=[jax.ShapeDtypeStruct(s, f32) for s in shapes],
        grid_spec=pltpu.PrefetchScalarGridSpec(
            num_scalar_prefetch=1,
            grid=(1,),
            in_specs=[pl.BlockSpec((extra, width), lambda i, a: (rows // extra, 0))] * depth,
            out_specs=[pl.BlockSpec(s, lambda i, a: (0, 0)) for s in shapes],
        ),
        name="unpack_small",
    )(jnp.stack([here, core]).astype(jnp.int32), *pieces)


def pack_grads_kernel(depth, sizes, index_ref, *refs):
    *sources, out_ref = refs
    core = index_ref[0]
    out_ref[...] = jnp.zeros_like(out_ref)
    for z in range(depth):
        for c in range(2):
            row = 16 * c
            for source, (size, of_core) in zip(sources, sizes):
                for start in range(0, size, LANES):
                    lanes = min(LANES, size - start)
                    at = (z if of_core else 2 * z + c) * size + start
                    value = source[0:1, at : at + lanes]
                    if of_core:
                        value = jnp.where(core == c, value, 0.0)
                    out_ref[z, row : row + 1, 0:lanes] = value
                    row += 1


def pack_grads(vectors, sizes, core, depth):
    return pl.pallas_call(
        functools.partial(pack_grads_kernel, depth, sizes),
        out_shape=jax.ShapeDtypeStruct((depth, 32, LANES), f32),
        grid_spec=pltpu.PrefetchScalarGridSpec(
            num_scalar_prefetch=1,
            grid=(1,),
            in_specs=whole_specs(vectors),
            out_specs=pl.BlockSpec((depth, 32, LANES), lambda i, a: (0, 0, 0)),
        ),
        name="pack_grads",
    )(core.reshape(1).astype(jnp.int32), *vectors)


def grad_blocks_kernel(orders, ranks, index_ref, a_ref, b_ref, *refs):
    outs, held = refs[:-1], refs[-1]
    rank = index_ref[0]
    held[...] = dot_tn(a_ref[...], b_ref[...]).astype(bf16)
    width = held.shape[1] // ranks
    share = held.shape[0] // len(orders)
    for n, order in enumerate(orders):
        for which, offsets in enumerate(halves(ranks, order[0], list(range(ranks)))):
            for i, o in enumerate(offsets):
                cols = pl.ds(pl.multiple_of((rank ^ o) * width, width), width)
                outs[2 * n + which][i, 0] = held[n * share : (n + 1) * share, cols]


def grad_blocks(a, b, rank, orders, name):
    depth, ranks = lax.axis_size("fsdp") // 2, lax.axis_size("rep")
    tokens, rows, cols = a.shape[0], a.shape[1] // depth, b.shape[1]
    if cols // ranks % LANES:
        return relative_blocks(dot_tn(a, b).astype(bf16), rank, orders)
    block = (ranks // 2, depth, rows // len(orders), cols // ranks)
    outs = pl.pallas_call(
        functools.partial(grad_blocks_kernel, orders, ranks),
        out_shape=[jax.ShapeDtypeStruct(block, bf16)] * (2 * len(orders)),
        grid_spec=pltpu.PrefetchScalarGridSpec(
            num_scalar_prefetch=1,
            grid=(depth,),
            in_specs=[
                pl.BlockSpec((tokens, rows), lambda i, s: (0, i)),
                pl.BlockSpec((tokens, cols), lambda i, s: (0, 0)),
            ],
            out_specs=[pl.BlockSpec((block[0], 1) + block[2:], lambda i, s: (0, i, 0, 0))] * (2 * len(orders)),
            scratch_shapes=[pltpu.VMEM((rows, cols), bf16)],
        ),
        compiler_params=pltpu.CompilerParams(vmem_limit_bytes=40 << 20),
        cost_estimate=SHORT,
        name=name,
    )(rank.reshape(1).astype(jnp.int32), a, b)
    return [(outs[2 * n], outs[2 * n + 1]) for n in range(len(orders))]


def pre_grad_kernel(g_ref, w_ref, slope_ref, out_ref, sum_ref):
    grad = dot_nt(g_ref[...], w_ref[...]) * slope_ref[...].astype(f32)
    out_ref[...] = grad.astype(bf16)
    sum_ref[...] = jnp.sum(grad, axis=0, keepdims=True)


def pre_grads(mlp_grad, fc2_matrix, slope):
    tokens, units = slope.shape
    tile = 256
    return pl.pallas_call(
        pre_grad_kernel,
        out_shape=[jax.ShapeDtypeStruct((tokens, units), bf16), jax.ShapeDtypeStruct((1, units), f32)],
        grid=(units // tile,),
        in_specs=[
            pl.BlockSpec((tokens, D), lambda i: (0, 0)),
            pl.BlockSpec((tile, D), lambda i: (i, 0)),
            pl.BlockSpec((tokens, tile), lambda i: (0, i)),
        ],
        out_specs=[pl.BlockSpec((tokens, tile), lambda i: (0, i)), pl.BlockSpec((1, tile), lambda i: (0, i))],
        compiler_params=pltpu.CompilerParams(vmem_limit_bytes=40 << 20),
        cost_estimate=SHORT,
        name="pre_grad",
    )(mlp_grad, fc2_matrix, slope)


def product_kernel(half_ref, first_ref, second_ref, w_ref, out1_ref, out2_ref):
    out1_ref[...] = dot(first_ref[...], w_ref[...])
    out2_ref[...] = dot(second_ref[...], w_ref[...])


def product_nt_kernel(half_ref, first_ref, second_ref, w_ref, out1_ref, out2_ref, held):
    @pl.when(pl.program_id(0) == 0)
    def _():
        held[...] = w_ref[...].T

    out1_ref[...] = dot(first_ref[...], held[...])
    out2_ref[...] = dot(second_ref[...], held[...])


def product(a, weight, flipped, half, name, cost=SHORT):
    rows, tile = a.shape[0] // 2, 128
    count = rows // tile
    out = pl.BlockSpec((tile, D), lambda i, h: (i, 0))
    return pl.pallas_call(
        product_nt_kernel if flipped else product_kernel,
        out_shape=[jax.ShapeDtypeStruct((rows, D), f32)] * 2,
        grid_spec=pltpu.PrefetchScalarGridSpec(
            num_scalar_prefetch=1,
            grid=(count,),
            in_specs=[
                pl.BlockSpec((tile, a.shape[1]), lambda i, h: (i + h[0] * count, 0)),
                pl.BlockSpec((tile, a.shape[1]), lambda i, h: (i + (1 - h[0]) * count, 0)),
                pl.BlockSpec(weight.shape, lambda i, h: (0, 0)),
            ],
            out_specs=[out, out],
            scratch_shapes=[pltpu.VMEM(weight.shape[::-1], bf16)] if flipped else [],
        ),
        compiler_params=pltpu.CompilerParams(vmem_limit_bytes=32 << 20),
        cost_estimate=cost,
        name=name,
    )(jnp.asarray(half, jnp.int32).reshape(1), a, a, weight)


def add_sums(sum_ref, values):
    @pl.when(pl.program_id(0) == 0)
    def _():
        sum_ref[...] = jnp.zeros_like(sum_ref)

    for row, value in enumerate(values):
        sum_ref[row : row + 1, :] += jnp.sum(value, axis=0, keepdims=True)


def input_kernel(own_ref, sent_ref, tok_ref, grad_ref, vec_ref, out_ref, sum_ref):
    grad = own_ref[...] + sent_ref[...]
    normal, inverse = normalize(tok_ref[...].astype(f32))
    out_ref[...] = grad_ref[...] + norm_back(grad, normal, inverse, vec_ref[0:1, :])
    add_sums(sum_ref, (grad * normal, grad))


def output_kernel(own_ref, sent_ref, cot_ref, resid_ref, vec_ref, out_ref, sum_ref):
    mlp = own_ref[...] + sent_ref[...] + vec_ref[8:9, :]
    out_ref[...] = (resid_ref[...] + vec_ref[9:10, :] * mlp).astype(bf16)
    out_grad = cot_ref[...].astype(f32)
    add_sums(sum_ref, (out_grad * vec_ref[9:10, :], out_grad * mlp))


def finish(kernel, dtype, parts, vecs, name):
    rows, tile = parts[0].shape[0], 128
    part = pl.BlockSpec((tile, D), lambda i: (i, 0))
    return pl.pallas_call(
        kernel,
        out_shape=[jax.ShapeDtypeStruct((rows, D), dtype), jax.ShapeDtypeStruct((8, D), f32)],
        grid=(rows // tile,),
        in_specs=[part] * len(parts) + [pl.BlockSpec(vecs.shape, lambda i: (0, 0))],
        out_specs=[part, pl.BlockSpec((8, D), lambda i: (0, 0))],
        compiler_params=pltpu.CompilerParams(vmem_limit_bytes=24 << 20),
        cost_estimate=SHORT,
        name=name,
    )(*parts, vecs)


def residual_kernel(own_ref, sent_ref, tok_ref, vec_ref, attn_ref, resid_ref, input_ref):
    attn = own_ref[...] + sent_ref[...] + vec_ref[4:5, :]
    resid = tok_ref[...].astype(f32) + vec_ref[5:6, :] * attn
    attn_ref[...] = attn
    resid_ref[...] = resid
    normal, _ = normalize(resid)
    input_ref[...] = (normal * vec_ref[6:7, :] + vec_ref[7:8, :]).astype(bf16)


def residual(own, sent, tok, vecs):
    rows, tile = own.shape[0], 128
    part = pl.BlockSpec((tile, D), lambda i: (i, 0))
    return pl.pallas_call(
        residual_kernel,
        out_shape=[jax.ShapeDtypeStruct((rows, D), t) for t in (f32, f32, bf16)],
        grid=(rows // tile,),
        in_specs=[part] * 3 + [pl.BlockSpec(vecs.shape, lambda i: (0, 0))],
        out_specs=[part] * 3,
        compiler_params=pltpu.CompilerParams(vmem_limit_bytes=24 << 20),
        cost_estimate=SHORT,
        name="residual",
    )(own, sent, tok, vecs)


def scaled_kernel(own_ref, other_ref, vec_ref, out_ref):
    rows = own_ref.shape[0]
    for n, ref in enumerate((own_ref, other_ref)):
        out_ref[n * rows : (n + 1) * rows, :] = (ref[...].astype(f32) * vec_ref[9:10, :]).astype(bf16)


def scaled(own, other, vecs):
    return pl.pallas_call(
        scaled_kernel,
        out_shape=jax.ShapeDtypeStruct((2 * own.shape[0], D), bf16),
        compiler_params=pltpu.CompilerParams(vmem_limit_bytes=24 << 20),
        cost_estimate=SHORT,
        name="scaled",
    )(own, other, vecs)


def units_kernel(n_ref, w_ref, b_ref, act_ref, slope_ref):
    act, slope = gelu_pair(dot(n_ref[...], w_ref[...]) + b_ref[...])
    act_ref[...] = act.astype(bf16)
    slope_ref[...] = slope.astype(bf16)


def hidden_units(normed, weight, bias):
    tokens, units = normed.shape[0], weight.shape[1]
    tile = 256
    part = pl.BlockSpec((tokens, tile), lambda i: (0, i))
    return pl.pallas_call(
        units_kernel,
        out_shape=[jax.ShapeDtypeStruct((tokens, units), bf16)] * 2,
        grid=(units // tile,),
        in_specs=[
            pl.BlockSpec((tokens, D), lambda i: (0, 0)),
            pl.BlockSpec((D, tile), lambda i: (0, i)),
            pl.BlockSpec((1, tile), lambda i: (0, i)),
        ],
        out_specs=[part, part],
        compiler_params=pltpu.CompilerParams(vmem_limit_bytes=32 << 20),
        cost_estimate=SHORT,
        name="units",
    )(normed, weight, bias)


def norm_grad_kernel(own_ref, sent_ref, resid_ref, cot_ref, attn_ref, vec_ref, grad_ref, scaled_ref, sum_ref):
    grad = own_ref[...] + sent_ref[...]
    normal, inverse = normalize(resid_ref[...])
    resid_grad = cot_ref[...].astype(f32) + norm_back(grad, normal, inverse, vec_ref[6:7, :])
    scaled = resid_grad * vec_ref[5:6, :]
    grad_ref[...] = resid_grad
    scaled_ref[...] = scaled.astype(bf16)

    @pl.when(pl.program_id(0) == 0)
    def _():
        sum_ref[...] = jnp.zeros_like(sum_ref)

    for row, value in enumerate((grad * normal, grad, scaled, resid_grad * attn_ref[...])):
        sum_ref[row : row + 1, :] += jnp.sum(value, axis=0, keepdims=True)


def norm_grads(own, sent, resid, cot, attn_out, vecs):
    rows, tile = own.shape[0], 128
    part = pl.BlockSpec((tile, D), lambda i: (i, 0))
    return pl.pallas_call(
        norm_grad_kernel,
        out_shape=[
            jax.ShapeDtypeStruct((rows, D), f32), jax.ShapeDtypeStruct((rows, D), bf16),
            jax.ShapeDtypeStruct((8, D), f32),
        ],
        grid=(rows // tile,),
        in_specs=[part] * 5 + [pl.BlockSpec(vecs.shape, lambda i: (0, 0))],
        out_specs=[part, part, pl.BlockSpec((8, D), lambda i: (0, 0))],
        compiler_params=pltpu.CompilerParams(vmem_limit_bytes=24 << 20),
        cost_estimate=SHORT,
        name="norm_grad",
    )(own, sent, resid, cot, attn_out, vecs)


def proj_grad_kernel(head_rows, c_ref, g_ref, out_ref):
    wide = out_ref.shape[1]
    for side in range(2):
        grad = dot_tn(c_ref[...], g_ref[:, side * wide : (side + 1) * wide]).astype(bf16)
        for z in range(grad.shape[0] // head_rows):
            at = (2 * z + side) * head_rows
            out_ref[at : at + head_rows, :] = grad[z * head_rows : (z + 1) * head_rows]


def packed_proj_grad(context, attn_grad, head_rows):
    wide = D // 2
    return pl.pallas_call(
        functools.partial(proj_grad_kernel, head_rows),
        out_shape=jax.ShapeDtypeStruct((D, wide), bf16),
        compiler_params=pltpu.CompilerParams(vmem_limit_bytes=32 << 20),
        cost_estimate=SHORT,
        name="proj_grad",
    )(context, attn_grad)


def qkv_grad_kernel(orders, ranks, depth, per, index_ref, n_ref, *refs):
    grads, p_ref = refs[: 3 * per], refs[3 * per]
    outs, held = refs[3 * per + 1 : -1], refs[-1]
    rank = index_ref[0]
    normed = n_ref[...]
    for number in range(3):
        pieces = [g[...] for g in grads[number * per : (number + 1) * per]]
        wide = per * LANES
        joined = pieces[0] if per == 1 else jnp.concatenate(pieces, axis=1)
        held[:, number * wide : (number + 1) * wide] = dot_tn(normed, joined).astype(bf16)
    held[:, 3 * per * LANES :] = p_ref[...]
    width = held.shape[1] // ranks
    rows = held.shape[0] // depth
    share = rows // len(orders)
    for n, order in enumerate(orders):
        for which, offsets in enumerate(halves(ranks, order[0], list(range(ranks)))):
            for i, o in enumerate(offsets):
                cols = pl.ds(pl.multiple_of((rank ^ o) * width, width), width)
                for z in range(depth):
                    at = z * rows + n * share
                    outs[2 * n + which][i, z] = held[at : at + share, cols]


def qkv_grad_blocks(normed, grads, proj_packed, part, parts, rank, orders):
    depth, ranks = lax.axis_size("fsdp") // 2, lax.axis_size("rep")
    per = len(grads) // 3
    cols = 4 * per * LANES
    block = (ranks // 2, depth, D // depth // len(orders), cols // ranks)
    tokens = normed.shape[0] // 3
    outs = pl.pallas_call(
        functools.partial(qkv_grad_kernel, orders, ranks, depth, per),
        out_shape=[jax.ShapeDtypeStruct(block, bf16)] * (2 * len(orders)),
        grid_spec=pltpu.PrefetchScalarGridSpec(
            num_scalar_prefetch=1,
            grid=(1,),
            in_specs=[pl.BlockSpec((tokens, D), lambda i, a: (1, 0))]
            + whole_specs(grads)
            + [pl.BlockSpec((D, per * LANES), lambda i, a: (0, part))],
            out_specs=[pl.BlockSpec(block, lambda i, a: (0, 0, 0, 0))] * (2 * len(orders)),
            scratch_shapes=[pltpu.VMEM((D, cols), bf16)],
        ),
        compiler_params=pltpu.CompilerParams(vmem_limit_bytes=40 << 20),
        cost_estimate=SHORT,
        name="qkv_grad",
    )(rank.reshape(1).astype(jnp.int32), normed, *grads, proj_packed)
    return [(outs[2 * n], outs[2 * n + 1]) for n in range(len(orders))]


def spread_lanes(tags, width):
    return jnp.concatenate([tags] * (width // LANES), axis=1)


def project_kernel(need_ref, n_ref, w_ref, b_ref, q_ref, k_ref, v_ref):
    row = pl.program_id(0)
    wide = q_ref.shape[1]

    @pl.when(need_ref[row] > 0)
    def _():
        n = n_ref[...]
        for i, ref in enumerate((q_ref, k_ref, v_ref)):
            out = dot(n, w_ref[:, i * wide : (i + 1) * wide]) + b_ref[0:1, i * wide : (i + 1) * wide]
            if i == 0:
                out = out.astype(bf16).astype(f32) * HEAD_DIM ** (-0.5)
            ref[...] = out.astype(bf16)

    @pl.when(need_ref[row] == 0)
    def _():
        for ref in (q_ref, k_ref, v_ref):
            ref[...] = jnp.zeros_like(ref)


def project(need, normed, weight, bias, wide):
    rows = normed.shape[0]
    return pl.pallas_call(
        project_kernel,
        out_shape=[jax.ShapeDtypeStruct((rows, wide), bf16)] * 3,
        grid_spec=pltpu.PrefetchScalarGridSpec(
            num_scalar_prefetch=1,
            grid=(rows // BLOCK,),
            in_specs=[
                pl.BlockSpec((BLOCK, D), lambda i, s: (i, 0)),
                pl.BlockSpec(weight.shape, lambda i, s: (0, 0)),
                pl.BlockSpec((1, 3 * wide), lambda i, s: (0, 0)),
            ],
            out_specs=[pl.BlockSpec((BLOCK, wide), lambda i, s: (i, 0))] * 3,
        ),
        compiler_params=pltpu.CompilerParams(vmem_limit_bytes=32 << 20),
        cost_estimate=SHORT,
        name="project",
    )(need, normed, weight, bias)


def norm_kernel(need_ref, info_ref, *refs):
    *sources, vec_ref, out_ref = refs
    row = pl.program_id(0)
    side = (row // info_ref[1]) % 2
    chip = row // (2 * info_ref[1])

    @pl.when(need_ref[row] > 0)
    def _():
        picked = jnp.where(chip == 0, sources[0][...], jnp.where(chip == 1, sources[2][...], sources[4][...]))
        theirs = jnp.where(chip == 0, sources[1][...], jnp.where(chip == 1, sources[3][...], sources[5][...]))
        picked = jnp.where(side == info_ref[0], picked, theirs)
        normal, _ = normalize(picked.astype(f32))
        out_ref[...] = (normal * vec_ref[0:1, :] + vec_ref[1:2, :]).astype(bf16)

    @pl.when(need_ref[row] == 0)
    def _():
        out_ref[...] = jnp.zeros_like(out_ref)


def norm_window(need, info, sources, vecs, window, count):
    per = count // BLOCK

    def spec(chip):
        def index(i, a, b):
            inside = jnp.clip(i - 2 * per * chip, 0, 2 * per - 1)
            return (inside % per, 0)

        return pl.BlockSpec((BLOCK, D), index)

    return pl.pallas_call(
        norm_kernel,
        out_shape=jax.ShapeDtypeStruct((window, D), bf16),
        grid_spec=pltpu.PrefetchScalarGridSpec(
            num_scalar_prefetch=2,
            grid=(window // BLOCK,),
            in_specs=[spec(i // 2) for i in range(6)] + [pl.BlockSpec(vecs.shape, lambda i, a, b: (0, 0))],
            out_specs=pl.BlockSpec((BLOCK, D), lambda i, a, b: (i, 0)),
        ),
        compiler_params=pltpu.CompilerParams(vmem_limit_bytes=24 << 20),
        cost_estimate=SHORT,
        name="norm_window",
    )(need, info, *sources, vecs)


def attend_kernel(lo_ref, hi_ref, first_ref, last_ref, q_ref, k_ref, v_ref, qt_ref, kt_ref, o_ref, lse_ref, s_ref, m_ref, acc_ref):
    i = pl.program_id(0)
    left = lax.broadcasted_iota(jnp.int32, (1, LANES), 1) < HEAD_DIM
    lo, hi = lo_ref[i], hi_ref[i]
    base = (first_ref.shape[0] - pl.num_programs(0)) // 2
    q = q_ref[...]
    zero = jnp.zeros_like(q)
    heads = (jnp.where(left, q, zero), jnp.where(left, zero, q))
    m_ref[...] = jnp.full_like(m_ref, MASKED)
    one_image = first_ref[base + i] == last_ref[base + i]
    folds = BLOCK // LANES

    def fold(value, combine):
        parts = [value[:, n * LANES : (n + 1) * LANES] for n in range(folds)]
        return functools.reduce(combine, parts)

    def scores(j, carry):
        at = pl.multiple_of(j * BLOCK, BLOCK)
        k = k_ref[pl.ds(at, BLOCK), :]
        inside = one_image & (first_ref[j] == first_ref[base + i]) & (last_ref[j] == first_ref[base + i])

        @pl.when(inside)
        def _():
            for h in range(2):
                s = dot_nt(heads[h], k)
                s_ref[h, j] = s
                m_ref[h] = jnp.maximum(m_ref[h], fold(s, jnp.maximum))

        @pl.when(jnp.logical_not(inside))
        def _():
            same = spread_lanes(qt_ref[...], BLOCK) == kt_ref[:, pl.ds(at, BLOCK)]
            for h in range(2):
                s = jnp.where(same, dot_nt(heads[h], k), MASKED)
                s_ref[h, j] = s
                m_ref[h] = jnp.maximum(m_ref[h], fold(s, jnp.maximum))

        return carry

    lax.fori_loop(lo, hi, scores, 0)
    tops = [jnp.max(m_ref[h], axis=1, keepdims=True) for h in range(2)]
    m_ref[...] = jnp.zeros_like(m_ref)
    acc_ref[...] = jnp.zeros_like(acc_ref)

    def mix(j, carry):
        at = pl.multiple_of(j * BLOCK, BLOCK)
        v = v_ref[pl.ds(at, BLOCK), :]
        for h in range(2):
            e = jnp.exp(s_ref[h, j] - tops[h])
            m_ref[h] += fold(e, jnp.add)
            acc_ref[h] += dot(e.astype(bf16), v)
        return carry

    lax.fori_loop(lo, hi, mix, 0)
    sums = [jnp.sum(m_ref[h], axis=1, keepdims=True) for h in range(2)]
    o_ref[...] = jnp.where(left, acc_ref[0] / sums[0], acc_ref[1] / sums[1]).astype(bf16)
    for h in range(2):
        lse = jnp.broadcast_to(tops[h] + jnp.log(sums[h]), (BLOCK, LANES))
        lse_ref[0, h : h + 1, :] = lse.T[0:1, :]


def attend(lo, hi, firsts, lasts, q, k, v, tag_cols, tag_row, own_rows, pair):
    window = q.shape[0]
    blocks = own_rows // BLOCK
    skip = (window - own_rows) // 2 // BLOCK
    return pl.pallas_call(
        attend_kernel,
        out_shape=[
            jax.ShapeDtypeStruct((own_rows, LANES), bf16),
            jax.ShapeDtypeStruct((1, 2, own_rows), f32),
        ],
        grid_spec=pltpu.PrefetchScalarGridSpec(
            num_scalar_prefetch=4,
            grid=(blocks,),
            in_specs=[
                pl.BlockSpec((BLOCK, LANES), lambda i, *_: (i + skip, pair)),
                pl.BlockSpec((window, LANES), lambda i, *_: (0, pair)),
                pl.BlockSpec((window, LANES), lambda i, *_: (0, pair)),
                pl.BlockSpec((BLOCK, LANES), lambda i, *_: (i + skip, 0)),
                pl.BlockSpec((1, window), lambda i, *_: (0, 0)),
            ],
            out_specs=[
                pl.BlockSpec((BLOCK, LANES), lambda i, *_: (i, 0)),
                pl.BlockSpec((1, 2, BLOCK), lambda i, *_: (0, 0, i)),
            ],
            scratch_shapes=[
                pltpu.VMEM((2, window // BLOCK, BLOCK, BLOCK), f32),
                pltpu.VMEM((2, BLOCK, LANES), f32),
                pltpu.VMEM((2, BLOCK, LANES), f32),
            ],
        ),
        compiler_params=pltpu.CompilerParams(vmem_limit_bytes=32 << 20),
        cost_estimate=SHORT,
        name="attend",
    )(lo, hi, firsts, lasts, q, k, v, tag_cols, tag_row)


def attend_back_kernel(
    start, stop, lo_ref, hi_ref, q_ref, k_ref, v_ref, g_ref, tc_ref, tr_ref, lse_ref, delta_ref,
    dq_ref, dk_ref, dv_ref, sum_ref, dk_acc, dv_acc, dq_acc,
):
    first = lax.broadcasted_iota(jnp.int32, (1, LANES), 1) < HEAD_DIM
    dk_acc[...] = jnp.zeros_like(dk_acc)
    dv_acc[...] = jnp.zeros_like(dv_acc)
    sum_ref[...] = jnp.zeros_like(sum_ref)

    def split(value):
        zero = jnp.zeros_like(value)
        return jnp.where(first, value, zero), jnp.where(first, zero, value)

    def visit(i, j, qs, gs, of_key, of_query):
        at_q, at_k = pl.multiple_of(i * BLOCK, BLOCK), pl.multiple_of(j * BLOCK, BLOCK)
        k = k_ref[pl.ds(at_k, BLOCK), :]
        v = v_ref[pl.ds(at_k, BLOCK), :]
        same = spread_lanes(tc_ref[pl.ds(at_k, BLOCK), :], BLOCK) == tr_ref[:, pl.ds(at_q, BLOCK)]
        ps, ds = [], []
        for h in range(2):
            s = dot_nt(k, qs[h])
            dp = dot_nt(v, gs[h])
            p = jnp.where(same, jnp.exp(s - lse_ref[0, h : h + 1, pl.ds(at_q, BLOCK)]), 0.0)
            d = p * (dp - delta_ref[0, h : h + 1, pl.ds(at_q, BLOCK)])
            ps.append(p.astype(bf16))
            ds.append(d.astype(bf16))
        if of_key:
            at = pl.multiple_of((j - start) * BLOCK, BLOCK)
            dv_acc[pl.ds(at, BLOCK), :] += dot(ps[0], gs[0]) + dot(ps[1], gs[1])
            dk_acc[pl.ds(at, BLOCK), :] += dot(ds[0], qs[0]) + dot(ds[1], qs[1])
        if of_query:
            ks = split(k)
            dq_acc[...] += dot_tn(ds[0], ks[0]) + dot_tn(ds[1], ks[1])

    def query_block(own_q, i, carry):
        at_q = pl.multiple_of(i * BLOCK, BLOCK)
        qs = split(q_ref[pl.ds(at_q, BLOCK), :])
        gs = split(g_ref[pl.ds(at_q, BLOCK), :])
        lo, hi = lo_ref[i], hi_ref[i]

        def keys(first_key, last_key, of_key):
            def body(j, carry):
                visit(i, j, qs, gs, of_key, own_q)
                return carry

            lax.fori_loop(first_key, last_key, body, 0)

        if own_q:
            dq_acc[...] = jnp.zeros_like(dq_acc)
            keys(lo, jnp.minimum(hi, start), False)
            keys(jnp.maximum(lo, stop), hi, False)
        keys(jnp.maximum(lo, start), jnp.minimum(hi, stop), True)
        if own_q:
            at = pl.multiple_of((i - start) * BLOCK, BLOCK)
            dq = dq_acc[...] * HEAD_DIM ** (-0.5)
            dq_ref[pl.ds(at, BLOCK), :] = dq.astype(bf16)
            sum_ref[0, 0:1, :] += jnp.sum(dq, axis=0, keepdims=True)
        return carry

    before = jnp.where(lo_ref[start] < start, lo_ref[start], start)
    after = jnp.maximum(hi_ref[stop - 1], stop)
    lax.fori_loop(before, start, functools.partial(query_block, False), 0)
    lax.fori_loop(start, stop, functools.partial(query_block, True), 0)
    lax.fori_loop(stop, after, functools.partial(query_block, False), 0)
    dk_ref[...] = dk_acc[...].astype(bf16)
    dv_ref[...] = dv_acc[...].astype(bf16)
    sum_ref[0, 1:2, :] = jnp.sum(dv_acc[...], axis=0, keepdims=True)


def attend_back(lo, hi, q, k, v, g, tag_cols, tag_row, lse, delta, own_rows, pair):
    window = q.shape[0]
    pairs, wide = 1, LANES
    grad_pair = pair % (g.shape[1] // LANES)
    start = (window - own_rows) // 2 // BLOCK
    stop = start + own_rows // BLOCK
    whole = lambda: pl.BlockSpec((window, LANES), lambda p, a, b: (0, pair))
    own = lambda: pl.BlockSpec((own_rows, LANES), lambda p, a, b: (0, p))
    stat = lambda: pl.BlockSpec((1, 2, window), lambda p, a, b: (pair, 0, 0))
    return pl.pallas_call(
        functools.partial(attend_back_kernel, start, stop),
        out_shape=[jax.ShapeDtypeStruct((own_rows, wide), bf16)] * 3
        + [jax.ShapeDtypeStruct((pairs, 8, LANES), f32)],
        grid_spec=pltpu.PrefetchScalarGridSpec(
            num_scalar_prefetch=2,
            grid=(pairs,),
            in_specs=[
                whole(), whole(), whole(),
                pl.BlockSpec((window, LANES), lambda p, a, b: (0, grad_pair)),
                pl.BlockSpec((window, LANES), lambda p, a, b: (0, 0)),
                pl.BlockSpec((1, window), lambda p, a, b: (0, 0)),
                stat(), stat(),
            ],
            out_specs=[own(), own(), own(), pl.BlockSpec((1, 8, LANES), lambda p, a, b: (p, 0, 0))],
            scratch_shapes=[
                pltpu.VMEM((own_rows, LANES), f32),
                pltpu.VMEM((own_rows, LANES), f32),
                pltpu.VMEM((BLOCK, LANES), f32),
            ],
        ),
        compiler_params=pltpu.CompilerParams(vmem_limit_bytes=40 << 20),
        cost_estimate=SHORT,
        name="attend_back",
    )(lo, hi, q, k, v, g, tag_cols, tag_row, lse, delta)


def on_device(
    tokens, image_ids, ln1_gain, ln1_bias, qkv_weight, query_bias, value_bias, proj_weight,
    proj_bias, scale_attn, ln2_gain, ln2_bias, fc1_weight, fc1_bias, fc2_weight, fc2_bias,
    scale_mlp, cotangent,
):
    devices = lax.axis_size("fsdp")
    depth, ranks = devices // 2, lax.axis_size("rep")
    place = lax.axis_index("fsdp")
    rank = lax.axis_index("rep")
    here, core = place // 2, place % 2
    count = tokens.shape[1]
    chip = 2 * count
    head_rows = D // devices
    ff = fc1_weight.shape[1]
    unit_rows = ff // devices
    half_heads = D // 2
    local_heads = half_heads // HEAD_DIM
    pairs = half_heads // LANES
    bits = list(range(rep_bits()))

    def in_order(own, other, axis=0):
        return jnp.where(
            core == 0,
            jnp.concatenate([own, other], axis=axis),
            jnp.concatenate([other, own], axis=axis),
        )

    def mine(value):
        return lax.dynamic_slice_in_dim(value, core * count, count, 0)

    def others(value):
        return lax.dynamic_slice_in_dim(value, (1 - core) * count, count, 0)

    def every_other(value, width, start):
        cuts = range(start * width, value.shape[1], 2 * width)
        return jnp.concatenate([value[:, c : c + width] for c in cuts], axis=1)

    def all_share(which):
        pick_cols = lambda v, w: jnp.where(which == 0, every_other(v, w, 0), every_other(v, w, 1))
        heads = lax.dynamic_slice_in_dim(
            jnp.concatenate(
                [
                    pick_cols(qkv_weight, head_rows),
                    lax.dynamic_slice_in_dim(proj_weight, which * half_heads, half_heads, 1),
                ],
                axis=1,
            ),
            rank * (2 * D // ranks), 2 * D // ranks, 1,
        )
        units = lax.dynamic_slice_in_dim(
            pick_cols(fc1_weight, unit_rows), rank * (ff // 2 // ranks), ff // 2 // ranks, 1
        )
        return jnp.concatenate([heads, units], axis=1)

    if head_rows % LANES:
        kept, given = all_share(core), all_share(1 - core)
    else:
        kept, given = weight_share(
            rank, core, qkv_weight, proj_weight, fc1_weight, ranks, head_rows, unit_rows
        )
    wide1 = 2 * D // ranks
    got = swap_cores(given)
    is_proj = rank * wide1 >= 3 * half_heads
    own1 = in_order(kept[:, :wide1], jnp.where(is_proj, given[:, :wide1], got[:, :wide1]))
    own2 = in_order(kept[:, wide1:], got[:, wide1:])
    own3 = lax.dynamic_slice_in_dim(fc2_weight, rank * (D // ranks), D // ranks, 1)
    small = (
        ln1_gain, ln1_bias, query_bias, value_bias, proj_bias, scale_attn, ln2_gain, ln2_bias,
        fc2_bias, scale_mlp, fc1_bias, (image_ids[0] + 1).astype(bf16),
    )
    sizes = [v.shape[0] for v in small]
    slots = slot_lists(sizes)
    width = 2 * D // ranks
    small = pack_small(small, width, slots)
    small_other = swap_cores(small)
    rows1, rows3 = own1.shape[0], own3.shape[0]
    tok, cot = tokens[0], cotangent[0]
    tok_other = swap_cores(tok)
    cot_other = swap_cores(cot)
    own1 = jnp.concatenate([own1, small, small_other])
    own1, own2, own3, tok = tie(own1, own2, own3, tok)
    pieces1 = fetch_z(own1)
    tok, pieces1[1] = tie(tok, pieces1[1])
    behind, ahead = from_chip(tok, 1), from_chip(tok, -1)
    gather1 = Gather(pieces1, rows1, "gather1")
    gather1.send()
    behind_other, ahead_other = swap_cores(behind), swap_cores(ahead)
    for _ in bits[1:]:
        gather1.send()

    vec_rows, fc1_shift, all_tags = unpack_small(
        pieces1, slots, rows1, here, core, ff // 2, devices * count
    )
    vector = lambda i: vec_rows[i : i + 1]
    (
        attn_gain, attn_shift, query_shift, value_shift, proj_shift, attn_scale, mlp_gain,
        mlp_shift, fc2_shift, mlp_scale,
    ) = map(vector, range(10))
    core_part = lambda vec: jnp.where(
        core == 0, every_other(vec, head_rows, 0), every_other(vec, head_rows, 1)
    )

    window = 3 * chip
    padded = jnp.concatenate(
        [jnp.zeros((1, chip), f32), all_tags, jnp.full((1, chip), 1e6, f32)], axis=1
    )
    tag_row = lax.dynamic_slice(padded, (0, here * chip), (1, window))
    tags = tag_row.reshape(window)
    firsts, lasts = tags[::BLOCK], tags[BLOCK - 1 :: BLOCK]
    real = firsts * (1e6 - firsts) > 0
    below = jnp.sum((tag_row < firsts[:, None]).astype(jnp.int32), axis=1)
    upto = jnp.sum((tag_row <= lasts[:, None]).astype(jnp.int32), axis=1)
    blocks = window // BLOCK
    block_lo = jnp.where(real, below // BLOCK, 0)
    block_hi = jnp.where(real, (upto + BLOCK - 1) // BLOCK, 0)
    own_lo, own_hi = chip // BLOCK, 2 * chip // BLOCK
    numbers = jnp.arange(blocks)
    need = jnp.logical_and(numbers >= block_lo[own_lo], numbers < block_hi[own_hi - 1]).astype(jnp.int32)
    firsts, lasts = firsts.astype(jnp.int32), lasts.astype(jnp.int32)
    tag_cols = jnp.broadcast_to(tags[:, None], (window, LANES))

    info = jnp.stack([core, jnp.int32(count // BLOCK)]).astype(jnp.int32)
    normed1 = norm_window(
        need, info, (behind, behind_other, tok, tok_other, ahead, ahead_other), vec_rows, window, count
    )

    normed1, own2 = tie(normed1, own2)
    pieces2 = fetch_z(own2)
    normed1 = gather1.arrive(normed1)
    qkv_matrix, proj_matrix = gather1.assemble(here, rank, head_rows)

    shifts = jnp.concatenate(
        [core_part(query_shift), jnp.zeros((1, half_heads), f32), core_part(value_shift)], axis=1
    )
    queries, keys, values = project(need, normed1, qkv_matrix, shifts, half_heads)

    contexts, lses = [], []
    los = block_lo[own_lo:own_hi]
    los, queries = tie(los, queries)
    for pair in range(pairs):
        if pair == 1:
            los, own3, *pieces2 = tie(los, own3, *pieces2)
            gather2 = Gather(pieces2, rows1, "gather2")
            los = gather2.send(los)
            pieces3 = fetch_z(own3)
        if pair == 2:
            los = gather2.arrive(los)
            los = gather2.send(los)
        if pair == 3:
            los = gather2.arrive(los)
            for _ in bits[2:]:
                los = gather2.arrive(gather2.send(los))
            los, *pieces3 = tie(los, *pieces3)
            gather3 = Gather(pieces3, rows3, "gather3")
            los = gather3.send(los)
        context, lse = attend(
            los, block_hi[own_lo:own_hi], firsts, lasts, queries, keys, values, tag_cols,
            tag_row, chip, pair,
        )
        los, context = tie(los, context)
        contexts.append(context)
        lses.append(lse)
    context = jnp.concatenate(contexts, axis=1)
    lse_rows = jnp.concatenate(lses).reshape(local_heads, chip)
    context = gather3.arrive(context)
    context = gather3.send(context)
    own, given = product(context, proj_matrix, False, core, "attn_out")
    attn_out, resid, mlp_input = residual(own, swap_cores(given), tok, vec_rows)
    mlp_input = jnp.concatenate([mlp_input, swap_cores(mlp_input)])
    fc1_matrix = gather2.assemble(here, rank)
    activated, slope = hidden_units(mlp_input, fc1_matrix, fc1_shift)
    mlp_grad = scaled(cot, cot_other, vec_rows)
    both = [bits, bits[::-1]]
    for _ in bits[2:]:
        activated = gather3.send(gather3.arrive(activated))
    fc2_blocks = gather3.arrive(grad_blocks(activated, mlp_grad, rank, both, "fc2_grad"))
    reduce3 = Reduce(fc2_blocks, here, both)
    mlp_grad = reduce3.send(mlp_grad)
    fc2_matrix = gather3.assemble(here, rank)
    pre_grad, fc1_bias_part = pre_grads(mlp_grad, fc2_matrix, slope)
    reduce2 = Reduce(grad_blocks(mlp_input, pre_grad, rank, both, "fc1_grad"), here, both)
    pre_grad, _ = tie(pre_grad, [give for _, _, give in reduce2.held])
    own, given = product(pre_grad, fc1_matrix, True, 0, "mlp_in_grad")
    own, given = reduce3.arrive(own, given)
    for _ in bits[2:]:
        own, given = reduce3.arrive(*reduce3.send(own, given))
    own, given = reduce3.send(own, given)
    sent = swap_cores(given)
    resid_grad, attn_grad, norm_sums = norm_grads(own, sent, resid, cot, attn_out, vec_rows)
    both_grads = jnp.zeros((chip, D), bf16)
    for part, which in ((attn_grad, core), (swap_cores(attn_grad), 1 - core)):
        both_grads = lax.dynamic_update_slice_in_dim(both_grads, part, which * count, 0)
    attn_grad = both_grads
    context_grad = dot_nt(attn_grad, proj_matrix).astype(bf16)
    head_of = (
        lax.broadcasted_iota(jnp.int32, (local_heads, half_heads), 1) // HEAD_DIM
        == lax.broadcasted_iota(jnp.int32, (local_heads, half_heads), 0)
    ).astype(f32)
    row_delta = lax.dot_general(
        head_of, context_grad.astype(f32) * context.astype(f32), (((1,), (1,)), ((), ())),
        precision=lax.Precision.HIGHEST, preferred_element_type=f32,
    )
    stats = jnp.concatenate([lse_rows, row_delta])
    context_grad, activated, attn_grad = tie(context_grad, activated, attn_grad)
    chunk = half_heads // 2
    chunks = [context_grad[:, :chunk], context_grad[:, chunk:]]
    grads_behind, grads_ahead = zip(*[(from_chip(c, 1), from_chip(c, -1)) for c in chunks])
    stats_behind, stats_ahead = from_chip(stats, 1), from_chip(stats, -1)
    proj_grad = packed_proj_grad(context, attn_grad, head_rows)
    stat_window = jnp.concatenate([stats_behind, stats, stats_ahead], axis=1)
    by_pair = lambda s: s.reshape(pairs, 2, window)
    lse_window, delta_window = by_pair(stat_window[:local_heads]), by_pair(stat_window[local_heads:])

    half_pairs = pairs // 2
    half_width = half_heads // 2

    def first_group(parts, number):
        grads = [g for kind in zip(*parts) for g in kind]
        return Reduce(
            qkv_grad_blocks(normed1, grads, proj_grad, number, 2, rank, both), here, both
        )

    parts, sums = [], []
    out_own, out_given = product(activated, fc2_matrix, False, 0, "mlp_out", FILLER)
    output_rows, out_sums = finish(
        output_kernel, bf16, (out_own, swap_cores(out_given), cot, resid), vec_rows, "output"
    )
    first, delta_window, lo, out_sums = settle(
        ((grads_behind[0], grads_ahead[0]), delta_window, block_lo, out_sums), (reduce3, "received")
    )
    grad_windows = [jnp.concatenate([first[0], chunks[0], first[1]])]
    for pair in range(pairs):
        if pair == 0:
            lo = reduce3.arrive(lo)
            lo = reduce2.send(lo)
        if pair == 1:
            lo, second = settle((lo, (grads_behind[1], grads_ahead[1])), (reduce2, "received"))
            grad_windows.append(jnp.concatenate([second[0], chunks[1], second[1]]))
            lo = reduce2.arrive(lo)
            lo = reduce3.send_z(lo)
            for _ in bits[2:]:
                lo = reduce2.arrive(reduce2.send(lo))
            lo = reduce2.send(lo)
        if pair == 2:
            lo = settle(lo, (reduce2, "received"), (reduce3, "pieces"))
            lo = reduce2.arrive(lo)
            lo = reduce2.send_z(lo)
            reduce1a = first_group(parts, 0)
            lo = reduce1a.send(lo)
        if pair == 3:
            lo = settle(lo, (reduce2, "pieces"), (reduce1a, "received"))
            lo = reduce3.arrive_z(lo)
            lo = reduce2.arrive_z(lo)
            fc2_part = reduce3.total.astype(bf16)
            fc1_part = reduce2.total.astype(bf16)
            split = fc2_part.shape[0] // fc1_part.shape[0]
            mlp_spread = Spread(jnp.concatenate([fc1_part, *jnp.split(fc2_part, split)], axis=1))
            lo = mlp_spread.send(lo)
            lo = reduce1a.arrive(lo)
            for _ in bits[2:]:
                lo = reduce1a.arrive(reduce1a.send(lo))
            lo = reduce1a.send(lo)
        *grads, total = attend_back(
            lo, block_hi, queries, keys, values, grad_windows[pair * 2 // pairs], tag_cols, tag_row, lse_window,
            delta_window, chip, pair,
        )
        lo, *grads = tie(lo, *grads)
        parts.append(grads)
        sums.append(total[0])

    parts[-1] = settle(parts[-1], (mlp_spread, "arrays"))
    parts[-1] = reduce1a.arrive(parts[-1])
    parts[-1] = reduce1a.send_z(parts[-1])
    reduce1b = first_group(parts[half_pairs:], 1)
    parts[-1] = reduce1b.send(parts[-1])
    every = [jnp.concatenate(p, axis=1) for p in zip(*parts)]

    factor = 1.0 / math.sqrt(count * devices * ranks)
    in_own, in_given = product(
        jnp.concatenate(every, axis=1), qkv_matrix, True, core, "attn_in_grad"
    )
    tail = (in_own, in_given)
    tail = settle(tail, (reduce1b, "received"), (reduce1a, "pieces"))
    for _ in bits[1:]:
        tail = reduce1b.arrive(tail)
        tail = reduce1b.send(tail)
    in_own, in_given = tail
    input_rows, in_sums = finish(
        input_kernel, f32, (in_own, swap_cores(in_given), tok, resid_grad), vec_rows, "input_grad"
    )

    vectors = (
        in_sums[0:1], in_sums[1:2],
        jnp.concatenate([s[0:1] for s in sums], axis=1), jnp.concatenate([s[1:2] for s in sums], axis=1),
        norm_sums[2:3], norm_sums[3:4], norm_sums[0:1], norm_sums[1:2],
        out_sums[0:1], out_sums[1:2], fc1_bias_part,
    )
    of_core = [number in (2, 3, 10) for number in range(11)]
    partial = pack_grads(vectors, list(zip(sizes, of_core)), core, depth)
    vec_width = D // ranks
    half_of = lambda which: lax.dynamic_slice_in_dim(partial, which * 16, 16, 1)
    partial = half_of(core) + swap_cores(half_of(1 - core))
    vec_high = lax.reduce_precision(partial, 8, 7)
    side_by_side = 2 if vec_width >= 2 * LANES else 1
    extra = jnp.concatenate([vec_high, partial - vec_high], axis=side_by_side).astype(bf16)
    extra = jnp.pad(extra, ((0, 0), (0, 0), (0, vec_width - extra.shape[2])))
    extra = reduce1b.arrive(extra)
    extra = reduce1b.send_z(extra, extra=extra)
    for _ in bits[1:]:
        mlp_spread.send(extra)

    reduce1a.arrive_z()
    reduce1b.arrive_z()
    rows = reduce1a.total.shape[0]
    vec_total = reduce1b.total[rows:]
    if side_by_side == 2:
        vec_total = vec_total[:, :LANES] + vec_total[:, LANES : 2 * LANES]
    else:
        vec_total = vec_total[:16] + vec_total[16:]
    vec_high = lax.reduce_precision(vec_total, 8, 7)
    sides = [jnp.pad(v, ((0, 16), (0, vec_width - LANES))) for v in (vec_high, vec_total - vec_high)]
    payload = jnp.concatenate(
        [
            jnp.concatenate([reduce1a.total, reduce1b.total[:rows]], axis=1),
            jnp.concatenate(sides, axis=1),
        ]
    ).astype(bf16)
    payload = settle(payload, (mlp_spread, "arrays"))
    first_spread = Spread(payload)
    for bit in bits:
        first_spread.send()

    mlp_cols = fc1_part.shape[1]
    fc1_full = mlp_spread.blocks(rank, 0, mlp_cols)
    fc2_width = fc2_part.shape[1]
    fc2_full = tie(*[mlp_spread.blocks(rank, mlp_cols + n * fc2_width, fc2_width) for n in range(split)])
    grad_fc2 = jnp.concatenate(fc2_full).astype(f32) * factor
    first_a = first_spread.blocks(rank, 0, vec_width)
    first_b = first_spread.blocks(rank, vec_width, vec_width)
    totals = sum(
        part[rows : rows + 16, r * vec_width : r * vec_width + LANES].astype(f32)
        for part in (first_a, first_b)
        for r in range(ranks)
    ) * factor
    first_a, first_b = first_a[:rows], first_b[:rows]

    def rows_of(value, index):
        return lax.dynamic_slice_in_dim(value, index * head_rows, head_rows, 0)

    def interleave(own, other, width):
        cuts = range(0, own.shape[1], width)
        zipped = lambda a, b: jnp.concatenate(
            [v[:, c : c + width] for c in cuts for v in (a, b)], axis=1
        )
        return jnp.where(core == 0, zipped(own, other), zipped(other, own)).astype(f32) * factor

    fc1_other = swap_cores(rows_of(fc1_full, 1 - core))
    grad_fc1 = interleave(rows_of(fc1_full, core), fc1_other, unit_rows)
    qkv_full = jnp.concatenate(
        [
            part[:, n * half_width : (n + 1) * half_width]
            for n in range(3)
            for part in (first_a, first_b)
        ],
        axis=1,
    )
    grad_qkv = interleave(rows_of(qkv_full, core), swap_cores(rows_of(qkv_full, 1 - core)), head_rows)
    proj_part = jnp.concatenate([first_a[:, 3 * half_width :], first_b[:, 3 * half_width :]], axis=1)
    grad_proj = jnp.concatenate([proj_part[:head_rows], proj_part[head_rows:]], axis=1).astype(f32) * factor

    small_grads = [totals[i, : sizes[i]] for i in range(10)]
    lines = -(-sizes[10] // LANES)
    small_grads.append(totals[10 : 10 + lines].reshape(-1))
    (
        grad_attn_gain, grad_attn_shift, grad_query_shift, grad_value_shift, grad_proj_shift,
        grad_attn_scale, grad_mlp_gain, grad_mlp_shift, grad_fc2_shift, grad_mlp_scale, grad_fc1_shift,
    ) = small_grads

    return (
        output_rows[None],
        input_rows[None],
        grad_attn_gain,
        grad_attn_shift,
        grad_qkv,
        grad_query_shift,
        grad_value_shift,
        grad_proj,
        grad_proj_shift,
        grad_attn_scale,
        grad_mlp_gain,
        grad_mlp_shift,
        grad_fc1,
        grad_fc1_shift,
        grad_fc2,
        grad_fc2_shift,
        grad_mlp_scale,
    )


def solution(mesh):
    rows = P("fsdp", None)
    vec = P("fsdp")
    tok = P("rep", "fsdp", None)
    return jax.shard_map(
        on_device,
        mesh=mesh,
        in_specs=(
            tok, P("rep", "fsdp"), vec, vec, rows, vec, vec, rows, vec, vec, vec, vec, rows, vec,
            rows, vec, vec, tok,
        ),
        out_specs=(
            tok, tok, vec, vec, rows, vec, vec, rows, vec, vec, vec, vec, rows, vec, rows, vec, vec,
        ),
        check_vma=False,
    )
```
